32 devices in a mesh: seq: 16 (over z, y, core), fsdp: 2 (over x).
Axes of the slice: x: 2, y: 2, z: 4, core: 2. Of those that a mesh axis runs over, the one named last changes fastest.
Arguments:
- first_half: float32 [2, 2048, 1024], P('fsdp', 'seq'), may hold values from -6 to 6
- second_half: float32 [2, 2048, 1024], P('fsdp', 'seq'), may hold values from -6 to 6
- first_cotangent: float32 [2, 2048, 1024], P('fsdp', 'seq'), may hold values from -6 to 6
- second_cotangent: float32 [2, 2048, 1024], P('fsdp', 'seq'), may hold values from -6 to 6
- bucket_ids: int32 [2, 4, 2048], P('fsdp', None, 'seq'), may hold values from 0 to 31, as said below
- slot_source: int32 [2, 4, 4096], P('fsdp', None, 'seq'), may hold values from 0 to 255, as said below
- live_slots: int32 [2, 4, 4096], P('fsdp', None, 'seq'), may hold values from 0 to 1, as said below
- mixer_gain: bfloat16 [1024], P(('seq', 'fsdp')), may hold values from 0.5 to 1.5
- mixer_shift: bfloat16 [1024], P(('seq', 'fsdp')), may hold values from -1.5 to 1.5
- query_weight: bfloat16 [1024, 1024], P(('seq', 'fsdp')), may hold values from -0.375 to 0.375
- value_weight: bfloat16 [1024, 1024], P(('seq', 'fsdp')), may hold values from -0.1875 to 0.1875
- output_weight: bfloat16 [1024, 1024], P(('seq', 'fsdp')), may hold values from -0.75 to 0.75
- feed_gain: bfloat16 [1024], P(('seq', 'fsdp')), may hold values from 0.5 to 1.5
- feed_shift: bfloat16 [1024], P(('seq', 'fsdp')), may hold values from -1.5 to 1.5
- expand_weight: bfloat16 [1024, 4096], P(('seq', 'fsdp')), may hold values from -0.1875 to 0.1875
- expand_bias: bfloat16 [4096], P(('seq', 'fsdp')), may hold values from -2.5 to 2.5
- contract_weight: bfloat16 [4096, 1024], P(('seq', 'fsdp')), may hold values from -0.09375 to 0.09375
- contract_bias: bfloat16 [1024], P(('seq', 'fsdp')), may hold values from -1.5 to 1.5
Outputs:
- first_out: float32 [2, 2048, 1024], P('fsdp', 'seq')
- second_out: float32 [2, 2048, 1024], P('fsdp', 'seq')
- first_grad: float32 [2, 2048, 1024], P('fsdp', 'seq')
- second_grad: float32 [2, 2048, 1024], P('fsdp', 'seq')
- mixer_gain_grad: float32 [1024], P(('seq', 'fsdp'))
- mixer_shift_grad: float32 [1024], P(('seq', 'fsdp'))
- query_weight_grad: float32 [1024, 1024], P(('seq', 'fsdp'))
- value_weight_grad: float32 [1024, 1024], P(('seq', 'fsdp'))
- output_weight_grad: float32 [1024, 1024], P(('seq', 'fsdp'))
- feed_gain_grad: float32 [1024], P(('seq', 'fsdp'))
- feed_shift_grad: float32 [1024], P(('seq', 'fsdp'))
- expand_weight_grad: float32 [1024, 4096], P(('seq', 'fsdp'))
- expand_bias_grad: float32 [4096], P(('seq', 'fsdp'))
- contract_weight_grad: float32 [4096, 1024], P(('seq', 'fsdp'))
- contract_bias_grad: float32 [1024], P(('seq', 'fsdp'))
The draws below stay inside these ranges and needn't reach their ends.
Inputs may be any that keep to these rules, and one draw needn't show every extreme that they name: `bucket_ids`: bucket // 2 is the bucket's group. In every round the 128 positions of one block send at most 16 tokens to one group, and in every sequence and round one group receives exactly 16 from every block. `slot_source`: each group's 256 entries are a permutation of its buffer rows: rows of tokens first, ordered by bucket and then position, empty rows after. `live_slots`: 1 exactly on a group's first slots, as many as tokens fall into the group; one group a round is full.
All inputs are finite; a program needn't handle non-finite values.
Results may differ from the reference program's by a relative error of at most 0.018.
Values may be sent and summed in bfloat16 or wider, within the bound.
A program may use at most 192 MiB of HBM per device.

```python
import jax
import jax.numpy as jnp
from jax import lax

D = 1024
FF = 4096
HEADS = 8
HEAD_DIM = 128
ROUNDS = 4
SPAN = 64
TOK_DEV = 128
SEQS = 2
LENGTH = 2048
GROUPS = 16
CAP = 16
SLOTS = 256
BUCKETS_GROUP = 2


def one_table(key):
    parts_key = jax.random.split(key, 5)
    hottest = jax.random.randint(parts_key[0], (), 0, GROUPS).astype(jnp.int32)

    def block_targets(block_key):
        pick_key, shuffle_key = jax.random.split(block_key)
        others = jnp.arange((GROUPS - 1) * CAP, dtype=jnp.int32) // CAP
        others = others + (others >= hottest).astype(jnp.int32)
        chosen = jax.random.permutation(pick_key, others)[:TOK_DEV - CAP]
        listed = jnp.concatenate([jnp.full((CAP,), hottest, jnp.int32), chosen])
        return jax.random.permutation(shuffle_key, listed)
    targets = jax.vmap(block_targets)(jax.random.split(parts_key[1], GROUPS)).reshape(LENGTH).astype(jnp.int32)
    bucket_order = jax.random.permutation(parts_key[2], BUCKETS_GROUP).astype(jnp.int32)
    first_pick = jax.random.randint(parts_key[3], (LENGTH,), 0, BUCKETS_GROUP)
    second_pick = jax.random.randint(parts_key[4], (LENGTH,), 0, BUCKETS_GROUP)
    local_bucket = bucket_order[jnp.minimum(first_pick, second_pick)]
    buckets = targets * BUCKETS_GROUP + local_bucket
    choose = (targets.reshape(GROUPS, TOK_DEV)[:, :, None] == jnp.arange(GROUPS, dtype=jnp.int32)[None, None, :]).astype(jnp.int32)
    ranked = jnp.sum(choose * (jnp.cumsum(choose, axis=1).astype(jnp.int32) - 1), axis=2).astype(jnp.int32).reshape(LENGTH)
    places = jnp.arange(LENGTH, dtype=jnp.int32)
    buffer_row = places // TOK_DEV * CAP + ranked
    empty_key = BUCKETS_GROUP * LENGTH
    sort_keys = empty_key + jnp.zeros((GROUPS, SLOTS), jnp.int32) + jnp.arange(SLOTS, dtype=jnp.int32)[None, :]
    sort_keys = sort_keys.at[targets, buffer_row].set(local_bucket * LENGTH + places)
    source_rows = jnp.argsort(sort_keys, axis=1, stable=True).astype(jnp.int32)
    live_flags = (jnp.take_along_axis(sort_keys, source_rows, axis=1) < empty_key).astype(jnp.int32)
    return (buckets.astype(jnp.int32), source_rows.reshape(GROUPS * SLOTS), live_flags.reshape(GROUPS * SLOTS))


def all_tables(key):
    base_key = jax.random.fold_in(key, 11)
    table_keys = jax.random.split(base_key, SEQS * ROUNDS)
    buckets, sources, lives = lax.map(one_table, table_keys)
    return (buckets.reshape(SEQS, ROUNDS, LENGTH), sources.reshape(SEQS, ROUNDS, GROUPS * SLOTS), lives.reshape(SEQS, ROUNDS, GROUPS * SLOTS))


def draw_bucket_ids(key, part):
    return all_tables(key)[0]


def draw_slot_source(key, part):
    return all_tables(key)[1]


def draw_live_slots(key, part):
    return all_tables(key)[2]


def block_scale(stream_key, extent, shards, least, largest):
    level = 1.0
    for dim, parts in shards:
        steps = jax.random.uniform(jax.random.fold_in(jax.random.fold_in(stream_key, 6), dim), (parts,), jnp.float32, least / len(shards), largest / len(shards))
        level = level * jnp.repeat(jnp.exp(steps), extent[dim] // parts).reshape((-1,) + (1,) * (len(extent) - 1 - dim))
    return level


def gaussian(stream_key, extent, scale, most, cuts=(), kind=jnp.bfloat16):
    level = block_scale(stream_key, extent, cuts, -0.22, 0.18) if cuts else 1.0
    drawn = jax.random.normal(stream_key, extent, jnp.float32) * scale * level
    return jnp.minimum(jnp.maximum(drawn, -most), most).astype(kind)


def setup_inputs(seed: int = 0) -> dict:
    keys = jax.random.split(jax.random.key(seed), 19)
    return {
        "first_half": gaussian(keys[0], (SEQS, LENGTH, D), 1.0, 6.0, ((0, 2), (1, 16)), jnp.float32),
        "second_half": gaussian(keys[1], (SEQS, LENGTH, D), 1.0, 6.0, ((0, 2), (1, 16)), jnp.float32),
        "first_cotangent": gaussian(keys[2], (SEQS, LENGTH, D), 1.0, 6.0, ((0, 2), (1, 16)), jnp.float32),
        "second_cotangent": gaussian(keys[3], (SEQS, LENGTH, D), 1.0, 6.0, ((0, 2), (1, 16)), jnp.float32),
        "bucket_ids": draw_bucket_ids(jax.random.fold_in(keys[18], 71), 0),
        "slot_source": draw_slot_source(jax.random.fold_in(keys[18], 71), 0),
        "live_slots": draw_live_slots(jax.random.fold_in(keys[18], 71), 0),
        "mixer_gain": jnp.clip(1.0 + 0.1 * jax.random.normal(keys[7], (D,), jnp.float32), 0.5, 1.5).astype(jnp.bfloat16),
        "mixer_shift": gaussian(keys[8], (D,), 0.3, 1.5, ((0, 32),)),
        "query_weight": gaussian(keys[9], (D, D), (D // 4) ** -0.5, 0.375, ((0, 32),)),
        "value_weight": gaussian(keys[10], (D, D), D ** -0.5, 0.1875, ((0, 32),)),
        "output_weight": gaussian(keys[11], (D, D), (D // 16) ** -0.5, 0.75, ((0, 32),)),
        "feed_gain": jnp.clip(1.0 + 0.1 * jax.random.normal(keys[12], (D,), jnp.float32), 0.5, 1.5).astype(jnp.bfloat16),
        "feed_shift": gaussian(keys[13], (D,), 0.3, 1.5, ((0, 32),)),
        "expand_weight": gaussian(keys[14], (D, FF), D ** -0.5, 0.1875, ((0, 32),)),
        "expand_bias": gaussian(keys[15], (FF,), 0.5, 2.5, ((0, 32),)),
        "contract_weight": gaussian(keys[16], (FF, D), FF ** -0.5, 0.09375, ((0, 32),)),
        "contract_bias": gaussian(keys[17], (D,), 0.3, 1.5, ((0, 32),)),
    }


@jax.custom_vjp
def low(v):
    return lax.optimization_barrier(v.astype(jnp.bfloat16)).astype(jnp.float32)

@jax.custom_vjp
def low_back(v):
    return v

def low_keep(v):
    return (low(v), None)

def low_pass(kept, grad):
    return (grad,)

def back_keep(v):
    return (v, None)

def back_low(kept, grad):
    return (low(grad),)
low.defvjp(low_keep, low_pass)
low_back.defvjp(back_keep, back_low)
highest = lax.Precision.HIGHEST

def layer_norm(values, gain, shift):
    center = values - lax.optimization_barrier(jnp.mean(values, axis=-1, keepdims=True))
    spread = lax.optimization_barrier(jnp.mean(center * center, axis=-1, keepdims=True))
    return center * lax.rsqrt(spread + 1e-05) * gain + shift

def unit_keys(queries):
    return queries * lax.rsqrt(lax.optimization_barrier(jnp.sum(queries * queries, axis=-1, keepdims=True)) + 1e-06)

def window(blocks):
    before = jnp.concatenate([jnp.zeros_like(blocks[:1]), blocks[:-1]], axis=0)
    return jnp.concatenate([before, blocks], axis=1)

def attend(rows_query, rows_value, rows_place, rows_live):
    blocks_count = SLOTS // SPAN
    query_blocks = rows_query.reshape(blocks_count, SPAN, HEADS, HEAD_DIM)
    value_blocks = rows_value.reshape(blocks_count, SPAN, HEADS, HEAD_DIM)
    key_window = window(low(unit_keys(query_blocks)))
    value_window = window(value_blocks)
    place_blocks = rows_place.reshape(blocks_count, SPAN)
    key_place = window(place_blocks)
    key_live = window(rows_live.reshape(blocks_count, SPAN)) > 0
    allowed = key_live[:, None, :] & (key_place[:, None, :] < place_blocks[:, :, None])
    selfish = key_live[:, None, :] & (key_place[:, None, :] == place_blocks[:, :, None])
    raw = low_back(jnp.einsum('cqhd,ckhd->hcqk', query_blocks, key_window, precision=highest))
    scores = jnp.where(allowed[None], raw, jnp.where(selfish[None], -10000.0, -1000000000.0))
    top = lax.optimization_barrier(jnp.max(scores, axis=-1, keepdims=True))
    log_total = jnp.log(lax.optimization_barrier(jnp.sum(jnp.exp(scores - top), axis=-1, keepdims=True))) + top
    probs = low(jnp.exp(scores - log_total))
    output = jnp.einsum('hcqk,ckhd->cqhd', probs, value_window, precision=highest)
    output = low_back(low(output.reshape(SLOTS, D)))
    totals = jnp.transpose(log_total[..., 0], (1, 2, 0)).reshape(SLOTS, HEADS)
    return (output, totals)

def tables(buckets, sources, lives):
    target = buckets // BUCKETS_GROUP
    choose = (target.reshape(GROUPS, TOK_DEV)[:, :, None] == jnp.arange(GROUPS, dtype=jnp.int32)[None, None, :]).astype(jnp.int32)
    ranked = lax.optimization_barrier(jnp.sum(choose * (jnp.cumsum(choose, axis=1).astype(jnp.int32) - 1), axis=2)).astype(jnp.int32).reshape(LENGTH)
    places = jnp.arange(LENGTH, dtype=jnp.int32)
    buffer_row = places // TOK_DEV * CAP + ranked
    token_table = jnp.zeros((GROUPS, SLOTS), jnp.int32).at[target, buffer_row].set(places)
    valid_table = jnp.zeros((GROUPS, SLOTS), jnp.int32).at[target, buffer_row].set(1)
    source_table = sources.reshape(GROUPS, SLOTS).astype(jnp.int32)
    slot_token = jnp.take_along_axis(token_table, source_table, axis=1)
    slot_valid = jnp.take_along_axis(valid_table, source_table, axis=1)
    return (slot_token, slot_valid, lives.reshape(GROUPS, SLOTS))

def forward(first, second, params, routes):
    mixer_gain, mixer_shift, query_weight, value_weight, output_weight, feed_gain, feed_shift, expand_weight, expand_bias, contract_weight, contract_bias = params
    normed = low(layer_norm(second, mixer_gain, mixer_shift))
    queries = low_back(low(jnp.dot(normed, query_weight, precision=highest)))
    values = low_back(low(jnp.dot(normed, value_weight, precision=highest)))
    places = jnp.arange(LENGTH, dtype=jnp.int32)

    def group_part(token_ids, valid_ids, live_ids):
        keeping = valid_ids[:, None].astype(jnp.float32)
        rows_query = low_back(jnp.take(queries, token_ids, axis=0) * keeping)
        rows_value = low_back(jnp.take(values, token_ids, axis=0) * keeping)
        rows_place = jnp.where(valid_ids > 0, jnp.take(places, token_ids), -1).astype(jnp.int32)
        return attend(rows_query, rows_value, rows_place, live_ids)
    checked = jax.checkpoint(group_part)

    def scan_step(carry, group_data):
        token_ids, valid_ids, live_ids = group_data
        outputs, totals = checked(token_ids, valid_ids, live_ids)
        keeping = valid_ids[:, None].astype(jnp.float32)
        out_sum = carry[0].at[token_ids].add(outputs * keeping)
        total_sum = carry[1].at[token_ids].add(totals * keeping)
        return ((out_sum, total_sum), None)
    round_outs = []
    round_totals = []
    for hashing in range(ROUNDS):
        start_carry = (jnp.zeros((LENGTH, D), jnp.float32), jnp.zeros((LENGTH, HEADS), jnp.float32))
        finals, unused = lax.scan(scan_step, start_carry, (routes[0][hashing], routes[1][hashing], routes[2][hashing]))
        round_outs.append(finals[0])
        round_totals.append(finals[1])
    stacked_totals = jnp.stack(round_totals)
    top_round = lax.optimization_barrier(jnp.max(stacked_totals, axis=0, keepdims=True))
    expo = jnp.exp(stacked_totals - top_round)
    mixing = expo / lax.optimization_barrier(jnp.sum(expo, axis=0, keepdims=True))
    stacked_outs = jnp.stack(round_outs).reshape(ROUNDS, LENGTH, HEADS, HEAD_DIM)
    mixed = low(lax.optimization_barrier(jnp.sum(mixing[..., None] * stacked_outs, axis=0)).reshape(LENGTH, D))
    branch = low_back(jnp.dot(mixed, output_weight, precision=highest))
    first_out = first + branch
    normed_feed = low(layer_norm(first_out, feed_gain, feed_shift))
    pre = low_back(jnp.dot(normed_feed, expand_weight, precision=highest) + expand_bias)
    active = low(jax.nn.gelu(pre))
    inner = low_back(jnp.dot(active, contract_weight, precision=highest) + contract_bias)
    return (first_out, second + inner)

def add_pair(total, extra):
    return total + extra

def reference(first_half, second_half, first_cotangent, second_cotangent, bucket_ids, slot_source, live_slots, mixer_gain, mixer_shift, query_weight, value_weight, output_weight, feed_gain, feed_shift, expand_weight, expand_bias, contract_weight, contract_bias):
    params = (mixer_gain.astype(jnp.float32), mixer_shift.astype(jnp.float32), query_weight.astype(jnp.float32), value_weight.astype(jnp.float32), output_weight.astype(jnp.float32), feed_gain.astype(jnp.float32), feed_shift.astype(jnp.float32), expand_weight.astype(jnp.float32), expand_bias.astype(jnp.float32), contract_weight.astype(jnp.float32), contract_bias.astype(jnp.float32))

    def per_sequence(carry, sequence_data):
        first, second, cot_first, cot_second, buckets, sources, lives = sequence_data
        routes = jax.vmap(tables)(buckets, sources, lives)

        def whole(stream_first, stream_second, weights):
            return forward(stream_first, stream_second, weights, routes)
        outputs, pullback = jax.vjp(whole, first, second, params)
        grad_first, grad_second, grad_params = pullback((cot_first, cot_second))
        carry = jax.tree.map(add_pair, carry, grad_params)
        return (carry, (outputs[0], outputs[1], grad_first, grad_second))
    zero_grads = tuple((jnp.zeros_like(param_value) for param_value in params))
    totals, stacked = lax.scan(per_sequence, zero_grads, (first_half, second_half, first_cotangent, second_cotangent, bucket_ids, slot_source, live_slots))
    return (stacked[0], stacked[1], stacked[2], stacked[3], totals[0], totals[1], totals[2], totals[3], totals[4], totals[5], totals[6], totals[7], totals[8], totals[9], totals[10])
```

```python
import functools
import types

import jax
import jax.numpy as jnp
from jax import lax
from jax.experimental import pallas as pl
from jax.experimental.pallas import tpu as pltpu
from jax.sharding import PartitionSpec as P

HEADS = 8
HEAD_DIM = 128
ROUNDS = 4
SPAN = 64
BF = jnp.bfloat16
F32 = jnp.float32
MESH = pl.DeviceIdType.MESH
DMA = pltpu.SemaphoreType.DMA
VM = pltpu.VMEM
MSG = 144


def dot(a, b):
    return lax.dot_general(a, b, (((1,), (0,)), ((), ())), preferred_element_type=F32)


def dot_nt(a, b):
    return lax.dot_general(a, b, (((1,), (1,)), ((), ())), preferred_element_type=F32)


def dot_tn(a, b):
    return lax.dot_general(a, b, (((0,), (0,)), ((), ())), preferred_element_type=F32)


def iota(shape, dim):
    return lax.broadcasted_iota(jnp.int32, shape, dim)


def iotaf(shape, dim):
    return iota(shape, dim).astype(F32)


def low(x):
    return x.astype(BF)


def split3(x):
    hi = x.astype(BF).astype(F32)
    rest = x - hi
    mid = rest.astype(BF).astype(F32)
    return hi, mid, rest - mid


def loop(count, body):
    def step(i, carry):
        body(i)
        return carry

    lax.fori_loop(0, count, step, 0)


def push(src, dst, send, recv, dev):
    pltpu.make_async_remote_copy(
        src_ref=src, dst_ref=dst, send_sem=send, recv_sem=recv, device_id=dev, device_id_type=MESH
    ).start()


def wait(ref, sem):
    pltpu.make_async_copy(ref, ref, sem).wait()


def to_column(row):
    size = row.shape[1]
    eye = iota((size, size), 0) == iota((size, size), 1)
    return jnp.sum(jnp.where(eye, row, 0.0), axis=1, keepdims=True)


def to_row(column):
    size = column.shape[0]
    eye = iota((size, size), 0) == iota((size, size), 1)
    return jnp.sum(jnp.where(eye, column, 0.0), axis=0, keepdims=True)


def message_rows(rows):
    at = iota((MSG - 128, 128), 0)
    out = jnp.zeros((MSG - 128, 128), F32)
    for i, row in enumerate(rows):
        out = jnp.where(at == i, row, out)
    return low(out)


def setup(seq, fsdp, width, hidden, tokens):
    n = types.SimpleNamespace()
    n.seq, n.fsdp, n.all = seq, fsdp, seq * fsdp
    n.chips = seq // 2
    n.b = 2 if n.chips <= 8 else 4
    n.a = n.chips // n.b
    n.sub = seq // HEADS
    n.rounds = ROUNDS // n.sub
    n.cap = 4 * SPAN // seq
    n.width, n.hidden, n.tokens = width, hidden, tokens
    n.rows = width // n.all
    n.units = hidden // n.all
    n.half = hidden // 2
    return n


def place(n):
    w = types.SimpleNamespace()
    w.s, w.f = lax.axis_index("seq"), lax.axis_index("fsdp")
    w.c, w.j = w.s // 2, lax.rem(w.s, 2)
    w.a, w.b = w.c // n.b, lax.rem(w.c, n.b)
    w.me = w.s * n.fsdp + w.f
    w.head, w.idx = w.s // n.sub, lax.rem(w.s, n.sub)
    w.sib = (w.s + 1 - 2 * w.j, w.f)
    return w


def plane(n, w, a, b, f):
    return ((a * n.b + b) * 2 + w.j, f)


def peer(n, w, i):
    d = lax.rem(w.me + i, n.all)
    return d, (d // n.fsdp, lax.rem(d, n.fsdp))


def meet_all(n, w):
    barrier = pltpu.get_barrier_semaphore()

    def greet(i):
        pl.semaphore_signal(barrier, inc=1, device_id=peer(n, w, i + 1)[1], device_id_type=MESH)

    loop(n.all - 1, greet)
    pl.semaphore_wait(barrier, n.all - 1)


class Gather:
    def __init__(self, n, w, unit, second, send, recv):
        self.n, self.w, self.unit, self.second = n, w, unit, second
        self.send, self.recv, self.k = send, recv, 0

    def at(self, i, q, v):
        n, w = self.n, self.w
        a = lax.rem(w.a + i, n.a)
        b = lax.rem(w.b + v, n.b)
        f = lax.rem(w.f + q, n.fsdp)
        return (a, b, f), (a * n.b + b) * n.fsdp + f

    def go(self, own, dev):
        spot, uid = own
        ref = self.unit(*spot)
        push(ref, ref, self.send.at[self.k], self.recv.at[uid], dev)
        self.k += 1

    def get(self, own):
        spot, uid = own
        wait(self.unit(*spot), self.recv.at[uid])

    def steps(self):
        n = self.n
        qs, vs = (n.fsdp, 1) if self.second == "f" else (1, n.b)
        return qs, vs

    def first(self):
        n, w = self.n, self.w
        for i in range(1, n.a):
            (a, b, f), _ = self.at(i, 0, 0)
            self.go(self.at(0, 0, 0), plane(n, w, a, w.b, w.f))

    def middle(self, arrived):
        n, w = self.n, self.w
        for i in range(n.a):
            own = self.at(i, 0, 0)
            if i:
                self.get(own)
                arrived(own)
            for m in range(1, n.fsdp if self.second == "f" else n.b):
                if self.second == "f":
                    self.go(own, plane(n, w, w.a, w.b, lax.rem(w.f + m, n.fsdp)))
                else:
                    self.go(own, plane(n, w, w.a, lax.rem(w.b + m, n.b), w.f))

    def last(self, arrived):
        n, w = self.n, self.w
        for i in range(n.a):
            for m in range(n.fsdp if self.second == "f" else n.b):
                own = self.at(i, m, 0) if self.second == "f" else self.at(i, 0, m)
                if m:
                    self.get(own)
                    arrived(own)
                for x in range(1, n.b if self.second == "f" else n.fsdp):
                    if self.second == "f":
                        self.go(own, plane(n, w, w.a, lax.rem(w.b + x, n.b), w.f))
                    else:
                        self.go(own, plane(n, w, w.a, w.b, lax.rem(w.f + x, n.fsdp)))

    def finish(self, arrived):
        n = self.n
        for i in range(n.a):
            for q in range(n.fsdp):
                for v in range(n.b):
                    if (v if self.second == "f" else q) == 0:
                        continue
                    own = self.at(i, q, v)
                    self.get(own)
                    arrived(own)
        for k in range(self.k):
            wait(self.unit(*self.at(0, 0, 0)[0]), self.send.at[k])


def nothing(own):
    pass


def tables(n, w, small_all, tab, own):
    nb = 2 * n.seq
    before = low((iota((128, 128), 0) < iota((128, 128), 1)).astype(F32))
    for r in range(n.rounds):
        def bucket_row(p):
            tile = small_all[p * n.fsdp + w.f].astype(F32)
            keep = iota((16, 128), 0) == 8 + w.idx * n.rounds + r
            return jnp.sum(jnp.where(keep, tile, 0.0), axis=0, keepdims=True)

        def count(p, run):
            row = bucket_row(p)
            hot = (iotaf((nb, 128), 0) == row).astype(F32)
            ahead = dot(low(hot), before)
            pos = jnp.sum(hot * (ahead + run), axis=0, keepdims=True)
            group = jnp.floor(row * 0.5)
            hotg = (iotaf((n.seq, 128), 0) == group).astype(F32)
            rank = jnp.sum(hotg * dot(low(hotg), before), axis=0, keepdims=True)
            line = group * n.cap + rank
            at = iota((8, 128), 0)
            tab[r, p] = jnp.where(at == 0, line, jnp.where(at == 1, pos, jnp.where(at == 2, row, 0.0)))
            return run + jnp.sum(hot, axis=1, keepdims=True)

        totals = lax.fori_loop(0, n.seq, count, jnp.zeros((nb, 1), F32))

        def settle(p):
            tile = tab[r, p]
            row = tile[2:3]
            odd = row - 2.0 * jnp.floor(row * 0.5)
            hot = (iotaf((nb, 128), 0) == row - 1.0).astype(F32)
            slot = tile[1:2] + odd * jnp.sum(hot * totals, axis=0, keepdims=True)
            block = jnp.floor(slot * (1.0 / SPAN))
            tab[r, p] = jnp.where(iota((8, 128), 0) == 1, block, tile)

        loop(n.seq, settle)


def picks(n, tile):
    return low((iotaf((n.seq * n.cap, 128), 0) == tile[0:1]).astype(F32))


def picks_back(n, tile):
    return low((iotaf((128, n.seq * n.cap), 1) == to_column(tile[0:1])).astype(F32))


def block_marks(tile):
    lane = iota((128, 128), 1)
    block = to_column(tile[1:2])
    ask = jnp.where(lane == 0, block, jnp.where(lane == 1, 1.0, 0.0))
    answer = jnp.where(lane == 0, 1.0, jnp.where(lane == 1, -8.0 - block, 0.0))
    return low(jnp.concatenate([ask, answer], axis=1))


def rows_of(n, ref):
    got = ref[...]
    if n.cap % 16:
        return low(got.astype(F32).reshape(n.seq * n.cap, got.shape[-1]))
    return got.reshape(n.seq * n.cap, got.shape[-1])


def put_rows(n, ref, value):
    ref[...] = value.reshape(n.seq, n.cap, value.shape[-1]).astype(ref.dtype)


def masked(n, marks, raw):
    size = n.seq * n.cap
    gap = dot_nt(marks[:, :128], marks[:, 128:])
    ahead = iota((size, size), 1) < iota((size, size), 0)
    allowed = ahead & ((gap == -8.0) | (gap == -7.0))
    same = iota((size, size), 1) == iota((size, size), 0)
    return allowed, jnp.where(allowed, raw, jnp.where(same, -1e4, -1e9))


def keys_of(query):
    wide = query.astype(F32)
    scale = lax.rsqrt(jnp.sum(wide * wide, axis=1, keepdims=True) + 1e-06)
    return low(wide * scale), scale


def fill_buffers(n, tab, qv, buf, marks):
    for r in range(n.rounds):
        def fill(p):
            tile = tab[r, p]
            hot = picks(n, tile)
            put_rows(n, buf.at[r, :, p], dot(hot, qv[p]))
            put_rows(n, marks.at[r, :, p], dot(hot, block_marks(tile)))

        loop(n.seq, fill)


def attend(n, r, g, buf, marks, obuf):
    both = rows_of(n, buf.at[r, g])
    query, value = both[:, :128], both[:, 128:]
    key, _ = keys_of(query)
    _, score = masked(n, rows_of(n, marks.at[r, g]), dot_nt(query, key))
    top = jnp.max(score, axis=1, keepdims=True)
    expo = jnp.exp(score - top)
    total = jnp.sum(expo, axis=1, keepdims=True)
    out = dot(low(expo), value) / total
    hi, mid, rest = split3(top + jnp.log(total))
    lane = iota((n.seq * n.cap, 128), 1)
    logs = jnp.where(lane == 0, hi, jnp.where(lane == 1, mid, jnp.where(lane == 2, rest, 0.0)))
    put_rows(n, obuf.at[r, :, g], jnp.concatenate([out, logs], axis=1))


def merge_rounds(n, p, tab, obuf, omsg):
    outs, logs = [], []
    for r in range(n.rounds):
        got = dot(picks_back(n, tab[r, p]), rows_of(n, obuf.at[r, p]))
        outs.append(got[:, :128])
        logs.append(jnp.sum(got[:, 128:], axis=1, keepdims=True))
    top = functools.reduce(jnp.maximum, logs)
    weights = [jnp.exp(v - top) for v in logs]
    total = sum(weights)
    omsg[p, :128] = low(sum(x * y for x, y in zip(weights, outs)) / total)
    omsg[p, 128:] = message_rows(split3(to_row(top + jnp.log(total))))


def normalize(x, gain, shift):
    center = x - jnp.mean(x, axis=1, keepdims=True)
    scale = lax.rsqrt(jnp.mean(center * center, axis=1, keepdims=True) + 1e-05)
    hat = center * scale
    return hat, scale, hat * gain + shift


def front_kernel(n, second, wqv_in, small_in, wo_in, wc_in, we_in,
                 mixed_o, logs_o, qv, nrm, wqv, tab, vec, shift_half, wo, wc, we,
                 small_all, buf, marks, obuf, omsg, home,
                 s_small, r_small, s_w, r_w, s_n, r_n, s_ns, r_ns, s_ag, r_ag, s_os, r_os, s_ex, r_ex, s_loc, s_out, r_out):
    w = place(n)
    own_spot = (w.a, w.b, w.f)
    small_all[w.me] = small_in[...]
    wqv[w.me] = wqv_in[w.head]
    locals_ = [
        pltpu.make_async_copy(wo_in, wo.at[w.me], s_loc.at[0]),
        pltpu.make_async_copy(wc_in, wc.at[w.c, w.f], s_loc.at[1]),
        pltpu.make_async_copy(we_in.at[w.j], we.at[w.c, w.j, w.f], s_loc.at[2]),
    ]
    for cp in locals_:
        cp.start()
    meet_all(n, w)

    def send_small(i):
        _, dev = peer(n, w, i + 1)
        push(small_all.at[w.me], small_all.at[w.me], s_small.at[i], r_small.at[w.me], dev)

    loop(n.all - 1, send_small)
    push(we_in.at[1 - w.j], we.at[w.c, w.j, w.f], s_ex.at[0], r_ex.at[0], w.sib)

    def send_w(i):
        _, dev = peer(n, w, i + 1)
        push(wqv_in.at[dev[0] // n.sub], wqv.at[w.me], s_w.at[i], r_w.at[w.me], dev)

    loop(n.all - 1, send_w)

    def wait_small(i):
        d, _ = peer(n, w, i + 1)
        wait(small_all.at[d], r_small.at[d])

    loop(n.all - 1, wait_small)
    group = 128 // n.rows
    for q in range(n.width // 128):
        vec[:, q * 128:(q + 1) * 128] = jnp.sum(
            small_all[q * group:(q + 1) * group].astype(F32), axis=0
        )
    per = 128 // n.units
    for q in range(n.chips * n.fsdp // per):
        chip, rest = q * per // n.fsdp, q * per % n.fsdp
        first = (2 * chip + w.j) * n.fsdp + rest
        total = sum(small_all[first + k].astype(F32) for k in range(per))
        shift_half[:, q * 128:(q + 1) * 128] = jnp.broadcast_to(total[5:6], (8, 128))

    _, _, normed = normalize(second[...], vec[0:1], vec[1:2])
    nrm[w.s] = low(normed)

    def spot(i, v):
        return (lax.rem(w.a + i, n.a) * n.b + lax.rem(w.b + v, n.b)) * 2 + w.j

    sent = 0
    for i in range(1, n.a):
        push(nrm.at[w.s], nrm.at[w.s], s_n.at[sent], r_n.at[w.c], (spot(i, 0), w.f))
        sent += 1
    for v in range(1, n.b):
        push(nrm.at[w.s], nrm.at[w.s], s_n.at[sent], r_n.at[w.c], (spot(0, v), w.f))
        sent += 1
    push(nrm.at[w.s], nrm.at[w.s], s_ns.at[0], r_ns.at[w.c], w.sib)
    shared = 1

    def wait_w(i):
        d, _ = peer(n, w, i + 1)
        wait(wqv.at[d], r_w.at[d])

    tables(n, w, small_all, tab, None)
    loop(n.all - 1, wait_w)
    weights = wqv.reshape(n.width, 256)

    def project(block):
        qv[block] = low(dot(nrm[block], weights[...]))

    for i in range(1, n.a):
        block = spot(i, 0)
        wait(nrm.at[block], r_n.at[block // 2])
        for v in range(1, n.b):
            push(nrm.at[block], nrm.at[block], s_n.at[sent], r_n.at[block // 2], (spot(0, v), w.f))
            sent += 1
        push(nrm.at[block], nrm.at[block], s_ns.at[shared], r_ns.at[block // 2], w.sib)
        shared += 1

    for cp in locals_:
        cp.wait()
    wait(we.at[w.c, 1 - w.j, w.f], r_ex.at[0])
    gather_o = Gather(n, w, lambda a, b, f: wo.at[((a * n.b + b) * 2 + w.j) * n.fsdp + f], "f", s_ag.at[0], r_ag.at[0])
    gather_c = Gather(n, w, lambda a, b, f: wc.at[a * n.b + b, f], "f", s_ag.at[1], r_ag.at[1])
    gather_e = Gather(n, w, lambda a, b, f: we.at[a * n.b + b, :, f], "b", s_ag.at[2], r_ag.at[2])
    gathers = (gather_o, gather_c, gather_e)

    def share(own):
        spot_, uid = own
        ref = gather_o.unit(*spot_)
        push(ref, ref, s_os.at[uid], r_os.at[uid], w.sib)

    share((own_spot, (w.a * n.b + w.b) * n.fsdp + w.f))
    for x in gathers:
        x.first()

    project(w.s)
    for i in range(1, n.a):
        project(spot(i, 0))
    for i in range(n.a):
        for v in range(1, n.b):
            block = spot(i, v)
            wait(nrm.at[block], r_n.at[block // 2])
            push(nrm.at[block], nrm.at[block], s_ns.at[shared], r_ns.at[block // 2], w.sib)
            shared += 1
            project(block)

    def from_sibling(c):
        block = 2 * c + 1 - w.j
        wait(nrm.at[block], r_ns.at[c])
        project(block)

    loop(n.chips, from_sibling)
    for k in range(sent):
        wait(nrm.at[w.s], s_n.at[k])
    for k in range(shared):
        wait(nrm.at[w.s], s_ns.at[k])

    gather_o.middle(share)
    gather_c.middle(nothing)
    gather_e.middle(nothing)
    fill_buffers(n, tab, qv, buf, marks)
    for r in range(n.rounds):
        loop(n.seq, lambda g: attend(n, r, g, buf, marks, obuf))
        if r == 0:
            gather_o.last(share)
            gather_c.last(nothing)
            gather_e.last(nothing)

    def give(i):
        p = lax.rem(w.s + 1 + i, n.seq)
        merge_rounds(n, p, tab, obuf, omsg)
        push(omsg.at[p], home.at[w.s], s_out.at[i], r_out.at[w.s], (p, w.f))

    loop(n.seq - 1, give)
    merge_rounds(n, w.s, tab, obuf, omsg)
    home[w.s] = omsg[w.s]

    def take(i):
        p = lax.rem(w.s + 1 + i, n.seq)
        wait(home.at[p], r_out.at[p])

    loop(n.seq - 1, take)

    def join(h):
        outs = [home[h * n.sub + i, :128].astype(F32) for i in range(n.sub)]
        logs = []
        for i in range(n.sub):
            lines = home[h * n.sub + i, 128:].astype(F32)
            logs.append(to_column(jnp.sum(lines, axis=0, keepdims=True)))
        top = functools.reduce(jnp.maximum, logs)
        parts = [jnp.exp(v - top) for v in logs]
        total = sum(parts)
        mixed_o[h] = sum(x * y for x, y in zip(parts, outs)) / total
        logs_o[h] = to_row(top + jnp.log(total))

    loop(HEADS, join)

    gather_o.finish(share)
    gather_c.finish(nothing)
    gather_e.finish(nothing)
    unit_o = wo.at[w.me]

    def wait_shared(u):
        wait(unit_o, r_os.at[u])
        wait(unit_o, s_os.at[u])

    loop(n.chips * n.fsdp, wait_shared)
    wait(we.at[w.c, w.j, w.f], s_ex.at[0])

    def wait_sends(i):
        wait(small_all.at[w.me], s_small.at[i])
        wait(wqv.at[w.me], s_w.at[i])

    loop(n.all - 1, wait_sends)
    loop(n.seq - 1, lambda i: wait(omsg.at[w.s], s_out.at[i]))


def front(n, second, wqv_in, small_in, wo_in, wc_in, we_in):
    anywhere = pl.BlockSpec(memory_space=pl.ANY)
    inside = pl.BlockSpec(memory_space=VM)
    shape = jax.ShapeDtypeStruct
    chip_units = n.chips * n.fsdp
    rows = n.seq * n.cap
    return pl.pallas_call(
        functools.partial(front_kernel, n),
        out_shape=(
            shape((HEADS, n.tokens, 128), F32),
            shape((HEADS, 1, 128), F32),
            shape((n.seq, 128, 256), BF),
            shape((n.seq, 128, n.width), BF),
            shape((n.all, n.rows, 256), BF),
            shape((n.rounds, n.seq, 8, 128), F32),
            shape((16, n.width), F32),
            shape((8, n.half), F32),
            shape((n.all, n.rows, n.width), BF),
            shape((n.chips, n.fsdp, n.units, n.width), BF),
            shape((n.chips, 2, n.fsdp, n.rows, n.half), BF),
        ),
        in_specs=[inside, inside, inside, anywhere, anywhere, anywhere],
        out_specs=(inside,) * 8 + (anywhere,) * 3,
        scratch_shapes=[
            VM((n.all, 16, 128), BF),
            VM((n.rounds, n.seq, n.seq, n.cap, 256), BF),
            VM((n.rounds, n.seq, n.seq, n.cap, 256), BF),
            VM((n.rounds, n.seq, n.seq, n.cap, 256), BF),
            VM((n.seq, MSG, 128), BF),
            VM((n.seq, MSG, 128), BF),
            DMA((n.all,)), DMA((n.all,)), DMA((n.all,)), DMA((n.all,)),
            DMA((n.chips + n.a + n.b,)), DMA((n.chips,)), DMA((n.chips,)), DMA((n.chips,)),
            DMA((3, chip_units)), DMA((3, chip_units)), DMA((chip_units,)), DMA((chip_units,)),
            DMA((1,)), DMA((1,)), DMA((3,)), DMA((n.seq,)), DMA((n.seq,)),
        ],
        compiler_params=pltpu.CompilerParams(collective_id=1, has_side_effects=True, vmem_limit_bytes=58 << 20),
        name="front",
    )(second, wqv_in, small_in, wo_in, wc_in, we_in)


def pack_front(n, buckets, mixer_gain, mixer_shift, query_weight, value_weight,
               feed_gain, feed_shift, expand_weight, expand_bias, contract_bias):
    me = lax.axis_index("seq") * n.fsdp + lax.axis_index("fsdp")

    def row(x):
        size = x.shape[0]
        tiled = jnp.tile(x, 128 // size)
        spot = lax.rem(me, 128 // size)
        return jnp.where(jnp.arange(128) // size == spot, tiled, jnp.zeros_like(tiled))

    rows = [row(x) for x in (mixer_gain, mixer_shift, feed_gain, feed_shift, contract_bias, expand_bias)]
    small = jnp.stack(rows + [jnp.zeros((128,), BF)] * 2)
    small = jnp.concatenate([small, buckets.astype(BF), jnp.zeros((8 - ROUNDS, 128), BF)])
    both = jnp.stack([query_weight, value_weight], axis=1).reshape(n.rows, 2, HEADS, HEAD_DIM)
    wqv_in = both.transpose(2, 0, 1, 3).reshape(HEADS, n.rows, 2 * HEAD_DIM)
    we_in = expand_weight.reshape(n.rows, n.chips, 2, n.hidden // n.seq)
    we_in = we_in.transpose(2, 0, 1, 3).reshape(2, n.rows, n.half)
    return wqv_in, small, we_in


def gelu_pair(x):
    k = 0.7978845608028654
    square = x * x
    t = jnp.tanh(k * (x + 0.044715 * (square * x)))
    half = 0.5 * (1.0 + t)
    return x * half, half + 0.5 * x * (1.0 - t * t) * (k * (1.0 + 0.134145 * square))


def feed_kernel(n, mixed, logs, first, second, cot1, cot2, vec, shift_half, wo, we, wc,
                first_o, second_o, grad1_o, gwc, gwe, gwo, message, vec_g, shift_g,
                mixed_low, n2, ci, act, gp, gn_part, gn_in, so_part, so_in, ssem, rsem):
    w = place(n)
    ci[w.j] = low(cot2[...])
    barrier = pltpu.get_barrier_semaphore()
    pl.semaphore_signal(barrier, inc=1, device_id=w.sib, device_id_type=MESH)
    pl.semaphore_wait(barrier, 1)
    push(ci.at[w.j], ci.at[w.j], ssem.at[0], rsem.at[0], w.sib)
    for h in range(HEADS):
        mixed_low[:, h * 128:(h + 1) * 128] = low(mixed[h])
    first_out = first[...] + dot(mixed_low[...], wo[...])
    first_o[...] = first_out
    hat, scale, normed = normalize(first_out, vec[2:3], vec[3:4])
    n2[w.j] = low(normed)
    push(n2.at[w.j], n2.at[w.j], ssem.at[1], rsem.at[1], w.sib)
    wait(ci.at[1 - w.j], rsem.at[0])
    wait(n2.at[1 - w.j], rsem.at[1])
    step = 512
    size = 2 * n.tokens
    for k in range(n.half // step):
        at = slice(k * step, (k + 1) * step)
        tokens = n2.reshape(size, n.width)[...]
        cots = ci.reshape(size, n.width)[...]
        pre = dot(tokens, we[:, at]) + shift_half[0:1, at]
        value, slope = gelu_pair(pre)
        act[:, at] = low(value)
        back = low(dot_nt(cots, wc[at]) * slope)
        gp[:, at] = back
        shift_g[:, at] = jnp.broadcast_to(jnp.sum(back.astype(F32), axis=0, keepdims=True), (8, step))
        part = dot_nt(back, we[:, at]).reshape(2, n.tokens, n.width)
        gn_part[...] = part if k == 0 else gn_part[...] + part
    push(gn_part.at[1 - w.j], gn_in, ssem.at[2], rsem.at[2], w.sib)
    so_part[...] = dot(act[...], wc[...]).reshape(2, n.tokens, n.width)
    push(so_part.at[1 - w.j], so_in, ssem.at[3], rsem.at[3], w.sib)
    for k in range(n.half // step):
        at = slice(k * step, (k + 1) * step)
        gwc[at] = low(dot_tn(act[:, at], ci.reshape(size, n.width)[...]))
    wait(gn_in, rsem.at[2])
    grad = gn_part[w.j] + gn_in[...]
    rest = grad * vec[2:3]
    mean = jnp.mean(rest, axis=1, keepdims=True)
    tilt = jnp.mean(rest * hat, axis=1, keepdims=True)
    grad1 = cot1[...] + scale * (rest - mean - hat * tilt)
    grad1_o[...] = grad1
    branch = low(grad1)
    zero = jnp.zeros((2, n.width), F32)
    vec_g[...] = jnp.concatenate([
        zero,
        jnp.sum(grad * hat, axis=0, keepdims=True),
        jnp.sum(grad, axis=0, keepdims=True),
        jnp.sum(ci[w.j].astype(F32), axis=0, keepdims=True),
        zero, zero[:1],
    ])
    for h in range(HEADS):
        gm = dot_nt(branch, wo[h * 128:(h + 1) * 128])
        message[h, :128] = low(gm)
        message[h, 128:] = message_rows(
            split3(logs[h])
            + split3(to_row(jnp.sum(gm * mixed[h], axis=1, keepdims=True)))
        )
    gwo[...] = low(dot_tn(mixed_low[...], branch))
    for k in range(n.half // step):
        at = slice(k * step, (k + 1) * step)
        gwe[:, at] = low(dot_tn(n2.reshape(size, n.width)[...], gp[:, at]))
    wait(so_in, rsem.at[3])
    second_o[...] = second[...] + (so_part[w.j] + so_in[...]) + vec[4:5]
    wait(ci.at[w.j], ssem.at[0])
    wait(n2.at[w.j], ssem.at[1])
    wait(gn_in, ssem.at[2])
    wait(so_in, ssem.at[3])


def feed(n, mixed, logs, first, second, cot1, cot2, vec, shift_half, wo, we, wc):
    inside = pl.BlockSpec(memory_space=VM)
    shape = jax.ShapeDtypeStruct
    t, d = n.tokens, n.width
    return pl.pallas_call(
        functools.partial(feed_kernel, n),
        out_shape=(
            shape((t, d), F32), shape((t, d), F32), shape((t, d), F32),
            shape((n.half, d), BF), shape((d, n.half), BF), shape((d, d), BF),
            shape((HEADS, MSG, 128), BF), shape((8, d), F32), shape((8, n.half), F32),
        ),
        in_specs=[inside] * 11,
        out_specs=(inside,) * 9,
        scratch_shapes=[
            VM((t, d), BF), VM((2, t, d), BF), VM((2, t, d), BF),
            VM((2 * t, n.half), BF), VM((2 * t, n.half), BF),
            VM((2, t, d), F32), VM((t, d), F32), VM((2, t, d), F32), VM((t, d), F32),
            DMA((4,)), DMA((4,)),
        ],
        compiler_params=pltpu.CompilerParams(collective_id=2, has_side_effects=True, vmem_limit_bytes=58 << 20),
        name="feed",
    )(mixed, logs, first, second, cot1, cot2, vec, shift_half, wo, we, wc)


class Scatter:
    def __init__(self, n, w, outer, part, got1, got2, got3, send, recv):
        self.n, self.w, self.outer, self.part = n, w, outer, part
        self.got1, self.got2, self.got3 = got1, got2, got3
        self.send, self.recv = send, recv
        self.one, self.two = (n.fsdp, n.b) if outer == "f" else (n.b, n.fsdp)
        self.me1, self.me2 = (w.f, w.b) if outer == "f" else (w.b, w.f)
        self.base2 = (self.one - 1) * n.a * self.two
        self.base3 = self.base2 + (self.two - 1) * n.a

    def mine(self, a, one, two):
        return self.part(a, two, one) if self.outer == "f" else self.part(a, one, two)

    def dev(self, a, one, two):
        if self.outer == "f":
            return plane(self.n, self.w, a, two, one)
        return plane(self.n, self.w, a, one, two)

    def first(self):
        for m in range(1, self.one):
            far = lax.rem(self.me1 + m, self.one)

            def body(i, m=m, far=far):
                a, two = i // self.two, lax.rem(i, self.two)
                k = (m - 1) * self.n.a * self.two + i
                push(self.mine(a, far, two), self.got1.at[m - 1, a, two], self.send.at[k], self.recv.at[k],
                     self.dev(self.w.a, far, self.me2))

            loop(self.n.a * self.two, body)

    def second(self):
        def body(i):
            m2, a = i // self.n.a, lax.rem(i, self.n.a)
            two = lax.rem(self.me2 + 1 + m2, self.two)
            for m in range(1, self.one):
                k = (m - 1) * self.n.a * self.two + a * self.two + two
                wait(self.got1.at[m - 1, a, two], self.recv.at[k])
            self.fold1(a, two)

            @pl.when(m2 < self.two - 1)
            def _():
                k = self.base2 + m2 * self.n.a + a
                push(self.got1.at[0, a, two], self.got2.at[m2, a], self.send.at[k], self.recv.at[k],
                     self.dev(self.w.a, self.me1, two))

        loop(self.n.a * self.two, body)

    def fold1(self, a, two):
        total = self.mine(a, self.me1, two)[...].astype(F32)
        for m in range(1, self.one):
            total += self.got1[m - 1, a, two].astype(F32)
        self.got1[0, a, two] = low(total)

    def third(self):
        def body(i):
            a = lax.rem(self.w.a + 1 + i, self.n.a)
            for m2 in range(self.two - 1):
                wait(self.got2.at[m2, a], self.recv.at[self.base2 + m2 * self.n.a + a])
            total = self.got1[0, a, self.me2].astype(F32)
            for m2 in range(self.two - 1):
                total += self.got2[m2, a].astype(F32)
            self.got2[0, a] = low(total)

            @pl.when(i < self.n.a - 1)
            def _():
                k = self.base3 + i
                push(self.got2.at[0, a], self.got3.at[i], self.send.at[k], self.recv.at[k],
                     self.dev(a, self.me1, self.me2))

        loop(self.n.a, body)

    def total(self):
        total = self.got2[0, self.w.a].astype(F32)
        for i in range(self.n.a - 1):
            wait(self.got3.at[i], self.recv.at[self.base3 + i])
            total += self.got3[i].astype(F32)
        return total

    def drain(self):
        loop(self.base3 + self.n.a - 1, lambda k: wait(self.got3.at[0], self.send.at[k]))


def spread(n, r, p, tab, dtok, dbuf, marks, buf, qv):
    tile = tab[r, p]
    hot = picks(n, tile)
    lines = dtok[p, 128:]
    embed = low((iota((MSG - 128, 128), 0) == iota((MSG - 128, 128), 1)).astype(F32))
    marked = low(dot_tn(lines, embed))
    put_rows(n, dbuf.at[r, :, p], dot(hot, jnp.concatenate([dtok[p, :128], marked], axis=1)))


def attend_back(n, r, g, buf, marks, dbuf, gbuf):
    both, back = rows_of(n, buf.at[r, g]), rows_of(n, dbuf.at[r, g])
    query, value, cot = both[:, :128], both[:, 128:], back[:, :128]
    aux = back[:, 128:].astype(F32)
    lane = iota(aux.shape, 1)
    log_all = jnp.sum(jnp.where(lane < 3, aux, 0.0), axis=1, keepdims=True)
    delta = jnp.sum(jnp.where(lane < 3, 0.0, aux), axis=1, keepdims=True)
    key, scale = keys_of(query)
    allowed, score = masked(n, rows_of(n, marks.at[r, g]), dot_nt(query, key))
    prob = jnp.exp(score - log_all)
    back_score = low(jnp.where(allowed, prob * (dot_nt(cot, value) - delta), 0.0))
    direct = dot(back_score, key)
    back_key = dot_tn(back_score, query)
    back_value = dot_tn(low(prob), cot)
    wide = query.astype(F32)
    inner = jnp.sum(wide * back_key, axis=1, keepdims=True)
    total = direct + scale * back_key - wide * (scale * scale * scale * inner)
    put_rows(n, gbuf.at[r, :, g], jnp.concatenate([total, back_value], axis=1))


def back_kernel(n, message, qv, nrm, wqv, tab, vec, gwc, gwe, gwo, vec_g, shift_g, second, cot2,
                grad2_o, small_o, gq_o, gv_o, go_o, ge_o, gc_o,
                dtok, nown, buf, marks, dbuf, gbuf, gout, gown, gin, dqv, wsum, wout, win, nsend, ngot1, ngot2,
                c1, c2, c3, e1, e2, e3, o0, o1, o2, o3, esw, egot, vsend, vgot,
                s_d, r_d, s_c, r_c, s_e, r_e, s_o, r_o, s_x, r_x, s_g, r_g, s_w, r_w, s_n1, r_n1, s_n2, r_n2, s_v, r_v, s_l):
    w = place(n)
    blocks = n.seq // n.sub

    def own_normed(i):
        return pltpu.make_async_copy(nrm.at[i * n.sub + w.idx], nown.at[i], s_l.at[i])

    for i in range(blocks):
        own_normed(i).start()
    meet_all(n, w)

    def give(i):
        s = lax.rem(w.s + 1 + i, n.seq)
        push(message.at[s // n.sub], dtok.at[w.s], s_d.at[i], r_d.at[w.s], (s, w.f))

    loop(n.seq - 1, give)
    dtok[w.s] = message[w.head]
    push(gwo.at[:, 1 - w.j], o0, s_x.at[0], r_x.at[0], w.sib)
    sum_c = Scatter(n, w, "f", lambda a, b, f: gwc.at[a * n.b + b, f], c1, c2, c3, s_c, r_c)
    sum_e = Scatter(n, w, "b", lambda a, b, f: gwe.at[a * n.b + b, :, f], e1, e2, e3, s_e, r_e)
    sum_o = Scatter(n, w, "f", lambda a, b, f: o0.at[a * n.b + b, f], o1, o2, o3, s_o, r_o)
    sum_c.first()
    sum_e.first()
    fill_buffers(n, tab, qv, buf, marks)
    wait(o0, r_x.at[0])

    def join_o(c):
        o0[c] = low(o0[c].astype(F32) + gwo[c, w.j].astype(F32))

    loop(n.chips, join_o)
    sum_o.first()

    def take(i):
        p = lax.rem(w.s + 1 + i, n.seq)
        wait(dtok.at[p], r_d.at[p])

    loop(n.seq - 1, take)
    for r in range(n.rounds):
        loop(n.seq, lambda p: spread(n, r, p, tab, dtok, dbuf, marks, buf, qv))
        loop(n.seq, lambda g: attend_back(n, r, g, buf, marks, dbuf, gbuf))
        if r == 0:
            for x in (sum_c, sum_e, sum_o):
                x.second()
    for x in (sum_c, sum_e, sum_o):
        x.third()

    def tokens_of(p):
        total = None
        for r in range(n.rounds):
            got = dot(picks_back(n, tab[r, p]), rows_of(n, gbuf.at[r, p]))
            total = got if total is None else total + got
        return total

    for m in range(1, n.sub):
        far = lax.rem(w.idx + m, n.sub)

        def offer(i, m=m, far=far):
            k = (m - 1) * blocks + i
            gout[k] = low(tokens_of(i * n.sub + far))
            push(gout.at[k], gin.at[k], s_g.at[k], r_g.at[k], (w.head * n.sub + far, w.f))

        loop(blocks, offer)

    def keep(i):
        gown[i] = tokens_of(i * n.sub + w.idx)

    loop(blocks, keep)

    weights = wqv.reshape(n.width, 256)
    bs = n.sub // 2
    nb = n.b // bs
    half_b = w.b // bs

    def finish_block(i):
        total = gown[i]
        for m in range(1, n.sub):
            k = (m - 1) * blocks + i
            wait(gin.at[k], r_g.at[k])
            total += gin[k].astype(F32)
        dqv[i] = low(total)
        nsend[i] = low(dot_nt(dqv[i], weights[...]))

    def chip_of(a, v):
        return plane(n, w, a, v * bs + lax.rem(w.b, bs), w.f)

    for m in range(1, nb):
        far = lax.rem(half_b + m, nb)

        def to_b(i, m=m, far=far):
            a = lax.rem(w.a + 1 + i, n.a)
            finish_block(a * nb + far)
            k = (m - 1) * n.a + a
            push(nsend.at[a * nb + far], ngot1.at[m - 1, a], s_n1.at[k], r_n1.at[k], chip_of(w.a, far))

        loop(n.a, to_b)
    loop(n.a, lambda i: finish_block(lax.rem(w.a + 1 + i, n.a) * nb + half_b))

    def to_a(i):
        a = lax.rem(w.a + 1 + i, n.a)
        total = nsend[a * nb + half_b].astype(F32)
        for m in range(1, nb):
            wait(ngot1.at[m - 1, a], r_n1.at[(m - 1) * n.a + a])
            total += ngot1[m - 1, a].astype(F32)
        nsend[a * nb + half_b] = low(total)

        @pl.when(i < n.a - 1)
        def _():
            push(nsend.at[a * nb + half_b], ngot2.at[i], s_n2.at[i], r_n2.at[i], chip_of(a, half_b))

    loop(n.a, to_a)

    for i in range(blocks):
        own_normed(i).wait()
        got = dot_tn(nown[i], dqv[i])
        wsum[...] = got if i == 0 else wsum[...] + got
    wout[...] = low(wsum[...]).reshape(n.all, n.rows, 256)

    def rows_out(i):
        d, dev = peer(n, w, i + 1)
        push(wout.at[d], win.at[w.me], s_w.at[i], r_w.at[w.me], dev)

    loop(n.all - 1, rows_out)
    win[w.me] = wout[w.me]

    hat, scale, _ = normalize(second[...], vec[0:1], vec[1:2])
    grad = nsend[w.a * nb + half_b].astype(F32)
    for i in range(n.a - 1):
        wait(ngot2.at[i], r_n2.at[i])
        grad += ngot2[i].astype(F32)
    rest = grad * vec[0:1]
    mean = jnp.mean(rest, axis=1, keepdims=True)
    tilt = jnp.mean(rest * hat, axis=1, keepdims=True)
    grad2_o[...] = cot2[...] + scale * (rest - mean - hat * tilt)
    gain_g = jnp.sum(grad * hat, axis=0, keepdims=True)
    shift1_g = jnp.sum(grad, axis=0, keepdims=True)
    group = 128 // n.rows
    per = 128 // n.units
    at = iota((8, 128), 0)
    for q in range(n.width // 128):
        cut = slice(q * 128, (q + 1) * 128)
        tile = jnp.where(at == 0, gain_g[:, cut], jnp.where(at == 1, shift1_g[:, cut], vec_g[:, cut]))
        for k in range(group):
            vsend[q * group + k] = tile
    for q in range(n.chips * n.fsdp // per):
        for k in range(per):
            u = q * per + k
            d = (2 * (u // n.fsdp) + w.j) * n.fsdp + u % n.fsdp
            vsend[d] = jnp.where(at == 5, shift_g[:, q * 128:(q + 1) * 128], vsend[d])

    def vec_out(i):
        d, dev = peer(n, w, i + 1)
        push(vsend.at[d], vgot.at[w.me], s_v.at[i], r_v.at[w.me], dev)

    loop(n.all - 1, vec_out)
    vgot[w.me] = vsend[w.me]

    go_o[...] = sum_o.total()
    gc_o[...] = sum_c.total()
    both = sum_e.total()
    esw[...] = both
    push(esw.at[1 - w.j], egot, s_x.at[1], r_x.at[1], w.sib)

    def take_rows(i):
        d, _ = peer(n, w, i + 1)
        wait(win.at[d], r_w.at[d])

    loop(n.all - 1, take_rows)
    for h in range(HEADS):
        total = 0.0
        for i in range(n.sub * n.fsdp):
            total += win[h * n.sub * n.fsdp + i].astype(F32)
        gq_o[:, h * 128:(h + 1) * 128] = total[:, :128]
        gv_o[:, h * 128:(h + 1) * 128] = total[:, 128:]
    wait(egot, r_x.at[1])
    wide = n.hidden // n.seq
    for c in range(n.chips):
        cut = slice(c * wide, (c + 1) * wide)
        ge_o[:, pl.ds(pl.multiple_of(c * 2 * wide + w.j * wide, 128), wide)] = esw[w.j, :, cut]
        ge_o[:, pl.ds(pl.multiple_of(c * 2 * wide + (1 - w.j) * wide, 128), wide)] = egot[:, cut]

    def take_vec(i):
        d, _ = peer(n, w, i + 1)
        wait(vgot.at[d], r_v.at[d])

    loop(n.all - 1, take_vec)
    small_o[...] = jnp.sum(vgot[...], axis=0)

    wait(o0, s_x.at[0])
    wait(egot, s_x.at[1])
    loop(n.seq - 1, lambda i: wait(dtok.at[0], s_d.at[i]))
    for x in (sum_c, sum_e, sum_o):
        x.drain()
    loop((n.sub - 1) * blocks, lambda k: wait(gin.at[0], s_g.at[k]))
    loop((nb - 1) * n.a, lambda k: wait(ngot1.at[0, 0], s_n1.at[k]))
    loop(n.a - 1, lambda k: wait(ngot2.at[0], s_n2.at[k]))

    def wait_all(i):
        wait(win.at[0], s_w.at[i])
        wait(vgot.at[0], s_v.at[i])

    loop(n.all - 1, wait_all)


def back(n, message, qv, nrm, wqv, tab, vec, gwc, gwe, gwo, vec_g, shift_g, second, cot2):
    inside = pl.BlockSpec(memory_space=VM)
    shape = jax.ShapeDtypeStruct
    t, d = n.tokens, n.width
    blocks = n.seq // n.sub
    nb = n.b // (n.sub // 2)
    pairs = (n.rounds, n.seq, n.seq, n.cap, 256)
    unit_c, unit_e, unit_o = (n.units, d), (2, n.rows, n.half), (n.rows, d)
    f1, b1, a = max(n.fsdp - 1, 1), max(n.b - 1, 1), n.a
    count_f = (n.fsdp - 1) * a * n.b + (n.b - 1) * a + a - 1
    count_b = (n.b - 1) * a * n.fsdp + (n.fsdp - 1) * a + a - 1

    def sems(k):
        return [DMA((k,)), DMA((k,))]

    return pl.pallas_call(
        functools.partial(back_kernel, n),
        out_shape=(
            shape((t, d), F32), shape((8, 128), F32), shape((n.rows, d), F32), shape((n.rows, d), F32),
            shape((n.rows, d), F32), shape((n.rows, n.hidden), F32), shape((n.units, d), F32),
        ),
        in_specs=[inside] * 2 + [pl.BlockSpec(memory_space=pl.ANY)] + [inside] * 10,
        out_specs=(inside,) * 7,
        scratch_shapes=[
            VM((n.seq, MSG, 128), BF), VM((blocks, 128, d), BF),
            VM(pairs, BF), VM(pairs, BF), VM(pairs, BF), VM(pairs, BF),
            VM(((n.sub - 1) * blocks, 128, 256), BF), VM((blocks, 128, 256), F32), VM(((n.sub - 1) * blocks, 128, 256), BF),
            VM((blocks, 128, 256), BF),
            VM((d, 256), F32), VM((n.all, n.rows, 256), BF), VM((n.all, n.rows, 256), BF),
            VM((blocks, 128, d), BF), VM((max(nb - 1, 1), a, 128, d), BF), VM((a - 1, 128, d), BF),
            VM((f1, a, n.b) + unit_c, BF), VM((b1, a) + unit_c, BF), VM((a - 1,) + unit_c, BF),
            VM((b1, a, n.fsdp) + unit_e, BF), VM((f1, a) + unit_e, BF), VM((a - 1,) + unit_e, BF),
            VM((n.chips, n.fsdp) + unit_o, BF),
            VM((f1, a, n.b) + unit_o, BF), VM((b1, a) + unit_o, BF), VM((a - 1,) + unit_o, BF),
            VM((2, n.rows, n.half), F32), VM((n.rows, n.half), F32),
            VM((n.all, 8, 128), F32), VM((n.all, 8, 128), F32),
            *sems(n.seq), *sems(count_f), *sems(count_b), *sems(count_f), *sems(2),
            *sems((n.sub - 1) * blocks), *sems(n.all), *sems(max((nb - 1) * a, 1)), *sems(a), *sems(n.all), DMA((blocks,)),
        ],
        compiler_params=pltpu.CompilerParams(collective_id=3, has_side_effects=True, vmem_limit_bytes=60 << 20),
        name="back",
    )(message, qv, nrm, wqv, tab, vec, gwc, gwe, gwo, vec_g, shift_g, second, cot2)


def on_device(
    first_half,
    second_half,
    first_cotangent,
    second_cotangent,
    bucket_ids,
    slot_source,
    live_slots,
    mixer_gain,
    mixer_shift,
    query_weight,
    value_weight,
    output_weight,
    feed_gain,
    feed_shift,
    expand_weight,
    expand_bias,
    contract_weight,
    contract_bias,
):
    seq, fsdp = lax.axis_size("seq"), lax.axis_size("fsdp")
    width, hidden = first_half.shape[2], expand_weight.shape[1]
    n = setup(seq, fsdp, width, hidden, first_half.shape[1])
    first, second = first_half[0], second_half[0]
    cot1, cot2 = first_cotangent[0], second_cotangent[0]
    wqv_in, small, we_in = pack_front(
        n, bucket_ids[0], mixer_gain, mixer_shift, query_weight, value_weight,
        feed_gain, feed_shift, expand_weight, expand_bias, contract_bias,
    )
    mixed, logs, qv, nrm, wqv, tab, vec, shift_half, wo, wc, we = front(
        n, second, wqv_in, small, output_weight, contract_weight, we_in
    )
    first_out, second_out, grad1, gwc, gwe, gwo, message, vec_g, shift_g = feed(
        n, mixed, logs, first, second, cot1, cot2, vec, shift_half,
        wo.reshape(width, width), we.reshape(width, n.half), wc.reshape(n.half, width),
    )
    grad2, small_g, gq, gv, go, ge, gc = back(
        n, message, qv, nrm, wqv, tab, vec,
        gwc.reshape(n.chips, fsdp, n.units, width),
        gwe.reshape(n.chips, 2, fsdp, n.rows, n.half),
        gwo.reshape(n.chips, 2, fsdp, n.rows, width),
        vec_g, shift_g, second, cot2,
    )
    me = lax.axis_index("seq") * fsdp + lax.axis_index("fsdp")

    def shard(row, size):
        return lax.dynamic_slice(small_g[row], (lax.rem(me, 128 // size) * size,), (size,))

    return (
        first_out[None], second_out[None], grad1[None], grad2[None],
        shard(0, n.rows), shard(1, n.rows), gq, gv, go,
        shard(2, n.rows), shard(3, n.rows), ge, shard(5, n.units), gc, shard(4, n.rows),
    )


def solution(mesh):
    tokens, slots = P("fsdp", "seq", None), P("fsdp", None, "seq")
    vector, matrix = P(("seq", "fsdp")), P(("seq", "fsdp"), None)
    return jax.shard_map(
        on_device,
        mesh=mesh,
        in_specs=(tokens,) * 4 + (slots,) * 3 + (vector, vector, matrix, matrix, matrix, vector, vector, matrix, vector, matrix, vector),
        out_specs=(tokens,) * 4 + (vector, vector, matrix, matrix, matrix, vector, vector, matrix, vector, matrix, vector),
        check_vma=False,
    )
```

```python
import functools
import types

import jax
import jax.numpy as jnp
from jax import lax
from jax.experimental import pallas as pl
from jax.experimental.pallas import tpu as pltpu
from jax.sharding import PartitionSpec as P

HEADS = 8
HEAD_DIM = 128
ROUNDS = 4
SPAN = 64
BF = jnp.bfloat16
F32 = jnp.float32
MESH = pl.DeviceIdType.MESH
DMA = pltpu.SemaphoreType.DMA
VM = pltpu.VMEM
MSG = 144


def dot(a, b):
    return lax.dot_general(a, b, (((1,), (0,)), ((), ())), preferred_element_type=F32)


def dot_nt(a, b):
    return lax.dot_general(a, b, (((1,), (1,)), ((), ())), preferred_element_type=F32)


def dot_tn(a, b):
    return lax.dot_general(a, b, (((0,), (0,)), ((), ())), preferred_element_type=F32)


def iota(shape, dim):
    return lax.broadcasted_iota(jnp.int32, shape, dim)


def iotaf(shape, dim):
    return iota(shape, dim).astype(F32)


def low(x):
    return x.astype(BF)


def split3(x):
    hi = x.astype(BF).astype(F32)
    rest = x - hi
    mid = rest.astype(BF).astype(F32)
    return hi, mid, rest - mid


def loop(count, body):
    def step(i, carry):
        body(i)
        return carry

    lax.fori_loop(0, count, step, 0)


def push(src, dst, send, recv, dev):
    pltpu.make_async_remote_copy(
        src_ref=src, dst_ref=dst, send_sem=send, recv_sem=recv, device_id=dev, device_id_type=MESH
    ).start()


def wait(ref, sem):
    pltpu.make_async_copy(ref, ref, sem).wait()


def to_column(row):
    size = row.shape[1]
    eye = iota((size, size), 0) == iota((size, size), 1)
    return jnp.sum(jnp.where(eye, row, 0.0), axis=1, keepdims=True)


def to_row(column):
    size = column.shape[0]
    eye = iota((size, size), 0) == iota((size, size), 1)
    return jnp.sum(jnp.where(eye, column, 0.0), axis=0, keepdims=True)


def message_rows(rows):
    at = iota((MSG - 128, 128), 0)
    out = jnp.zeros((MSG - 128, 128), F32)
    for i, row in enumerate(rows):
        out = jnp.where(at == i, row, out)
    return low(out)


def setup(seq, fsdp, width, hidden, tokens):
    n = types.SimpleNamespace()
    n.seq, n.fsdp, n.all = seq, fsdp, seq * fsdp
    n.chips = seq // 2
    n.b = 2 if n.chips <= 8 else 4
    n.a = n.chips // n.b
    n.sub = seq // HEADS
    n.rounds = ROUNDS // n.sub
    n.cap = 4 * SPAN // seq
    n.width, n.hidden, n.tokens = width, hidden, tokens
    n.rows = width // n.all
    n.units = hidden // n.all
    n.group = 2 * n.b
    n.part = hidden // n.group
    n.wide = hidden // seq
    return n


def place(n):
    w = types.SimpleNamespace()
    w.s, w.f = lax.axis_index("seq"), lax.axis_index("fsdp")
    w.c, w.j = w.s // 2, lax.rem(w.s, 2)
    w.a, w.b = w.c // n.b, lax.rem(w.c, n.b)
    w.me = w.s * n.fsdp + w.f
    w.head, w.idx = w.s // n.sub, lax.rem(w.s, n.sub)
    w.sib = (w.s + 1 - 2 * w.j, w.f)
    w.t = w.b * 2 + w.j
    return w


def plane(n, w, a, b, f):
    return ((a * n.b + b) * 2 + w.j, f)


def member(n, w, t):
    return ((w.a * n.b) * 2 + t, w.f)


def peer(n, w, i):
    d = lax.rem(w.me + i, n.all)
    return d, (d // n.fsdp, lax.rem(d, n.fsdp))


def meet_all(n, w):
    barrier = pltpu.get_barrier_semaphore()

    def greet(i):
        pl.semaphore_signal(barrier, inc=1, device_id=peer(n, w, i + 1)[1], device_id_type=MESH)

    loop(n.all - 1, greet)
    pl.semaphore_wait(barrier, n.all - 1)


class Gather:
    def __init__(self, n, w, unit, second, send, recv, arrived=None):
        self.n, self.w, self.unit, self.second = n, w, unit, second
        self.send, self.recv, self.k, self.arrived = send, recv, 0, arrived

    def spot(self, i, q, v):
        n, w = self.n, self.w
        a, b, f = lax.rem(w.a + i, n.a), lax.rem(w.b + v, n.b), lax.rem(w.f + q, n.fsdp)
        return (a, b, f), (a * n.b + b) * n.fsdp + f

    def go(self, at, dev):
        spot, uid = self.spot(*at)
        ref = self.unit(*spot)
        push(ref, ref, self.send.at[self.k], self.recv.at[uid], dev)
        self.k += 1

    def get(self, at):
        spot, uid = self.spot(*at)
        wait(self.unit(*spot), self.recv.at[uid])
        if self.arrived:
            self.arrived(self.unit(*spot), uid)

    def to_a(self):
        n, w = self.n, self.w
        for i in range(1, n.a):
            self.go((0, 0, 0), plane(n, w, lax.rem(w.a + i, n.a), w.b, w.f))

    def to_f(self, at):
        n, w = self.n, self.w
        for m in range(1, n.fsdp):
            self.go(at, plane(n, w, w.a, w.b, lax.rem(w.f + m, n.fsdp)))

    def to_b(self, at):
        n, w = self.n, self.w
        for m in range(1, n.b):
            self.go(at, plane(n, w, w.a, lax.rem(w.b + m, n.b), w.f))

    def column(self, i):
        if i:
            self.get((i, 0, 0))
        if self.second == "f":
            self.to_f((i, 0, 0))
            self.to_b((i, 0, 0))
        else:
            self.to_b((i, 0, 0))
            self.to_f((i, 0, 0))

    def corner(self, i):
        if self.second == "f":
            for q in range(1, self.n.fsdp):
                self.get((i, q, 0))
                self.to_b((i, q, 0))
        else:
            for v in range(1, self.n.b):
                self.get((i, 0, v))
                self.to_f((i, 0, v))

    def finish(self):
        n = self.n
        for i in range(n.a):
            for q in range(n.fsdp):
                for v in range(n.b):
                    if (v if self.second == "f" else q) != 0:
                        self.get((i, q, v))

    def drain(self):
        ref = self.unit(*self.spot(0, 0, 0)[0])
        for k in range(self.k):
            wait(ref, self.send.at[k])


class PlaneGather:
    def __init__(self, n, w, unit, send, recv):
        self.n, self.w, self.unit, self.send, self.recv, self.k = n, w, unit, send, recv, 0

    def spot(self, i, q):
        a, f = lax.rem(self.w.a + i, self.n.a), lax.rem(self.w.f + q, self.n.fsdp)
        return (a, f), a * self.n.fsdp + f

    def go(self, at, dev):
        spot, uid = self.spot(*at)
        ref = self.unit(*spot)
        push(ref, ref, self.send.at[self.k], self.recv.at[uid], dev)
        self.k += 1

    def get(self, at):
        spot, uid = self.spot(*at)
        wait(self.unit(*spot), self.recv.at[uid])

    def to_a(self):
        for i in range(1, self.n.a):
            self.go((0, 0), plane(self.n, self.w, lax.rem(self.w.a + i, self.n.a), self.w.b, self.w.f))

    def column(self, i):
        if i:
            self.get((i, 0))
        for m in range(1, self.n.fsdp):
            self.go((i, 0), plane(self.n, self.w, self.w.a, self.w.b, lax.rem(self.w.f + m, self.n.fsdp)))

    def corner(self, i):
        pass

    def finish(self):
        for i in range(self.n.a):
            for q in range(1, self.n.fsdp):
                self.get((i, q))

    def drain(self):
        ref = self.unit(*self.spot(0, 0)[0])
        for k in range(self.k):
            wait(ref, self.send.at[k])


def tables(n, w, small_all, tab):
    nb = 2 * n.seq
    before = low((iota((128, 128), 0) < iota((128, 128), 1)).astype(F32))
    for r in range(n.rounds):
        def bucket_row(p):
            tile = small_all[p * n.fsdp + w.f].astype(F32)
            keep = iota((16, 128), 0) == 8 + w.idx * n.rounds + r
            return jnp.sum(jnp.where(keep, tile, 0.0), axis=0, keepdims=True)

        def count(p, run):
            row = bucket_row(p)
            hot = (iotaf((nb, 128), 0) == row).astype(F32)
            ahead = dot(low(hot), before)
            pos = jnp.sum(hot * (ahead + run), axis=0, keepdims=True)
            group = jnp.floor(row * 0.5)
            hotg = (iotaf((n.seq, 128), 0) == group).astype(F32)
            rank = jnp.sum(hotg * dot(low(hotg), before), axis=0, keepdims=True)
            line = group * n.cap + rank
            at = iota((8, 128), 0)
            tab[r, p] = jnp.where(at == 0, line, jnp.where(at == 1, pos, jnp.where(at == 2, row, 0.0)))
            return run + jnp.sum(hot, axis=1, keepdims=True)

        totals = lax.fori_loop(0, n.seq, count, jnp.zeros((nb, 1), F32))

        def settle(p):
            tile = tab[r, p]
            row = tile[2:3]
            odd = row - 2.0 * jnp.floor(row * 0.5)
            hot = (iotaf((nb, 128), 0) == row - 1.0).astype(F32)
            slot = tile[1:2] + odd * jnp.sum(hot * totals, axis=0, keepdims=True)
            block = jnp.floor(slot * (1.0 / SPAN))
            tab[r, p] = jnp.where(iota((8, 128), 0) == 1, block, tile)

        loop(n.seq, settle)


def picks(n, tile):
    return low((iotaf((n.seq * n.cap, 128), 0) == tile[0:1]).astype(F32))


def picks_back(n, tile):
    return low((iotaf((128, n.seq * n.cap), 1) == to_column(tile[0:1])).astype(F32))


def block_marks(tile):
    lane = iota((128, 128), 1)
    block = to_column(tile[1:2])
    ask = jnp.where(lane == 0, block, jnp.where(lane == 1, 1.0, 0.0))
    answer = jnp.where(lane == 0, 1.0, jnp.where(lane == 1, -8.0 - block, 0.0))
    return low(jnp.concatenate([ask, answer], axis=1))


def rows_of(n, ref):
    got = ref[...]
    if n.cap % 16:
        return low(got.astype(F32).reshape(n.seq * n.cap, got.shape[-1]))
    return got.reshape(n.seq * n.cap, got.shape[-1])


def put_rows(n, ref, value):
    ref[...] = value.reshape(n.seq, n.cap, value.shape[-1]).astype(ref.dtype)


def masked(n, marks, raw):
    size = n.seq * n.cap
    gap = dot_nt(marks[:, :128], marks[:, 128:])
    ahead = iota((size, size), 1) < iota((size, size), 0)
    allowed = ahead & ((gap == -8.0) | (gap == -7.0))
    same = iota((size, size), 1) == iota((size, size), 0)
    return allowed, jnp.where(allowed, raw, jnp.where(same, -1e4, -1e9))


def keys_of(query):
    wide = query.astype(F32)
    scale = lax.rsqrt(jnp.sum(wide * wide, axis=1, keepdims=True) + 1e-06)
    return low(wide * scale), scale


def fill_block(n, r, p, tab, qv, buf, marks):
    tile = tab[r, p]
    hot = picks(n, tile)
    put_rows(n, buf.at[r, :, p], dot(hot, qv[p]))
    put_rows(n, marks.at[r, :, p], dot(hot, block_marks(tile)))


def attend(n, r, g, buf, marks, obuf):
    both = rows_of(n, buf.at[r, g])
    query, value = both[:, :128], both[:, 128:]
    key, _ = keys_of(query)
    _, score = masked(n, rows_of(n, marks.at[r, g]), dot_nt(query, key))
    top = jnp.max(score, axis=1, keepdims=True)
    expo = jnp.exp(score - top)
    total = jnp.sum(expo, axis=1, keepdims=True)
    out = dot(low(expo), value) / total
    hi, mid, rest = split3(top + jnp.log(total))
    lane = iota((n.seq * n.cap, 128), 1)
    logs = jnp.where(lane == 0, hi, jnp.where(lane == 1, mid, jnp.where(lane == 2, rest, 0.0)))
    put_rows(n, obuf.at[r, :, g], jnp.concatenate([out, logs], axis=1))


def merge(outs, logs):
    top = functools.reduce(jnp.maximum, logs)
    weights = [jnp.exp(v - top) for v in logs]
    total = sum(weights)
    return sum(x * y for x, y in zip(weights, outs)) / total, top + jnp.log(total)


def merge_rounds(n, p, tab, obuf):
    outs, logs = [], []
    for r in range(n.rounds):
        got = dot(picks_back(n, tab[r, p]), rows_of(n, obuf.at[r, p]))
        outs.append(got[:, :128])
        logs.append(jnp.sum(got[:, 128:], axis=1, keepdims=True))
    return merge(outs, logs)


def write_message(ref, out, log):
    ref[:128] = low(out)
    ref[128:] = message_rows(split3(to_row(log)))


def read_log(ref):
    return to_column(jnp.sum(ref[128:].astype(F32), axis=0, keepdims=True))


def hat_of(x):
    center = x - jnp.mean(x, axis=1, keepdims=True)
    scale = lax.rsqrt(jnp.mean(center * center, axis=1, keepdims=True) + 1e-05)
    return center * scale, scale


def normalize(x, gain, shift):
    hat, scale = hat_of(x)
    return hat, scale, hat * gain + shift


def placed(row, spot):
    size = row.shape[1]
    put = (iota((size, 128), 1) == iota((size, 128), 0) + spot * size).astype(F32)
    return dot(row, low(put))


def front_kernel(n, second, cot2, vectors, bias, buckets, query_w, value_w, expand_w, wo_in, wc_in,
                 home, qv, nrm, wqv, tab, vec, shift_part, ci, wo, wc, we,
                 xh, wqv_in, we_in, small_all, buf, marks, obuf, pmsg, pin, omsg,
                 s_small, r_small, s_w, r_w, s_n, r_n, s_ns, r_ns, s_ag, r_ag, s_os, r_os, s_ex, r_ex, s_loc,
                 s_p, r_p, s_out, r_out, s_ci, r_ci):
    w = place(n)
    barrier = pltpu.get_barrier_semaphore()

    def greet(i):
        pl.semaphore_signal(barrier, inc=1, device_id=peer(n, w, i + 1)[1], device_id_type=MESH)

    loop(n.all - 1, greet)
    hat, _ = hat_of(second[...])
    xh[w.s] = low(hat)
    ci[w.t] = low(cot2[...])
    for t in range(n.group):
        for a in range(n.a):
            s = a * n.group + t
            we_in[t, :, a * n.wide:(a + 1) * n.wide] = expand_w[:, s * n.wide:(s + 1) * n.wide]
    for h in range(HEADS):
        wqv_in[h, :, :128] = query_w[:, h * 128:(h + 1) * 128]
        wqv_in[h, :, 128:] = value_w[:, h * 128:(h + 1) * 128]
    lead = placed(vectors[...], lax.rem(w.me, 128 // n.rows))
    extra = placed(jnp.broadcast_to(bias[...], (8, n.units)), lax.rem(w.me, 128 // n.units))
    lead = jnp.where(iota((8, 128), 0) == 5, extra, lead)
    small_all[w.me] = low(jnp.concatenate([lead, buckets[...].astype(F32), jnp.zeros((8 - ROUNDS, 128), F32)]))
    wqv[w.me] = wqv_in[w.head]
    locals_ = [
        pltpu.make_async_copy(wo_in, wo.at[w.me], s_loc.at[0]),
        pltpu.make_async_copy(wc_in, wc.at[w.a, w.f], s_loc.at[1]),
        pltpu.make_async_copy(we_in.at[w.t], we.at[w.a, w.t, w.f], s_loc.at[2]),
    ]
    for cp in locals_:
        cp.start()
    pl.semaphore_wait(barrier, n.all - 1)

    def spot(i, v):
        return (lax.rem(w.a + i, n.a) * n.b + lax.rem(w.b + v, n.b)) * 2 + w.j

    sent = [0, 0]

    def send_hat(block, dev):
        push(xh.at[block], xh.at[block], s_n.at[sent[0]], r_n.at[block // 2], dev)
        sent[0] += 1

    def share_hat(block):
        push(xh.at[block], xh.at[block], s_ns.at[sent[1]], r_ns.at[block // 2], w.sib)
        sent[1] += 1

    for i in range(1, n.a):
        send_hat(w.s, (spot(i, 0), w.f))
    for v in range(1, n.b):
        send_hat(w.s, (spot(0, v), w.f))
    share_hat(w.s)
    for m in range(1, n.group):
        t = lax.rem(w.t + m, n.group)
        push(we_in.at[t], we.at[w.a, w.t, w.f], s_ex.at[m], r_ex.at[w.t], member(n, w, t))

    def send_small(i):
        _, dev = peer(n, w, i + 1)
        push(small_all.at[w.me], small_all.at[w.me], s_small.at[i], r_small.at[w.me], dev)

    loop(n.all - 1, send_small)

    def send_w(i):
        _, dev = peer(n, w, i + 1)
        push(wqv_in.at[dev[0] // n.sub], wqv.at[w.me], s_w.at[i], r_w.at[w.me], dev)

    loop(n.all - 1, send_w)

    def shared_o(ref, uid):
        push(ref, ref, s_os.at[uid], r_os.at[uid], w.sib)

    g_o = Gather(n, w, lambda a, b, f: wo.at[((a * n.b + b) * 2 + w.j) * n.fsdp + f], "f", s_ag.at[0], r_ag.at[0], shared_o)
    g_c = PlaneGather(n, w, lambda a, f: wc.at[a, f], s_ag.at[1], r_ag.at[1])
    g_e = PlaneGather(n, w, lambda a, f: we.at[a, :, f], s_ag.at[2], r_ag.at[2])
    gathers = (g_c, g_e, g_o)

    def wait_small(i):
        d, _ = peer(n, w, i + 1)
        wait(small_all.at[d], r_small.at[d])

    for cp in locals_:
        cp.wait()
    for m in range(1, n.group):
        t = lax.rem(w.t + m, n.group)
        wait(we.at[w.a, t, w.f], r_ex.at[t])
        push(ci.at[w.t], ci.at[w.t], s_ci.at[m], r_ci.at[w.t], member(n, w, t))
    g_o.arrived(wo.at[w.me], (w.a * n.b + w.b) * n.fsdp + w.f)
    for x in gathers:
        x.column(0)
    loop(n.all - 1, wait_small)
    group = 128 // n.rows
    for q in range(n.width // 128):
        vec[:, q * 128:(q + 1) * 128] = jnp.sum(
            small_all[q * group:(q + 1) * group].astype(F32), axis=0
        )
    per = 128 // n.units
    for q in range(n.a * n.fsdp // per):
        a, rest = q * per // n.fsdp, q * per % n.fsdp
        first = (a * n.group + w.t) * n.fsdp + rest
        total = sum(small_all[first + k].astype(F32) for k in range(per))
        shift_part[:, q * 128:(q + 1) * 128] = jnp.broadcast_to(total[5:6], (8, 128))
    tables(n, w, small_all, tab)
    weights = wqv.reshape(n.width, 256)

    def project(block):
        normed = low(xh[block].astype(F32) * vec[0:1] + vec[1:2])
        nrm[block] = normed
        qv[block] = low(dot(normed, weights[...]))

    for i in range(1, n.a):
        block = spot(i, 0)
        wait(xh.at[block], r_n.at[block // 2])
        for v in range(1, n.b):
            send_hat(block, (spot(0, v), w.f))
        share_hat(block)
    for x in gathers:
        x.to_a()

    def wait_w(i):
        d, _ = peer(n, w, i + 1)
        wait(wqv.at[d], r_w.at[d])

    loop(n.all - 1, wait_w)
    project(w.s)
    for i in range(1, n.a):
        project(spot(i, 0))
    for i in range(n.a):
        for v in range(1, n.b):
            block = spot(i, v)
            wait(xh.at[block], r_n.at[block // 2])
            share_hat(block)
            project(block)

    def from_sibling(c):
        block = 2 * c + 1 - w.j
        wait(xh.at[block], r_ns.at[c])
        project(block)

    loop(n.chips, from_sibling)

    tasks = []
    for i in range(n.a):
        if i:
            tasks.append(lambda i=i: [x.column(i) for x in gathers])
        tasks.append(lambda i=i: [x.corner(i) for x in gathers])

    def relay(count):
        for _ in range(count):
            if tasks:
                tasks.pop(0)()

    for r in range(n.rounds):
        loop(n.seq, lambda p: fill_block(n, r, p, tab, qv, buf, marks))
    relay(RELAYS[0])
    parts = 4
    slot = 1
    for r in range(n.rounds):
        for q in range(parts):
            loop(n.seq // parts, lambda g: attend(n, r, q * (n.seq // parts) + g, buf, marks, obuf))
            relay(RELAYS[slot] if slot < len(RELAYS) else 0)
            slot += 1

    blocks = n.seq // n.sub
    for m in range(1, n.sub):
        far = lax.rem(w.idx + m, n.sub)

        def offer(i, m=m, far=far):
            k = (m - 1) * blocks + i
            write_message(pmsg.at[k], *merge_rounds(n, i * n.sub + far, tab, obuf))
            push(pmsg.at[k], pin.at[k], s_p.at[k], r_p.at[k], (w.head * n.sub + far, w.f))

        loop(blocks, offer)

    def settle(i):
        out, log = merge_rounds(n, i * n.sub + w.idx, tab, obuf)
        outs, logs = [out], [log]
        for m in range(1, n.sub):
            k = (m - 1) * blocks + i
            wait(pin.at[k], r_p.at[k])
            outs.append(pin[k, :128].astype(F32))
            logs.append(read_log(pin.at[k]))
        write_message(omsg.at[i], *merge(outs, logs))

    def give(i):
        to = lax.rem(w.head + 1 + i, blocks)
        settle(to)
        push(omsg.at[to], home.at[w.head], s_out.at[i], r_out.at[w.head], (to * n.sub + w.idx, w.f))

    loop(blocks - 1, give)
    settle(w.head)
    home[w.head] = omsg[w.head]
    relay(len(tasks))

    def take(i):
        h = lax.rem(w.head + 1 + i, HEADS)
        wait(home.at[h], r_out.at[h])

    loop(HEADS - 1, take)

    for x in gathers:
        x.finish()
    unit_o = wo.at[w.me]

    def wait_shared(u):
        wait(unit_o, r_os.at[u])
        wait(unit_o, s_os.at[u])

    loop(n.chips * n.fsdp, wait_shared)
    for x in gathers:
        x.drain()
    for m in range(1, n.group):
        t = lax.rem(w.t + m, n.group)
        wait(we_in.at[0], s_ex.at[m])
        wait(ci.at[t], r_ci.at[t])
        wait(ci.at[t], s_ci.at[m])

    def wait_sends(i):
        wait(small_all.at[w.me], s_small.at[i])
        wait(wqv.at[w.me], s_w.at[i])

    loop(n.all - 1, wait_sends)
    for k in range(sent[0]):
        wait(xh.at[w.s], s_n.at[k])
    for k in range(sent[1]):
        wait(xh.at[w.s], s_ns.at[k])
    loop((n.sub - 1) * blocks, lambda k: wait(pmsg.at[0], s_p.at[k]))
    loop(blocks - 1, lambda k: wait(omsg.at[0], s_out.at[k]))


RELAYS = (0, 0, 0, 0, 0, 2, 1, 1, 3)


def front(n, second, cot2, vectors, bias, buckets, query_w, value_w, expand_w, wo_in, wc_in):
    anywhere = pl.BlockSpec(memory_space=pl.ANY)
    inside = pl.BlockSpec(memory_space=VM)
    shape = jax.ShapeDtypeStruct
    units = n.chips * n.fsdp
    blocks = n.seq // n.sub
    pairs = (n.rounds, n.seq, n.seq, n.cap, 256)

    def sems(*k):
        return [DMA(k), DMA(k)]

    return pl.pallas_call(
        functools.partial(front_kernel, n),
        out_shape=(
            shape((HEADS, MSG, 128), BF),
            shape((n.seq, 128, 256), BF),
            shape((n.seq, 128, n.width), BF),
            shape((n.all, n.rows, 256), BF),
            shape((n.rounds, n.seq, 8, 128), F32),
            shape((16, n.width), F32),
            shape((8, n.part), F32),
            shape((n.group, 128, n.width), BF),
            shape((n.all, n.rows, n.width), BF),
            shape((n.a, n.fsdp, n.units, n.width), BF),
            shape((n.a, n.group, n.fsdp, n.rows, n.part), BF),
        ),
        in_specs=[inside] * 8 + [anywhere] * 2,
        out_specs=(inside,) * 8 + (anywhere,) * 3,
        scratch_shapes=[
            VM((n.seq, 128, n.width), BF),
            VM((HEADS, n.rows, 256), BF), VM((n.group, n.rows, n.part), BF),
            VM((n.all, 16, 128), BF),
            VM(pairs, BF), VM(pairs, BF), VM(pairs, BF),
            VM(((n.sub - 1) * blocks, MSG, 128), BF), VM(((n.sub - 1) * blocks, MSG, 128), BF), VM((blocks, MSG, 128), BF),
            *sems(n.all), *sems(n.all), *sems(n.chips + n.a + n.b), *sems(n.chips),
            *sems(3, units), *sems(units), *sems(n.group), DMA((3,)), *sems((n.sub - 1) * blocks), *sems(HEADS), *sems(n.group),
        ],
        compiler_params=pltpu.CompilerParams(collective_id=1, has_side_effects=True, vmem_limit_bytes=58 << 20),
        name="front",
    )(second, cot2, vectors, bias, buckets, query_w, value_w, expand_w, wo_in, wc_in)


def gelu_pair(x):
    k = 0.7978845608028654
    square = x * x
    t = jnp.tanh(k * (x + 0.044715 * (square * x)))
    half = 0.5 * (1.0 + t)
    return x * half, half + 0.5 * x * (1.0 - t * t) * (k * (1.0 + 0.134145 * square))


class GroupSum:
    def __init__(self, n, w, part, out, got1, got2, send, recv):
        self.n, self.w, self.part, self.out, self.got1, self.got2 = n, w, part, out, got1, got2
        self.send, self.recv = send, recv

    def cores(self):
        for b in range(self.n.b):
            t = b * 2 + 1 - self.w.j
            self.out[t] = low(self.part[t])
            push(self.out.at[t], self.got1.at[b], self.send.at[b], self.recv.at[b], self.w.sib)

    def chips(self):
        n, w = self.n, self.w
        for m in range(1, n.b):
            b = lax.rem(w.b + m, n.b)
            t = b * 2 + w.j
            wait(self.got1.at[b], self.recv.at[b])
            self.out[t] = low(self.part[t] + self.got1[b].astype(F32))
            k = n.b + m - 1
            push(self.out.at[t], self.got2.at[m - 1], self.send.at[k], self.recv.at[k], member(n, w, t))

    def total(self):
        n, w = self.n, self.w
        wait(self.got1.at[w.b], self.recv.at[w.b])
        total = self.part[w.t] + self.got1[w.b].astype(F32)
        for m in range(1, n.b):
            wait(self.got2.at[m - 1], self.recv.at[n.b + m - 1])
            total += self.got2[m - 1].astype(F32)
        return total

    def drain(self):
        for k in range(2 * self.n.b - 1):
            wait(self.got1.at[0], self.send.at[k])


def feed_kernel(n, home, first, second, cot1, ci, vec, shift_part, wo, we, wc,
                first_o, second_o, grad1_o, gwc, gwe, gwo, message, vec_g, shift_g,
                mixed_low, n2, act, gp, gn_part, gn_out, gn_got1, gn_got2, so_part, so_out, so_got1, so_got2,
                s_x, r_x, s_gn, r_gn, s_so, r_so):
    w = place(n)
    barrier = pltpu.get_barrier_semaphore()
    for m in range(1, n.group):
        pl.semaphore_signal(barrier, inc=1, device_id=member(n, w, lax.rem(w.t + m, n.group)), device_id_type=MESH)
    for h in range(HEADS):
        mixed_low[:, h * 128:(h + 1) * 128] = home[h, :128]
    first_out = first[...] + dot(mixed_low[...], wo[...])
    first_o[...] = first_out
    hat, scale, normed = normalize(first_out, vec[2:3], vec[3:4])
    n2[w.t] = low(normed)
    pl.semaphore_wait(barrier, n.group - 1)
    k = 0
    for m in range(1, n.b):
        t = lax.rem(w.b + m, n.b) * 2 + w.j
        push(n2.at[w.t], n2.at[w.t], s_x.at[k], r_x.at[w.t], member(n, w, t))
        k += 1
    push(n2.at[w.t], n2.at[w.t], s_x.at[k], r_x.at[w.t], w.sib)
    k += 1
    for m in range(1, n.b):
        t = lax.rem(w.b + m, n.b) * 2 + w.j
        wait(n2.at[t], r_x.at[t])
        push(n2.at[t], n2.at[t], s_x.at[k], r_x.at[t], w.sib)
        k += 1
    for b in range(n.b):
        t = b * 2 + 1 - w.j
        wait(n2.at[t], r_x.at[t])
    size = n.group * n.tokens
    step = min(512, n.part)
    tokens = n2.reshape(size, n.width)
    cots = ci.reshape(size, n.width)
    for q in range(n.part // step):
        at = slice(q * step, (q + 1) * step)
        pre = dot(tokens[...], we[:, at]) + shift_part[0:1, at]
        value, slope = gelu_pair(pre)
        act[:, at] = low(value)
        back = low(dot_nt(cots[...], wc[at]) * slope)
        gp[:, at] = back
        shift_g[:, at] = jnp.broadcast_to(jnp.sum(back.astype(F32), axis=0, keepdims=True), (8, step))
    gn_part[...] = dot_nt(gp[...], we[...]).reshape(n.group, n.tokens, n.width)
    gn = GroupSum(n, w, gn_part, gn_out, gn_got1, gn_got2, s_gn, r_gn)
    so = GroupSum(n, w, so_part, so_out, so_got1, so_got2, s_so, r_so)
    gn.cores()
    so_part[...] = dot(act[...], wc[...]).reshape(n.group, n.tokens, n.width)
    gn.chips()
    so.cores()
    gwc[...] = low(dot_tn(act[...], cots[...]))
    so.chips()
    gwe[...] = low(dot_tn(tokens[...], gp[...]))
    grad = gn.total()
    rest = grad * vec[2:3]
    mean = jnp.mean(rest, axis=1, keepdims=True)
    tilt = jnp.mean(rest * hat, axis=1, keepdims=True)
    grad1 = cot1[...] + scale * (rest - mean - hat * tilt)
    grad1_o[...] = grad1
    branch = low(grad1)
    zero = jnp.zeros((2, n.width), F32)
    vec_g[...] = jnp.concatenate([
        zero,
        jnp.sum(grad * hat, axis=0, keepdims=True),
        jnp.sum(grad, axis=0, keepdims=True),
        jnp.sum(ci[w.t].astype(F32), axis=0, keepdims=True),
        zero, zero[:1],
    ])
    for h in range(HEADS):
        gm = dot_nt(branch, wo[h * 128:(h + 1) * 128])
        message[h, :128] = low(gm)
        delta = jnp.sum(gm * home[h, :128].astype(F32), axis=1, keepdims=True)
        logs = home[h, 128:].astype(F32)
        message[h, 128:] = message_rows((logs[0:1], logs[1:2], logs[2:3]) + split3(to_row(delta)))
    gwo[...] = low(dot_tn(mixed_low[...], branch))
    second_o[...] = second[...] + so.total() + vec[4:5]
    for i in range(k):
        wait(n2.at[0], s_x.at[i])
    gn.drain()
    so.drain()


def feed(n, home, first, second, cot1, ci, vec, shift_part, wo, we, wc):
    inside = pl.BlockSpec(memory_space=VM)
    shape = jax.ShapeDtypeStruct
    t, d, g = n.tokens, n.width, n.group
    more = max(n.b - 1, 1)
    sums = [VM((g, t, d), F32), VM((g, t, d), BF), VM((n.b, t, d), BF), VM((more, t, d), BF)]
    return pl.pallas_call(
        functools.partial(feed_kernel, n),
        out_shape=(
            shape((t, d), F32), shape((t, d), F32), shape((t, d), F32),
            shape((n.part, d), BF), shape((d, n.part), BF), shape((d, d), BF),
            shape((HEADS, MSG, 128), BF), shape((8, d), F32), shape((8, n.part), F32),
        ),
        in_specs=[inside] * 10,
        out_specs=(inside,) * 9,
        scratch_shapes=[
            VM((t, d), BF), VM((g, t, d), BF), VM((g * t, n.part), BF), VM((g * t, n.part), BF),
            *sums, *sums,
            DMA((2 * n.b,)), DMA((g,)), DMA((2 * n.b,)), DMA((2 * n.b,)), DMA((2 * n.b,)), DMA((2 * n.b,)),
        ],
        compiler_params=pltpu.CompilerParams(collective_id=2, has_side_effects=True, vmem_limit_bytes=58 << 20),
        name="feed",
    )(home, first, second, cot1, ci, vec, shift_part, wo, we, wc)


class Scatter:
    def __init__(self, n, w, outer, part, got1, got2, got3, send, recv):
        self.n, self.w, self.outer, self.part = n, w, outer, part
        self.got1, self.got2, self.got3 = got1, got2, got3
        self.send, self.recv = send, recv
        self.one, self.two = (n.fsdp, n.b) if outer == "f" else (n.b, n.fsdp)
        self.me1, self.me2 = (w.f, w.b) if outer == "f" else (w.b, w.f)
        self.base2 = (self.one - 1) * n.a * self.two
        self.base3 = self.base2 + (self.two - 1) * n.a

    def mine(self, a, one, two):
        return self.part(a, two, one) if self.outer == "f" else self.part(a, one, two)

    def dev(self, a, one, two):
        if self.outer == "f":
            return plane(self.n, self.w, a, two, one)
        return plane(self.n, self.w, a, one, two)

    def first(self):
        for m in range(1, self.one):
            far = lax.rem(self.me1 + m, self.one)

            def body(i, m=m, far=far):
                a, two = i // self.two, lax.rem(i, self.two)
                k = (m - 1) * self.n.a * self.two + i
                push(self.mine(a, far, two), self.got1.at[m - 1, a, two], self.send.at[k], self.recv.at[k],
                     self.dev(self.w.a, far, self.me2))

            loop(self.n.a * self.two, body)

    def second(self):
        def body(i):
            m2, a = i // self.n.a, lax.rem(i, self.n.a)
            two = lax.rem(self.me2 + 1 + m2, self.two)
            for m in range(1, self.one):
                k = (m - 1) * self.n.a * self.two + a * self.two + two
                wait(self.got1.at[m - 1, a, two], self.recv.at[k])
            self.fold1(a, two)

            @pl.when(m2 < self.two - 1)
            def _():
                k = self.base2 + m2 * self.n.a + a
                push(self.got1.at[0, a, two], self.got2.at[m2, a], self.send.at[k], self.recv.at[k],
                     self.dev(self.w.a, self.me1, two))

        loop(self.n.a * self.two, body)

    def fold1(self, a, two):
        total = self.mine(a, self.me1, two)[...].astype(F32)
        for m in range(1, self.one):
            total += self.got1[m - 1, a, two].astype(F32)
        self.got1[0, a, two] = low(total)

    def third(self):
        def body(i):
            a = lax.rem(self.w.a + 1 + i, self.n.a)
            for m2 in range(self.two - 1):
                wait(self.got2.at[m2, a], self.recv.at[self.base2 + m2 * self.n.a + a])
            total = self.got1[0, a, self.me2].astype(F32)
            for m2 in range(self.two - 1):
                total += self.got2[m2, a].astype(F32)
            self.got2[0, a] = low(total)

            @pl.when(i < self.n.a - 1)
            def _():
                k = self.base3 + i
                push(self.got2.at[0, a], self.got3.at[i], self.send.at[k], self.recv.at[k],
                     self.dev(a, self.me1, self.me2))

        loop(self.n.a, body)

    def total(self):
        total = self.got2[0, self.w.a].astype(F32)
        for i in range(self.n.a - 1):
            wait(self.got3.at[i], self.recv.at[self.base3 + i])
            total += self.got3[i].astype(F32)
        return total

    def drain(self):
        loop(self.base3 + self.n.a - 1, lambda k: wait(self.got3.at[0], self.send.at[k]))


class PlaneScatter:
    def __init__(self, n, w, part, got1, got2, send, recv):
        self.n, self.w, self.part, self.got1, self.got2, self.send, self.recv = n, w, part, got1, got2, send, recv
        self.base = (n.fsdp - 1) * n.a

    def first(self):
        n, w = self.n, self.w
        for m in range(1, n.fsdp):
            far = lax.rem(w.f + m, n.fsdp)

            def body(i, m=m, far=far):
                a = lax.rem(w.a + 1 + i, n.a)
                k = (m - 1) * n.a + a
                push(self.part(a, far), self.got1.at[m - 1, a], self.send.at[k], self.recv.at[k], plane(n, w, w.a, w.b, far))

            loop(n.a, body)

    def second(self, i):
        n, w = self.n, self.w
        a = lax.rem(w.a + 1 + i, n.a)
        total = self.part(a, w.f)[...].astype(F32)
        for m in range(1, n.fsdp):
            wait(self.got1.at[m - 1, a], self.recv.at[(m - 1) * n.a + a])
            total += self.got1[m - 1, a].astype(F32)
        self.got1[0, a] = low(total)
        if i < n.a - 1:
            k = self.base + i
            push(self.got1.at[0, a], self.got2.at[i], self.send.at[k], self.recv.at[k], plane(n, w, a, w.b, w.f))

    def total(self):
        total = self.got1[0, self.w.a].astype(F32)
        for i in range(self.n.a - 1):
            wait(self.got2.at[i], self.recv.at[self.base + i])
            total += self.got2[i].astype(F32)
        return total

    def drain(self):
        loop(self.base + self.n.a - 1, lambda k: wait(self.got2.at[0], self.send.at[k]))


def spread(n, r, p, tab, dtok, dbuf, marks, buf, qv):
    tile = tab[r, p]
    hot = picks(n, tile)
    lines = dtok[p, 128:]
    embed = low((iota((MSG - 128, 128), 0) == iota((MSG - 128, 128), 1)).astype(F32))
    marked = low(dot_tn(lines, embed))
    put_rows(n, dbuf.at[r, :, p], dot(hot, jnp.concatenate([dtok[p, :128], marked], axis=1)))


def attend_back(n, r, g, buf, marks, dbuf, gbuf):
    both, back = rows_of(n, buf.at[r, g]), rows_of(n, dbuf.at[r, g])
    query, value, cot = both[:, :128], both[:, 128:], back[:, :128]
    aux = back[:, 128:].astype(F32)
    lane = iota(aux.shape, 1)
    log_all = jnp.sum(jnp.where(lane < 3, aux, 0.0), axis=1, keepdims=True)
    delta = jnp.sum(jnp.where(lane < 3, 0.0, aux), axis=1, keepdims=True)
    key, scale = keys_of(query)
    allowed, score = masked(n, rows_of(n, marks.at[r, g]), dot_nt(query, key))
    prob = jnp.exp(score - log_all)
    back_score = low(jnp.where(allowed, prob * (dot_nt(cot, value) - delta), 0.0))
    direct = dot(back_score, key)
    back_key = dot_tn(back_score, query)
    back_value = dot_tn(low(prob), cot)
    wide = query.astype(F32)
    inner = jnp.sum(wide * back_key, axis=1, keepdims=True)
    total = direct + scale * back_key - wide * (scale * scale * scale * inner)
    put_rows(n, gbuf.at[r, :, g], jnp.concatenate([total, back_value], axis=1))


SUMS = (0, 0, 1, 1, 1, 1, 1, 1)


def back_kernel(n, message, qv, nrm, wqv, tab, vec, gwc, gwe, gwo, vec_g, shift_g, second, cot2,
                grad2_o, small_o, gq_o, gv_o, go_o, ge_o, gc_o,
                dtok, nown, buf, marks, dbuf, gbuf, gout, gown, gin, dqv, wsum, wout, win, nsend, ngot1, ngot2,
                c1, c2, e1, e2, o0, o1, o2, o3, esw, egot, vsend, vgot,
                s_d, r_d, s_c, r_c, s_e, r_e, s_o, r_o, s_x, r_x, s_g, r_g, s_w, r_w, s_n1, r_n1, s_n2, r_n2, s_v, r_v, s_l, s_y, r_y):
    w = place(n)
    blocks = n.seq // n.sub

    def own_normed(i):
        return pltpu.make_async_copy(nrm.at[i * n.sub + w.idx], nown.at[i], s_l.at[i])

    for i in range(blocks):
        own_normed(i).start()
    meet_all(n, w)

    def give(i):
        s = lax.rem(w.s + 1 + i, n.seq)
        push(message.at[s // n.sub], dtok.at[w.s], s_d.at[i], r_d.at[w.s], (s, w.f))

    loop(n.seq - 1, give)
    dtok[w.s] = message[w.head]
    push(gwo.at[:, 1 - w.j], o0, s_x.at[0], r_x.at[0], w.sib)
    sum_c = PlaneScatter(n, w, lambda a, f: gwc.at[a, f], c1, c2, s_c, r_c)
    sum_e = PlaneScatter(n, w, lambda a, f: gwe.at[a, :, f], e1, e2, s_e, r_e)
    sum_o = Scatter(n, w, "f", lambda a, b, f: o0.at[a * n.b + b, f], o1, o2, o3, s_o, r_o)
    sum_c.first()
    sum_e.first()
    for r in range(n.rounds):
        loop(n.seq, lambda p: fill_block(n, r, p, tab, qv, buf, marks))
    wait(o0, r_x.at[0])

    def join_o(c):
        o0[c] = low(o0[c].astype(F32) + gwo[c, w.j].astype(F32))

    loop(n.chips, join_o)
    sum_o.first()

    def take(i):
        p = lax.rem(w.s + 1 + i, n.seq)
        wait(dtok.at[p], r_d.at[p])

    loop(n.seq - 1, take)
    tasks = []
    for i in range(n.a):
        tasks.append(lambda i=i: (sum_c.second(i), sum_e.second(i)))
    tasks.insert(2, sum_o.second)
    tasks.append(sum_o.third)

    def relay(count):
        for _ in range(count):
            if tasks:
                tasks.pop(0)()

    slot = 0
    parts = 4
    for r in range(n.rounds):
        loop(n.seq, lambda p: spread(n, r, p, tab, dtok, dbuf, marks, buf, qv))
        for q in range(parts):
            loop(n.seq // parts, lambda g: attend_back(n, r, q * (n.seq // parts) + g, buf, marks, dbuf, gbuf))
            relay(SUMS[slot] if slot < len(SUMS) else 0)
            slot += 1
    relay(len(tasks))

    def tokens_of(p):
        total = None
        for r in range(n.rounds):
            got = dot(picks_back(n, tab[r, p]), rows_of(n, gbuf.at[r, p]))
            total = got if total is None else total + got
        return total

    for m in range(1, n.sub):
        far = lax.rem(w.idx + m, n.sub)

        def offer(i, m=m, far=far):
            k = (m - 1) * blocks + i
            gout[k] = low(tokens_of(i * n.sub + far))
            push(gout.at[k], gin.at[k], s_g.at[k], r_g.at[k], (w.head * n.sub + far, w.f))

        loop(blocks, offer)

    def keep(i):
        gown[i] = tokens_of(i * n.sub + w.idx)

    loop(blocks, keep)

    weights = wqv.reshape(n.width, 256)
    bs = n.sub // 2
    nb = n.b // bs
    half_b = w.b // bs

    def finish_block(i):
        total = gown[i]
        for m in range(1, n.sub):
            k = (m - 1) * blocks + i
            wait(gin.at[k], r_g.at[k])
            total += gin[k].astype(F32)
        dqv[i] = low(total)
        nsend[i] = low(dot_nt(dqv[i], weights[...]))

    def chip_of(a, v):
        return plane(n, w, a, v * bs + lax.rem(w.b, bs), w.f)

    for m in range(1, nb):
        far = lax.rem(half_b + m, nb)

        def to_b(i, m=m, far=far):
            a = lax.rem(w.a + 1 + i, n.a)
            finish_block(a * nb + far)
            k = (m - 1) * n.a + a
            push(nsend.at[a * nb + far], ngot1.at[m - 1, a], s_n1.at[k], r_n1.at[k], chip_of(w.a, far))

        loop(n.a, to_b)
    loop(n.a, lambda i: finish_block(lax.rem(w.a + 1 + i, n.a) * nb + half_b))

    def to_a(i):
        a = lax.rem(w.a + 1 + i, n.a)
        total = nsend[a * nb + half_b].astype(F32)
        for m in range(1, nb):
            wait(ngot1.at[m - 1, a], r_n1.at[(m - 1) * n.a + a])
            total += ngot1[m - 1, a].astype(F32)
        nsend[a * nb + half_b] = low(total)

        @pl.when(i < n.a - 1)
        def _():
            push(nsend.at[a * nb + half_b], ngot2.at[i], s_n2.at[i], r_n2.at[i], chip_of(a, half_b))

    loop(n.a, to_a)

    for i in range(blocks):
        own_normed(i).wait()
        got = dot_tn(nown[i], dqv[i])
        wsum[...] = got if i == 0 else wsum[...] + got
    wout[...] = low(wsum[...]).reshape(n.all, n.rows, 256)

    def rows_out(i):
        d, dev = peer(n, w, i + 1)
        push(wout.at[d], win.at[w.me], s_w.at[i], r_w.at[w.me], dev)

    loop(n.all - 1, rows_out)
    win[w.me] = wout[w.me]

    hat, scale, _ = normalize(second[...], vec[0:1], vec[1:2])
    grad = nsend[w.a * nb + half_b].astype(F32)
    for i in range(n.a - 1):
        wait(ngot2.at[i], r_n2.at[i])
        grad += ngot2[i].astype(F32)
    rest = grad * vec[0:1]
    mean = jnp.mean(rest, axis=1, keepdims=True)
    tilt = jnp.mean(rest * hat, axis=1, keepdims=True)
    grad2_o[...] = cot2[...] + scale * (rest - mean - hat * tilt)
    gain_g = jnp.sum(grad * hat, axis=0, keepdims=True)
    shift1_g = jnp.sum(grad, axis=0, keepdims=True)
    group = 128 // n.rows
    per = 128 // n.units
    at = iota((8, 128), 0)
    for q in range(n.width // 128):
        cut = slice(q * 128, (q + 1) * 128)
        tile = jnp.where(at == 0, gain_g[:, cut], jnp.where(at == 1, shift1_g[:, cut], vec_g[:, cut]))
        for k in range(group):
            vsend[q * group + k] = tile
    for q in range(n.a * n.fsdp // per):
        for k in range(per):
            u = q * per + k
            d = (u // n.fsdp * n.group + w.t) * n.fsdp + u % n.fsdp
            vsend[d] = jnp.where(at == 5, shift_g[:, q * 128:(q + 1) * 128], vsend[d])

    def vec_out(i):
        d, dev = peer(n, w, i + 1)
        push(vsend.at[d], vgot.at[w.me], s_v.at[i], r_v.at[w.me], dev)

    loop(n.all - 1, vec_out)
    vgot[w.me] = vsend[w.me]

    go_o[...] = sum_o.total()
    gc_o[...] = sum_c.total()
    both = sum_e.total()
    esw[...] = both
    egot[w.t] = esw[w.t]
    for m in range(1, n.group):
        t = lax.rem(w.t + m, n.group)
        push(esw.at[t], egot.at[w.t], s_y.at[m], r_y.at[w.t], member(n, w, t))

    def take_rows(i):
        d, _ = peer(n, w, i + 1)
        wait(win.at[d], r_w.at[d])

    loop(n.all - 1, take_rows)
    for h in range(HEADS):
        total = 0.0
        for i in range(n.sub * n.fsdp):
            total += win[h * n.sub * n.fsdp + i].astype(F32)
        gq_o[:, h * 128:(h + 1) * 128] = total[:, :128]
        gv_o[:, h * 128:(h + 1) * 128] = total[:, 128:]
    for m in range(1, n.group):
        t = lax.rem(w.t + m, n.group)
        wait(egot.at[t], r_y.at[t])
    for t in range(n.group):
        for a in range(n.a):
            c = (a * n.group + t) * n.wide
            ge_o[:, c:c + n.wide] = egot[t, :, a * n.wide:(a + 1) * n.wide]

    def take_vec(i):
        d, _ = peer(n, w, i + 1)
        wait(vgot.at[d], r_v.at[d])

    loop(n.all - 1, take_vec)
    small_o[...] = jnp.sum(vgot[...], axis=0)

    wait(o0, s_x.at[0])
    for m in range(1, n.group):
        wait(egot.at[0], s_y.at[m])
    loop(n.seq - 1, lambda i: wait(dtok.at[0], s_d.at[i]))
    for x in (sum_c, sum_e, sum_o):
        x.drain()
    loop((n.sub - 1) * blocks, lambda k: wait(gin.at[0], s_g.at[k]))
    loop((nb - 1) * n.a, lambda k: wait(ngot1.at[0, 0], s_n1.at[k]))
    loop(n.a - 1, lambda k: wait(ngot2.at[0], s_n2.at[k]))

    def wait_all(i):
        wait(win.at[0], s_w.at[i])
        wait(vgot.at[0], s_v.at[i])

    loop(n.all - 1, wait_all)


def back(n, message, qv, nrm, wqv, tab, vec, gwc, gwe, gwo, vec_g, shift_g, second, cot2):
    inside = pl.BlockSpec(memory_space=VM)
    shape = jax.ShapeDtypeStruct
    t, d = n.tokens, n.width
    blocks = n.seq // n.sub
    nb = n.b // (n.sub // 2)
    pairs = (n.rounds, n.seq, n.seq, n.cap, 256)
    unit_c, unit_e, unit_o = (n.units, d), (n.group, n.rows, n.part), (n.rows, d)
    f1, b1, a = max(n.fsdp - 1, 1), max(n.b - 1, 1), n.a
    count_f = (n.fsdp - 1) * a * n.b + (n.b - 1) * a + a - 1
    count_p = (n.fsdp - 1) * a + a - 1

    def sems(k):
        return [DMA((k,)), DMA((k,))]

    return pl.pallas_call(
        functools.partial(back_kernel, n),
        out_shape=(
            shape((t, d), F32), shape((8, 128), F32), shape((n.rows, d), F32), shape((n.rows, d), F32),
            shape((n.rows, d), F32), shape((n.rows, n.hidden), F32), shape((n.units, d), F32),
        ),
        in_specs=[inside] * 2 + [pl.BlockSpec(memory_space=pl.ANY)] + [inside] * 10,
        out_specs=(inside,) * 7,
        scratch_shapes=[
            VM((n.seq, MSG, 128), BF), VM((blocks, 128, d), BF),
            VM(pairs, BF), VM(pairs, BF), VM(pairs, BF), VM(pairs, BF),
            VM(((n.sub - 1) * blocks, 128, 256), BF), VM((blocks, 128, 256), F32), VM(((n.sub - 1) * blocks, 128, 256), BF),
            VM((blocks, 128, 256), BF),
            VM((d, 256), F32), VM((n.all, n.rows, 256), BF), VM((n.all, n.rows, 256), BF),
            VM((blocks, 128, d), BF), VM((max(nb - 1, 1), a, 128, d), BF), VM((a - 1, 128, d), BF),
            VM((f1, a) + unit_c, BF), VM((a - 1,) + unit_c, BF),
            VM((f1, a) + unit_e, BF), VM((a - 1,) + unit_e, BF),
            VM((n.chips, n.fsdp) + unit_o, BF),
            VM((f1, a, n.b) + unit_o, BF), VM((b1, a) + unit_o, BF), VM((a - 1,) + unit_o, BF),
            VM(unit_e, F32), VM(unit_e, F32),
            VM((n.all, 8, 128), F32), VM((n.all, 8, 128), F32),
            *sems(n.seq), *sems(count_p), *sems(count_p), *sems(count_f), *sems(1),
            *sems((n.sub - 1) * blocks), *sems(n.all), *sems(max((nb - 1) * a, 1)), *sems(a), *sems(n.all), DMA((blocks,)), *sems(n.group),
        ],
        compiler_params=pltpu.CompilerParams(collective_id=3, has_side_effects=True, vmem_limit_bytes=60 << 20),
        name="back",
    )(message, qv, nrm, wqv, tab, vec, gwc, gwe, gwo, vec_g, shift_g, second, cot2)


def on_device(
    first_half,
    second_half,
    first_cotangent,
    second_cotangent,
    bucket_ids,
    slot_source,
    live_slots,
    mixer_gain,
    mixer_shift,
    query_weight,
    value_weight,
    output_weight,
    feed_gain,
    feed_shift,
    expand_weight,
    expand_bias,
    contract_weight,
    contract_bias,
):
    seq, fsdp = lax.axis_size("seq"), lax.axis_size("fsdp")
    width, hidden = first_half.shape[2], expand_weight.shape[1]
    n = setup(seq, fsdp, width, hidden, first_half.shape[1])
    first, second = first_half[0], second_half[0]
    cot1, cot2 = first_cotangent[0], second_cotangent[0]
    vectors = jnp.stack([mixer_gain, mixer_shift, feed_gain, feed_shift, contract_bias] + [jnp.zeros_like(mixer_gain)] * 3)
    home, qv, nrm, wqv, tab, vec, shift_part, ci, wo, wc, we = front(
        n, second, cot2, vectors, expand_bias.reshape(1, -1), bucket_ids[0], query_weight, value_weight, expand_weight,
        output_weight, contract_weight,
    )
    first_out, second_out, grad1, gwc, gwe, gwo, message, vec_g, shift_g = feed(
        n, home, first, second, cot1, ci, vec, shift_part,
        wo.reshape(width, width), we.reshape(width, n.part), wc.reshape(n.part, width),
    )
    grad2, small_g, gq, gv, go, ge, gc = back(
        n, message, qv, nrm, wqv, tab, vec,
        gwc.reshape(n.a, fsdp, n.units, width),
        gwe.reshape(n.a, n.group, fsdp, n.rows, n.part),
        gwo.reshape(n.chips, 2, fsdp, n.rows, width),
        vec_g, shift_g, second, cot2,
    )
    me = lax.axis_index("seq") * fsdp + lax.axis_index("fsdp")

    def shard(row, size):
        return lax.dynamic_slice(small_g[row], (lax.rem(me, 128 // size) * size,), (size,))

    return (
        first_out[None], second_out[None], grad1[None], grad2[None],
        shard(0, n.rows), shard(1, n.rows), gq, gv, go,
        shard(2, n.rows), shard(3, n.rows), ge, shard(5, n.units), gc, shard(4, n.rows),
    )


def solution(mesh):
    tokens, slots = P("fsdp", "seq", None), P("fsdp", None, "seq")
    vector, matrix = P(("seq", "fsdp")), P(("seq", "fsdp"), None)
    return jax.shard_map(
        on_device,
        mesh=mesh,
        in_specs=(tokens,) * 4 + (slots,) * 3 + (vector, vector, matrix, matrix, matrix, vector, vector, matrix, vector, matrix, vector),
        out_specs=(tokens,) * 4 + (vector, vector, matrix, matrix, matrix, vector, vector, matrix, vector, matrix, vector),
        check_vma=False,
    )
```

```python
import functools
import types

import jax
import jax.numpy as jnp
from jax import lax
from jax.experimental import pallas as pl
from jax.experimental.pallas import tpu as pltpu
from jax.sharding import PartitionSpec as P

HEADS = 8
HEAD_DIM = 128
ROUNDS = 4
SPAN = 64
BF = jnp.bfloat16
F32 = jnp.float32
MESH = pl.DeviceIdType.MESH
DMA = pltpu.SemaphoreType.DMA
VM = pltpu.VMEM
MSG = 144


def dot(a, b):
    return lax.dot_general(a, b, (((1,), (0,)), ((), ())), preferred_element_type=F32)


def dot_nt(a, b):
    return lax.dot_general(a, b, (((1,), (1,)), ((), ())), preferred_element_type=F32)


def dot_tn(a, b):
    return lax.dot_general(a, b, (((0,), (0,)), ((), ())), preferred_element_type=F32)


def iota(shape, dim):
    return lax.broadcasted_iota(jnp.int32, shape, dim)


def iotaf(shape, dim):
    return iota(shape, dim).astype(F32)


def low(x):
    return x.astype(BF)


def split3(x):
    hi = x.astype(BF).astype(F32)
    rest = x - hi
    mid = rest.astype(BF).astype(F32)
    return hi, mid, rest - mid


def loop(count, body):
    def step(i, carry):
        body(i)
        return carry

    lax.fori_loop(0, count, step, 0)


def push(src, dst, send, recv, dev):
    pltpu.make_async_remote_copy(
        src_ref=src, dst_ref=dst, send_sem=send, recv_sem=recv, device_id=dev, device_id_type=MESH
    ).start()


def wait(ref, sem):
    pltpu.make_async_copy(ref, ref, sem).wait()


def to_column(row):
    size = row.shape[1]
    eye = iota((size, size), 0) == iota((size, size), 1)
    return jnp.sum(jnp.where(eye, row, 0.0), axis=1, keepdims=True)


def to_row(column):
    size = column.shape[0]
    eye = iota((size, size), 0) == iota((size, size), 1)
    return jnp.sum(jnp.where(eye, column, 0.0), axis=0, keepdims=True)


def message_rows(rows):
    at = iota((MSG - 128, 128), 0)
    out = jnp.zeros((MSG - 128, 128), F32)
    for i, row in enumerate(rows):
        out = jnp.where(at == i, row, out)
    return low(out)


def setup(seq, fsdp, width, hidden, tokens):
    n = types.SimpleNamespace()
    n.seq, n.fsdp, n.all = seq, fsdp, seq * fsdp
    n.chips = seq // 2
    n.b = 2 if n.chips <= 8 else 4
    n.a = n.chips // n.b
    n.sub = seq // HEADS
    n.rounds = ROUNDS // n.sub
    n.cap = 4 * SPAN // seq
    n.width, n.hidden, n.tokens = width, hidden, tokens
    n.rows = width // n.all
    n.units = hidden // n.all
    n.group = 2 * n.b
    n.part = hidden // n.group
    n.wide = hidden // seq
    return n


def place(n):
    w = types.SimpleNamespace()
    w.s, w.f = lax.axis_index("seq"), lax.axis_index("fsdp")
    w.c, w.j = w.s // 2, lax.rem(w.s, 2)
    w.a, w.b = w.c // n.b, lax.rem(w.c, n.b)
    w.me = w.s * n.fsdp + w.f
    w.head, w.idx = w.s // n.sub, lax.rem(w.s, n.sub)
    w.sib = (w.s + 1 - 2 * w.j, w.f)
    w.t = w.b * 2 + w.j
    return w


def plane(n, w, a, b, f):
    return ((a * n.b + b) * 2 + w.j, f)


def member(n, w, t):
    return ((w.a * n.b) * 2 + t, w.f)


def peer(n, w, i):
    d = lax.rem(w.me + i, n.all)
    return d, (d // n.fsdp, lax.rem(d, n.fsdp))


def meet_all(n, w):
    barrier = pltpu.get_barrier_semaphore()

    def greet(i):
        pl.semaphore_signal(barrier, inc=1, device_id=peer(n, w, i + 1)[1], device_id_type=MESH)

    loop(n.all - 1, greet)
    pl.semaphore_wait(barrier, n.all - 1)


class Gather:
    def __init__(self, n, w, unit, second, send, recv, arrived=None):
        self.n, self.w, self.unit, self.second = n, w, unit, second
        self.send, self.recv, self.k, self.arrived = send, recv, 0, arrived

    def spot(self, i, q, v):
        n, w = self.n, self.w
        a, b, f = lax.rem(w.a + i, n.a), lax.rem(w.b + v, n.b), lax.rem(w.f + q, n.fsdp)
        return (a, b, f), (a * n.b + b) * n.fsdp + f

    def go(self, at, dev):
        spot, uid = self.spot(*at)
        ref = self.unit(*spot)
        push(ref, ref, self.send(self.k), self.recv(uid), dev)
        self.k += 1

    def get(self, at):
        spot, uid = self.spot(*at)
        wait(self.unit(*spot), self.recv(uid))
        if self.arrived:
            self.arrived(self.unit(*spot), uid)

    def to_a(self):
        n, w = self.n, self.w
        for i in range(1, n.a):
            self.go((0, 0, 0), plane(n, w, lax.rem(w.a + i, n.a), w.b, w.f))

    def to_f(self, at):
        n, w = self.n, self.w
        for m in range(1, n.fsdp):
            self.go(at, plane(n, w, w.a, w.b, lax.rem(w.f + m, n.fsdp)))

    def to_b(self, at):
        n, w = self.n, self.w
        for m in range(1, n.b):
            self.go(at, plane(n, w, w.a, lax.rem(w.b + m, n.b), w.f))

    def column(self, i):
        if i:
            self.get((i, 0, 0))
        if self.second == "f":
            self.to_f((i, 0, 0))
            self.to_b((i, 0, 0))
        else:
            self.to_b((i, 0, 0))
            self.to_f((i, 0, 0))

    def corner(self, i):
        if self.second == "f":
            for q in range(1, self.n.fsdp):
                self.get((i, q, 0))
                self.to_b((i, q, 0))
        else:
            for v in range(1, self.n.b):
                self.get((i, 0, v))
                self.to_f((i, 0, v))

    def finish(self):
        n = self.n
        for i in range(n.a):
            for q in range(n.fsdp):
                for v in range(n.b):
                    if (v if self.second == "f" else q) != 0:
                        self.get((i, q, v))

    def drain(self):
        ref = self.unit(*self.spot(0, 0, 0)[0])
        for k in range(self.k):
            wait(ref, self.send(k))


class PlaneGather:
    def __init__(self, n, w, unit, send, recv):
        self.n, self.w, self.unit, self.send, self.recv, self.k = n, w, unit, send, recv, 0

    def spot(self, i, q):
        a, f = lax.rem(self.w.a + i, self.n.a), lax.rem(self.w.f + q, self.n.fsdp)
        return (a, f), a * self.n.fsdp + f

    def go(self, at, dev):
        spot, uid = self.spot(*at)
        ref = self.unit(*spot)
        push(ref, ref, self.send(self.k), self.recv(uid), dev)
        self.k += 1

    def get(self, at):
        spot, uid = self.spot(*at)
        wait(self.unit(*spot), self.recv(uid))

    def to_a(self):
        for i in range(1, self.n.a):
            self.go((0, 0), plane(self.n, self.w, lax.rem(self.w.a + i, self.n.a), self.w.b, self.w.f))

    def column(self, i):
        if i:
            self.get((i, 0))
        for m in range(1, self.n.fsdp):
            self.go((i, 0), plane(self.n, self.w, self.w.a, self.w.b, lax.rem(self.w.f + m, self.n.fsdp)))

    def corner(self, i):
        pass

    def finish(self):
        for i in range(self.n.a):
            for q in range(1, self.n.fsdp):
                self.get((i, q))

    def drain(self):
        ref = self.unit(*self.spot(0, 0)[0])
        for k in range(self.k):
            wait(ref, self.send(k))


def tables(n, w, small_all, tab):
    nb = 2 * n.seq
    before = low((iota((128, 128), 0) < iota((128, 128), 1)).astype(F32))
    for r in range(n.rounds):
        def bucket_row(p):
            tile = small_all[p * n.fsdp + w.f].astype(F32)
            keep = iota((16, 128), 0) == 8 + w.idx * n.rounds + r
            return jnp.sum(jnp.where(keep, tile, 0.0), axis=0, keepdims=True)

        def count(p, run):
            row = bucket_row(p)
            hot = (iotaf((nb, 128), 0) == row).astype(F32)
            ahead = dot(low(hot), before)
            pos = jnp.sum(hot * (ahead + run), axis=0, keepdims=True)
            group = jnp.floor(row * 0.5)
            hotg = (iotaf((n.seq, 128), 0) == group).astype(F32)
            rank = jnp.sum(hotg * dot(low(hotg), before), axis=0, keepdims=True)
            line = group * n.cap + rank
            at = iota((8, 128), 0)
            tab[r, p] = jnp.where(at == 0, line, jnp.where(at == 1, pos, jnp.where(at == 2, row, 0.0)))
            return run + jnp.sum(hot, axis=1, keepdims=True)

        totals = lax.fori_loop(0, n.seq, count, jnp.zeros((nb, 1), F32))

        def settle(p):
            tile = tab[r, p]
            row = tile[2:3]
            odd = row - 2.0 * jnp.floor(row * 0.5)
            hot = (iotaf((nb, 128), 0) == row - 1.0).astype(F32)
            slot = tile[1:2] + odd * jnp.sum(hot * totals, axis=0, keepdims=True)
            block = jnp.floor(slot * (1.0 / SPAN))
            tab[r, p] = jnp.where(iota((8, 128), 0) == 1, block, tile)

        loop(n.seq, settle)


def picks(n, tile):
    return low((iotaf((n.seq * n.cap, 128), 0) == tile[0:1]).astype(F32))


def picks_back(n, tile):
    return low((iotaf((128, n.seq * n.cap), 1) == to_column(tile[0:1])).astype(F32))


def block_marks(tile):
    lane = iota((128, 128), 1)
    return low(jnp.where(lane == 0, to_column(tile[1:2]), jnp.where(lane == 1, 1.0, 0.0)))


def gap_form():
    i, k = iota((128, 128), 0), iota((128, 128), 1)
    value = jnp.where((i == 0) & (k == 1), 1.0, jnp.where((i == 1) & (k == 0), -1.0, 0.0))
    return low(jnp.where((i == 1) & (k == 1), -8.0, value))


def rows_of(n, ref):
    got = ref[...]
    if n.cap % 16:
        return low(got.astype(F32).reshape(n.seq * n.cap, got.shape[-1]))
    return got.reshape(n.seq * n.cap, got.shape[-1])


def put_rows(n, ref, value):
    ref[...] = value.reshape(n.seq, n.cap, value.shape[-1]).astype(ref.dtype)


def masked(n, marks, raw):
    size = n.seq * n.cap
    gap = dot_nt(low(dot(marks, gap_form())), marks)
    ahead = iota((size, size), 1) < iota((size, size), 0)
    allowed = ahead & ((gap == -8.0) | (gap == -7.0))
    same = iota((size, size), 1) == iota((size, size), 0)
    return allowed, jnp.where(allowed, raw, jnp.where(same, -1e4, -1e9))


def keys_of(query):
    wide = query.astype(F32)
    scale = lax.rsqrt(jnp.sum(wide * wide, axis=1, keepdims=True) + 1e-06)
    return low(wide * scale), scale


def fill_block(n, r, p, tab, qv, buf, marks):
    tile = tab[r, p]
    hot = picks(n, tile)
    got = dot(hot, jnp.concatenate([qv[p], block_marks(tile)], axis=1))
    put_rows(n, buf.at[r, :, p], got[:, :256])
    put_rows(n, marks.at[r, :, p], got[:, 256:])


def attend(n, r, g, buf, marks, obuf):
    both = rows_of(n, buf.at[r, g])
    query, value = both[:, :128], both[:, 128:]
    key, _ = keys_of(query)
    _, score = masked(n, rows_of(n, marks.at[r, g]), dot_nt(query, key))
    top = jnp.max(score, axis=1, keepdims=True)
    expo = jnp.exp(score - top)
    total = jnp.sum(expo, axis=1, keepdims=True)
    out = dot(low(expo), value) / total
    hi, mid, rest = split3(top + jnp.log(total))
    lane = iota((n.seq * n.cap, 128), 1)
    logs = jnp.where(lane == 0, hi, jnp.where(lane == 1, mid, jnp.where(lane == 2, rest, 0.0)))
    put_rows(n, obuf.at[r, :, g], jnp.concatenate([out, logs], axis=1))


def merge(outs, logs):
    top = functools.reduce(jnp.maximum, logs)
    weights = [jnp.exp(v - top) for v in logs]
    total = sum(weights)
    return sum(x * y for x, y in zip(weights, outs)) / total, top + jnp.log(total)


def merge_rounds(n, p, tab, obuf):
    outs, logs = [], []
    for r in range(n.rounds):
        got = dot(picks_back(n, tab[r, p]), rows_of(n, obuf.at[r, p]))
        outs.append(got[:, :128])
        logs.append(jnp.sum(got[:, 128:], axis=1, keepdims=True))
    return merge(outs, logs)


def write_message(ref, out, log):
    ref[:128] = low(out)
    ref[128:] = message_rows(split3(to_row(log)))


def read_log(ref):
    return to_column(jnp.sum(ref[128:].astype(F32), axis=0, keepdims=True))


def hat_of(x):
    center = x - jnp.mean(x, axis=1, keepdims=True)
    scale = lax.rsqrt(jnp.mean(center * center, axis=1, keepdims=True) + 1e-05)
    return center * scale, scale


def normalize(x, gain, shift):
    hat, scale = hat_of(x)
    return hat, scale, hat * gain + shift


def placed(row, spot):
    size = row.shape[1]
    put = (iota((size, 128), 1) == iota((size, 128), 0) + spot * size).astype(F32)
    return dot(row, low(put))


def gelu_pair(x):
    k = 0.7978845608028654
    square = x * x
    t = jnp.tanh(k * (x + 0.044715 * (square * x)))
    half = 0.5 * (1.0 + t)
    return x * half, half + 0.5 * x * (1.0 - t * t) * (k * (1.0 + 0.134145 * square))


class GroupSum:
    def __init__(self, n, w, out, got1, got2, send, recv):
        self.n, self.w, self.out, self.got1, self.got2 = n, w, out, got1, got2
        self.send, self.recv = send, recv

    def fill(self, product):
        n, w = self.n, self.w
        for m in range(n.b):
            b = lax.rem(w.b + 1 + m, n.b)
            self.out[pl.ds(2 * b, 2)] = low(product(b)).reshape(2, n.tokens, n.width)
            t = b * 2 + 1 - w.j
            push(self.out.at[t], self.got1.at[b], self.send.at[m], self.recv.at[b], w.sib)

    def chips(self):
        n, w = self.n, self.w
        for m in range(1, n.b):
            b = lax.rem(w.b + m, n.b)
            t = b * 2 + w.j
            wait(self.got1.at[b], self.recv.at[b])
            self.out[t] = low(self.out[t].astype(F32) + self.got1[b].astype(F32))
            k = n.b + m - 1
            push(self.out.at[t], self.got2.at[m - 1], self.send.at[k], self.recv.at[k], member(n, w, t))

    def total(self):
        n, w = self.n, self.w
        wait(self.got1.at[w.b], self.recv.at[w.b])
        total = self.out[w.t].astype(F32) + self.got1[w.b].astype(F32)
        for m in range(1, n.b):
            wait(self.got2.at[m - 1], self.recv.at[n.b + m - 1])
            total += self.got2[m - 1].astype(F32)
        return total

    def drain(self):
        for k in range(2 * self.n.b - 1):
            wait(self.got1.at[0], self.send.at[k])


class Scatter:
    def __init__(self, n, w, outer, part, got1, got2, got3, send, recv):
        self.n, self.w, self.outer, self.part = n, w, outer, part
        self.got1, self.got2, self.got3 = got1, got2, got3
        self.send, self.recv = send, recv
        self.one, self.two = (n.fsdp, n.b) if outer == "f" else (n.b, n.fsdp)
        self.me1, self.me2 = (w.f, w.b) if outer == "f" else (w.b, w.f)
        self.base2 = (self.one - 1) * n.a * self.two
        self.base3 = self.base2 + (self.two - 1) * n.a

    def mine(self, a, one, two):
        return self.part(a, two, one) if self.outer == "f" else self.part(a, one, two)

    def dev(self, a, one, two):
        if self.outer == "f":
            return plane(self.n, self.w, a, two, one)
        return plane(self.n, self.w, a, one, two)

    def first(self):
        for m in range(1, self.one):
            far = lax.rem(self.me1 + m, self.one)

            def body(i, m=m, far=far):
                a, two = i // self.two, lax.rem(i, self.two)
                k = (m - 1) * self.n.a * self.two + i
                push(self.mine(a, far, two), self.got1.at[m - 1, a, two], self.send.at[k], self.recv.at[k],
                     self.dev(self.w.a, far, self.me2))

            loop(self.n.a * self.two, body)

    def second(self):
        def body(i):
            m2, a = i // self.n.a, lax.rem(i, self.n.a)
            two = lax.rem(self.me2 + 1 + m2, self.two)
            for m in range(1, self.one):
                k = (m - 1) * self.n.a * self.two + a * self.two + two
                wait(self.got1.at[m - 1, a, two], self.recv.at[k])
            self.fold1(a, two)

            @pl.when(m2 < self.two - 1)
            def _():
                k = self.base2 + m2 * self.n.a + a
                push(self.got1.at[0, a, two], self.got2.at[m2, a], self.send.at[k], self.recv.at[k],
                     self.dev(self.w.a, self.me1, two))

        loop(self.n.a * self.two, body)

    def fold1(self, a, two):
        total = self.mine(a, self.me1, two)[...].astype(F32)
        for m in range(1, self.one):
            total += self.got1[m - 1, a, two].astype(F32)
        self.got1[0, a, two] = low(total)

    def third(self):
        def body(i):
            a = lax.rem(self.w.a + 1 + i, self.n.a)
            for m2 in range(self.two - 1):
                wait(self.got2.at[m2, a], self.recv.at[self.base2 + m2 * self.n.a + a])
            total = self.got1[0, a, self.me2].astype(F32)
            for m2 in range(self.two - 1):
                total += self.got2[m2, a].astype(F32)
            self.got2[0, a] = low(total)

            @pl.when(i < self.n.a - 1)
            def _():
                k = self.base3 + i
                push(self.got2.at[0, a], self.got3.at[i], self.send.at[k], self.recv.at[k],
                     self.dev(a, self.me1, self.me2))

        loop(self.n.a, body)

    def total(self):
        total = self.got2[0, self.w.a].astype(F32)
        for i in range(self.n.a - 1):
            wait(self.got3.at[i], self.recv.at[self.base3 + i])
            total += self.got3[i].astype(F32)
        return total

    def drain(self):
        loop(self.base3 + self.n.a - 1, lambda k: wait(self.got3.at[0], self.send.at[k]))


class PlaneScatter:
    def __init__(self, n, w, part, got1, got2, send, recv):
        self.n, self.w, self.part, self.got1, self.got2, self.send, self.recv = n, w, part, got1, got2, send, recv
        self.base = (n.fsdp - 1) * n.a

    def first(self):
        n, w = self.n, self.w
        for m in range(1, n.fsdp):
            far = lax.rem(w.f + m, n.fsdp)

            def body(i, m=m, far=far):
                a = lax.rem(w.a + 1 + i, n.a)
                k = (m - 1) * n.a + a
                push(self.part(a, far), self.got1.at[m - 1, a], self.send.at[k], self.recv.at[k], plane(n, w, w.a, w.b, far))

            loop(n.a, body)

    def second(self, i):
        n, w = self.n, self.w
        a = lax.rem(w.a + 1 + i, n.a)
        total = self.part(a, w.f)[...].astype(F32)
        for m in range(1, n.fsdp):
            wait(self.got1.at[m - 1, a], self.recv.at[(m - 1) * n.a + a])
            total += self.got1[m - 1, a].astype(F32)
        self.got1[0, a] = low(total)
        if i < n.a - 1:
            k = self.base + i
            push(self.got1.at[0, a], self.got2.at[i], self.send.at[k], self.recv.at[k], plane(n, w, a, w.b, w.f))

    def total(self):
        total = self.got1[0, self.w.a].astype(F32)
        for i in range(self.n.a - 1):
            wait(self.got2.at[i], self.recv.at[self.base + i])
            total += self.got2[i].astype(F32)
        return total

    def drain(self):
        loop(self.base + self.n.a - 1, lambda k: wait(self.got2.at[0], self.send.at[k]))


def spread(n, r, p, tab, dtok, dbuf, marks):
    tile = tab[r, p]
    shift = low((iota((MSG - 128, 128), 0) + 2 == iota((MSG - 128, 128), 1)).astype(F32))
    marked = block_marks(tile) + low(dot_tn(dtok[p, 128:], shift))
    got = dot(picks(n, tile), jnp.concatenate([dtok[p, :128], marked], axis=1))
    put_rows(n, dbuf.at[r, :, p], got[:, :128])
    put_rows(n, marks.at[r, :, p], got[:, 128:])


def attend_back(n, r, g, buf, marks, dbuf, gbuf):
    both, cot, marked = rows_of(n, buf.at[r, g]), rows_of(n, dbuf.at[r, g]), rows_of(n, marks.at[r, g])
    query, value = both[:, :128], both[:, 128:]
    aux = marked.astype(F32)
    lane = iota(aux.shape, 1)
    log_all = jnp.sum(jnp.where((lane >= 2) & (lane < 5), aux, 0.0), axis=1, keepdims=True)
    delta = jnp.sum(jnp.where(lane >= 5, aux, 0.0), axis=1, keepdims=True)
    key, scale = keys_of(query)
    allowed, score = masked(n, marked, dot_nt(query, key))
    prob = jnp.exp(score - log_all)
    back_score = low(jnp.where(allowed, prob * (dot_nt(cot, value) - delta), 0.0))
    direct = dot(back_score, key)
    back_key = dot_tn(back_score, query)
    back_value = dot_tn(low(prob), cot)
    wide = query.astype(F32)
    inner = jnp.sum(wide * back_key, axis=1, keepdims=True)
    total = direct + scale * back_key - wide * (scale * scale * scale * inner)
    put_rows(n, gbuf.at[r, :, g], jnp.concatenate([total, back_value], axis=1))


RELAYS = (0, 0, 0, 0, 0, 1, 1, 1, 1)
SUMS = (0, 0, 1, 1, 1, 1, 1, 1)


def greet_all(n, w, barrier):
    def greet(i):
        pl.semaphore_signal(barrier, inc=1, device_id=peer(n, w, i + 1)[1], device_id_type=MESH)

    loop(n.all - 1, greet)


def pack(n, w, x):
    x.ci[w.t] = low(x.cot2[...])
    for t in range(n.group):
        for a in range(n.a):
            s = a * n.group + t
            x.we_in[t, :, a * n.wide:(a + 1) * n.wide] = x.expand_w[:, s * n.wide:(s + 1) * n.wide]
    for h in range(HEADS):
        x.wqv_in[h, :, :128] = x.query_w[:, h * 128:(h + 1) * 128]
        x.wqv_in[h, :, 128:] = x.value_w[:, h * 128:(h + 1) * 128]
    lead = placed(x.vectors[...], lax.rem(w.me, 128 // n.rows))
    extra = placed(jnp.broadcast_to(x.bias[...], (8, n.units)), lax.rem(w.me, 128 // n.units))
    lead = jnp.where(iota((8, 128), 0) == 5, extra, lead)
    x.small_all[w.me] = low(jnp.concatenate([lead, x.buckets[...].astype(F32), jnp.zeros((8 - ROUNDS, 128), F32)]))
    x.wqv[w.me] = x.wqv_in[w.head]
    x.wo[w.me] = x.wo_in[...]
    x.wc[w.a, w.f] = x.wc_in[...]
    x.we[w.a, w.t, w.f] = x.we_in[w.t]


def vectors_of(n, w, x):
    group = 128 // n.rows
    for q in range(n.width // 128):
        x.vec[:, q * 128:(q + 1) * 128] = jnp.sum(
            x.small_all[q * group:(q + 1) * group].astype(F32), axis=0
        )
    per = 128 // n.units
    for q in range(n.a * n.fsdp // per):
        a, rest = q * per // n.fsdp, q * per % n.fsdp
        first = (a * n.group + w.t) * n.fsdp + rest
        total = sum(x.small_all[first + k].astype(F32) for k in range(per))
        x.shift_part[:, q * 128:(q + 1) * 128] = jnp.broadcast_to(total[5:6], (8, 128))


def front_part(n, w, x, obuf, pmsg, omsg):
    barrier = pltpu.get_barrier_semaphore()
    greet_all(n, w, barrier)
    hat, _ = hat_of(x.second[...])
    x.xh[w.s] = low(hat)
    pack(n, w, x)
    pl.semaphore_wait(barrier, n.all - 1)

    def spot(i, v):
        return (lax.rem(w.a + i, n.a) * n.b + lax.rem(w.b + v, n.b)) * 2 + w.j

    sent = [0, 0]

    def send_hat(block, dev):
        push(x.xh.at[block], x.xh.at[block], x.s_n.at[sent[0]], x.r_n.at[block // 2], dev)
        sent[0] += 1

    def share_hat(block):
        push(x.xh.at[block], x.xh.at[block], x.s_ns.at[sent[1]], x.r_ns.at[block // 2], w.sib)
        sent[1] += 1

    for i in range(1, n.a):
        send_hat(w.s, (spot(i, 0), w.f))
    for v in range(1, n.b):
        send_hat(w.s, (spot(0, v), w.f))
    share_hat(w.s)
    for m in range(1, n.group):
        t = lax.rem(w.t + m, n.group)
        push(x.we_in.at[t], x.we.at[w.a, w.t, w.f], x.s_ex.at[m], x.r_ex.at[w.t], member(n, w, t))

    def send_small(i):
        _, dev = peer(n, w, i + 1)
        push(x.small_all.at[w.me], x.small_all.at[w.me], x.s_small.at[i], x.r_small.at[w.me], dev)

    loop(n.all - 1, send_small)

    def send_w(i):
        _, dev = peer(n, w, i + 1)
        push(x.wqv_in.at[dev[0] // n.sub], x.wqv.at[w.me], x.s_w.at[i], x.r_w.at[w.me], dev)

    loop(n.all - 1, send_w)

    def shared_o(ref, uid):
        push(ref, ref, x.s_os.at[uid], x.r_os.at[uid], w.sib)

    g_o = Gather(n, w, lambda a, b, f: x.wo.at[((a * n.b + b) * 2 + w.j) * n.fsdp + f], "f", lambda k: x.s_ag.at[0, k], lambda u: x.r_ag.at[0, u], shared_o)
    g_c = PlaneGather(n, w, lambda a, f: x.wc.at[a, f], lambda k: x.s_ag.at[1, k], lambda u: x.r_ag.at[1, u])
    g_e = PlaneGather(n, w, lambda a, f: x.we.at[a, :, f], lambda k: x.s_ag.at[2, k], lambda u: x.r_ag.at[2, u])
    gathers = (g_o, g_c, g_e)
    for m in range(1, n.group):
        t = lax.rem(w.t + m, n.group)
        wait(x.we.at[w.a, t, w.f], x.r_ex.at[t])
        push(x.ci.at[w.t], x.ci.at[w.t], x.s_ci.at[m], x.r_ci.at[w.t], member(n, w, t))
    shared_o(x.wo.at[w.me], (w.a * n.b + w.b) * n.fsdp + w.f)
    for y in gathers:
        y.column(0)

    def wait_small(i):
        d, _ = peer(n, w, i + 1)
        wait(x.small_all.at[d], x.r_small.at[d])

    loop(n.all - 1, wait_small)
    vectors_of(n, w, x)
    tables(n, w, x.small_all, x.tab)
    weights = x.wqv.reshape(n.width, 256)

    def project(block):
        normed = low(x.xh[block].astype(F32) * x.vec[0:1] + x.vec[1:2])

        @pl.when(lax.rem(block, n.sub) == w.idx)
        def _():
            x.nown[block // n.sub] = normed

        x.qv[block] = low(dot(normed, weights[...]))

    for i in range(1, n.a):
        block = spot(i, 0)
        wait(x.xh.at[block], x.r_n.at[block // 2])
        for v in range(1, n.b):
            send_hat(block, (spot(0, v), w.f))
        share_hat(block)
    for y in gathers:
        y.to_a()

    def wait_w(i):
        d, _ = peer(n, w, i + 1)
        wait(x.wqv.at[d], x.r_w.at[d])

    loop(n.all - 1, wait_w)
    project(w.s)
    for i in range(1, n.a):
        project(spot(i, 0))
    for i in range(n.a):
        for v in range(1, n.b):
            block = spot(i, v)
            wait(x.xh.at[block], x.r_n.at[block // 2])
            share_hat(block)
            project(block)

    def from_sibling(c):
        block = 2 * c + 1 - w.j
        wait(x.xh.at[block], x.r_ns.at[c])
        project(block)

    loop(n.chips, from_sibling)

    tasks = []
    for i in range(n.a):
        if i:
            tasks.append(lambda i=i: [y.column(i) for y in gathers])
        tasks.append(lambda i=i: g_o.corner(i))

    def relay(count):
        for _ in range(count):
            if tasks:
                tasks.pop(0)()

    for r in range(n.rounds):
        loop(n.seq, lambda p: fill_block(n, r, p, x.tab, x.qv, x.buf, x.marks))
    relay(RELAYS[0])
    parts = 4
    slot = 1
    for r in range(n.rounds):
        for q in range(parts):
            loop(n.seq // parts, lambda g: attend(n, r, q * (n.seq // parts) + g, x.buf, x.marks, obuf))
            relay(RELAYS[slot])
            slot += 1

    blocks = n.seq // n.sub
    for m in range(1, n.sub):
        far = lax.rem(w.idx + m, n.sub)

        def offer(i, m=m, far=far):
            k = (m - 1) * blocks + i
            write_message(pmsg.at[k], *merge_rounds(n, i * n.sub + far, x.tab, obuf))
            push(pmsg.at[k], x.pin.at[k], x.s_p.at[k], x.r_p.at[k], (w.head * n.sub + far, w.f))

        loop(blocks, offer)

    def settle(i):
        out, log = merge_rounds(n, i * n.sub + w.idx, x.tab, obuf)
        outs, logs = [out], [log]
        for m in range(1, n.sub):
            k = (m - 1) * blocks + i
            wait(x.pin.at[k], x.r_p.at[k])
            outs.append(x.pin[k, :128].astype(F32))
            logs.append(read_log(x.pin.at[k]))
        write_message(omsg.at[i], *merge(outs, logs))

    def give(i):
        to = lax.rem(w.head + 1 + i, blocks)
        settle(to)
        push(omsg.at[to], x.home.at[w.head], x.s_out.at[i], x.r_out.at[w.head], (to * n.sub + w.idx, w.f))

    loop(blocks - 1, give)
    settle(w.head)
    x.home[w.head] = omsg[w.head]
    relay(len(tasks))

    def take(i):
        h = lax.rem(w.head + 1 + i, HEADS)
        wait(x.home.at[h], x.r_out.at[h])

    loop(HEADS - 1, take)
    g_o.finish()
    loop(n.chips * n.fsdp, lambda u: wait(x.wo.at[w.me], x.r_os.at[u]))

    loop((n.sub - 1) * blocks, lambda k: wait(pmsg.at[0], x.s_p.at[k]))
    loop(blocks - 1, lambda k: wait(omsg.at[0], x.s_out.at[k]))

    def drain():
        g_c.finish()
        g_e.finish()
        for y in gathers:
            y.drain()
        loop(n.chips * n.fsdp, lambda u: wait(x.wo.at[w.me], x.s_os.at[u]))
        for m in range(1, n.group):
            t = lax.rem(w.t + m, n.group)
            wait(x.we_in.at[0], x.s_ex.at[m])
            wait(x.ci.at[t], x.r_ci.at[t])
            wait(x.ci.at[t], x.s_ci.at[m])

        def wait_sends(i):
            wait(x.small_all.at[w.me], x.s_small.at[i])
            wait(x.wqv.at[w.me], x.s_w.at[i])

        loop(n.all - 1, wait_sends)
        for k in range(sent[0]):
            wait(x.xh.at[w.s], x.s_n.at[k])
        for k in range(sent[1]):
            wait(x.xh.at[w.s], x.s_ns.at[k])

    return drain


def feed_part(n, w, x, sums, drain, mixed_low, act, gp, out):
    sum_c, sum_e, _ = sums
    for h in range(HEADS):
        mixed_low[:, h * 128:(h + 1) * 128] = x.home[h, :128]
    first_out = x.first[...] + dot(mixed_low[...], x.wo.reshape(n.width, n.width)[...])
    x.first_o[...] = first_out
    hat, scale, normed = normalize(first_out, x.vec[2:3], x.vec[3:4])
    x.n2[w.t] = low(normed)
    k = 0
    for m in range(1, n.b):
        t = lax.rem(w.b + m, n.b) * 2 + w.j
        push(x.n2.at[w.t], x.n2.at[w.t], x.s_x.at[k], x.r_x.at[w.t], member(n, w, t))
        k += 1
    push(x.n2.at[w.t], x.n2.at[w.t], x.s_x.at[k], x.r_x.at[w.t], w.sib)
    k += 1
    drain()
    for m in range(1, n.b):
        t = lax.rem(w.b + m, n.b) * 2 + w.j
        wait(x.n2.at[t], x.r_x.at[t])
        push(x.n2.at[t], x.n2.at[t], x.s_x.at[k], x.r_x.at[t], w.sib)
        k += 1
    for b in range(n.b):
        t = b * 2 + 1 - w.j
        wait(x.n2.at[t], x.r_x.at[t])
    size = n.group * n.tokens
    step = min(512, n.part)
    tokens = x.n2.reshape(size, n.width)
    cots = x.ci.reshape(size, n.width)
    we = x.we.reshape(n.width, n.part)
    wc = x.wc.reshape(n.part, n.width)
    for q in range(n.part // step):
        at = slice(q * step, (q + 1) * step)
        pre = dot(tokens[...], we[:, at]) + x.shift_part[0:1, at]
        value, slope = gelu_pair(pre)
        act[:, at] = low(value)
        back = low(dot_nt(cots[...], wc[at]) * slope)
        gp[:, at] = back
        x.shift_g[:, at] = jnp.broadcast_to(jnp.sum(back.astype(F32), axis=0, keepdims=True), (8, step))
    gn = GroupSum(n, w, out, x.gn_got1, x.gn_got2, x.s_gn, x.r_gn)
    so = GroupSum(n, w, out, x.so_got1, x.so_got2, x.s_so, x.r_so)
    pair = 2 * n.tokens
    gn.fill(lambda b: dot_nt(gp[pl.ds(pl.multiple_of(b * pair, pair), pair)], we[...]))
    x.gwc.reshape(n.part, n.width)[...] = low(dot_tn(act[...], cots[...]))
    sum_c.first()
    gn.chips()
    x.gwe.reshape(n.width, n.part)[...] = low(dot_tn(tokens[...], gp[...]))
    sum_e.first()
    grad = gn.total()
    rest = grad * x.vec[2:3]
    mean = jnp.mean(rest, axis=1, keepdims=True)
    tilt = jnp.mean(rest * hat, axis=1, keepdims=True)
    grad1 = x.cot1[...] + scale * (rest - mean - hat * tilt)
    x.grad1_o[...] = grad1
    branch = low(grad1)
    wo = x.wo.reshape(n.width, n.width)
    for h in range(HEADS):
        gm = dot_nt(branch, wo[h * 128:(h + 1) * 128])
        x.message[h, :128] = low(gm)
        delta = jnp.sum(gm * x.home[h, :128].astype(F32), axis=1, keepdims=True)
        logs = x.home[h, 128:].astype(F32)
        x.message[h, 128:] = message_rows((logs[0:1], logs[1:2], logs[2:3]) + split3(to_row(delta)))

    def give(i):
        s = lax.rem(w.s + 1 + i, n.seq)
        push(x.message.at[s // n.sub], x.dtok.at[w.s], x.s_d.at[i], x.r_d.at[w.s], (s, w.f))

    loop(n.seq - 1, give)
    x.dtok[w.s] = x.message[w.head]
    gwo = low(dot_tn(mixed_low[...], branch)).reshape(n.chips, 2, n.fsdp * n.rows, n.width)
    x.gwo[...] = gwo.reshape(n.chips, 2, n.fsdp, n.rows, n.width)
    push(x.gwo.at[:, 1 - w.j], x.o0, x.s_o0.at[0], x.r_o0.at[0], w.sib)
    gn.drain()
    so.fill(lambda b: dot(act[pl.ds(pl.multiple_of(b * pair, pair), pair)], wc[...]))
    zero = jnp.zeros((2, n.width), F32)
    x.vec_g[...] = jnp.concatenate([
        zero,
        jnp.sum(grad * hat, axis=0, keepdims=True),
        jnp.sum(grad, axis=0, keepdims=True),
        jnp.sum(x.ci[w.t].astype(F32), axis=0, keepdims=True),
        zero, zero[:1],
    ])
    so.chips()
    x.second_o[...] = x.second[...] + so.total() + x.vec[4:5]
    for i in range(k):
        wait(x.n2.at[0], x.s_x.at[i])
    so.drain()


def back_attention(n, w, x, sums, dbuf, gbuf, gout):
    sum_c, sum_e, sum_o = sums
    blocks = n.seq // n.sub
    wait(x.o0, x.r_o0.at[0])

    def join_o(c):
        x.o0[c] = low(x.o0[c].astype(F32) + x.gwo[c, w.j].astype(F32))

    loop(n.chips, join_o)
    sum_o.first()

    def take(i):
        p = lax.rem(w.s + 1 + i, n.seq)
        wait(x.dtok.at[p], x.r_d.at[p])

    loop(n.seq - 1, take)
    tasks = []
    for i in range(n.a):
        tasks.append(lambda i=i: (sum_c.second(i), sum_e.second(i)))
    tasks.insert(2, sum_o.second)
    tasks.append(sum_o.third)

    def relay(count):
        for _ in range(count):
            if tasks:
                tasks.pop(0)()

    slot = 0
    parts = 4
    for r in range(n.rounds):
        loop(n.seq, lambda p: spread(n, r, p, x.tab, x.dtok, dbuf, x.marks))
        for q in range(parts):
            loop(n.seq // parts, lambda g: attend_back(n, r, q * (n.seq // parts) + g, x.buf, x.marks, dbuf, gbuf))
            relay(SUMS[slot])
            slot += 1
    relay(len(tasks))

    def tokens_of(p):
        total = None
        for r in range(n.rounds):
            got = dot(picks_back(n, x.tab[r, p]), rows_of(n, gbuf.at[r, p]))
            total = got if total is None else total + got
        return total

    for m in range(1, n.sub):
        far = lax.rem(w.idx + m, n.sub)

        def offer(i, m=m, far=far):
            k = (m - 1) * blocks + i
            gout[k] = low(tokens_of(i * n.sub + far))
            push(gout.at[k], x.gin.at[k], x.s_g.at[k], x.r_g.at[k], (w.head * n.sub + far, w.f))

        loop(blocks, offer)

    def keep(i):
        x.gown[i] = tokens_of(i * n.sub + w.idx)

    loop(blocks, keep)
    loop((n.sub - 1) * blocks, lambda k: wait(gout.at[0], x.s_g.at[k]))


def back_rest(n, w, x, sums, dqv, wsum, wout, esw, vsend):
    sum_c, sum_e, sum_o = sums
    blocks = n.seq // n.sub
    weights = x.wqv.reshape(n.width, 256)
    bs = n.sub // 2
    nb = n.b // bs
    half_b = w.b // bs
    base1 = blocks
    base2 = base1 + (nb - 1) * n.a

    def finish_block(i):
        total = x.gown[i]
        for m in range(1, n.sub):
            k = (m - 1) * blocks + i
            wait(x.gin.at[k], x.r_g.at[k])
            total += x.gin[k].astype(F32)
        dqv[i] = low(total)
        x.xh[i] = low(dot_nt(dqv[i], weights[...]))

    def chip_of(a, v):
        return plane(n, w, a, v * bs + lax.rem(w.b, bs), w.f)

    for m in range(1, nb):
        far = lax.rem(half_b + m, nb)

        def to_b(i, m=m, far=far):
            a = lax.rem(w.a + 1 + i, n.a)
            finish_block(a * nb + far)
            k = (m - 1) * n.a + a
            push(x.xh.at[a * nb + far], x.xh.at[base1 + k], x.s_n1.at[k], x.r_n1.at[k], chip_of(w.a, far))

        loop(n.a, to_b)
    loop(n.a, lambda i: finish_block(lax.rem(w.a + 1 + i, n.a) * nb + half_b))

    def to_a(i):
        a = lax.rem(w.a + 1 + i, n.a)
        total = x.xh[a * nb + half_b].astype(F32)
        for m in range(1, nb):
            k = (m - 1) * n.a + a
            wait(x.xh.at[base1 + k], x.r_n1.at[k])
            total += x.xh[base1 + k].astype(F32)
        x.xh[a * nb + half_b] = low(total)

        @pl.when(i < n.a - 1)
        def _():
            push(x.xh.at[a * nb + half_b], x.xh.at[base2 + i], x.s_n2.at[i], x.r_n2.at[i], chip_of(a, half_b))

    loop(n.a, to_a)

    for i in range(blocks):
        got = dot_tn(x.nown[i], dqv[i])
        wsum[...] = got if i == 0 else wsum[...] + got
    wout[...] = low(wsum[...]).reshape(n.all, n.rows, 256)

    def rows_out(i):
        d, dev = peer(n, w, i + 1)
        push(wout.at[d], x.win.at[w.me], x.s_small.at[i], x.r_w2.at[w.me], dev)

    loop(n.all - 1, rows_out)
    x.win[w.me] = wout[w.me]

    hat, scale = hat_of(x.second[...])
    grad = x.xh[w.a * nb + half_b].astype(F32)
    for i in range(n.a - 1):
        wait(x.xh.at[base2 + i], x.r_n2.at[i])
        grad += x.xh[base2 + i].astype(F32)
    rest = grad * x.vec[0:1]
    mean = jnp.mean(rest, axis=1, keepdims=True)
    tilt = jnp.mean(rest * hat, axis=1, keepdims=True)
    x.grad2_o[...] = x.cot2[...] + scale * (rest - mean - hat * tilt)
    gain_g = jnp.sum(grad * hat, axis=0, keepdims=True)
    shift1_g = jnp.sum(grad, axis=0, keepdims=True)
    group = 128 // n.rows
    per = 128 // n.units
    at = iota((8, 128), 0)

    def rolled(tile, lanes):
        return pltpu.roll(tile, 128 - lanes, 1) if lanes else tile

    for q in range(n.width // 128):
        cut = slice(q * 128, (q + 1) * 128)
        tile = jnp.where(at == 0, gain_g[:, cut], jnp.where(at == 1, shift1_g[:, cut], x.vec_g[:, cut]))
        for k in range(group):
            vsend[q * group + k] = rolled(tile, k * n.rows)
    for q in range(n.a * n.fsdp // per):
        for k in range(per):
            u = q * per + k
            d = (u // n.fsdp * n.group + w.t) * n.fsdp + u % n.fsdp
            tile = rolled(x.shift_g[:, q * 128:(q + 1) * 128], k * n.units)
            vsend[d] = jnp.where(at == 5, tile, vsend[d])

    def vec_out(i):
        d, dev = peer(n, w, i + 1)
        push(vsend.at[d], x.vgot.at[w.me], x.s_w.at[i], x.r_v.at[w.me], dev)

    loop(n.all - 1, vec_out)
    x.vgot[w.me] = vsend[w.me]

    esw[...] = sum_e.total()
    x.egot[w.t] = esw[w.t]
    for m in range(1, n.group):
        t = lax.rem(w.t + m, n.group)
        push(esw.at[t], x.egot.at[w.t], x.s_y.at[m], x.r_y.at[w.t], member(n, w, t))
    x.go_o[...] = sum_o.total()
    x.gc_o[...] = sum_c.total()

    def take_rows(i):
        d, _ = peer(n, w, i + 1)
        wait(x.win.at[d], x.r_w2.at[d])

    loop(n.all - 1, take_rows)
    for h in range(HEADS):
        total = 0.0
        for i in range(n.sub * n.fsdp):
            total += x.win[h * n.sub * n.fsdp + i].astype(F32)
        x.gq_o[:, h * 128:(h + 1) * 128] = total[:, :128]
        x.gv_o[:, h * 128:(h + 1) * 128] = total[:, 128:]
    for m in range(1, n.group):
        t = lax.rem(w.t + m, n.group)
        wait(x.egot.at[t], x.r_y.at[t])
    for t in range(n.group):
        for a in range(n.a):
            c = (a * n.group + t) * n.wide
            x.ge_o[:, c:c + n.wide] = x.egot[t, :, a * n.wide:(a + 1) * n.wide]

    wait(x.o0, x.s_o0.at[0])
    for m in range(1, n.group):
        wait(x.egot.at[0], x.s_y.at[m])
    loop(n.seq - 1, lambda i: wait(x.dtok.at[0], x.s_d.at[i]))
    for y in (sum_c, sum_e, sum_o):
        y.drain()
    loop((nb - 1) * n.a, lambda k: wait(x.xh.at[0], x.s_n1.at[k]))
    loop(n.a - 1, lambda k: wait(x.xh.at[0], x.s_n2.at[k]))

    def wait_all(i):
        wait(x.win.at[0], x.s_small.at[i])
        wait(x.vgot.at[0], x.s_w.at[i])

    loop(n.all - 1, wait_all)

    def take_vec(i):
        d, _ = peer(n, w, i + 1)
        wait(x.vgot.at[d], x.r_v.at[d])

    loop(n.all - 1, take_vec)
    x.small_o[...] = jnp.sum(x.vgot[...], axis=0)


def layer_kernel(n, names, *refs):
    x = types.SimpleNamespace(**dict(zip(names, refs, strict=True)))
    w = place(n)
    t, d, g = n.tokens, n.width, n.group
    blocks = n.seq // n.sub
    pairs = (n.rounds, n.seq, n.seq, n.cap, 256)
    sums = (
        PlaneScatter(n, w, lambda a, f: x.gwc.at[a, f], x.c1, x.c2, x.s_c, x.r_c),
        PlaneScatter(n, w, lambda a, f: x.gwe.at[a, :, f], x.e1, x.e2, x.s_e, x.r_e),
        Scatter(n, w, "f", lambda a, b, f: x.o0.at[a * n.b + b, f], x.o1, x.o2, x.o3, x.s_o, x.r_o),
    )
    drains = []
    pl.run_scoped(
        lambda *r: drains.append(front_part(n, w, x, *r)),
        VM(pairs, BF), VM(((n.sub - 1) * blocks, MSG, 128), BF), VM((blocks, MSG, 128), BF),
    )
    pl.run_scoped(
        lambda *r: feed_part(n, w, x, sums, drains[0], *r),
        VM((t, d), BF), VM((g * t, n.part), BF), VM((g * t, n.part), BF),
        VM((g, t, d), BF),
    )
    pl.run_scoped(
        lambda *r: back_attention(n, w, x, sums, *r),
        VM(pairs[:-1] + (128,), BF), VM(pairs, BF), VM(((n.sub - 1) * blocks, 128, 256), BF),
    )
    pl.run_scoped(
        lambda *r: back_rest(n, w, x, sums, *r),
        VM((blocks, 128, 256), BF), VM((d, 256), F32), VM((n.all, n.rows, 256), BF), VM((g, n.rows, n.part), F32),
        VM((n.all, 8, 128), F32),
    )


def layer(n, inputs):
    inside = pl.BlockSpec(memory_space=VM)
    t, d, g, a = n.tokens, n.width, n.group, n.a
    units = n.chips * n.fsdp
    blocks = n.seq // n.sub
    nb = n.b // (n.sub // 2)
    f1, b1 = max(n.fsdp - 1, 1), max(n.b - 1, 1)
    pairs = (n.rounds, n.seq, n.seq, n.cap)
    unit_c, unit_e, unit_o = (n.units, d), (g, n.rows, n.part), (n.rows, d)
    count_f = (n.fsdp - 1) * a * n.b + (n.b - 1) * a + a - 1
    count_p = (n.fsdp - 1) * a + a - 1
    outputs = {
        "first_o": (t, d), "second_o": (t, d), "grad1_o": (t, d), "grad2_o": (t, d),
        "gq_o": (n.rows, d), "gv_o": (n.rows, d), "go_o": (n.rows, d), "ge_o": (n.rows, n.hidden), "gc_o": (n.units, d),
        "small_o": (8, 128),
    }
    scratch = {
        "xh": VM((n.seq, 128, d), BF),
        "nown": VM((blocks, 128, d), BF), "qv": VM((n.seq, 128, 256), BF),
        "wqv": VM((n.all, n.rows, 256), BF), "wqv_in": VM((HEADS, n.rows, 256), BF), "we_in": VM((g, n.rows, n.part), BF),
        "small_all": VM((n.all, 16, 128), BF), "tab": VM((n.rounds, n.seq, 8, 128), F32), "vec": VM((16, d), F32),
        "shift_part": VM((8, n.part), F32), "ci": VM((g, t, d), BF),
        "buf": VM(pairs + (256,), BF), "marks": VM(pairs + (128,), BF),
        "pin": VM(((n.sub - 1) * blocks, MSG, 128), BF),
        "home": VM((HEADS, MSG, 128), BF), "dtok": VM((n.seq, MSG, 128), BF),
        "wo": VM((n.all, n.rows, d), BF), "wc": VM((a, n.fsdp, n.units, d), BF), "we": VM((a, g, n.fsdp, n.rows, n.part), BF),
        "n2": VM((g, t, d), BF),
        "gn_got1": VM((n.b, t, d), BF), "gn_got2": VM((b1, t, d), BF), "so_got1": VM((n.b, t, d), BF), "so_got2": VM((b1, t, d), BF),
        "gwc": VM((a, n.fsdp, n.units, d), BF), "gwe": VM((a, g, n.fsdp, n.rows, n.part), BF),
        "gwo": VM((n.chips, 2, n.fsdp, n.rows, d), BF), "message": VM((HEADS, MSG, 128), BF),
        "vec_g": VM((8, d), F32), "shift_g": VM((8, n.part), F32),
        "gown": VM((blocks, 128, 256), F32),
        "gin": VM(((n.sub - 1) * blocks, 128, 256), BF), "win": VM((n.all, n.rows, 256), BF),
        "c1": VM((f1, a) + unit_c, BF), "c2": VM((a - 1,) + unit_c, BF),
        "e1": VM((f1, a) + unit_e, BF), "e2": VM((a - 1,) + unit_e, BF),
        "o0": VM((n.chips, n.fsdp) + unit_o, BF), "o1": VM((f1, a, n.b) + unit_o, BF),
        "o2": VM((b1, a) + unit_o, BF), "o3": VM((a - 1,) + unit_o, BF),
        "egot": VM(unit_e, F32), "vgot": VM((n.all, 8, 128), F32),
    }
    sems = {
        "small": n.all, "w": n.all, "n": n.chips + a + n.b, "ns": n.chips, "ag": (3, units), "os": units, "ex": g, "ci": g,
        "p": (n.sub - 1) * blocks, "out": HEADS, "x": 2 * n.b, "gn": 2 * n.b, "so": 2 * n.b, "d": n.seq, "o0": 1,
        "c": count_p, "e": count_p, "o": count_f, "g": (n.sub - 1) * blocks, "w2": n.all, "n1": max((nb - 1) * a, 1), "n2": a,
        "v": n.all, "y": g,
    }
    for key, count in sems.items():
        for side in ("s_", "r_"):
            if side == "s_" and key in ("w2", "v"):
                continue
            if key == "x" and side == "r_":
                count = g
            scratch[side + key] = DMA(count if isinstance(count, tuple) else (count,))
    names = list(inputs) + list(outputs) + list(scratch)
    return pl.pallas_call(
        functools.partial(layer_kernel, n, names),
        out_shape=tuple(jax.ShapeDtypeStruct(s, F32) for s in outputs.values()),
        in_specs=[inside] * len(inputs),
        out_specs=(inside,) * len(outputs),
        scratch_shapes=list(scratch.values()),
        compiler_params=pltpu.CompilerParams(collective_id=1, has_side_effects=True, vmem_limit_bytes=60 << 20),
        name="layer",
    )(*inputs.values())


def deliver_kernel(n, count, *refs):
    arrays, small, outs = refs[:count], refs[count], refs[count + 1:2 * count + 1]
    vectors, held, come, leave = refs[2 * count + 1:-count - 2], refs[-count - 2:-2], refs[-2], refs[-1]
    ins = [pltpu.make_async_copy(arrays[i], held[i], come.at[i]) for i in range(count)]
    ends = [pltpu.make_async_copy(held[i], outs[i], leave.at[i]) for i in range(count)]
    for cp in ins:
        cp.start()
    for row, ref in zip((0, 1, 2, 3, 5, 4), vectors, strict=True):
        ref[...] = small[row:row + 1, :ref.shape[1]]
    for before, after in zip(ins, ends, strict=True):
        before.wait()
        after.start()
    for cp in ends:
        cp.wait()


def deliver(n, arrays, small):
    anywhere = pl.BlockSpec(memory_space=pl.ANY)
    inside = pl.BlockSpec(memory_space=VM)
    shape = jax.ShapeDtypeStruct
    sizes = (n.rows, n.rows, n.rows, n.rows, n.units, n.rows)
    count = len(arrays)
    return pl.pallas_call(
        functools.partial(deliver_kernel, n, count),
        out_shape=tuple(shape(y.shape, F32) for y in arrays) + tuple(shape((1, k), F32) for k in sizes),
        in_specs=[anywhere] * count + [inside],
        out_specs=(anywhere,) * count + (inside,) * len(sizes),
        scratch_shapes=[VM(y.shape, F32) for y in arrays] + [DMA((count,)), DMA((count,))],
        compiler_params=pltpu.CompilerParams(vmem_limit_bytes=60 << 20),
        name="deliver",
    )(*arrays, small)


def on_device(
    first_half,
    second_half,
    first_cotangent,
    second_cotangent,
    bucket_ids,
    slot_source,
    live_slots,
    mixer_gain,
    mixer_shift,
    query_weight,
    value_weight,
    output_weight,
    feed_gain,
    feed_shift,
    expand_weight,
    expand_bias,
    contract_weight,
    contract_bias,
):
    seq, fsdp = lax.axis_size("seq"), lax.axis_size("fsdp")
    n = setup(seq, fsdp, first_half.shape[2], expand_weight.shape[1], first_half.shape[1])
    vectors = jnp.stack([mixer_gain, mixer_shift, feed_gain, feed_shift, contract_bias] + [jnp.zeros_like(mixer_gain)] * 3)
    *arrays, small = layer(n, {
        "first": first_half[0], "second": second_half[0], "cot1": first_cotangent[0], "cot2": second_cotangent[0],
        "vectors": vectors, "bias": expand_bias.reshape(1, -1), "buckets": bucket_ids[0],
        "query_w": query_weight, "value_w": value_weight, "expand_w": expand_weight,
        "wo_in": output_weight, "wc_in": contract_weight,
    })
    outs = deliver(n, arrays, small)
    first_out, second_out, grad1, grad2, gq, gv, go, ge, gc = outs[:9]
    gain1, shift1, gain2, shift2, up_bias, down_bias = [y.reshape(-1) for y in outs[9:]]
    return (
        first_out[None], second_out[None], grad1[None], grad2[None],
        gain1, shift1, gq, gv, go, gain2, shift2, ge, up_bias, gc, down_bias,
    )


def solution(mesh):
    tokens, slots = P("fsdp", "seq", None), P("fsdp", None, "seq")
    vector, matrix = P(("seq", "fsdp")), P(("seq", "fsdp"), None)
    return jax.shard_map(
        on_device,
        mesh=mesh,
        in_specs=(tokens,) * 4 + (slots,) * 3 + (vector, vector, matrix, matrix, matrix, vector, vector, matrix, vector, matrix, vector),
        out_specs=(tokens,) * 4 + (vector, vector, matrix, matrix, matrix, vector, vector, matrix, vector, matrix, vector),
        check_vma=False,
    )
```

```python
import functools
import types

import jax
import jax.numpy as jnp
from jax import lax
from jax.experimental import pallas as pl
from jax.experimental.pallas import tpu as pltpu
from jax.sharding import PartitionSpec as P

HEADS = 8
HEAD_DIM = 128
ROUNDS = 4
SPAN = 64
BF = jnp.bfloat16
F32 = jnp.float32
MESH = pl.DeviceIdType.MESH
DMA = pltpu.SemaphoreType.DMA
VM = pltpu.VMEM
MSG = 144


def dot(a, b):
    return lax.dot_general(a, b, (((1,), (0,)), ((), ())), preferred_element_type=F32)


def dot_nt(a, b):
    return lax.dot_general(a, b, (((1,), (1,)), ((), ())), preferred_element_type=F32)


def dot_tn(a, b):
    return lax.dot_general(a, b, (((0,), (0,)), ((), ())), preferred_element_type=F32)


def iota(shape, dim):
    return lax.broadcasted_iota(jnp.int32, shape, dim)


def iotaf(shape, dim):
    return iota(shape, dim).astype(F32)


def low(x):
    return x.astype(BF)


def split3(x):
    hi = x.astype(BF).astype(F32)
    rest = x - hi
    mid = rest.astype(BF).astype(F32)
    return hi, mid, rest - mid


def loop(count, body):
    def step(i, carry):
        body(i)
        return carry

    lax.fori_loop(0, count, step, 0)


def loop_by(k, count, body):
    k = k if count % k == 0 else 1

    def several(i):
        for u in range(k):
            body(i * k + u)

    loop(count // k, several)


def push(src, dst, send, recv, dev):
    pltpu.make_async_remote_copy(
        src_ref=src, dst_ref=dst, send_sem=send, recv_sem=recv, device_id=dev, device_id_type=MESH
    ).start()


def wait(ref, sem):
    pltpu.make_async_copy(ref, ref, sem).wait()


def to_column(row):
    size = row.shape[1]
    eye = iota((size, size), 0) == iota((size, size), 1)
    return jnp.sum(jnp.where(eye, row, 0.0), axis=1, keepdims=True)


def to_row(column):
    size = column.shape[0]
    eye = iota((size, size), 0) == iota((size, size), 1)
    return jnp.sum(jnp.where(eye, column, 0.0), axis=0, keepdims=True)


def message_rows(rows):
    at = iota((MSG - 128, 128), 0)
    out = jnp.zeros((MSG - 128, 128), F32)
    for i, row in enumerate(rows):
        out = jnp.where(at == i, row, out)
    return low(out)


def setup(seq, fsdp, width, hidden, tokens):
    n = types.SimpleNamespace()
    n.seq, n.fsdp, n.all = seq, fsdp, seq * fsdp
    n.chips = seq // 2
    n.b = 2 if n.chips <= 8 else 4
    n.a = n.chips // n.b
    n.sub = seq // HEADS
    n.rounds = ROUNDS // n.sub
    n.cap = 4 * SPAN // seq
    n.width, n.hidden, n.tokens = width, hidden, tokens
    n.rows = width // n.all
    n.units = hidden // n.all
    n.group = 2 * n.b
    n.part = hidden // n.group
    n.wide = hidden // seq
    return n


def place(n):
    w = types.SimpleNamespace()
    w.s, w.f = lax.axis_index("seq"), lax.axis_index("fsdp")
    w.c, w.j = w.s // 2, lax.rem(w.s, 2)
    w.a, w.b = w.c // n.b, lax.rem(w.c, n.b)
    w.me = w.s * n.fsdp + w.f
    w.head, w.idx = w.s // n.sub, lax.rem(w.s, n.sub)
    w.sib = (w.s + 1 - 2 * w.j, w.f)
    w.t = w.b * 2 + w.j
    return w


def plane(n, w, a, b, f):
    return ((a * n.b + b) * 2 + w.j, f)


def member(n, w, t):
    return ((w.a * n.b) * 2 + t, w.f)


def peer(n, w, i):
    d = lax.rem(w.me + i, n.all)
    return d, (d // n.fsdp, lax.rem(d, n.fsdp))


def meet_all(n, w):
    barrier = pltpu.get_barrier_semaphore()

    def greet(i):
        pl.semaphore_signal(barrier, inc=1, device_id=peer(n, w, i + 1)[1], device_id_type=MESH)

    loop(n.all - 1, greet)
    pl.semaphore_wait(barrier, n.all - 1)


class Line:
    def __init__(self, n, w):
        self.n, self.w, self.k, self.sent = n, w, 0, []

    def inside(self, shift):
        a = self.w.a + shift
        return (a >= 0) & (a < self.n.a)

    def send(self, ref, recv, dev, *shifts):
        push(ref, ref, self.send_sem(self.k), recv, dev)
        self.sent.append((self.k, shifts))
        self.k += 1

    def both(self, shifts):
        return functools.reduce(jnp.logical_and, [self.inside(v) for v in shifts])

    def start(self, own, neighbour):
        for sign in (-1, 1):
            @pl.when(self.inside(-sign))
            def _(sign=sign):
                self.send(*own(), neighbour(self.w.a - sign), -sign)

    def step(self, far, take, neighbour, more):
        for sign in (-1, 1):
            @pl.when(self.inside(sign * far))
            def _(sign=sign):
                ref, recv = take(self.w.a + sign * far)
                if far < self.n.a - 1:
                    @pl.when(self.inside(-sign))
                    def _():
                        self.send(ref, recv, neighbour(self.w.a - sign), sign * far, -sign)
                for dev in more:
                    self.send(ref, recv, dev, sign * far)

    def drain_sends(self, ref):
        for k, shifts in self.sent:
            if shifts:
                @pl.when(self.both(shifts))
                def _(k=k):
                    wait(ref(), self.send_sem(k))
            else:
                wait(ref(), self.send_sem(k))


class Gather(Line):
    def __init__(self, n, w, unit, index, send_sem, recv_sem, over_b=False, arrived=None):
        super().__init__(n, w)
        self.unit, self.index, self.send_sem, self.recv_sem = unit, index, send_sem, recv_sem
        self.over_b, self.arrived = over_b, arrived

    def entry(self, a, b, f):
        return self.unit(a, b, f), self.recv_sem(self.index(a, b, f))

    def take(self, a, b, f):
        ref, recv = self.entry(a, b, f)
        wait(ref, recv)
        if self.arrived:
            self.arrived(ref, self.index(a, b, f))
        return ref, recv

    def neighbour(self, a):
        return plane(self.n, self.w, a, self.w.b, self.w.f)

    def others(self, over_f=True):
        n, w = self.n, self.w
        out = []
        if over_f:
            out += [plane(n, w, w.a, w.b, lax.rem(w.f + m, n.fsdp)) for m in range(1, n.fsdp)]
        if self.over_b:
            out += [plane(n, w, w.a, lax.rem(w.b + m, n.b), w.f) for m in range(1, n.b)]
        return out

    def to_a(self):
        self.start(lambda: self.entry(self.w.a, self.w.b, self.w.f), self.neighbour)

    def column(self, far):
        w = self.w
        if far == 0:
            for dev in self.others():
                self.send(*self.entry(w.a, w.b, w.f), dev)
        else:
            self.step(far, lambda a: self.take(a, w.b, w.f), self.neighbour, self.others())

    def corner(self, far):
        if not self.over_b:
            return

        def pass_on(shift, *shifts):
            for q in range(1, self.n.fsdp):
                ref, recv = self.take(self.w.a + shift, self.w.b, lax.rem(self.w.f + q, self.n.fsdp))
                for dev in self.others(False):
                    self.send(ref, recv, dev, *shifts)

        if far == 0:
            pass_on(0)
        else:
            for sign in (-1, 1):
                @pl.when(self.inside(sign * far))
                def _(sign=sign):
                    pass_on(sign * far, sign * far)

    def finish(self):
        n, w = self.n, self.w
        for i in range(n.a):
            a = lax.rem(w.a + i, n.a)
            for q in range(n.fsdp):
                for v in range(n.b):
                    if (v if self.over_b else q) != 0 and (self.over_b or v == 0):
                        self.take(a, lax.rem(w.b + v, n.b), lax.rem(w.f + q, n.fsdp))

    def drain(self):
        self.drain_sends(lambda: self.unit(self.w.a, self.w.b, self.w.f))


def tables(n, w, small_all, tab):
    nb = 2 * n.seq
    before = low((iota((128, 128), 0) < iota((128, 128), 1)).astype(F32))
    for r in range(n.rounds):
        def bucket_row(p):
            tile = small_all[p * n.fsdp + w.f].astype(F32)
            keep = iota((16, 128), 0) == 8 + w.idx * n.rounds + r
            return jnp.sum(jnp.where(keep, tile, 0.0), axis=0, keepdims=True)

        def count(p, run):
            row = bucket_row(p)
            hot = (iotaf((nb, 128), 0) == row).astype(F32)
            ahead = dot(low(hot), before)
            pos = jnp.sum(hot * (ahead + run), axis=0, keepdims=True)
            group = jnp.floor(row * 0.5)
            hotg = (iotaf((n.seq, 128), 0) == group).astype(F32)
            rank = jnp.sum(hotg * dot(low(hotg), before), axis=0, keepdims=True)
            line = group * n.cap + rank
            at = iota((8, 128), 0)
            tab[r, p] = jnp.where(at == 0, line, jnp.where(at == 1, pos, jnp.where(at == 2, row, 0.0)))
            return run + jnp.sum(hot, axis=1, keepdims=True)

        totals = lax.fori_loop(0, n.seq, count, jnp.zeros((nb, 1), F32))

        def settle(p):
            tile = tab[r, p]
            row = tile[2:3]
            odd = row - 2.0 * jnp.floor(row * 0.5)
            hot = (iotaf((nb, 128), 0) == row - 1.0).astype(F32)
            slot = tile[1:2] + odd * jnp.sum(hot * totals, axis=0, keepdims=True)
            block = jnp.floor(slot * (1.0 / SPAN))
            tab[r, p] = jnp.where(iota((8, 128), 0) == 1, block, tile)

        loop(n.seq, settle)


def picks(n, tile):
    return low((iotaf((n.seq * n.cap, 128), 0) == tile[0:1]).astype(F32))


def picks_back(n, tile):
    return low((iotaf((128, n.seq * n.cap), 1) == to_column(tile[0:1])).astype(F32))


def block_marks(tile):
    return low((iotaf((128, 128), 1) == to_column(tile[1:2])).astype(F32))


FAR = 2.0 ** 30


def with_blocks(marks, query, key):
    i, k = iota((128, 128), 0), iota((128, 128), 1)
    seen = dot(marks, low((((k == i) | (k == i + 1)) & (i < 4)).astype(F32)))
    lane = iota(marks.shape, 1)
    ask = low(jnp.where(lane < 4, marks.astype(F32) * -FAR, 0.0))
    answer = low(jnp.where(lane < 4, 1.0 - seen, 0.0))
    return jnp.concatenate([query, ask], axis=1), jnp.concatenate([key, answer], axis=1)


def halves(wide_query, wide_key):
    size = wide_query.shape[0]
    cut = size // 2
    row, col = iota((cut, cut), 0), iota((cut, cut), 1)

    def ordered(raw):
        return jnp.where(col < row, raw, jnp.where(col == row, -1e4, -1e9))

    first = ordered(dot_nt(wide_query[:cut], wide_key[:cut]))
    rest = dot_nt(wide_query[cut:], wide_key)
    return first, jnp.concatenate([rest[:, :cut], ordered(rest[:, cut:])], axis=1)


def rows_of(n, ref):
    got = ref[...]
    if n.cap % 16:
        return low(got.astype(F32).reshape(n.seq * n.cap, got.shape[-1]))
    return got.reshape(n.seq * n.cap, got.shape[-1])


def put_rows(n, ref, value):
    ref[...] = value.reshape(n.seq, n.cap, value.shape[-1]).astype(ref.dtype)


def keys_of(query):
    wide = query.astype(F32)
    scale = lax.rsqrt(jnp.sum(wide * wide, axis=1, keepdims=True) + 1e-06)
    return low(wide * scale), scale


def fill_block(n, r, p, tab, qv, buf, marks):
    tile = tab[r, p]
    hot = picks(n, tile)
    got = dot(hot, jnp.concatenate([qv[p], block_marks(tile)], axis=1))
    put_rows(n, buf.at[r, :, p], got[:, :256])
    put_rows(n, marks.at[r, :, p], got[:, 256:])


def attend(n, r, g, buf, marks, obuf):
    both = rows_of(n, buf.at[r, g])
    query, value = both[:, :128], both[:, 128:]
    key, _ = keys_of(query)
    cut = query.shape[0] // 2
    outs = []
    for score, values in zip(halves(*with_blocks(rows_of(n, marks.at[r, g]), query, key)), (value[:cut], value)):
        top = jnp.max(score, axis=1, keepdims=True)
        expo = jnp.exp(score - top)
        total = jnp.sum(expo, axis=1, keepdims=True)
        out = dot(low(expo), values) / total
        hi, mid, rest = split3(top + jnp.log(total))
        lane = iota((cut, 128), 1)
        logs = jnp.where(lane == 0, hi, jnp.where(lane == 1, mid, jnp.where(lane == 2, rest, 0.0)))
        outs.append(jnp.concatenate([out, logs], axis=1))
    put_rows(n, obuf.at[r, :, g], jnp.concatenate(outs, axis=0))


def merge(outs, logs):
    top = functools.reduce(jnp.maximum, logs)
    weights = [jnp.exp(v - top) for v in logs]
    total = sum(weights)
    return sum(x * y for x, y in zip(weights, outs)) / total, top + jnp.log(total)


def merge_rounds(n, p, tab, obuf):
    outs, logs = [], []
    for r in range(n.rounds):
        got = dot(picks_back(n, tab[r, p]), rows_of(n, obuf.at[r, p]))
        outs.append(got[:, :128])
        logs.append(jnp.sum(got[:, 128:], axis=1, keepdims=True))
    return merge(outs, logs)


def write_message(ref, out, log):
    ref[:128] = low(out)
    ref[128:] = message_rows(split3(to_row(log)))


def read_log(ref):
    return to_column(jnp.sum(ref[128:].astype(F32), axis=0, keepdims=True))


def hat_of(x):
    center = x - jnp.mean(x, axis=1, keepdims=True)
    scale = lax.rsqrt(jnp.mean(center * center, axis=1, keepdims=True) + 1e-05)
    return center * scale, scale


def normalize(x, gain, shift):
    hat, scale = hat_of(x)
    return hat, scale, hat * gain + shift


def placed(row, spot):
    size = row.shape[1]
    put = (iota((size, 128), 1) == iota((size, 128), 0) + spot * size).astype(F32)
    return dot(row, low(put))


def gelu_pair(x):
    k = 0.7978845608028654
    square = x * x
    t = jnp.tanh(k * (x + 0.044715 * (square * x)))
    half = 0.5 * (1.0 + t)
    return x * half, half + 0.5 * x * (1.0 - t * t) * (k * (1.0 + 0.134145 * square))


class GroupSum:
    def __init__(self, n, w, out, got1, got2, send, recv):
        self.n, self.w, self.out, self.got1, self.got2 = n, w, out, got1, got2
        self.send, self.recv = send, recv

    def fill(self, product):
        n, w = self.n, self.w
        for m in range(n.b):
            b = lax.rem(w.b + 1 + m, n.b)
            self.out[pl.ds(2 * b, 2)] = low(product(b)).reshape(2, n.tokens, n.width)
            t = b * 2 + 1 - w.j
            push(self.out.at[t], self.got1.at[b], self.send.at[m], self.recv.at[b], w.sib)

    def chips(self):
        n, w = self.n, self.w
        for m in range(1, n.b):
            b = lax.rem(w.b + m, n.b)
            t = b * 2 + w.j
            wait(self.got1.at[b], self.recv.at[b])
            self.out[t] = low(self.out[t].astype(F32) + self.got1[b].astype(F32))
            k = n.b + m - 1
            push(self.out.at[t], self.got2.at[m - 1], self.send.at[k], self.recv.at[k], member(n, w, t))

    def total(self):
        n, w = self.n, self.w
        wait(self.got1.at[w.b], self.recv.at[w.b])
        total = self.out[w.t].astype(F32) + self.got1[w.b].astype(F32)
        for m in range(1, n.b):
            wait(self.got2.at[m - 1], self.recv.at[n.b + m - 1])
            total += self.got2[m - 1].astype(F32)
        return total

    def drain(self):
        for k in range(2 * self.n.b - 1):
            wait(self.got1.at[0], self.send.at[k])


class Scatter:
    def __init__(self, n, w, outer, part, got1, got2, got3, send, recv):
        self.n, self.w, self.outer, self.part = n, w, outer, part
        self.got1, self.got2, self.got3 = got1, got2, got3
        self.send, self.recv = send, recv
        self.one, self.two = (n.fsdp, n.b) if outer == "f" else (n.b, n.fsdp)
        self.me1, self.me2 = (w.f, w.b) if outer == "f" else (w.b, w.f)
        self.base2 = (self.one - 1) * n.a * self.two
        self.base3 = self.base2 + (self.two - 1) * n.a

    def mine(self, a, one, two):
        return self.part(a, two, one) if self.outer == "f" else self.part(a, one, two)

    def dev(self, a, one, two):
        if self.outer == "f":
            return plane(self.n, self.w, a, two, one)
        return plane(self.n, self.w, a, one, two)

    def first(self):
        for m in range(1, self.one):
            far = lax.rem(self.me1 + m, self.one)

            def body(i, m=m, far=far):
                a, two = i // self.two, lax.rem(i, self.two)
                k = (m - 1) * self.n.a * self.two + i
                push(self.mine(a, far, two), self.got1.at[m - 1, a, two], self.send.at[k], self.recv.at[k],
                     self.dev(self.w.a, far, self.me2))

            loop(self.n.a * self.two, body)

    def second(self):
        def body(i):
            m2, a = i // self.n.a, lax.rem(i, self.n.a)
            two = lax.rem(self.me2 + 1 + m2, self.two)
            for m in range(1, self.one):
                k = (m - 1) * self.n.a * self.two + a * self.two + two
                wait(self.got1.at[m - 1, a, two], self.recv.at[k])
            self.fold1(a, two)

            @pl.when(m2 < self.two - 1)
            def _():
                k = self.base2 + m2 * self.n.a + a
                push(self.got1.at[0, a, two], self.got2.at[m2, a], self.send.at[k], self.recv.at[k],
                     self.dev(self.w.a, self.me1, two))

        loop(self.n.a * self.two, body)

    def fold1(self, a, two):
        total = self.mine(a, self.me1, two)[...].astype(F32)
        for m in range(1, self.one):
            total += self.got1[m - 1, a, two].astype(F32)
        self.got1[0, a, two] = low(total)

    def third(self):
        def body(i):
            a = lax.rem(self.w.a + 1 + i, self.n.a)
            for m2 in range(self.two - 1):
                wait(self.got2.at[m2, a], self.recv.at[self.base2 + m2 * self.n.a + a])
            total = self.got1[0, a, self.me2].astype(F32)
            for m2 in range(self.two - 1):
                total += self.got2[m2, a].astype(F32)
            self.got2[0, a] = low(total)

            @pl.when(i < self.n.a - 1)
            def _():
                k = self.base3 + i
                push(self.got2.at[0, a], self.got3.at[i], self.send.at[k], self.recv.at[k],
                     self.dev(a, self.me1, self.me2))

        loop(self.n.a, body)

    def total(self):
        total = self.got2[0, self.w.a].astype(F32)
        for i in range(self.n.a - 1):
            wait(self.got3.at[i], self.recv.at[self.base3 + i])
            total += self.got3[i].astype(F32)
        return total

    def drain(self):
        loop(self.base3 + self.n.a - 1, lambda k: wait(self.got3.at[0], self.send.at[k]))


class PlaneScatter:
    def __init__(self, n, w, part, got1, got2, send, recv):
        self.n, self.w, self.part, self.got1, self.got2, self.send, self.recv = n, w, part, got1, got2, send, recv
        self.base = (n.fsdp - 1) * n.a

    def first(self):
        n, w = self.n, self.w
        for m in range(1, n.fsdp):
            far = lax.rem(w.f + m, n.fsdp)

            def body(i, m=m, far=far):
                a = lax.rem(w.a + 1 + i, n.a)
                k = (m - 1) * n.a + a
                push(self.part(a, far), self.got1.at[m - 1, a], self.send.at[k], self.recv.at[k], plane(n, w, w.a, w.b, far))

            loop(n.a, body)

    def second(self, i):
        n, w = self.n, self.w
        a = lax.rem(w.a + 1 + i, n.a)
        total = self.part(a, w.f)[...].astype(F32)
        for m in range(1, n.fsdp):
            wait(self.got1.at[m - 1, a], self.recv.at[(m - 1) * n.a + a])
            total += self.got1[m - 1, a].astype(F32)
        self.got1[0, a] = low(total)
        if i < n.a - 1:
            k = self.base + i
            push(self.got1.at[0, a], self.got2.at[i], self.send.at[k], self.recv.at[k], plane(n, w, a, w.b, w.f))

    def total(self):
        total = self.got1[0, self.w.a].astype(F32)
        for i in range(self.n.a - 1):
            wait(self.got2.at[i], self.recv.at[self.base + i])
            total += self.got2[i].astype(F32)
        return total

    def drain(self):
        loop(self.base + self.n.a - 1, lambda k: wait(self.got2.at[0], self.send.at[k]))


def spread(n, r, p, tab, dtok, dbuf, marks):
    tile = tab[r, p]
    shift = low((iota((MSG - 128, 128), 0) + 4 == iota((MSG - 128, 128), 1)).astype(F32))
    marked = block_marks(tile) + low(dot_tn(dtok[p, 128:], shift))
    got = dot(picks(n, tile), jnp.concatenate([dtok[p, :128], marked], axis=1))
    put_rows(n, dbuf.at[r, :, p], got[:, :128])
    put_rows(n, marks.at[r, :, p], got[:, 128:])


def attend_back(n, r, g, buf, marks, dbuf, gbuf):
    both, cot, marked = rows_of(n, buf.at[r, g]), rows_of(n, dbuf.at[r, g]), rows_of(n, marks.at[r, g])
    query, value = both[:, :128], both[:, 128:]
    aux = marked.astype(F32)
    lane = iota(aux.shape, 1)
    log_all = jnp.sum(jnp.where((lane >= 4) & (lane < 7), aux, 0.0), axis=1, keepdims=True)
    delta = jnp.sum(jnp.where(lane >= 7, aux, 0.0), axis=1, keepdims=True)
    key, scale = keys_of(query)
    cut = query.shape[0] // 2
    score0, score1 = halves(*with_blocks(marked, query, key))
    under = iota((cut, cut), 1) < iota((cut, cut), 0)
    prob0 = jnp.exp(score0 - log_all[:cut])
    prob1 = jnp.exp(score1 - log_all[cut:])
    back0 = low(jnp.where(under, prob0 * (dot_nt(cot[:cut], value[:cut]) - delta[:cut]), 0.0))
    back1 = prob1 * (dot_nt(cot[cut:], value) - delta[cut:])
    back1 = low(jnp.concatenate([back1[:, :cut], jnp.where(under, back1[:, cut:], 0.0)], axis=1))
    direct = jnp.concatenate([dot(back0, key[:cut]), dot(back1, key)], axis=0)

    def both_halves(first, rest, rows):
        total = dot_tn(rest, rows[cut:])
        return jnp.concatenate([total[:cut] + dot_tn(first, rows[:cut]), total[cut:]], axis=0)

    back_key = both_halves(back0, back1, query)
    back_value = both_halves(low(prob0), low(prob1), cot)
    wide = query.astype(F32)
    inner = jnp.sum(wide * back_key, axis=1, keepdims=True)
    total = direct + scale * back_key - wide * (scale * scale * scale * inner)
    put_rows(n, gbuf.at[r, :, g], jnp.concatenate([total, back_value], axis=1))


UNROLL = 2
RELAYS = (0, 0, 0, 0, 0, 1, 1, 1, 1)
SUMS = (1, 1, 1, 1, 1, 1, 0, 0)


def greet_all(n, w, barrier):
    def greet(i):
        pl.semaphore_signal(barrier, inc=1, device_id=peer(n, w, i + 1)[1], device_id_type=MESH)

    loop(n.all - 1, greet)


def pack(n, w, x):
    x.ci[w.t] = low(x.cot2[...])
    for t in range(n.group):
        for a in range(n.a):
            s = a * n.group + t
            x.we_in[t, :, a * n.wide:(a + 1) * n.wide] = x.expand_w[:, s * n.wide:(s + 1) * n.wide]
    lead = placed(x.vectors[...], lax.rem(w.me, 128 // n.rows))
    extra = placed(jnp.broadcast_to(x.bias[...], (8, n.units)), lax.rem(w.me, 128 // n.units))
    lead = jnp.where(iota((8, 128), 0) == 5, extra, lead)
    x.small_all[w.me] = low(jnp.concatenate([lead, x.buckets[...].astype(F32), jnp.zeros((8 - ROUNDS, 128), F32)]))
    for h in range(HEADS):
        x.wqv_in[w.f, h, :, :128] = x.query_w[:, h * 128:(h + 1) * 128]
        x.wqv_in[w.f, h, :, 128:] = x.value_w[:, h * 128:(h + 1) * 128]
    x.wo[w.me] = x.wo_in[...]
    x.wc[w.a, w.f] = x.wc_in[...]
    x.we[w.a, w.t, w.f] = x.we_in[w.t]


def vectors_of(n, w, x):
    group = 128 // n.rows
    for q in range(n.width // 128):
        x.vec[:, q * 128:(q + 1) * 128] = jnp.sum(
            x.small_all[q * group:(q + 1) * group].astype(F32), axis=0
        )
    per = 128 // n.units
    for q in range(n.a * n.fsdp // per):
        a, rest = q * per // n.fsdp, q * per % n.fsdp
        first = (a * n.group + w.t) * n.fsdp + rest
        total = sum(x.small_all[first + k].astype(F32) for k in range(per))
        x.shift_part[:, q * 128:(q + 1) * 128] = jnp.broadcast_to(total[5:6], (8, 128))


def front_part(n, w, x, obuf, pmsg, omsg):
    barrier = pltpu.get_barrier_semaphore()
    greet_all(n, w, barrier)
    hat, _ = hat_of(x.second[...])
    x.xh[w.s] = low(hat)
    pack(n, w, x)
    pl.semaphore_wait(barrier, n.all - 1)

    def spot(i, v):
        return (lax.rem(w.a + i, n.a) * n.b + lax.rem(w.b + v, n.b)) * 2 + w.j

    def hat_at(a):
        block = (a * n.b + w.b) * 2 + w.j
        return x.xh.at[block], x.r_n.at[block // 2]

    def hat_chip(a):
        return ((a * n.b + w.b) * 2 + w.j, w.f)

    hats = Line(n, w)
    hats.send_sem = lambda k: x.s_n.at[k]
    shares = Line(n, w)
    shares.send_sem = lambda k: x.s_ns.at[k]

    def share_hat(block, *shifts):
        shares.send(x.xh.at[block], x.r_ns.at[block // 2], w.sib, *shifts)

    far_b = [(spot(0, v), w.f) for v in range(1, n.b)]
    hats.start(lambda: hat_at(w.a), hat_chip)
    for dev in far_b:
        hats.send(*hat_at(w.a), dev)
    share_hat(w.s)
    for m in range(1, n.group):
        t = lax.rem(w.t + m, n.group)
        push(x.we_in.at[t], x.we.at[w.a, w.t, w.f], x.s_ex.at[m], x.r_ex.at[w.t], member(n, w, t))

    mine = pl.ds(w.s * n.fsdp, n.fsdp)
    for q in range(1, n.fsdp):
        far = (w.s, lax.rem(w.f + q, n.fsdp))
        push(x.small_all.at[w.me], x.small_all.at[w.me], x.s_f.at[0, q], x.r_f.at[0, w.f], far)
        push(x.wqv_in.at[w.f], x.wqv_in.at[w.f], x.s_f.at[1, q], x.r_f.at[1, w.f], far)
    for q in range(1, n.fsdp):
        f = lax.rem(w.f + q, n.fsdp)
        wait(x.small_all.at[w.me], x.r_f.at[0, f])

    def send_small(i):
        s = lax.rem(w.s + 1 + i, n.seq)
        push(x.small_all.at[mine], x.small_all.at[mine], x.s_small.at[i], x.r_small.at[w.s], (s, w.f))

    loop(n.seq - 1, send_small)
    for q in range(1, n.fsdp):
        f = lax.rem(w.f + q, n.fsdp)
        wait(x.wqv_in.at[f], x.r_f.at[1, f])

    def send_w(i):
        s = lax.rem(w.s + 1 + i, n.seq)
        push(x.wqv_in.at[:, s // n.sub], x.wqv.at[mine], x.s_wq.at[i], x.r_wq.at[w.s], (s, w.f))

    loop(n.seq - 1, send_w)
    x.wqv[mine] = x.wqv_in[:, w.head]

    def shared_o(ref, uid):
        push(ref, ref, x.s_os.at[uid], x.r_os.at[uid], w.sib)

    def ag(k):
        return (lambda i: x.s_ag.at[k, i]), (lambda u: x.r_ag.at[k, u])

    def all_index(a, b, f):
        return (a * n.b + b) * n.fsdp + f

    def part_index(a, b, f):
        return a * n.fsdp + f

    g_o = Gather(n, w, lambda a, b, f: x.wo.at[((a * n.b + b) * 2 + w.j) * n.fsdp + f], all_index, *ag(0), True, shared_o)
    g_c = Gather(n, w, lambda a, b, f: x.wc.at[a, f], part_index, *ag(1))
    g_e = Gather(n, w, lambda a, b, f: x.we.at[a, :, f], part_index, *ag(2))
    gathers = (g_o, g_c, g_e)
    for m in range(1, n.group):
        t = lax.rem(w.t + m, n.group)
        wait(x.we.at[w.a, t, w.f], x.r_ex.at[t])
        push(x.ci.at[w.t], x.ci.at[w.t], x.s_ci.at[m], x.r_ci.at[w.t], member(n, w, t))
    shared_o(x.wo.at[w.me], (w.a * n.b + w.b) * n.fsdp + w.f)
    for y in gathers:
        y.column(0)

    def wait_small(i):
        s = lax.rem(w.s + 1 + i, n.seq)
        wait(x.small_all.at[mine], x.r_small.at[s])

    loop(n.seq - 1, wait_small)
    vectors_of(n, w, x)
    tables(n, w, x.small_all, x.tab)
    weights = x.wqv.reshape(n.width, 256)

    def project(block):
        normed = low(x.xh[block].astype(F32) * x.vec[0:1] + x.vec[1:2])

        @pl.when(lax.rem(block, n.sub) == w.idx)
        def _():
            x.nown[block // n.sub] = normed

        x.qv[block] = low(dot(normed, weights[...]))

    for far in range(1, n.a):
        def take_hat(a):
            ref, recv = hat_at(a)
            wait(ref, recv)
            return ref, recv

        hats.step(far, take_hat, hat_chip, far_b)
        for sign in (-1, 1):
            @pl.when(hats.inside(sign * far))
            def _(sign=sign):
                share_hat(((w.a + sign * far) * n.b + w.b) * 2 + w.j, sign * far)
    for y in gathers:
        y.to_a()

    def wait_w(i):
        s = lax.rem(w.s + 1 + i, n.seq)
        wait(x.wqv.at[mine], x.r_wq.at[s])

    loop(n.seq - 1, wait_w)
    project(w.s)
    for i in range(1, n.a):
        project(spot(i, 0))
    for i in range(n.a):
        for v in range(1, n.b):
            block = spot(i, v)
            wait(x.xh.at[block], x.r_n.at[block // 2])
            share_hat(block)
            project(block)

    def from_sibling(c):
        block = 2 * c + 1 - w.j
        wait(x.xh.at[block], x.r_ns.at[c])
        project(block)

    loop(n.chips, from_sibling)

    tasks = []
    for i in range(n.a):
        if i:
            tasks.append(lambda i=i: [y.column(i) for y in gathers])
        tasks.append(lambda i=i: g_o.corner(i))

    def relay(count):
        for _ in range(count):
            if tasks:
                tasks.pop(0)()

    for r in range(n.rounds):
        loop_by(UNROLL, n.seq, lambda p: fill_block(n, r, p, x.tab, x.qv, x.buf, x.marks))
    relay(RELAYS[0])
    parts = 4
    slot = 1
    for r in range(n.rounds):
        for q in range(parts):
            loop_by(UNROLL, n.seq // parts, lambda g: attend(n, r, q * (n.seq // parts) + g, x.buf, x.marks, obuf))
            relay(RELAYS[slot])
            slot += 1

    blocks = n.seq // n.sub
    for m in range(1, n.sub):
        far = lax.rem(w.idx + m, n.sub)

        def offer(i, m=m, far=far):
            k = (m - 1) * blocks + i
            write_message(pmsg.at[k], *merge_rounds(n, i * n.sub + far, x.tab, obuf))
            push(pmsg.at[k], x.pin.at[k], x.s_p.at[k], x.r_p.at[k], (w.head * n.sub + far, w.f))

        loop_by(UNROLL, blocks, offer)

    def settle(i):
        out, log = merge_rounds(n, i * n.sub + w.idx, x.tab, obuf)
        outs, logs = [out], [log]
        for m in range(1, n.sub):
            k = (m - 1) * blocks + i
            wait(x.pin.at[k], x.r_p.at[k])
            outs.append(x.pin[k, :128].astype(F32))
            logs.append(read_log(x.pin.at[k]))
        write_message(omsg.at[i], *merge(outs, logs))

    def give(i):
        to = lax.rem(w.head + 1 + i, blocks)
        settle(to)
        push(omsg.at[to], x.home.at[w.head], x.s_out.at[i], x.r_out.at[w.head], (to * n.sub + w.idx, w.f))

    loop(blocks - 1, give)
    settle(w.head)
    x.home[w.head] = omsg[w.head]
    relay(len(tasks))

    def take(i):
        h = lax.rem(w.head + 1 + i, HEADS)
        wait(x.home.at[h], x.r_out.at[h])

    loop(HEADS - 1, take)
    g_o.finish()
    loop(n.chips * n.fsdp, lambda u: wait(x.wo.at[w.me], x.r_os.at[u]))

    loop((n.sub - 1) * blocks, lambda k: wait(pmsg.at[0], x.s_p.at[k]))
    loop(blocks - 1, lambda k: wait(omsg.at[0], x.s_out.at[k]))

    def drain():
        g_c.finish()
        g_e.finish()
        for y in gathers:
            y.drain()
        loop(n.chips * n.fsdp, lambda u: wait(x.wo.at[w.me], x.s_os.at[u]))
        for m in range(1, n.group):
            t = lax.rem(w.t + m, n.group)
            wait(x.we_in.at[0], x.s_ex.at[m])
            wait(x.ci.at[t], x.r_ci.at[t])
            wait(x.ci.at[t], x.s_ci.at[m])

        def wait_sends(i):
            wait(x.small_all.at[pl.ds(0, n.fsdp)], x.s_small.at[i])
            wait(x.wqv.at[pl.ds(0, n.fsdp)], x.s_wq.at[i])

        loop(n.seq - 1, wait_sends)
        for q in range(1, n.fsdp):
            wait(x.small_all.at[0], x.s_f.at[0, q])
            wait(x.wqv_in.at[0], x.s_f.at[1, q])
        hats.drain_sends(lambda: x.xh.at[w.s])
        shares.drain_sends(lambda: x.xh.at[w.s])

    return drain


def feed_part(n, w, x, sums, drain, mixed_low, act, gp, out, out2):
    sum_c, sum_e, _ = sums
    for h in range(HEADS):
        mixed_low[:, h * 128:(h + 1) * 128] = x.home[h, :128]
    first_out = x.first[...] + dot(mixed_low[...], x.wo.reshape(n.width, n.width)[...])
    x.first_o[...] = first_out
    hat, scale, normed = normalize(first_out, x.vec[2:3], x.vec[3:4])
    x.n2[w.t] = low(normed)
    k = 0
    for m in range(1, n.b):
        t = lax.rem(w.b + m, n.b) * 2 + w.j
        push(x.n2.at[w.t], x.n2.at[w.t], x.s_x.at[k], x.r_x.at[w.t], member(n, w, t))
        k += 1
    push(x.n2.at[w.t], x.n2.at[w.t], x.s_x.at[k], x.r_x.at[w.t], w.sib)
    k += 1
    drain()
    for m in range(1, n.b):
        t = lax.rem(w.b + m, n.b) * 2 + w.j
        wait(x.n2.at[t], x.r_x.at[t])
        push(x.n2.at[t], x.n2.at[t], x.s_x.at[k], x.r_x.at[t], w.sib)
        k += 1
    for b in range(n.b):
        t = b * 2 + 1 - w.j
        wait(x.n2.at[t], x.r_x.at[t])
    size = n.group * n.tokens
    step = min(512, n.part)
    tokens = x.n2.reshape(size, n.width)
    cots = x.ci.reshape(size, n.width)
    we = x.we.reshape(n.width, n.part)
    wc = x.wc.reshape(n.part, n.width)
    for q in range(n.part // step):
        at = slice(q * step, (q + 1) * step)
        pre = dot(tokens[...], we[:, at]) + x.shift_part[0:1, at]
        value, slope = gelu_pair(pre)
        act[:, at] = low(value)
        back = low(dot_nt(cots[...], wc[at]) * slope)
        gp[:, at] = back
        x.shift_g[:, at] = jnp.broadcast_to(jnp.sum(back.astype(F32), axis=0, keepdims=True), (8, step))
    gn = GroupSum(n, w, out, x.gn_got1, x.gn_got2, x.s_gn, x.r_gn)
    so = GroupSum(n, w, out2, x.so_got1, x.so_got2, x.s_so, x.r_so)
    pair = 2 * n.tokens
    gn.fill(lambda b: dot_nt(gp[pl.ds(pl.multiple_of(b * pair, pair), pair)], we[...]))
    x.gwc.reshape(n.part, n.width)[...] = low(dot_tn(act[...], cots[...]))
    sum_c.first()
    gn.chips()
    so.fill(lambda b: dot(act[pl.ds(pl.multiple_of(b * pair, pair), pair)], wc[...]))
    x.gwe.reshape(n.width, n.part)[...] = low(dot_tn(tokens[...], gp[...]))
    so.chips()
    sum_e.first()
    grad = gn.total()
    rest = grad * x.vec[2:3]
    mean = jnp.mean(rest, axis=1, keepdims=True)
    tilt = jnp.mean(rest * hat, axis=1, keepdims=True)
    grad1 = x.cot1[...] + scale * (rest - mean - hat * tilt)
    x.grad1_o[...] = grad1
    branch = low(grad1)
    wo = x.wo.reshape(n.width, n.width)
    for h in range(HEADS):
        gm = dot_nt(branch, wo[h * 128:(h + 1) * 128])
        x.message[h, :128] = low(gm)
        delta = jnp.sum(gm * x.home[h, :128].astype(F32), axis=1, keepdims=True)
        logs = x.home[h, 128:].astype(F32)
        x.message[h, 128:] = message_rows((logs[0:1], logs[1:2], logs[2:3]) + split3(to_row(delta)))

    def give(i):
        s = lax.rem(w.s + 1 + i, n.seq)
        push(x.message.at[s // n.sub], x.dtok.at[w.s], x.s_d.at[i], x.r_d.at[w.s], (s, w.f))

    loop(n.seq - 1, give)
    x.dtok[w.s] = x.message[w.head]
    gwo = low(dot_tn(mixed_low[...], branch)).reshape(n.chips, 2, n.fsdp * n.rows, n.width)
    x.gwo[...] = gwo.reshape(n.chips, 2, n.fsdp, n.rows, n.width)
    push(x.gwo.at[:, 1 - w.j], x.o0, x.s_o0.at[0], x.r_o0.at[0], w.sib)
    zero = jnp.zeros((2, n.width), F32)
    x.vec_g[...] = jnp.concatenate([
        zero,
        jnp.sum(grad * hat, axis=0, keepdims=True),
        jnp.sum(grad, axis=0, keepdims=True),
        jnp.sum(x.ci[w.t].astype(F32), axis=0, keepdims=True),
        zero, zero[:1],
    ])
    x.second_o[...] = x.second[...] + so.total() + x.vec[4:5]
    for i in range(k):
        wait(x.n2.at[0], x.s_x.at[i])
    gn.drain()
    so.drain()


def back_attention(n, w, x, sums, dbuf, gbuf, gout):
    sum_c, sum_e, sum_o = sums
    blocks = n.seq // n.sub
    wait(x.o0, x.r_o0.at[0])

    def join_o(c):
        x.o0[c] = low(x.o0[c].astype(F32) + x.gwo[c, w.j].astype(F32))

    loop(n.chips, join_o)
    sum_o.first()

    def take(i):
        p = lax.rem(w.s + 1 + i, n.seq)
        wait(x.dtok.at[p], x.r_d.at[p])

    loop(n.seq - 1, take)
    tasks = []
    for i in range(n.a):
        tasks.append(lambda i=i: (sum_c.second(i), sum_e.second(i)))
    tasks.insert(2, sum_o.second)
    tasks.append(sum_o.third)

    def relay(count):
        for _ in range(count):
            if tasks:
                tasks.pop(0)()

    slot = 0
    parts = 4
    for r in range(n.rounds):
        loop_by(UNROLL, n.seq, lambda p: spread(n, r, p, x.tab, x.dtok, dbuf, x.marks))
        for q in range(parts):
            loop_by(UNROLL, n.seq // parts, lambda g: attend_back(n, r, q * (n.seq // parts) + g, x.buf, x.marks, dbuf, gbuf))
            relay(SUMS[slot])
            slot += 1
    relay(len(tasks))

    def tokens_of(p):
        total = None
        for r in range(n.rounds):
            got = dot(picks_back(n, x.tab[r, p]), rows_of(n, gbuf.at[r, p]))
            total = got if total is None else total + got
        return total

    for m in range(1, n.sub):
        far = lax.rem(w.idx + m, n.sub)

        def offer(i, m=m, far=far):
            k = (m - 1) * blocks + i
            gout[k] = low(tokens_of(i * n.sub + far))
            push(gout.at[k], x.gin.at[k], x.s_g.at[k], x.r_g.at[k], (w.head * n.sub + far, w.f))

        loop_by(UNROLL, blocks, offer)

    def keep(i):
        x.gown[i] = tokens_of(i * n.sub + w.idx)

    loop_by(UNROLL, blocks, keep)
    loop((n.sub - 1) * blocks, lambda k: wait(gout.at[0], x.s_g.at[k]))


def back_rest(n, w, x, sums, dqv, wsum, wout, esw, vsend):
    sum_c, sum_e, sum_o = sums
    blocks = n.seq // n.sub
    weights = x.wqv.reshape(n.width, 256)
    bs = n.sub // 2
    nb = n.b // bs
    half_b = w.b // bs
    base1 = blocks
    base2 = base1 + (nb - 1) * n.a

    def finish_block(i):
        total = x.gown[i]
        for m in range(1, n.sub):
            k = (m - 1) * blocks + i
            wait(x.gin.at[k], x.r_g.at[k])
            total += x.gin[k].astype(F32)
        dqv[i] = low(total)
        x.xh[i] = low(dot_nt(dqv[i], weights[...]))

    def chip_of(a, v):
        return plane(n, w, a, v * bs + lax.rem(w.b, bs), w.f)

    for m in range(1, nb):
        far = lax.rem(half_b + m, nb)

        def to_b(i, m=m, far=far):
            a = lax.rem(w.a + 1 + i, n.a)
            finish_block(a * nb + far)
            k = (m - 1) * n.a + a
            push(x.xh.at[a * nb + far], x.xh.at[base1 + k], x.s_n1.at[k], x.r_n1.at[k], chip_of(w.a, far))

        loop(n.a, to_b)
    loop(n.a, lambda i: finish_block(lax.rem(w.a + 1 + i, n.a) * nb + half_b))

    def to_a(i):
        a = lax.rem(w.a + 1 + i, n.a)
        total = x.xh[a * nb + half_b].astype(F32)
        for m in range(1, nb):
            k = (m - 1) * n.a + a
            wait(x.xh.at[base1 + k], x.r_n1.at[k])
            total += x.xh[base1 + k].astype(F32)
        x.xh[a * nb + half_b] = low(total)

        @pl.when(i < n.a - 1)
        def _():
            push(x.xh.at[a * nb + half_b], x.xh.at[base2 + i], x.s_n2.at[i], x.r_n2.at[i], chip_of(a, half_b))

    loop(n.a, to_a)

    for i in range(blocks):
        got = dot_tn(x.nown[i], dqv[i])
        wsum[...] = got if i == 0 else wsum[...] + got
    wout[...] = low(wsum[...]).reshape(n.all, n.rows, 256)

    def rows_out(i):
        d, dev = peer(n, w, i + 1)
        push(wout.at[d], x.win.at[w.me], x.s_w2.at[i], x.r_w2.at[w.me], dev)

    loop(n.all - 1, rows_out)
    x.win[w.me] = wout[w.me]

    esw[...] = sum_e.total()
    x.egot[w.t] = esw[w.t]
    for m in range(1, n.group):
        t = lax.rem(w.t + m, n.group)
        push(esw.at[t], x.egot.at[w.t], x.s_y.at[m], x.r_y.at[w.t], member(n, w, t))
    x.go_o[...] = sum_o.total()
    x.gc_o[...] = sum_c.total()

    hat, scale = hat_of(x.second[...])
    grad = x.xh[w.a * nb + half_b].astype(F32)
    for i in range(n.a - 1):
        wait(x.xh.at[base2 + i], x.r_n2.at[i])
        grad += x.xh[base2 + i].astype(F32)
    rest = grad * x.vec[0:1]
    mean = jnp.mean(rest, axis=1, keepdims=True)
    tilt = jnp.mean(rest * hat, axis=1, keepdims=True)
    x.grad2_o[...] = x.cot2[...] + scale * (rest - mean - hat * tilt)
    gain_g = jnp.sum(grad * hat, axis=0, keepdims=True)
    shift1_g = jnp.sum(grad, axis=0, keepdims=True)
    group = 128 // n.rows
    per = 128 // n.units
    at = iota((8, 128), 0)

    def rolled(tile, lanes):
        return pltpu.roll(tile, 128 - lanes, 1) if lanes else tile

    for q in range(n.width // 128):
        cut = slice(q * 128, (q + 1) * 128)
        tile = jnp.where(at == 0, gain_g[:, cut], jnp.where(at == 1, shift1_g[:, cut], x.vec_g[:, cut]))
        for k in range(group):
            vsend[q * group + k] = rolled(tile, k * n.rows)
    for q in range(n.a * n.fsdp // per):
        for k in range(per):
            u = q * per + k
            d = (u // n.fsdp * n.group + w.t) * n.fsdp + u % n.fsdp
            tile = rolled(x.shift_g[:, q * 128:(q + 1) * 128], k * n.units)
            vsend[d] = jnp.where(at == 5, tile, vsend[d])

    def vec_out(i):
        d, dev = peer(n, w, i + 1)
        push(vsend.at[d], x.vgot.at[w.me], x.s_v.at[i], x.r_v.at[w.me], dev)

    loop(n.all - 1, vec_out)
    x.vgot[w.me] = vsend[w.me]

    def take_rows(i):
        d, _ = peer(n, w, i + 1)
        wait(x.win.at[d], x.r_w2.at[d])

    loop(n.all - 1, take_rows)
    for h in range(HEADS):
        total = 0.0
        for i in range(n.sub * n.fsdp):
            total += x.win[h * n.sub * n.fsdp + i].astype(F32)
        x.gq_o[:, h * 128:(h + 1) * 128] = total[:, :128]
        x.gv_o[:, h * 128:(h + 1) * 128] = total[:, 128:]
    for m in range(1, n.group):
        t = lax.rem(w.t + m, n.group)
        wait(x.egot.at[t], x.r_y.at[t])
    for t in range(n.group):
        for a in range(n.a):
            c = (a * n.group + t) * n.wide
            x.ge_o[:, c:c + n.wide] = x.egot[t, :, a * n.wide:(a + 1) * n.wide]

    wait(x.o0, x.s_o0.at[0])
    for m in range(1, n.group):
        wait(x.egot.at[0], x.s_y.at[m])
    loop(n.seq - 1, lambda i: wait(x.dtok.at[0], x.s_d.at[i]))
    for y in (sum_c, sum_e, sum_o):
        y.drain()
    loop((nb - 1) * n.a, lambda k: wait(x.xh.at[0], x.s_n1.at[k]))
    loop(n.a - 1, lambda k: wait(x.xh.at[0], x.s_n2.at[k]))

    def wait_all(i):
        wait(x.win.at[0], x.s_w2.at[i])
        wait(x.vgot.at[0], x.s_v.at[i])

    loop(n.all - 1, wait_all)

    def take_vec(i):
        d, _ = peer(n, w, i + 1)
        wait(x.vgot.at[d], x.r_v.at[d])

    loop(n.all - 1, take_vec)
    x.small_o[...] = jnp.sum(x.vgot[...], axis=0)


def layer_kernel(n, names, *refs):
    x = types.SimpleNamespace(**dict(zip(names, refs, strict=True)))
    w = place(n)
    t, d, g = n.tokens, n.width, n.group
    blocks = n.seq // n.sub
    pairs = (n.rounds, n.seq, n.seq, n.cap, 256)
    sums = (
        PlaneScatter(n, w, lambda a, f: x.gwc.at[a, f], x.c1, x.c2, x.s_c, x.r_c),
        PlaneScatter(n, w, lambda a, f: x.gwe.at[a, :, f], x.e1, x.e2, x.s_e, x.r_e),
        Scatter(n, w, "f", lambda a, b, f: x.o0.at[a * n.b + b, f], x.o1, x.o2, x.o3, x.s_o, x.r_o),
    )
    drains = []
    pl.run_scoped(
        lambda *r: drains.append(front_part(n, w, x, *r)),
        VM(pairs, BF), VM(((n.sub - 1) * blocks, MSG, 128), BF), VM((blocks, MSG, 128), BF),
    )
    pl.run_scoped(
        lambda *r: feed_part(n, w, x, sums, drains[0], *r),
        VM((t, d), BF), VM((g * t, n.part), BF), VM((g * t, n.part), BF),
        VM((g, t, d), BF), VM((g, t, d), BF),
    )
    pl.run_scoped(
        lambda *r: back_attention(n, w, x, sums, *r),
        VM(pairs[:-1] + (128,), BF), VM(pairs, BF), VM(((n.sub - 1) * blocks, 128, 256), BF),
    )
    pl.run_scoped(
        lambda *r: back_rest(n, w, x, sums, *r),
        VM((blocks, 128, 256), BF), VM((d, 256), F32), VM((n.all, n.rows, 256), BF), VM((g, n.rows, n.part), F32),
        VM((n.all, 8, 128), F32),
    )


def layer(n, inputs):
    inside = pl.BlockSpec(memory_space=VM)
    t, d, g, a = n.tokens, n.width, n.group, n.a
    units = n.chips * n.fsdp
    blocks = n.seq // n.sub
    nb = n.b // (n.sub // 2)
    f1, b1 = max(n.fsdp - 1, 1), max(n.b - 1, 1)
    pairs = (n.rounds, n.seq, n.seq, n.cap)
    unit_c, unit_e, unit_o = (n.units, d), (g, n.rows, n.part), (n.rows, d)
    count_f = (n.fsdp - 1) * a * n.b + (n.b - 1) * a + a - 1
    count_p = (n.fsdp - 1) * a + a - 1
    outputs = {
        "first_o": (t, d), "second_o": (t, d), "grad1_o": (t, d), "grad2_o": (t, d),
        "gq_o": (n.rows, d), "gv_o": (n.rows, d), "go_o": (n.rows, d), "ge_o": (n.rows, n.hidden), "gc_o": (n.units, d),
        "small_o": (8, 128),
    }
    scratch = {
        "xh": VM((n.seq, 128, d), BF),
        "nown": VM((blocks, 128, d), BF), "qv": VM((n.seq, 128, 256), BF),
        "wqv": VM((n.all, n.rows, 256), BF), "wqv_in": VM((n.fsdp, HEADS, n.rows, 256), BF), "we_in": VM((g, n.rows, n.part), BF),
        "small_all": VM((n.all, 16, 128), BF), "tab": VM((n.rounds, n.seq, 8, 128), F32), "vec": VM((16, d), F32),
        "shift_part": VM((8, n.part), F32), "ci": VM((g, t, d), BF),
        "buf": VM(pairs + (256,), BF), "marks": VM(pairs + (128,), BF),
        "pin": VM(((n.sub - 1) * blocks, MSG, 128), BF),
        "home": VM((HEADS, MSG, 128), BF), "dtok": VM((n.seq, MSG, 128), BF),
        "wo": VM((n.all, n.rows, d), BF), "wc": VM((a, n.fsdp, n.units, d), BF), "we": VM((a, g, n.fsdp, n.rows, n.part), BF),
        "n2": VM((g, t, d), BF),
        "gn_got1": VM((n.b, t, d), BF), "gn_got2": VM((b1, t, d), BF), "so_got1": VM((n.b, t, d), BF), "so_got2": VM((b1, t, d), BF),
        "gwc": VM((a, n.fsdp, n.units, d), BF), "gwe": VM((a, g, n.fsdp, n.rows, n.part), BF),
        "gwo": VM((n.chips, 2, n.fsdp, n.rows, d), BF), "message": VM((HEADS, MSG, 128), BF),
        "vec_g": VM((8, d), F32), "shift_g": VM((8, n.part), F32),
        "gown": VM((blocks, 128, 256), F32),
        "gin": VM(((n.sub - 1) * blocks, 128, 256), BF), "win": VM((n.all, n.rows, 256), BF),
        "c1": VM((f1, a) + unit_c, BF), "c2": VM((a - 1,) + unit_c, BF),
        "e1": VM((f1, a) + unit_e, BF), "e2": VM((a - 1,) + unit_e, BF),
        "o0": VM((n.chips, n.fsdp) + unit_o, BF), "o1": VM((f1, a, n.b) + unit_o, BF),
        "o2": VM((b1, a) + unit_o, BF), "o3": VM((a - 1,) + unit_o, BF),
        "egot": VM(unit_e, F32), "vgot": VM((n.all, 8, 128), F32),
    }
    sems = {
        "small": n.seq, "wq": n.seq, "f": (2, n.fsdp), "n": 2 * n.chips + 2 * a + n.b, "ns": n.chips + 2 * a, "ag": (3, units + 4 * a * n.b), "os": units, "ex": g, "ci": g,
        "p": (n.sub - 1) * blocks, "out": HEADS, "x": 2 * n.b, "gn": 2 * n.b, "so": 2 * n.b, "d": n.seq, "o0": 1,
        "c": count_p, "e": count_p, "o": count_f, "g": (n.sub - 1) * blocks, "w2": n.all, "n1": max((nb - 1) * a, 1), "n2": a,
        "v": n.all, "y": g,
    }
    for key, count in sems.items():
        for side in ("s_", "r_"):
            if key == "x" and side == "r_":
                count = g
            scratch[side + key] = DMA(count if isinstance(count, tuple) else (count,))
    names = list(inputs) + list(outputs) + list(scratch)
    return pl.pallas_call(
        functools.partial(layer_kernel, n, names),
        out_shape=tuple(jax.ShapeDtypeStruct(s, F32) for s in outputs.values()),
        in_specs=[inside] * len(inputs),
        out_specs=(inside,) * len(outputs),
        scratch_shapes=list(scratch.values()),
        compiler_params=pltpu.CompilerParams(collective_id=1, has_side_effects=True, vmem_limit_bytes=60 << 20),
        name="layer",
    )(*inputs.values())


def deliver_kernel(n, count, *refs):
    arrays, small, outs = refs[:count], refs[count], refs[count + 1:2 * count + 1]
    vectors, held, come, leave = refs[2 * count + 1:-count - 2], refs[-count - 2:-2], refs[-2], refs[-1]
    ins = [pltpu.make_async_copy(arrays[i], held[i], come.at[i]) for i in range(count)]
    ends = [pltpu.make_async_copy(held[i], outs[i], leave.at[i]) for i in range(count)]
    for cp in ins:
        cp.start()
    for row, ref in zip((0, 1, 2, 3, 5, 4), vectors, strict=True):
        ref[...] = small[row:row + 1, :ref.shape[1]]
    for before, after in zip(ins, ends, strict=True):
        before.wait()
        after.start()
    for cp in ends:
        cp.wait()


def deliver(n, arrays, small):
    anywhere = pl.BlockSpec(memory_space=pl.ANY)
    inside = pl.BlockSpec(memory_space=VM)
    shape = jax.ShapeDtypeStruct
    sizes = (n.rows, n.rows, n.rows, n.rows, n.units, n.rows)
    count = len(arrays)
    return pl.pallas_call(
        functools.partial(deliver_kernel, n, count),
        out_shape=tuple(shape(y.shape, F32) for y in arrays) + tuple(shape((1, k), F32) for k in sizes),
        in_specs=[anywhere] * count + [inside],
        out_specs=(anywhere,) * count + (inside,) * len(sizes),
        scratch_shapes=[VM(y.shape, F32) for y in arrays] + [DMA((count,)), DMA((count,))],
        compiler_params=pltpu.CompilerParams(vmem_limit_bytes=60 << 20),
        name="deliver",
    )(*arrays, small)


def on_device(
    first_half,
    second_half,
    first_cotangent,
    second_cotangent,
    bucket_ids,
    slot_source,
    live_slots,
    mixer_gain,
    mixer_shift,
    query_weight,
    value_weight,
    output_weight,
    feed_gain,
    feed_shift,
    expand_weight,
    expand_bias,
    contract_weight,
    contract_bias,
):
    seq, fsdp = lax.axis_size("seq"), lax.axis_size("fsdp")
    n = setup(seq, fsdp, first_half.shape[2], expand_weight.shape[1], first_half.shape[1])
    vectors = jnp.stack([mixer_gain, mixer_shift, feed_gain, feed_shift, contract_bias] + [jnp.zeros_like(mixer_gain)] * 3)
    *arrays, small = layer(n, {
        "first": first_half[0], "second": second_half[0], "cot1": first_cotangent[0], "cot2": second_cotangent[0],
        "vectors": vectors, "bias": expand_bias.reshape(1, -1), "buckets": bucket_ids[0],
        "query_w": query_weight, "value_w": value_weight, "expand_w": expand_weight,
        "wo_in": output_weight, "wc_in": contract_weight,
    })
    outs = deliver(n, arrays, small)
    first_out, second_out, grad1, grad2, gq, gv, go, ge, gc = outs[:9]
    gain1, shift1, gain2, shift2, up_bias, down_bias = [y.reshape(-1) for y in outs[9:]]
    return (
        first_out[None], second_out[None], grad1[None], grad2[None],
        gain1, shift1, gq, gv, go, gain2, shift2, ge, up_bias, gc, down_bias,
    )


def solution(mesh):
    tokens, slots = P("fsdp", "seq", None), P("fsdp", None, "seq")
    vector, matrix = P(("seq", "fsdp")), P(("seq", "fsdp"), None)
    return jax.shard_map(
        on_device,
        mesh=mesh,
        in_specs=(tokens,) * 4 + (slots,) * 3 + (vector, vector, matrix, matrix, matrix, vector, vector, matrix, vector, matrix, vector),
        out_specs=(tokens,) * 4 + (vector, vector, matrix, matrix, matrix, vector, vector, matrix, vector, matrix, vector),
        check_vma=False,
    )
```

```python
import functools
import types

import jax
import jax.numpy as jnp
from jax import lax
from jax.experimental import pallas as pl
from jax.experimental.pallas import tpu as pltpu
from jax.sharding import PartitionSpec as P

HEADS = 8
HEAD_DIM = 128
ROUNDS = 4
SPAN = 64
BF = jnp.bfloat16
F32 = jnp.float32
MESH = pl.DeviceIdType.MESH
DMA = pltpu.SemaphoreType.DMA
VM = pltpu.VMEM
MSG = 144


def dot(a, b):
    return lax.dot_general(a, b, (((1,), (0,)), ((), ())), preferred_element_type=F32)


def dot_nt(a, b):
    return lax.dot_general(a, b, (((1,), (1,)), ((), ())), preferred_element_type=F32)


def dot_tn(a, b):
    return lax.dot_general(a, b, (((0,), (0,)), ((), ())), preferred_element_type=F32)


def iota(shape, dim):
    return lax.broadcasted_iota(jnp.int32, shape, dim)


def iotaf(shape, dim):
    return iota(shape, dim).astype(F32)


def low(x):
    return x.astype(BF)


def split3(x):
    hi = x.astype(BF).astype(F32)
    rest = x - hi
    mid = rest.astype(BF).astype(F32)
    return hi, mid, rest - mid


def loop(count, body):
    def step(i, carry):
        body(i)
        return carry

    lax.fori_loop(0, count, step, 0)


def loop_by(k, count, body):
    k = k if count % k == 0 else 1

    def several(i):
        for u in range(k):
            body(i * k + u)

    loop(count // k, several)


def push(src, dst, send, recv, dev):
    pltpu.make_async_remote_copy(
        src_ref=src, dst_ref=dst, send_sem=send, recv_sem=recv, device_id=dev, device_id_type=MESH
    ).start()


def wait(ref, sem):
    pltpu.make_async_copy(ref, ref, sem).wait()


def to_column(row):
    size = row.shape[1]
    eye = iota((size, size), 0) == iota((size, size), 1)
    return jnp.sum(jnp.where(eye, row, 0.0), axis=1, keepdims=True)


def to_row(column):
    size = column.shape[0]
    eye = iota((size, size), 0) == iota((size, size), 1)
    return jnp.sum(jnp.where(eye, column, 0.0), axis=0, keepdims=True)


def message_rows(rows):
    at = iota((MSG - 128, 128), 0)
    out = jnp.zeros((MSG - 128, 128), F32)
    for i, row in enumerate(rows):
        out = jnp.where(at == i, row, out)
    return low(out)


def setup(seq, fsdp, width, hidden, tokens):
    n = types.SimpleNamespace()
    n.seq, n.fsdp, n.all = seq, fsdp, seq * fsdp
    n.chips = seq // 2
    n.b = 2 if n.chips <= 8 else 4
    n.a = n.chips // n.b
    n.sub = seq // HEADS
    n.rounds = ROUNDS // n.sub
    n.cap = 4 * SPAN // seq
    n.width, n.hidden, n.tokens = width, hidden, tokens
    n.rows = width // n.all
    n.units = hidden // n.all
    n.group = 2 * n.b
    n.part = hidden // n.group
    n.wide = hidden // seq
    return n


def place(n):
    w = types.SimpleNamespace()
    w.s, w.f = lax.axis_index("seq"), lax.axis_index("fsdp")
    w.c, w.j = w.s // 2, lax.rem(w.s, 2)
    w.a, w.b = w.c // n.b, lax.rem(w.c, n.b)
    w.me = w.s * n.fsdp + w.f
    w.head, w.idx = w.s // n.sub, lax.rem(w.s, n.sub)
    w.sib = (w.s + 1 - 2 * w.j, w.f)
    w.t = w.b * 2 + w.j
    return w


def plane(n, w, a, b, f):
    return ((a * n.b + b) * 2 + w.j, f)


def member(n, w, t):
    return ((w.a * n.b) * 2 + t, w.f)


def peer(n, w, i):
    d = lax.rem(w.me + i, n.all)
    return d, (d // n.fsdp, lax.rem(d, n.fsdp))


def meet_all(n, w):
    barrier = pltpu.get_barrier_semaphore()

    def greet(i):
        pl.semaphore_signal(barrier, inc=1, device_id=peer(n, w, i + 1)[1], device_id_type=MESH)

    loop(n.all - 1, greet)
    pl.semaphore_wait(barrier, n.all - 1)


class Line:
    def __init__(self, n, w, send_sem, per_unit):
        self.n, self.w, self.send_sem, self.per_unit, self.sent = n, w, send_sem, per_unit, []

    def inside(self, shift):
        a = self.w.a + shift
        return (a >= 0) & (a < self.n.a)

    def slot(self, shift, k):
        return 2 + (self.w.a + shift) * self.per_unit + k

    def send(self, ref, recv, dev, slot, *shifts):
        push(ref, ref, self.send_sem(slot()), recv, dev)
        self.sent.append((slot, shifts))

    def both(self, shifts):
        return functools.reduce(jnp.logical_and, [self.inside(v) for v in shifts])

    def start(self, own, neighbour):
        for sign in (-1, 1):
            @pl.when(self.inside(-sign))
            def _(sign=sign):
                self.send(*own(), neighbour(self.w.a - sign), lambda: (1 + sign) // 2, -sign)

    def step(self, far, take, neighbour, more):
        for sign in (-1, 1):
            @pl.when(self.inside(sign * far))
            def _(sign=sign):
                ref, recv = take(self.w.a + sign * far)
                if far < self.n.a - 1:
                    @pl.when(self.inside(-sign))
                    def _():
                        self.send(ref, recv, neighbour(self.w.a - sign), lambda: self.slot(sign * far, 0), sign * far, -sign)
                for k, dev in enumerate(more):
                    self.send(ref, recv, dev, lambda k=k: self.slot(sign * far, 1 + k), sign * far)

    def drain_sends(self, ref):
        for slot, shifts in self.sent:
            if shifts:
                @pl.when(self.both(shifts))
                def _(slot=slot):
                    wait(ref(), self.send_sem(slot()))
            else:
                wait(ref(), self.send_sem(slot()))


class Gather(Line):
    def __init__(self, n, w, unit, index, send_sem, recv_sem, over_b=False, arrived=None):
        super().__init__(n, w, send_sem, n.fsdp + (n.b - 1 if over_b else 0))
        self.unit, self.index, self.recv_sem = unit, index, recv_sem
        self.over_b, self.arrived = over_b, arrived

    def entry(self, a, b, f):
        return self.unit(a, b, f), self.recv_sem(self.index(a, b, f))

    def own(self):
        w = self.w
        return self.unit(w.a, w.b, w.f), self.index(w.a, w.b, w.f)

    def take(self, a, b, f):
        ref, recv = self.entry(a, b, f)
        wait(ref, recv)
        if self.arrived:
            self.arrived(ref, self.index(a, b, f))
        return ref, recv

    def neighbour(self, a):
        return plane(self.n, self.w, a, self.w.b, self.w.f)

    def others(self, over_f=True):
        n, w = self.n, self.w
        out = []
        if over_f:
            out += [plane(n, w, w.a, w.b, lax.rem(w.f + m, n.fsdp)) for m in range(1, n.fsdp)]
        if self.over_b:
            out += [plane(n, w, w.a, lax.rem(w.b + m, n.b), w.f) for m in range(1, n.b)]
        return out

    def to_a(self):
        self.start(lambda: self.entry(self.w.a, self.w.b, self.w.f), self.neighbour)

    def column(self, far):
        w = self.w
        if far == 0:
            for k, dev in enumerate(self.others()):
                self.send(*self.entry(w.a, w.b, w.f), dev, lambda k=k: self.slot(0, 1 + k))
        else:
            self.step(far, lambda a: self.take(a, w.b, w.f), self.neighbour, self.others())

    def corner_slot(self, shift, q, k):
        base = 2 + self.n.a * self.per_unit
        return base + ((self.w.a + shift) * (self.n.fsdp - 1) + q - 1) * (self.n.b - 1) + k

    def corner(self, far):
        if not self.over_b:
            return

        def pass_on(shift, *shifts):
            for q in range(1, self.n.fsdp):
                ref, recv = self.take(self.w.a + shift, self.w.b, lax.rem(self.w.f + q, self.n.fsdp))
                for k, dev in enumerate(self.others(False)):
                    self.send(ref, recv, dev, lambda q=q, k=k: self.corner_slot(shift, q, k), *shifts)

        if far == 0:
            pass_on(0)
        else:
            for sign in (-1, 1):
                @pl.when(self.inside(sign * far))
                def _(sign=sign):
                    pass_on(sign * far, sign * far)

    def finish(self):
        n, w = self.n, self.w
        for i in range(n.a):
            a = lax.rem(w.a + i, n.a)
            for q in range(n.fsdp):
                for v in range(n.b):
                    if (v if self.over_b else q) != 0 and (self.over_b or v == 0):
                        self.take(a, lax.rem(w.b + v, n.b), lax.rem(w.f + q, n.fsdp))

    def drain(self):
        self.drain_sends(lambda: self.unit(self.w.a, self.w.b, self.w.f))


def tables(n, w, small_all, tab):
    nb = 2 * n.seq
    before = low((iota((128, 128), 0) < iota((128, 128), 1)).astype(F32))
    for r in range(n.rounds):
        def bucket_row(p):
            tile = small_all[p * n.fsdp + w.f].astype(F32)
            keep = iota((16, 128), 0) == 8 + w.idx * n.rounds + r
            return jnp.sum(jnp.where(keep, tile, 0.0), axis=0, keepdims=True)

        def count(p, run):
            row = bucket_row(p)
            hot = (iotaf((nb, 128), 0) == row).astype(F32)
            ahead = dot(low(hot), before)
            pos = jnp.sum(hot * (ahead + run), axis=0, keepdims=True)
            group = jnp.floor(row * 0.5)
            hotg = (iotaf((n.seq, 128), 0) == group).astype(F32)
            rank = jnp.sum(hotg * dot(low(hotg), before), axis=0, keepdims=True)
            line = group * n.cap + rank
            at = iota((8, 128), 0)
            tab[r, p] = jnp.where(at == 0, line, jnp.where(at == 1, pos, jnp.where(at == 2, row, 0.0)))
            return run + jnp.sum(hot, axis=1, keepdims=True)

        totals = lax.fori_loop(0, n.seq, count, jnp.zeros((nb, 1), F32))

        def settle(p):
            tile = tab[r, p]
            row = tile[2:3]
            odd = row - 2.0 * jnp.floor(row * 0.5)
            hot = (iotaf((nb, 128), 0) == row - 1.0).astype(F32)
            slot = tile[1:2] + odd * jnp.sum(hot * totals, axis=0, keepdims=True)
            block = jnp.floor(slot * (1.0 / SPAN))
            tab[r, p] = jnp.where(iota((8, 128), 0) == 1, block, tile)

        loop(n.seq, settle)


def picks(n, tile):
    return low((iotaf((n.seq * n.cap, 128), 0) == tile[0:1]).astype(F32))


def picks_back(n, tile):
    return low((iotaf((128, n.seq * n.cap), 1) == to_column(tile[0:1])).astype(F32))


def block_marks(tile):
    return low((iotaf((128, 128), 1) == to_column(tile[1:2])).astype(F32))


FAR = 2.0 ** 30


def with_blocks(marks, query, key):
    i, k = iota((128, 128), 0), iota((128, 128), 1)
    seen = dot(marks, low((((k == i) | (k == i + 1)) & (i < 4)).astype(F32)))
    lane = iota(marks.shape, 1)
    ask = low(jnp.where(lane < 4, marks.astype(F32) * -FAR, 0.0))
    answer = low(jnp.where(lane < 4, 1.0 - seen, 0.0))
    return jnp.concatenate([query, ask], axis=1), jnp.concatenate([key, answer], axis=1)


def halves(wide_query, wide_key):
    size = wide_query.shape[0]
    cut = size // 2
    row, col = iota((cut, cut), 0), iota((cut, cut), 1)

    def ordered(raw):
        return jnp.where(col < row, raw, jnp.where(col == row, -1e4, -1e9))

    first = ordered(dot_nt(wide_query[:cut], wide_key[:cut]))
    rest = dot_nt(wide_query[cut:], wide_key)
    return first, jnp.concatenate([rest[:, :cut], ordered(rest[:, cut:])], axis=1)


def rows_of(n, ref):
    got = ref[...]
    if n.cap % 16:
        return low(got.astype(F32).reshape(n.seq * n.cap, got.shape[-1]))
    return got.reshape(n.seq * n.cap, got.shape[-1])


def put_rows(n, ref, value):
    ref[...] = value.reshape(n.seq, n.cap, value.shape[-1]).astype(ref.dtype)


def keys_of(query):
    wide = query.astype(F32)
    scale = lax.rsqrt(jnp.sum(wide * wide, axis=1, keepdims=True) + 1e-06)
    return low(wide * scale), scale


def fill_block(n, r, p, tab, qv, buf, marks):
    tile = tab[r, p]
    hot = picks(n, tile)
    got = dot(hot, jnp.concatenate([qv[p], block_marks(tile)], axis=1))
    put_rows(n, buf.at[r, :, p], got[:, :256])
    put_rows(n, marks.at[r, :, p], got[:, 256:])


def attend(n, r, g, buf, marks, obuf):
    both = rows_of(n, buf.at[r, g])
    query, value = both[:, :128], both[:, 128:]
    key, _ = keys_of(query)
    cut = query.shape[0] // 2
    outs = []
    for score, values in zip(halves(*with_blocks(rows_of(n, marks.at[r, g]), query, key)), (value[:cut], value)):
        top = jnp.max(score, axis=1, keepdims=True)
        expo = jnp.exp(score - top)
        total = jnp.sum(expo, axis=1, keepdims=True)
        out = dot(low(expo), values) / total
        hi, mid, rest = split3(top + jnp.log(total))
        lane = iota((cut, 128), 1)
        logs = jnp.where(lane == 0, hi, jnp.where(lane == 1, mid, jnp.where(lane == 2, rest, 0.0)))
        outs.append(jnp.concatenate([out, logs], axis=1))
    put_rows(n, obuf.at[r, :, g], jnp.concatenate(outs, axis=0))


def merge(outs, logs):
    top = functools.reduce(jnp.maximum, logs)
    weights = [jnp.exp(v - top) for v in logs]
    total = sum(weights)
    return sum(x * y for x, y in zip(weights, outs)) / total, top + jnp.log(total)


def merge_rounds(n, p, tab, obuf):
    outs, logs = [], []
    for r in range(n.rounds):
        got = dot(picks_back(n, tab[r, p]), rows_of(n, obuf.at[r, p]))
        outs.append(got[:, :128])
        logs.append(jnp.sum(got[:, 128:], axis=1, keepdims=True))
    return merge(outs, logs)


def write_message(ref, out, log):
    ref[:128] = low(out)
    ref[128:] = message_rows(split3(to_row(log)))


def read_log(ref):
    return to_column(jnp.sum(ref[128:].astype(F32), axis=0, keepdims=True))


def hat_of(x):
    center = x - jnp.mean(x, axis=1, keepdims=True)
    scale = lax.rsqrt(jnp.mean(center * center, axis=1, keepdims=True) + 1e-05)
    return center * scale, scale


def normalize(x, gain, shift):
    hat, scale = hat_of(x)
    return hat, scale, hat * gain + shift


def placed(row, spot):
    size = row.shape[1]
    put = (iota((size, 128), 1) == iota((size, 128), 0) + spot * size).astype(F32)
    return dot(row, low(put))


def gelu_pair(x):
    k = 0.7978845608028654
    square = x * x
    t = jnp.tanh(k * (x + 0.044715 * (square * x)))
    half = 0.5 * (1.0 + t)
    return x * half, half + 0.5 * x * (1.0 - t * t) * (k * (1.0 + 0.134145 * square))


class GroupSum:
    def __init__(self, n, w, out, got1, got2, send, recv):
        self.n, self.w, self.out, self.got1, self.got2 = n, w, out, got1, got2
        self.send, self.recv = send, recv

    def fill(self, product):
        n, w = self.n, self.w
        for m in range(n.b):
            b = lax.rem(w.b + 1 + m, n.b)
            self.out[pl.ds(2 * b, 2)] = low(product(b)).reshape(2, n.tokens, n.width)
            t = b * 2 + 1 - w.j
            push(self.out.at[t], self.got1.at[b], self.send.at[m], self.recv.at[b], w.sib)

    def chips(self):
        n, w = self.n, self.w
        for m in range(1, n.b):
            b = lax.rem(w.b + m, n.b)
            t = b * 2 + w.j
            wait(self.got1.at[b], self.recv.at[b])
            self.out[t] = low(self.out[t].astype(F32) + self.got1[b].astype(F32))
            k = n.b + m - 1
            push(self.out.at[t], self.got2.at[m - 1], self.send.at[k], self.recv.at[k], member(n, w, t))

    def total(self):
        n, w = self.n, self.w
        wait(self.got1.at[w.b], self.recv.at[w.b])
        total = self.out[w.t].astype(F32) + self.got1[w.b].astype(F32)
        for m in range(1, n.b):
            wait(self.got2.at[m - 1], self.recv.at[n.b + m - 1])
            total += self.got2[m - 1].astype(F32)
        return total

    def drain(self):
        for k in range(2 * self.n.b - 1):
            wait(self.got1.at[0], self.send.at[k])


class Scatter:
    def __init__(self, n, w, outer, part, got1, got2, got3, send, recv):
        self.n, self.w, self.outer, self.part = n, w, outer, part
        self.got1, self.got2, self.got3 = got1, got2, got3
        self.send, self.recv = send, recv
        self.one, self.two = (n.fsdp, n.b) if outer == "f" else (n.b, n.fsdp)
        self.me1, self.me2 = (w.f, w.b) if outer == "f" else (w.b, w.f)
        self.base2 = (self.one - 1) * n.a * self.two
        self.base3 = self.base2 + (self.two - 1) * n.a

    def mine(self, a, one, two):
        return self.part(a, two, one) if self.outer == "f" else self.part(a, one, two)

    def dev(self, a, one, two):
        if self.outer == "f":
            return plane(self.n, self.w, a, two, one)
        return plane(self.n, self.w, a, one, two)

    def first(self):
        for m in range(1, self.one):
            far = lax.rem(self.me1 + m, self.one)

            def body(i, m=m, far=far):
                a, two = i // self.two, lax.rem(i, self.two)
                k = (m - 1) * self.n.a * self.two + i
                push(self.mine(a, far, two), self.got1.at[m - 1, a, two], self.send.at[k], self.recv.at[k],
                     self.dev(self.w.a, far, self.me2))

            loop(self.n.a * self.two, body)

    def second(self):
        def body(i):
            m2, a = i // self.n.a, lax.rem(i, self.n.a)
            two = lax.rem(self.me2 + 1 + m2, self.two)
            for m in range(1, self.one):
                k = (m - 1) * self.n.a * self.two + a * self.two + two
                wait(self.got1.at[m - 1, a, two], self.recv.at[k])
            self.fold1(a, two)

            @pl.when(m2 < self.two - 1)
            def _():
                k = self.base2 + m2 * self.n.a + a
                push(self.got1.at[0, a, two], self.got2.at[m2, a], self.send.at[k], self.recv.at[k],
                     self.dev(self.w.a, self.me1, two))

        loop(self.n.a * self.two, body)

    def fold1(self, a, two):
        total = self.mine(a, self.me1, two)[...].astype(F32)
        for m in range(1, self.one):
            total += self.got1[m - 1, a, two].astype(F32)
        self.got1[0, a, two] = low(total)

    def third(self):
        def body(i):
            a = lax.rem(self.w.a + 1 + i, self.n.a)
            for m2 in range(self.two - 1):
                wait(self.got2.at[m2, a], self.recv.at[self.base2 + m2 * self.n.a + a])
            total = self.got1[0, a, self.me2].astype(F32)
            for m2 in range(self.two - 1):
                total += self.got2[m2, a].astype(F32)
            self.got2[0, a] = low(total)

            @pl.when(i < self.n.a - 1)
            def _():
                k = self.base3 + i
                push(self.got2.at[0, a], self.got3.at[i], self.send.at[k], self.recv.at[k],
                     self.dev(a, self.me1, self.me2))

        loop(self.n.a, body)

    def total(self):
        total = self.got2[0, self.w.a].astype(F32)
        for i in range(self.n.a - 1):
            wait(self.got3.at[i], self.recv.at[self.base3 + i])
            total += self.got3[i].astype(F32)
        return total

    def drain(self):
        loop(self.base3 + self.n.a - 1, lambda k: wait(self.got3.at[0], self.send.at[k]))


class PlaneScatter:
    def __init__(self, n, w, part, got1, got2, send, recv):
        self.n, self.w, self.part, self.got1, self.got2, self.send, self.recv = n, w, part, got1, got2, send, recv
        self.base = (n.fsdp - 1) * n.a

    def first(self):
        n, w = self.n, self.w
        for m in range(1, n.fsdp):
            far = lax.rem(w.f + m, n.fsdp)

            def body(i, m=m, far=far):
                a = lax.rem(w.a + 1 + i, n.a)
                k = (m - 1) * n.a + a
                push(self.part(a, far), self.got1.at[m - 1, a], self.send.at[k], self.recv.at[k], plane(n, w, w.a, w.b, far))

            loop(n.a, body)

    def second(self, i):
        n, w = self.n, self.w
        a = lax.rem(w.a + 1 + i, n.a)
        total = self.part(a, w.f)[...].astype(F32)
        for m in range(1, n.fsdp):
            wait(self.got1.at[m - 1, a], self.recv.at[(m - 1) * n.a + a])
            total += self.got1[m - 1, a].astype(F32)
        self.got1[0, a] = low(total)
        if i < n.a - 1:
            k = self.base + i
            push(self.got1.at[0, a], self.got2.at[i], self.send.at[k], self.recv.at[k], plane(n, w, a, w.b, w.f))

    def total(self):
        total = self.got1[0, self.w.a].astype(F32)
        for i in range(self.n.a - 1):
            wait(self.got2.at[i], self.recv.at[self.base + i])
            total += self.got2[i].astype(F32)
        return total

    def drain(self):
        loop(self.base + self.n.a - 1, lambda k: wait(self.got2.at[0], self.send.at[k]))


def spread(n, r, p, tab, dtok, dbuf, marks):
    tile = tab[r, p]
    shift = low((iota((MSG - 128, 128), 0) + 4 == iota((MSG - 128, 128), 1)).astype(F32))
    marked = block_marks(tile) + low(dot_tn(dtok[p, 128:], shift))
    got = dot(picks(n, tile), jnp.concatenate([dtok[p, :128], marked], axis=1))
    put_rows(n, dbuf.at[r, :, p], got[:, :128])
    put_rows(n, marks.at[r, :, p], got[:, 128:])


def attend_back(n, r, g, buf, marks, dbuf, gbuf):
    both, cot, marked = rows_of(n, buf.at[r, g]), rows_of(n, dbuf.at[r, g]), rows_of(n, marks.at[r, g])
    query, value = both[:, :128], both[:, 128:]
    aux = marked.astype(F32)
    lane = iota(aux.shape, 1)
    log_all = jnp.sum(jnp.where((lane >= 4) & (lane < 7), aux, 0.0), axis=1, keepdims=True)
    delta = jnp.sum(jnp.where(lane >= 7, aux, 0.0), axis=1, keepdims=True)
    key, scale = keys_of(query)
    cut = query.shape[0] // 2
    score0, score1 = halves(*with_blocks(marked, query, key))
    under = iota((cut, cut), 1) < iota((cut, cut), 0)
    prob0 = jnp.exp(score0 - log_all[:cut])
    prob1 = jnp.exp(score1 - log_all[cut:])
    back0 = low(jnp.where(under, prob0 * (dot_nt(cot[:cut], value[:cut]) - delta[:cut]), 0.0))
    back1 = prob1 * (dot_nt(cot[cut:], value) - delta[cut:])
    back1 = low(jnp.concatenate([back1[:, :cut], jnp.where(under, back1[:, cut:], 0.0)], axis=1))
    direct = jnp.concatenate([dot(back0, key[:cut]), dot(back1, key)], axis=0)

    def both_halves(first, rest, rows):
        total = dot_tn(rest, rows[cut:])
        return jnp.concatenate([total[:cut] + dot_tn(first, rows[:cut]), total[cut:]], axis=0)

    back_key = both_halves(back0, back1, query)
    back_value = both_halves(low(prob0), low(prob1), cot)
    wide = query.astype(F32)
    inner = jnp.sum(wide * back_key, axis=1, keepdims=True)
    total = direct + scale * back_key - wide * (scale * scale * scale * inner)
    put_rows(n, gbuf.at[r, :, g], jnp.concatenate([total, back_value], axis=1))


UNROLL = 2
RELAYS = (0, 0, 0, 0, 0, 1, 1, 1, 1)
SUMS = (1, 1, 2, 2, 1, 1, 1, 1)


def greet_all(n, w, barrier):
    def greet(i):
        pl.semaphore_signal(barrier, inc=1, device_id=peer(n, w, i + 1)[1], device_id_type=MESH)

    loop(n.all - 1, greet)


def pack(n, w, x):
    x.ci[w.t] = low(x.cot2[...])
    for t in range(n.group):
        for a in range(n.a):
            s = a * n.group + t
            x.we_in[t, :, a * n.wide:(a + 1) * n.wide] = x.expand_w[:, s * n.wide:(s + 1) * n.wide]
    lead = placed(x.vectors[...], lax.rem(w.me, 128 // n.rows))
    extra = placed(jnp.broadcast_to(x.bias[...], (8, n.units)), lax.rem(w.me, 128 // n.units))
    lead = jnp.where(iota((8, 128), 0) == 5, extra, lead)
    x.small_all[w.me] = low(jnp.concatenate([lead, x.buckets[...].astype(F32), jnp.zeros((8 - ROUNDS, 128), F32)]))
    for h in range(HEADS):
        x.wqv_in[w.f, h, :, :128] = x.query_w[:, h * 128:(h + 1) * 128]
        x.wqv_in[w.f, h, :, 128:] = x.value_w[:, h * 128:(h + 1) * 128]
    x.wo[w.me] = x.wo_in[...]
    for q, ref in enumerate((x.query_w, x.value_w)):
        pltpu.make_async_copy(ref, x.full.at[q, w.me], x.s_loc.at[q]).start()
    x.wc[w.a, w.f] = x.wc_in[...]
    x.we[w.a, w.t, w.f] = x.we_in[w.t]


def vectors_of(n, w, x):
    group = 128 // n.rows
    for q in range(n.width // 128):
        x.vec[:, q * 128:(q + 1) * 128] = jnp.sum(
            x.small_all[q * group:(q + 1) * group].astype(F32), axis=0
        )
    per = 128 // n.units
    for q in range(n.a * n.fsdp // per):
        a, rest = q * per // n.fsdp, q * per % n.fsdp
        first = (a * n.group + w.t) * n.fsdp + rest
        total = sum(x.small_all[first + k].astype(F32) for k in range(per))
        x.shift_part[:, q * 128:(q + 1) * 128] = jnp.broadcast_to(total[5:6], (8, 128))


def front_part(n, w, x, obuf, pmsg, omsg):
    barrier = pltpu.get_barrier_semaphore()
    greet_all(n, w, barrier)
    hat, _ = hat_of(x.second[...])
    x.xh[w.s] = low(hat)
    pack(n, w, x)
    pl.semaphore_wait(barrier, n.all - 1)

    def spot(i, v):
        return (lax.rem(w.a + i, n.a) * n.b + lax.rem(w.b + v, n.b)) * 2 + w.j

    def hat_at(a):
        block = (a * n.b + w.b) * 2 + w.j
        return x.xh.at[block], x.r_n.at[block // 2]

    def hat_chip(a):
        return ((a * n.b + w.b) * 2 + w.j, w.f)

    hats = Line(n, w, lambda k: x.s_n.at[k], n.b)

    def share_hat(block):
        push(x.xh.at[block], x.xh.at[block], x.s_ns.at[block // 2], x.r_ns.at[block // 2], w.sib)

    far_b = [(spot(0, v), w.f) for v in range(1, n.b)]
    hats.start(lambda: hat_at(w.a), hat_chip)
    for k, dev in enumerate(far_b):
        hats.send(*hat_at(w.a), dev, lambda k=k: hats.slot(0, 1 + k))
    share_hat(w.s)
    for m in range(1, n.group):
        t = lax.rem(w.t + m, n.group)
        push(x.we_in.at[t], x.we.at[w.a, w.t, w.f], x.s_ex.at[m], x.r_ex.at[w.t], member(n, w, t))

    mine = pl.ds(w.s * n.fsdp, n.fsdp)
    for q in range(1, n.fsdp):
        far = (w.s, lax.rem(w.f + q, n.fsdp))
        push(x.small_all.at[w.me], x.small_all.at[w.me], x.s_f.at[0, q], x.r_f.at[0, w.f], far)
        push(x.wqv_in.at[w.f], x.wqv_in.at[w.f], x.s_f.at[1, q], x.r_f.at[1, w.f], far)
    for q in range(1, n.fsdp):
        f = lax.rem(w.f + q, n.fsdp)
        wait(x.small_all.at[w.me], x.r_f.at[0, f])

    def send_small(i):
        s = lax.rem(w.s + 1 + i, n.seq)
        push(x.small_all.at[mine], x.small_all.at[mine], x.s_small.at[i], x.r_small.at[w.s], (s, w.f))

    loop(n.seq - 1, send_small)
    for q in range(1, n.fsdp):
        f = lax.rem(w.f + q, n.fsdp)
        wait(x.wqv_in.at[f], x.r_f.at[1, f])

    def send_w(i):
        s = lax.rem(w.s + 1 + i, n.seq)
        push(x.wqv_in.at[:, s // n.sub], x.wqv.at[mine], x.s_wq.at[i], x.r_wq.at[w.s], (s, w.f))

    loop(n.seq - 1, send_w)
    x.wqv[mine] = x.wqv_in[:, w.head]

    def shared_o(ref, uid):
        push(ref, ref, x.s_os.at[uid], x.r_os.at[uid], w.sib)

    def all_index(a, b, f):
        return (a * n.b + b) * n.fsdp + f

    def part_index(a, b, f):
        return a * n.fsdp + f

    g_o = Gather(n, w, lambda a, b, f: x.wo.at[((a * n.b + b) * 2 + w.j) * n.fsdp + f], all_index, lambda i: x.s_go.at[i], lambda u: x.r_go.at[u], True, shared_o)
    g_c = Gather(n, w, lambda a, b, f: x.wc.at[a, f], part_index, lambda i: x.s_gc.at[i], lambda u: x.r_gc.at[u])
    g_e = Gather(n, w, lambda a, b, f: x.we.at[a, :, f], part_index, lambda i: x.s_ge.at[i], lambda u: x.r_ge.at[u])
    gathers = (g_o, g_c, g_e)
    for m in range(1, n.group):
        t = lax.rem(w.t + m, n.group)
        wait(x.we.at[w.a, t, w.f], x.r_ex.at[t])
        push(x.ci.at[w.t], x.ci.at[w.t], x.s_ci.at[m], x.r_ci.at[w.t], member(n, w, t))
    shared_o(x.wo.at[w.me], (w.a * n.b + w.b) * n.fsdp + w.f)
    for y in gathers:
        y.column(0)

    def wait_small(i):
        s = lax.rem(w.s + 1 + i, n.seq)
        wait(x.small_all.at[mine], x.r_small.at[s])

    loop(n.seq - 1, wait_small)
    vectors_of(n, w, x)
    tables(n, w, x.small_all, x.tab)
    weights = x.wqv.reshape(n.width, 256)

    def project(block):
        normed = low(x.xh[block].astype(F32) * x.vec[0:1] + x.vec[1:2])

        @pl.when(lax.rem(block, n.sub) == w.idx)
        def _():
            x.nown[block // n.sub] = normed

        x.qv[block] = low(dot(normed, weights[...]))

    for far in range(1, n.a):
        def take_hat(a):
            ref, recv = hat_at(a)
            wait(ref, recv)
            return ref, recv

        hats.step(far, take_hat, hat_chip, far_b)
        for sign in (-1, 1):
            @pl.when(hats.inside(sign * far))
            def _(sign=sign):
                share_hat(((w.a + sign * far) * n.b + w.b) * 2 + w.j)
    for y in gathers:
        y.to_a()

    def wait_w(i):
        s = lax.rem(w.s + 1 + i, n.seq)
        wait(x.wqv.at[mine], x.r_wq.at[s])

    loop(n.seq - 1, wait_w)
    project(w.s)
    for i in range(1, n.a):
        project(spot(i, 0))
    for i in range(n.a):
        for v in range(1, n.b):
            block = spot(i, v)
            wait(x.xh.at[block], x.r_n.at[block // 2])
            share_hat(block)
            project(block)

    def from_sibling(c):
        block = 2 * c + 1 - w.j
        wait(x.xh.at[block], x.r_ns.at[c])
        project(block)

    loop(n.chips, from_sibling)

    tasks = []
    for i in range(n.a):
        if i:
            tasks.append(lambda i=i: [y.column(i) for y in gathers])
        tasks.append(lambda i=i: g_o.corner(i))

    def relay(count):
        for _ in range(count):
            if tasks:
                tasks.pop(0)()

    for r in range(n.rounds):
        loop_by(UNROLL, n.seq, lambda p: fill_block(n, r, p, x.tab, x.qv, x.buf, x.marks))
    relay(RELAYS[0])
    parts = 4
    slot = 1
    for r in range(n.rounds):
        for q in range(parts):
            loop_by(UNROLL, n.seq // parts, lambda g: attend(n, r, q * (n.seq // parts) + g, x.buf, x.marks, obuf))
            relay(RELAYS[slot])
            slot += 1

    blocks = n.seq // n.sub
    for m in range(1, n.sub):
        far = lax.rem(w.idx + m, n.sub)

        def offer(i, m=m, far=far):
            k = (m - 1) * blocks + i
            write_message(pmsg.at[k], *merge_rounds(n, i * n.sub + far, x.tab, obuf))
            push(pmsg.at[k], x.pin.at[k], x.s_p.at[k], x.r_p.at[k], (w.head * n.sub + far, w.f))

        loop_by(UNROLL, blocks, offer)

    def settle(i):
        out, log = merge_rounds(n, i * n.sub + w.idx, x.tab, obuf)
        outs, logs = [out], [log]
        for m in range(1, n.sub):
            k = (m - 1) * blocks + i
            wait(x.pin.at[k], x.r_p.at[k])
            outs.append(x.pin[k, :128].astype(F32))
            logs.append(read_log(x.pin.at[k]))
        write_message(omsg.at[i], *merge(outs, logs))

    def give(i):
        to = lax.rem(w.head + 1 + i, blocks)
        settle(to)
        push(omsg.at[to], x.home.at[w.head], x.s_out.at[i], x.r_out.at[w.head], (to * n.sub + w.idx, w.f))

    loop(blocks - 1, give)
    settle(w.head)
    x.home[w.head] = omsg[w.head]
    relay(len(tasks))

    def take(i):
        h = lax.rem(w.head + 1 + i, HEADS)
        wait(x.home.at[h], x.r_out.at[h])

    loop(HEADS - 1, take)
    g_o.finish()
    loop(n.chips * n.fsdp, lambda u: wait(x.wo.at[w.me], x.r_os.at[u]))

    loop((n.sub - 1) * blocks, lambda k: wait(pmsg.at[0], x.s_p.at[k]))
    loop(blocks - 1, lambda k: wait(omsg.at[0], x.s_out.at[k]))

    def drain():
        g_c.finish()
        g_e.finish()
        for y in gathers:
            y.drain()
        loop(n.chips * n.fsdp, lambda u: wait(x.wo.at[w.me], x.s_os.at[u]))
        for m in range(1, n.group):
            t = lax.rem(w.t + m, n.group)
            wait(x.we_in.at[0], x.s_ex.at[m])
            wait(x.ci.at[t], x.r_ci.at[t])
            wait(x.ci.at[t], x.s_ci.at[m])

        def wait_sends(i):
            wait(x.small_all.at[pl.ds(0, n.fsdp)], x.s_small.at[i])
            wait(x.wqv.at[pl.ds(0, n.fsdp)], x.s_wq.at[i])

        loop(n.seq - 1, wait_sends)
        for q in range(1, n.fsdp):
            wait(x.small_all.at[0], x.s_f.at[0, q])
            wait(x.wqv_in.at[0], x.s_f.at[1, q])
        hats.drain_sends(lambda: x.xh.at[w.s])
        loop(n.chips, lambda c: wait(x.xh.at[w.s], x.s_ns.at[c]))

    return drain


def feed_part(n, w, x, sums, whole, drain, mixed_low, act, gp, out, out2):
    sum_c, sum_e, _ = sums
    for h in range(HEADS):
        mixed_low[:, h * 128:(h + 1) * 128] = x.home[h, :128]
    first_out = x.first[...] + dot(mixed_low[...], x.wo.reshape(n.width, n.width)[...])
    x.first_o[...] = first_out
    hat, scale, normed = normalize(first_out, x.vec[2:3], x.vec[3:4])
    x.n2[w.t] = low(normed)
    k = 0
    for m in range(1, n.b):
        t = lax.rem(w.b + m, n.b) * 2 + w.j
        push(x.n2.at[w.t], x.n2.at[w.t], x.s_x.at[k], x.r_x.at[w.t], member(n, w, t))
        k += 1
    push(x.n2.at[w.t], x.n2.at[w.t], x.s_x.at[k], x.r_x.at[w.t], w.sib)
    k += 1
    for q, ref in enumerate((x.query_w, x.value_w)):
        pltpu.make_async_copy(ref, x.full.at[q, w.me], x.s_loc.at[q]).wait()
    whole.arrived(*whole.own())
    whole.to_a()
    whole.column(0)
    drain()
    for m in range(1, n.b):
        t = lax.rem(w.b + m, n.b) * 2 + w.j
        wait(x.n2.at[t], x.r_x.at[t])
        push(x.n2.at[t], x.n2.at[t], x.s_x.at[k], x.r_x.at[t], w.sib)
        k += 1
    for b in range(n.b):
        t = b * 2 + 1 - w.j
        wait(x.n2.at[t], x.r_x.at[t])
    size = n.group * n.tokens
    step = min(512, n.part)
    tokens = x.n2.reshape(size, n.width)
    cots = x.ci.reshape(size, n.width)
    we = x.we.reshape(n.width, n.part)
    wc = x.wc.reshape(n.part, n.width)
    for q in range(n.part // step):
        at = slice(q * step, (q + 1) * step)
        pre = dot(tokens[...], we[:, at]) + x.shift_part[0:1, at]
        value, slope = gelu_pair(pre)
        act[:, at] = low(value)
        back = low(dot_nt(cots[...], wc[at]) * slope)
        gp[:, at] = back
        x.shift_g[:, at] = jnp.broadcast_to(jnp.sum(back.astype(F32), axis=0, keepdims=True), (8, step))
    gn = GroupSum(n, w, out, x.gn_got1, x.gn_got2, x.s_gn, x.r_gn)
    so = GroupSum(n, w, out2, x.so_got1, x.so_got2, x.s_so, x.r_so)
    pair = 2 * n.tokens
    gn.fill(lambda b: dot_nt(gp[pl.ds(pl.multiple_of(b * pair, pair), pair)], we[...]))
    x.gwc.reshape(n.part, n.width)[...] = low(dot_tn(act[...], cots[...]))
    sum_c.first()
    gn.chips()
    so.fill(lambda b: dot(act[pl.ds(pl.multiple_of(b * pair, pair), pair)], wc[...]))
    x.gwe.reshape(n.width, n.part)[...] = low(dot_tn(tokens[...], gp[...]))
    so.chips()
    sum_e.first()
    whole.column(1)
    grad = gn.total()
    rest = grad * x.vec[2:3]
    mean = jnp.mean(rest, axis=1, keepdims=True)
    tilt = jnp.mean(rest * hat, axis=1, keepdims=True)
    grad1 = x.cot1[...] + scale * (rest - mean - hat * tilt)
    x.grad1_o[...] = grad1
    branch = low(grad1)
    wo = x.wo.reshape(n.width, n.width)
    for h in range(HEADS):
        gm = dot_nt(branch, wo[h * 128:(h + 1) * 128])
        x.message[h, :128] = low(gm)
        delta = jnp.sum(gm * x.home[h, :128].astype(F32), axis=1, keepdims=True)
        logs = x.home[h, 128:].astype(F32)
        x.message[h, 128:] = message_rows((logs[0:1], logs[1:2], logs[2:3]) + split3(to_row(delta)))

    def give(i):
        s = lax.rem(w.s + 1 + i, n.seq)
        push(x.message.at[s // n.sub], x.dtok.at[w.s], x.s_d.at[i], x.r_d.at[w.s], (s, w.f))

    loop(n.seq - 1, give)
    x.dtok[w.s] = x.message[w.head]
    whole.corner(0)
    gwo = low(dot_tn(mixed_low[...], branch)).reshape(n.chips, 2, n.fsdp * n.rows, n.width)
    x.gwo[...] = gwo.reshape(n.chips, 2, n.fsdp, n.rows, n.width)
    push(x.gwo.at[:, 1 - w.j], x.o0, x.s_o0.at[0], x.r_o0.at[0], w.sib)
    zero = jnp.zeros((2, n.width), F32)
    x.vec_g[...] = jnp.concatenate([
        zero,
        jnp.sum(grad * hat, axis=0, keepdims=True),
        jnp.sum(grad, axis=0, keepdims=True),
        jnp.sum(x.ci[w.t].astype(F32), axis=0, keepdims=True),
        zero, zero[:1],
    ])
    x.second_o[...] = x.second[...] + so.total() + x.vec[4:5]
    for i in range(k):
        wait(x.n2.at[0], x.s_x.at[i])
    gn.drain()
    so.drain()


def back_attention(n, w, x, sums, whole, dbuf, gbuf, gout):
    sum_c, sum_e, sum_o = sums
    blocks = n.seq // n.sub
    wait(x.o0, x.r_o0.at[0])

    def join_o(c):
        x.o0[c] = low(x.o0[c].astype(F32) + x.gwo[c, w.j].astype(F32))

    loop(n.chips, join_o)
    sum_o.first()

    def take(i):
        p = lax.rem(w.s + 1 + i, n.seq)
        wait(x.dtok.at[p], x.r_d.at[p])

    loop(n.seq - 1, take)
    tasks = []
    for i in range(n.a):
        tasks.append(lambda i=i: (sum_c.second(i), sum_e.second(i)))
        if 0 < i < n.a - 1:
            tasks.append(lambda i=i: whole.column(i + 1))
        if i:
            tasks.append(lambda i=i: whole.corner(i))
        if i == 1:
            tasks.append(sum_o.second)
    tasks.append(sum_o.third)

    def relay(count):
        for _ in range(count):
            if tasks:
                tasks.pop(0)()

    slot = 0
    parts = 4
    for r in range(n.rounds):
        loop_by(UNROLL, n.seq, lambda p: spread(n, r, p, x.tab, x.dtok, dbuf, x.marks))
        for q in range(parts):
            loop_by(UNROLL, n.seq // parts, lambda g: attend_back(n, r, q * (n.seq // parts) + g, x.buf, x.marks, dbuf, gbuf))
            relay(SUMS[slot])
            slot += 1
    relay(len(tasks))

    def tokens_of(p):
        total = None
        for r in range(n.rounds):
            got = dot(picks_back(n, x.tab[r, p]), rows_of(n, gbuf.at[r, p]))
            total = got if total is None else total + got
        return total

    for m in range(1, n.sub):
        far = lax.rem(w.idx + m, n.sub)

        def offer(i, m=m, far=far):
            k = (m - 1) * blocks + i
            gout[k] = low(tokens_of(i * n.sub + far))
            push(gout.at[k], x.gin.at[k], x.s_g.at[k], x.r_g.at[k], (w.head * n.sub + far, w.f))

        loop_by(UNROLL, blocks, offer)

    def keep(i):
        x.gown[i] = tokens_of(i * n.sub + w.idx)

    loop_by(UNROLL, blocks, keep)
    loop((n.sub - 1) * blocks, lambda k: wait(gout.at[0], x.s_g.at[k]))


def back_rest(n, w, x, sums, whole, dqv, wsum, wout, esw, vsend, full):
    sum_c, sum_e, sum_o = sums
    blocks = n.seq // n.sub
    whole.finish()
    loop(n.chips * n.fsdp, lambda u: wait(whole.own()[0], x.r_ps.at[u]))
    load = pltpu.make_async_copy(x.full, full, x.s_loc.at[0])
    load.start()

    def finish_block(i):
        total = x.gown[i]
        for m in range(1, n.sub):
            k = (m - 1) * blocks + i
            wait(x.gin.at[k], x.r_g.at[k])
            total += x.gin[k].astype(F32)
        dqv[i] = low(total)

    def arrived(h):
        return x.xh.at[h, :, pl.ds(0, 256)]

    def send_home(k):
        i = lax.rem(w.head + 1 + k, blocks)
        finish_block(i)
        push(dqv.at[i], arrived(w.head), x.s_h.at[k], x.r_h.at[w.head], (i * n.sub + w.idx, w.f))

    loop(blocks - 1, send_home)
    finish_block(w.head)
    x.xh[w.head, :, :256] = dqv[w.head]

    for i in range(blocks):
        got = dot_tn(x.nown[i], dqv[i])
        wsum[...] = got if i == 0 else wsum[...] + got
    wout[...] = low(wsum[...]).reshape(n.all, n.rows, 256)

    def rows_out(i):
        d, dev = peer(n, w, i + 1)
        push(wout.at[d], x.win.at[w.me], x.s_w2.at[i], x.r_w2.at[w.me], dev)

    loop(n.all - 1, rows_out)
    x.win[w.me] = wout[w.me]

    esw[...] = sum_e.total()
    x.egot[w.t] = esw[w.t]
    for m in range(1, n.group):
        t = lax.rem(w.t + m, n.group)
        push(esw.at[t], x.egot.at[w.t], x.s_y.at[m], x.r_y.at[w.t], member(n, w, t))
    x.go_o[...] = sum_o.total()
    x.gc_o[...] = sum_c.total()

    hat, scale = hat_of(x.second[...])

    def take_home(k):
        h = lax.rem(w.head + 1 + k, HEADS)
        wait(arrived(h), x.r_h.at[h])

    loop(HEADS - 1, take_home)
    for h in range(HEADS):
        for q in range(2):
            x.xh[HEADS + q, :, h * 128:(h + 1) * 128] = x.xh[h, :, q * 128:(q + 1) * 128]
    load.wait()
    grad = sum(dot_nt(x.xh[HEADS + q], full[q].reshape(n.width, n.width)) for q in range(2))
    rest = grad * x.vec[0:1]
    mean = jnp.mean(rest, axis=1, keepdims=True)
    tilt = jnp.mean(rest * hat, axis=1, keepdims=True)
    x.grad2_o[...] = x.cot2[...] + scale * (rest - mean - hat * tilt)
    gain_g = jnp.sum(grad * hat, axis=0, keepdims=True)
    shift1_g = jnp.sum(grad, axis=0, keepdims=True)
    group = 128 // n.rows
    per = 128 // n.units
    at = iota((8, 128), 0)

    def rolled(tile, lanes):
        return pltpu.roll(tile, 128 - lanes, 1) if lanes else tile

    for q in range(n.width // 128):
        cut = slice(q * 128, (q + 1) * 128)
        tile = jnp.where(at == 0, gain_g[:, cut], jnp.where(at == 1, shift1_g[:, cut], x.vec_g[:, cut]))
        for k in range(group):
            vsend[q * group + k] = rolled(tile, k * n.rows)
    for q in range(n.a * n.fsdp // per):
        for k in range(per):
            u = q * per + k
            d = (u // n.fsdp * n.group + w.t) * n.fsdp + u % n.fsdp
            tile = rolled(x.shift_g[:, q * 128:(q + 1) * 128], k * n.units)
            vsend[d] = jnp.where(at == 5, tile, vsend[d])

    def vec_out(i):
        d, dev = peer(n, w, i + 1)
        push(vsend.at[d], x.vgot.at[w.me], x.s_v.at[i], x.r_v.at[w.me], dev)

    loop(n.all - 1, vec_out)
    x.vgot[w.me] = vsend[w.me]

    def take_rows(i):
        d, _ = peer(n, w, i + 1)
        wait(x.win.at[d], x.r_w2.at[d])

    loop(n.all - 1, take_rows)
    for h in range(HEADS):
        total = 0.0
        for i in range(n.sub * n.fsdp):
            total += x.win[h * n.sub * n.fsdp + i].astype(F32)
        x.gq_o[:, h * 128:(h + 1) * 128] = total[:, :128]
        x.gv_o[:, h * 128:(h + 1) * 128] = total[:, 128:]
    for m in range(1, n.group):
        t = lax.rem(w.t + m, n.group)
        wait(x.egot.at[t], x.r_y.at[t])
    for t in range(n.group):
        for a in range(n.a):
            c = (a * n.group + t) * n.wide
            x.ge_o[:, c:c + n.wide] = x.egot[t, :, a * n.wide:(a + 1) * n.wide]

    wait(x.o0, x.s_o0.at[0])
    for m in range(1, n.group):
        wait(x.egot.at[0], x.s_y.at[m])
    loop(n.seq - 1, lambda i: wait(x.dtok.at[0], x.s_d.at[i]))
    for y in (sum_c, sum_e, sum_o):
        y.drain()
    loop(blocks - 1, lambda k: wait(dqv.at[0], x.s_h.at[k]))
    whole.drain()
    loop(n.chips * n.fsdp, lambda u: wait(whole.own()[0], x.s_ps.at[u]))

    def wait_all(i):
        wait(x.win.at[0], x.s_w2.at[i])
        wait(x.vgot.at[0], x.s_v.at[i])

    loop(n.all - 1, wait_all)

    def take_vec(i):
        d, _ = peer(n, w, i + 1)
        wait(x.vgot.at[d], x.r_v.at[d])

    loop(n.all - 1, take_vec)
    x.small_o[...] = jnp.sum(x.vgot[...], axis=0)


def layer_kernel(n, names, *refs):
    x = types.SimpleNamespace(**dict(zip(names, refs, strict=True)))
    w = place(n)
    t, d, g = n.tokens, n.width, n.group
    blocks = n.seq // n.sub
    pairs = (n.rounds, n.seq, n.seq, n.cap, 256)
    sums = (
        PlaneScatter(n, w, lambda a, f: x.gwc.at[a, f], x.c1, x.c2, x.s_c, x.r_c),
        PlaneScatter(n, w, lambda a, f: x.gwe.at[a, :, f], x.e1, x.e2, x.s_e, x.r_e),
        Scatter(n, w, "f", lambda a, b, f: x.o0.at[a * n.b + b, f], x.o1, x.o2, x.o3, x.s_o, x.r_o),
    )
    drains = []

    def shared(ref, uid):
        push(ref, ref, x.s_ps.at[uid], x.r_ps.at[uid], w.sib)

    whole = Gather(
        n, w, lambda a, b, f: x.full.at[:, ((a * n.b + b) * 2 + w.j) * n.fsdp + f], lambda a, b, f: (a * n.b + b) * n.fsdp + f,
        lambda i: x.s_gp.at[i], lambda u: x.r_gp.at[u], True, shared,
    )
    pl.run_scoped(
        lambda *r: drains.append(front_part(n, w, x, *r)),
        VM(pairs, BF), VM(((n.sub - 1) * blocks, MSG, 128), BF), VM((blocks, MSG, 128), BF),
    )
    pl.run_scoped(
        lambda *r: feed_part(n, w, x, sums, whole, drains[0], *r),
        VM((t, d), BF), VM((g * t, n.part), BF), VM((g * t, n.part), BF),
        VM((g, t, d), BF), VM((g, t, d), BF),
    )
    pl.run_scoped(
        lambda *r: back_attention(n, w, x, sums, whole, *r),
        VM(pairs[:-1] + (128,), BF), VM(pairs, BF), VM(((n.sub - 1) * blocks, 128, 256), BF),
    )
    pl.run_scoped(
        lambda *r: back_rest(n, w, x, sums, whole, *r),
        VM((blocks, 128, 256), BF), VM((d, 256), F32), VM((n.all, n.rows, 256), BF), VM((g, n.rows, n.part), F32),
        VM((n.all, 8, 128), F32), VM((2, n.all, n.rows, d), BF),
    )


def layer(n, inputs):
    inside = pl.BlockSpec(memory_space=VM)
    t, d, g, a = n.tokens, n.width, n.group, n.a
    units = n.chips * n.fsdp
    blocks = n.seq // n.sub
    f1, b1 = max(n.fsdp - 1, 1), max(n.b - 1, 1)
    pairs = (n.rounds, n.seq, n.seq, n.cap)
    unit_c, unit_e, unit_o = (n.units, d), (g, n.rows, n.part), (n.rows, d)
    count_f = (n.fsdp - 1) * a * n.b + (n.b - 1) * a + a - 1
    count_p = (n.fsdp - 1) * a + a - 1
    outputs = {
        "first_o": (t, d), "second_o": (t, d), "grad1_o": (t, d), "grad2_o": (t, d),
        "gq_o": (n.rows, d), "gv_o": (n.rows, d), "go_o": (n.rows, d), "ge_o": (n.rows, n.hidden), "gc_o": (n.units, d),
        "small_o": (8, 128),
    }
    scratch = {
        "xh": VM((n.seq, 128, d), BF),
        "nown": VM((blocks, 128, d), BF), "qv": VM((n.seq, 128, 256), BF),
        "wqv": VM((n.all, n.rows, 256), BF), "wqv_in": VM((n.fsdp, HEADS, n.rows, 256), BF), "we_in": VM((g, n.rows, n.part), BF),
        "small_all": VM((n.all, 16, 128), BF), "tab": VM((n.rounds, n.seq, 8, 128), F32), "vec": VM((16, d), F32),
        "shift_part": VM((8, n.part), F32), "ci": VM((g, t, d), BF),
        "buf": VM(pairs + (256,), BF), "marks": VM(pairs + (128,), BF),
        "pin": VM(((n.sub - 1) * blocks, MSG, 128), BF),
        "home": VM((HEADS, MSG, 128), BF), "dtok": VM((n.seq, MSG, 128), BF),
        "wo": VM((n.all, n.rows, d), BF), "wc": VM((a, n.fsdp, n.units, d), BF), "we": VM((a, g, n.fsdp, n.rows, n.part), BF),
        "n2": VM((g, t, d), BF),
        "gn_got1": VM((n.b, t, d), BF), "gn_got2": VM((b1, t, d), BF), "so_got1": VM((n.b, t, d), BF), "so_got2": VM((b1, t, d), BF),
        "gwc": VM((a, n.fsdp, n.units, d), BF), "gwe": VM((a, g, n.fsdp, n.rows, n.part), BF),
        "gwo": VM((n.chips, 2, n.fsdp, n.rows, d), BF), "message": VM((HEADS, MSG, 128), BF),
        "vec_g": VM((8, d), F32), "shift_g": VM((8, n.part), F32),
        "gown": VM((blocks, 128, 256), F32),
        "gin": VM(((n.sub - 1) * blocks, 128, 256), BF), "win": VM((n.all, n.rows, 256), BF),
        "c1": VM((f1, a) + unit_c, BF), "c2": VM((a - 1,) + unit_c, BF),
        "e1": VM((f1, a) + unit_e, BF), "e2": VM((a - 1,) + unit_e, BF),
        "o0": VM((n.chips, n.fsdp) + unit_o, BF), "o1": VM((f1, a, n.b) + unit_o, BF),
        "o2": VM((b1, a) + unit_o, BF), "o3": VM((a - 1,) + unit_o, BF),
        "egot": VM(unit_e, F32), "vgot": VM((n.all, 8, 128), F32),
    }
    sems = {
        "small": n.seq, "wq": n.seq, "f": (2, n.fsdp), "ns": n.chips, "os": units, "ex": g, "ci": g,
        "p": (n.sub - 1) * blocks, "out": HEADS, "x": 2 * n.b, "gn": 2 * n.b, "so": 2 * n.b, "d": n.seq, "o0": 1,
        "c": count_p, "e": count_p, "o": count_f, "g": (n.sub - 1) * blocks, "w2": n.all, "h": HEADS, "ps": units,
        "v": n.all, "y": g,
    }
    for key, count in sems.items():
        for side in ("s_", "r_"):
            if key == "x" and side == "r_":
                count = g
            scratch[side + key] = DMA(count if isinstance(count, tuple) else (count,))
    scratch["s_loc"] = DMA((2,))
    part, every = 2 + a * n.fsdp, 2 + a * (n.fsdp + n.b - 1) + a * (n.fsdp - 1) * (n.b - 1)
    for key, sends, gets in (("n", 2 + n.chips, n.chips), ("go", every, units), ("gp", every, units), ("gc", part, a * n.fsdp), ("ge", part, a * n.fsdp)):
        scratch["s_" + key], scratch["r_" + key] = DMA((sends,)), DMA((gets,))
    names = list(inputs) + list(outputs) + ["full"] + list(scratch)
    return pl.pallas_call(
        functools.partial(layer_kernel, n, names),
        out_shape=tuple(jax.ShapeDtypeStruct(s, F32) for s in outputs.values()) + (jax.ShapeDtypeStruct((2, n.all, n.rows, d), BF),),
        in_specs=[inside] * len(inputs),
        out_specs=(inside,) * len(outputs) + (pl.BlockSpec(memory_space=pl.ANY),),
        scratch_shapes=list(scratch.values()),
        compiler_params=pltpu.CompilerParams(collective_id=1, has_side_effects=True, vmem_limit_bytes=60 << 20),
        name="layer",
    )(*inputs.values())


def deliver_kernel(n, count, *refs):
    arrays, small, outs = refs[:count], refs[count], refs[count + 1:2 * count + 1]
    vectors, held, come, leave = refs[2 * count + 1:-count - 2], refs[-count - 2:-2], refs[-2], refs[-1]
    ins = [pltpu.make_async_copy(arrays[i], held[i], come.at[i]) for i in range(count)]
    ends = [pltpu.make_async_copy(held[i], outs[i], leave.at[i]) for i in range(count)]
    for cp in ins:
        cp.start()
    for row, ref in zip((0, 1, 2, 3, 5, 4), vectors, strict=True):
        ref[...] = small[row:row + 1, :ref.shape[1]]
    for before, after in zip(ins, ends, strict=True):
        before.wait()
        after.start()
    for cp in ends:
        cp.wait()


def deliver(n, arrays, small):
    anywhere = pl.BlockSpec(memory_space=pl.ANY)
    inside = pl.BlockSpec(memory_space=VM)
    shape = jax.ShapeDtypeStruct
    sizes = (n.rows, n.rows, n.rows, n.rows, n.units, n.rows)
    count = len(arrays)
    return pl.pallas_call(
        functools.partial(deliver_kernel, n, count),
        out_shape=tuple(shape(y.shape, F32) for y in arrays) + tuple(shape((1, k), F32) for k in sizes),
        in_specs=[anywhere] * count + [inside],
        out_specs=(anywhere,) * count + (inside,) * len(sizes),
        scratch_shapes=[VM(y.shape, F32) for y in arrays] + [DMA((count,)), DMA((count,))],
        compiler_params=pltpu.CompilerParams(vmem_limit_bytes=60 << 20),
        name="deliver",
    )(*arrays, small)


def on_device(
    first_half,
    second_half,
    first_cotangent,
    second_cotangent,
    bucket_ids,
    slot_source,
    live_slots,
    mixer_gain,
    mixer_shift,
    query_weight,
    value_weight,
    output_weight,
    feed_gain,
    feed_shift,
    expand_weight,
    expand_bias,
    contract_weight,
    contract_bias,
):
    seq, fsdp = lax.axis_size("seq"), lax.axis_size("fsdp")
    n = setup(seq, fsdp, first_half.shape[2], expand_weight.shape[1], first_half.shape[1])
    vectors = jnp.stack([mixer_gain, mixer_shift, feed_gain, feed_shift, contract_bias] + [jnp.zeros_like(mixer_gain)] * 3)
    *arrays, small, _ = layer(n, {
        "first": first_half[0], "second": second_half[0], "cot1": first_cotangent[0], "cot2": second_cotangent[0],
        "vectors": vectors, "bias": expand_bias.reshape(1, -1), "buckets": bucket_ids[0],
        "query_w": query_weight, "value_w": value_weight, "expand_w": expand_weight,
        "wo_in": output_weight, "wc_in": contract_weight,
    })
    outs = deliver(n, arrays, small)
    first_out, second_out, grad1, grad2, gq, gv, go, ge, gc = outs[:9]
    gain1, shift1, gain2, shift2, up_bias, down_bias = [y.reshape(-1) for y in outs[9:]]
    return (
        first_out[None], second_out[None], grad1[None], grad2[None],
        gain1, shift1, gq, gv, go, gain2, shift2, ge, up_bias, gc, down_bias,
    )


def solution(mesh):
    tokens, slots = P("fsdp", "seq", None), P("fsdp", None, "seq")
    vector, matrix = P(("seq", "fsdp")), P(("seq", "fsdp"), None)
    return jax.shard_map(
        on_device,
        mesh=mesh,
        in_specs=(tokens,) * 4 + (slots,) * 3 + (vector, vector, matrix, matrix, matrix, vector, vector, matrix, vector, matrix, vector),
        out_specs=(tokens,) * 4 + (vector, vector, matrix, matrix, matrix, vector, vector, matrix, vector, matrix, vector),
        check_vma=False,
    )
```

```python
import functools
import types

import jax
import jax.numpy as jnp
from jax import lax
from jax.experimental import pallas as pl
from jax.experimental.pallas import tpu as pltpu
from jax.sharding import PartitionSpec as P

HEADS = 8
HEAD_DIM = 128
ROUNDS = 4
SPAN = 64
BF = jnp.bfloat16
F32 = jnp.float32
MESH = pl.DeviceIdType.MESH
DMA = pltpu.SemaphoreType.DMA
VM = pltpu.VMEM
MSG = 144


def dot(a, b):
    return lax.dot_general(a, b, (((1,), (0,)), ((), ())), preferred_element_type=F32)


def dot_nt(a, b):
    return lax.dot_general(a, b, (((1,), (1,)), ((), ())), preferred_element_type=F32)


def dot_tn(a, b):
    return lax.dot_general(a, b, (((0,), (0,)), ((), ())), preferred_element_type=F32)


def iota(shape, dim):
    return lax.broadcasted_iota(jnp.int32, shape, dim)


def iotaf(shape, dim):
    return iota(shape, dim).astype(F32)


def low(x):
    return x.astype(BF)


def split3(x):
    hi = x.astype(BF).astype(F32)
    rest = x - hi
    mid = rest.astype(BF).astype(F32)
    return hi, mid, rest - mid


def loop(count, body):
    def step(i, carry):
        body(i)
        return carry

    lax.fori_loop(0, count, step, 0)


def loop_by(k, count, body):
    k = k if count % k == 0 else 1

    def several(i):
        for u in range(k):
            body(i * k + u)

    loop(count // k, several)


def push(src, dst, send, recv, dev):
    pltpu.make_async_remote_copy(
        src_ref=src, dst_ref=dst, send_sem=send, recv_sem=recv, device_id=dev, device_id_type=MESH
    ).start()


def wait(ref, sem):
    pltpu.make_async_copy(ref, ref, sem).wait()


def to_column(row):
    size = row.shape[1]
    eye = iota((size, size), 0) == iota((size, size), 1)
    return jnp.sum(jnp.where(eye, row, 0.0), axis=1, keepdims=True)


def to_row(column):
    size = column.shape[0]
    eye = iota((size, size), 0) == iota((size, size), 1)
    return jnp.sum(jnp.where(eye, column, 0.0), axis=0, keepdims=True)


def message_rows(rows):
    at = iota((MSG - 128, 128), 0)
    out = jnp.zeros((MSG - 128, 128), F32)
    for i, row in enumerate(rows):
        out = jnp.where(at == i, row, out)
    return low(out)


def setup(seq, fsdp, width, hidden, tokens):
    n = types.SimpleNamespace()
    n.seq, n.fsdp, n.all = seq, fsdp, seq * fsdp
    n.chips = seq // 2
    n.b = 2 if n.chips <= 8 else 4
    n.a = n.chips // n.b
    n.sub = seq // HEADS
    n.rounds = ROUNDS // n.sub
    n.cap = 4 * SPAN // seq
    n.width, n.hidden, n.tokens = width, hidden, tokens
    n.rows = width // n.all
    n.units = hidden // n.all
    n.group = 2 * n.b
    n.part = hidden // n.group
    n.wide = hidden // seq
    return n


def place(n):
    w = types.SimpleNamespace()
    w.s, w.f = lax.axis_index("seq"), lax.axis_index("fsdp")
    w.c, w.j = w.s // 2, lax.rem(w.s, 2)
    w.a, w.b = w.c // n.b, lax.rem(w.c, n.b)
    w.me = w.s * n.fsdp + w.f
    w.head, w.idx = w.s // n.sub, lax.rem(w.s, n.sub)
    w.sib = (w.s + 1 - 2 * w.j, w.f)
    w.t = w.b * 2 + w.j
    return w


def plane(n, w, a, b, f):
    return ((a * n.b + b) * 2 + w.j, f)


def member(n, w, t):
    return ((w.a * n.b) * 2 + t, w.f)


def peer(n, w, i):
    d = lax.rem(w.me + i, n.all)
    return d, (d // n.fsdp, lax.rem(d, n.fsdp))


def meet_all(n, w):
    barrier = pltpu.get_barrier_semaphore()

    def greet(i):
        pl.semaphore_signal(barrier, inc=1, device_id=peer(n, w, i + 1)[1], device_id_type=MESH)

    loop(n.all - 1, greet)
    pl.semaphore_wait(barrier, n.all - 1)


class Line:
    def __init__(self, n, w, send_sem, per_unit):
        self.n, self.w, self.send_sem, self.per_unit, self.sent = n, w, send_sem, per_unit, []

    def inside(self, shift):
        a = self.w.a + shift
        return (a >= 0) & (a < self.n.a)

    def slot(self, shift, k):
        return 2 + (self.w.a + shift) * self.per_unit + k

    def send(self, ref, recv, dev, slot, *shifts):
        push(ref, ref, self.send_sem(slot()), recv, dev)
        self.sent.append((slot, shifts))

    def both(self, shifts):
        return functools.reduce(jnp.logical_and, [self.inside(v) for v in shifts])

    def start(self, own, neighbour):
        for sign in (-1, 1):
            @pl.when(self.inside(-sign))
            def _(sign=sign):
                self.send(*own(), neighbour(self.w.a - sign), lambda: (1 + sign) // 2, -sign)

    def step(self, far, take, neighbour, more):
        for sign in (-1, 1):
            @pl.when(self.inside(sign * far))
            def _(sign=sign):
                ref, recv = take(self.w.a + sign * far)
                if far < self.n.a - 1:
                    @pl.when(self.inside(-sign))
                    def _():
                        self.send(ref, recv, neighbour(self.w.a - sign), lambda: self.slot(sign * far, 0), sign * far, -sign)
                for k, dev in enumerate(more):
                    self.send(ref, recv, dev, lambda k=k: self.slot(sign * far, 1 + k), sign * far)

    def drain_sends(self, ref):
        for slot, shifts in self.sent:
            if shifts:
                @pl.when(self.both(shifts))
                def _(slot=slot):
                    wait(ref(), self.send_sem(slot()))
            else:
                wait(ref(), self.send_sem(slot()))


class Gather(Line):
    def __init__(self, n, w, unit, index, send_sem, recv_sem, over_b=False, arrived=None):
        super().__init__(n, w, send_sem, n.fsdp + (n.b - 1 if over_b else 0))
        self.unit, self.index, self.recv_sem = unit, index, recv_sem
        self.over_b, self.arrived = over_b, arrived

    def entry(self, a, b, f):
        return self.unit(a, b, f), self.recv_sem(self.index(a, b, f))

    def own(self):
        w = self.w
        return self.unit(w.a, w.b, w.f), self.index(w.a, w.b, w.f)

    def take(self, a, b, f):
        ref, recv = self.entry(a, b, f)
        wait(ref, recv)
        if self.arrived:
            self.arrived(ref, self.index(a, b, f))
        return ref, recv

    def neighbour(self, a):
        return plane(self.n, self.w, a, self.w.b, self.w.f)

    def others(self, over_f=True):
        n, w = self.n, self.w
        out = []
        if over_f:
            out += [plane(n, w, w.a, w.b, lax.rem(w.f + m, n.fsdp)) for m in range(1, n.fsdp)]
        if self.over_b:
            out += [plane(n, w, w.a, lax.rem(w.b + m, n.b), w.f) for m in range(1, n.b)]
        return out

    def to_a(self):
        self.start(lambda: self.entry(self.w.a, self.w.b, self.w.f), self.neighbour)

    def column(self, far):
        w = self.w
        if far == 0:
            for k, dev in enumerate(self.others()):
                self.send(*self.entry(w.a, w.b, w.f), dev, lambda k=k: self.slot(0, 1 + k))
        else:
            self.step(far, lambda a: self.take(a, w.b, w.f), self.neighbour, self.others())

    def corner_slot(self, shift, q, k):
        base = 2 + self.n.a * self.per_unit
        return base + ((self.w.a + shift) * (self.n.fsdp - 1) + q - 1) * (self.n.b - 1) + k

    def corner(self, far):
        if not self.over_b:
            return

        def pass_on(shift, *shifts):
            for q in range(1, self.n.fsdp):
                ref, recv = self.take(self.w.a + shift, self.w.b, lax.rem(self.w.f + q, self.n.fsdp))
                for k, dev in enumerate(self.others(False)):
                    self.send(ref, recv, dev, lambda q=q, k=k: self.corner_slot(shift, q, k), *shifts)

        if far == 0:
            pass_on(0)
        else:
            for sign in (-1, 1):
                @pl.when(self.inside(sign * far))
                def _(sign=sign):
                    pass_on(sign * far, sign * far)

    def finish(self):
        n, w = self.n, self.w
        for i in range(n.a):
            a = lax.rem(w.a + i, n.a)
            for q in range(n.fsdp):
                for v in range(n.b):
                    if (v if self.over_b else q) != 0 and (self.over_b or v == 0):
                        self.take(a, lax.rem(w.b + v, n.b), lax.rem(w.f + q, n.fsdp))

    def drain(self):
        self.drain_sends(lambda: self.unit(self.w.a, self.w.b, self.w.f))


def tables(n, w, small_all, tab):
    nb = 2 * n.seq
    before = low((iota((128, 128), 0) < iota((128, 128), 1)).astype(F32))
    for r in range(n.rounds):
        def bucket_row(p):
            tile = small_all[p * n.fsdp + w.f].astype(F32)
            keep = iota((16, 128), 0) == 8 + w.idx * n.rounds + r
            return jnp.sum(jnp.where(keep, tile, 0.0), axis=0, keepdims=True)

        def count(p, run):
            row = bucket_row(p)
            hot = (iotaf((nb, 128), 0) == row).astype(F32)
            ahead = dot(low(hot), before)
            pos = jnp.sum(hot * (ahead + run), axis=0, keepdims=True)
            group = jnp.floor(row * 0.5)
            hotg = (iotaf((n.seq, 128), 0) == group).astype(F32)
            rank = jnp.sum(hotg * dot(low(hotg), before), axis=0, keepdims=True)
            line = group * n.cap + rank
            at = iota((8, 128), 0)
            tab[r, p] = jnp.where(at == 0, line, jnp.where(at == 1, pos, jnp.where(at == 2, row, 0.0)))
            return run + jnp.sum(hot, axis=1, keepdims=True)

        totals = lax.fori_loop(0, n.seq, count, jnp.zeros((nb, 1), F32))

        def settle(p):
            tile = tab[r, p]
            row = tile[2:3]
            odd = row - 2.0 * jnp.floor(row * 0.5)
            hot = (iotaf((nb, 128), 0) == row - 1.0).astype(F32)
            slot = tile[1:2] + odd * jnp.sum(hot * totals, axis=0, keepdims=True)
            block = jnp.floor(slot * (1.0 / SPAN))
            tab[r, p] = jnp.where(iota((8, 128), 0) == 1, block, tile)

        loop(n.seq, settle)


def picks(n, tile):
    return low((iotaf((n.seq * n.cap, 128), 0) == tile[0:1]).astype(F32))


def picks_back(n, tile):
    return low((iotaf((128, n.seq * n.cap), 1) == to_column(tile[0:1])).astype(F32))


def block_marks(tile):
    return low((iotaf((128, 128), 1) == to_column(tile[1:2])).astype(F32))


FAR = 2.0 ** 30


def with_blocks(marks, query, key):
    i, k = iota((128, 128), 0), iota((128, 128), 1)
    seen = dot(marks, low((((k == i) | (k == i + 1)) & (i < 4)).astype(F32)))
    lane = iota(marks.shape, 1)
    ask = low(jnp.where(lane < 4, marks.astype(F32) * -FAR, 0.0))
    answer = low(jnp.where(lane < 4, 1.0 - seen, 0.0))
    return jnp.concatenate([query, ask], axis=1), jnp.concatenate([key, answer], axis=1)


def halves(wide_query, wide_key):
    size = wide_query.shape[0]
    cut = size // 2
    row, col = iota((cut, cut), 0), iota((cut, cut), 1)

    def ordered(raw):
        return jnp.where(col < row, raw, jnp.where(col == row, -1e4, -1e9))

    first = ordered(dot_nt(wide_query[:cut], wide_key[:cut]))
    rest = dot_nt(wide_query[cut:], wide_key)
    return first, jnp.concatenate([rest[:, :cut], ordered(rest[:, cut:])], axis=1)


def rows_of(n, ref):
    got = ref[...]
    if n.cap % 16:
        return low(got.astype(F32).reshape(n.seq * n.cap, got.shape[-1]))
    return got.reshape(n.seq * n.cap, got.shape[-1])


def put_rows(n, ref, value):
    ref[...] = value.reshape(n.seq, n.cap, value.shape[-1]).astype(ref.dtype)


def keys_of(query):
    wide = query.astype(F32)
    scale = lax.rsqrt(jnp.sum(wide * wide, axis=1, keepdims=True) + 1e-06)
    return low(wide * scale), scale


def fill_block(n, r, p, tab, qv, buf, marks):
    tile = tab[r, p]
    hot = picks(n, tile)
    got = dot(hot, jnp.concatenate([qv[p], block_marks(tile)], axis=1))
    put_rows(n, buf.at[r, :, p], got[:, :256])
    put_rows(n, marks.at[r, :, p], got[:, 256:])


def attend(n, r, g, buf, marks, obuf):
    both = rows_of(n, buf.at[r, g])
    query, value = both[:, :128], both[:, 128:]
    key, _ = keys_of(query)
    cut = query.shape[0] // 2
    outs = []
    for score, values in zip(halves(*with_blocks(rows_of(n, marks.at[r, g]), query, key)), (value[:cut], value)):
        top = jnp.max(score, axis=1, keepdims=True)
        expo = jnp.exp(score - top)
        total = jnp.sum(expo, axis=1, keepdims=True)
        out = dot(low(expo), values) / total
        hi, mid, rest = split3(top + jnp.log(total))
        lane = iota((cut, 128), 1)
        logs = jnp.where(lane == 0, hi, jnp.where(lane == 1, mid, jnp.where(lane == 2, rest, 0.0)))
        outs.append(jnp.concatenate([out, logs], axis=1))
    put_rows(n, obuf.at[r, :, g], jnp.concatenate(outs, axis=0))


def merge(outs, logs):
    top = functools.reduce(jnp.maximum, logs)
    weights = [jnp.exp(v - top) for v in logs]
    total = sum(weights)
    return sum(x * y for x, y in zip(weights, outs)) / total, top + jnp.log(total)


def merge_rounds(n, p, tab, obuf):
    outs, logs = [], []
    for r in range(n.rounds):
        got = dot(picks_back(n, tab[r, p]), rows_of(n, obuf.at[r, p]))
        outs.append(got[:, :128])
        logs.append(jnp.sum(got[:, 128:], axis=1, keepdims=True))
    return merge(outs, logs)


def write_message(ref, out, log):
    ref[:128] = low(out)
    ref[128:] = message_rows(split3(to_row(log)))


def read_log(ref):
    return to_column(jnp.sum(ref[128:].astype(F32), axis=0, keepdims=True))


def hat_of(x):
    center = x - jnp.mean(x, axis=1, keepdims=True)
    scale = lax.rsqrt(jnp.mean(center * center, axis=1, keepdims=True) + 1e-05)
    return center * scale, scale


def normalize(x, gain, shift):
    hat, scale = hat_of(x)
    return hat, scale, hat * gain + shift


def placed(row, spot):
    size = row.shape[1]
    put = (iota((size, 128), 1) == iota((size, 128), 0) + spot * size).astype(F32)
    return dot(row, low(put))


def gelu_pair(x):
    k = 0.7978845608028654
    square = x * x
    t = jnp.tanh(k * (x + 0.044715 * (square * x)))
    half = 0.5 * (1.0 + t)
    return x * half, half + 0.5 * x * (1.0 - t * t) * (k * (1.0 + 0.134145 * square))


class GroupSum:
    def __init__(self, n, w, out, got1, got2, send, recv):
        self.n, self.w, self.out, self.got1, self.got2 = n, w, out, got1, got2
        self.send, self.recv = send, recv

    def fill(self, product):
        n, w = self.n, self.w
        for m in range(n.b):
            b = lax.rem(w.b + 1 + m, n.b)
            self.out[pl.ds(2 * b, 2)] = low(product(b)).reshape(2, n.tokens, n.width)
            t = b * 2 + 1 - w.j
            push(self.out.at[t], self.got1.at[b], self.send.at[m], self.recv.at[b], w.sib)

    def chips(self):
        n, w = self.n, self.w
        for m in range(1, n.b):
            b = lax.rem(w.b + m, n.b)
            t = b * 2 + w.j
            wait(self.got1.at[b], self.recv.at[b])
            self.out[t] = low(self.out[t].astype(F32) + self.got1[b].astype(F32))
            k = n.b + m - 1
            push(self.out.at[t], self.got2.at[m - 1], self.send.at[k], self.recv.at[k], member(n, w, t))

    def total(self):
        n, w = self.n, self.w
        wait(self.got1.at[w.b], self.recv.at[w.b])
        total = self.out[w.t].astype(F32) + self.got1[w.b].astype(F32)
        for m in range(1, n.b):
            wait(self.got2.at[m - 1], self.recv.at[n.b + m - 1])
            total += self.got2[m - 1].astype(F32)
        return total

    def drain(self):
        for k in range(2 * self.n.b - 1):
            wait(self.got1.at[0], self.send.at[k])


class Scatter:
    def __init__(self, n, w, outer, part, got1, got2, got3, send, recv):
        self.n, self.w, self.outer, self.part = n, w, outer, part
        self.got1, self.got2, self.got3 = got1, got2, got3
        self.send, self.recv = send, recv
        self.one, self.two = (n.fsdp, n.b) if outer == "f" else (n.b, n.fsdp)
        self.me1, self.me2 = (w.f, w.b) if outer == "f" else (w.b, w.f)
        self.base2 = (self.one - 1) * n.a * self.two
        self.base3 = self.base2 + (self.two - 1) * n.a

    def mine(self, a, one, two):
        return self.part(a, two, one) if self.outer == "f" else self.part(a, one, two)

    def dev(self, a, one, two):
        if self.outer == "f":
            return plane(self.n, self.w, a, two, one)
        return plane(self.n, self.w, a, one, two)

    def first(self):
        for m in range(1, self.one):
            far = lax.rem(self.me1 + m, self.one)

            def body(i, m=m, far=far):
                a, two = i // self.two, lax.rem(i, self.two)
                k = (m - 1) * self.n.a * self.two + i
                push(self.mine(a, far, two), self.got1.at[m - 1, a, two], self.send.at[k], self.recv.at[k],
                     self.dev(self.w.a, far, self.me2))

            loop(self.n.a * self.two, body)

    def second(self):
        def body(i):
            m2, a = i // self.n.a, lax.rem(i, self.n.a)
            two = lax.rem(self.me2 + 1 + m2, self.two)
            for m in range(1, self.one):
                k = (m - 1) * self.n.a * self.two + a * self.two + two
                wait(self.got1.at[m - 1, a, two], self.recv.at[k])
            self.fold1(a, two)

            @pl.when(m2 < self.two - 1)
            def _():
                k = self.base2 + m2 * self.n.a + a
                push(self.got1.at[0, a, two], self.got2.at[m2, a], self.send.at[k], self.recv.at[k],
                     self.dev(self.w.a, self.me1, two))

        loop(self.n.a * self.two, body)

    def fold1(self, a, two):
        total = self.mine(a, self.me1, two)[...].astype(F32)
        for m in range(1, self.one):
            total += self.got1[m - 1, a, two].astype(F32)
        self.got1[0, a, two] = low(total)

    def third(self):
        def body(i):
            a = lax.rem(self.w.a + 1 + i, self.n.a)
            for m2 in range(self.two - 1):
                wait(self.got2.at[m2, a], self.recv.at[self.base2 + m2 * self.n.a + a])
            total = self.got1[0, a, self.me2].astype(F32)
            for m2 in range(self.two - 1):
                total += self.got2[m2, a].astype(F32)
            self.got2[0, a] = low(total)

            @pl.when(i < self.n.a - 1)
            def _():
                k = self.base3 + i
                push(self.got2.at[0, a], self.got3.at[i], self.send.at[k], self.recv.at[k],
                     self.dev(a, self.me1, self.me2))

        loop(self.n.a, body)

    def total(self):
        total = self.got2[0, self.w.a].astype(F32)
        for i in range(self.n.a - 1):
            wait(self.got3.at[i], self.recv.at[self.base3 + i])
            total += self.got3[i].astype(F32)
        return total

    def drain(self):
        loop(self.base3 + self.n.a - 1, lambda k: wait(self.got3.at[0], self.send.at[k]))


class PlaneScatter:
    def __init__(self, n, w, part, got1, got2, send, recv):
        self.n, self.w, self.part, self.got1, self.got2, self.send, self.recv = n, w, part, got1, got2, send, recv
        self.base = (n.fsdp - 1) * n.a

    def first(self):
        n, w = self.n, self.w
        for m in range(1, n.fsdp):
            far = lax.rem(w.f + m, n.fsdp)

            def body(i, m=m, far=far):
                a = lax.rem(w.a + 1 + i, n.a)
                k = (m - 1) * n.a + a
                push(self.part(a, far), self.got1.at[m - 1, a], self.send.at[k], self.recv.at[k], plane(n, w, w.a, w.b, far))

            loop(n.a, body)

    def second(self, i):
        n, w = self.n, self.w
        a = lax.rem(w.a + 1 + i, n.a)
        total = self.part(a, w.f)[...].astype(F32)
        for m in range(1, n.fsdp):
            wait(self.got1.at[m - 1, a], self.recv.at[(m - 1) * n.a + a])
            total += self.got1[m - 1, a].astype(F32)
        self.got1[0, a] = low(total)
        if i < n.a - 1:
            k = self.base + i
            push(self.got1.at[0, a], self.got2.at[i], self.send.at[k], self.recv.at[k], plane(n, w, a, w.b, w.f))

    def total(self):
        total = self.got1[0, self.w.a].astype(F32)
        for i in range(self.n.a - 1):
            wait(self.got2.at[i], self.recv.at[self.base + i])
            total += self.got2[i].astype(F32)
        return total

    def drain(self):
        loop(self.base + self.n.a - 1, lambda k: wait(self.got2.at[0], self.send.at[k]))


def spread(n, r, p, tab, dtok, dbuf, marks):
    tile = tab[r, p]
    shift = low((iota((MSG - 128, 128), 0) + 4 == iota((MSG - 128, 128), 1)).astype(F32))
    marked = block_marks(tile) + low(dot_tn(dtok[p, 128:], shift))
    got = dot(picks(n, tile), jnp.concatenate([dtok[p, :128], marked], axis=1))
    put_rows(n, dbuf.at[r, :, p], got[:, :128])
    put_rows(n, marks.at[r, :, p], got[:, 128:])


def attend_back(n, r, g, buf, marks, dbuf, gbuf):
    both, cot, marked = rows_of(n, buf.at[r, g]), rows_of(n, dbuf.at[r, g]), rows_of(n, marks.at[r, g])
    query, value = both[:, :128], both[:, 128:]
    aux = marked.astype(F32)
    lane = iota(aux.shape, 1)
    log_all = jnp.sum(jnp.where((lane >= 4) & (lane < 7), aux, 0.0), axis=1, keepdims=True)
    delta = jnp.sum(jnp.where(lane >= 7, aux, 0.0), axis=1, keepdims=True)
    key, scale = keys_of(query)
    cut = query.shape[0] // 2
    score0, score1 = halves(*with_blocks(marked, query, key))
    under = iota((cut, cut), 1) < iota((cut, cut), 0)
    prob0 = jnp.exp(score0 - log_all[:cut])
    prob1 = jnp.exp(score1 - log_all[cut:])
    back0 = low(jnp.where(under, prob0 * (dot_nt(cot[:cut], value[:cut]) - delta[:cut]), 0.0))
    back1 = prob1 * (dot_nt(cot[cut:], value) - delta[cut:])
    back1 = low(jnp.concatenate([back1[:, :cut], jnp.where(under, back1[:, cut:], 0.0)], axis=1))
    direct = jnp.concatenate([dot(back0, key[:cut]), dot(back1, key)], axis=0)

    def both_halves(first, rest, rows):
        total = dot_tn(rest, rows[cut:])
        return jnp.concatenate([total[:cut] + dot_tn(first, rows[:cut]), total[cut:]], axis=0)

    back_key = both_halves(back0, back1, query)
    back_value = both_halves(low(prob0), low(prob1), cot)
    wide = query.astype(F32)
    inner = jnp.sum(wide * back_key, axis=1, keepdims=True)
    total = direct + scale * back_key - wide * (scale * scale * scale * inner)
    put_rows(n, gbuf.at[r, :, g], jnp.concatenate([total, back_value], axis=1))


UNROLL = 2
RELAYS = (0, 0, 0, 0, 0, 1, 1, 1, 1)
SUMS = (1, 1, 2, 2, 1, 1, 1, 1)


def greet_all(n, w, barrier):
    def greet(i):
        pl.semaphore_signal(barrier, inc=1, device_id=peer(n, w, i + 1)[1], device_id_type=MESH)

    loop(n.all - 1, greet)


def pack(n, w, x):
    x.ci[w.t] = low(x.cot2[...])
    for t in range(n.group):
        for a in range(n.a):
            s = a * n.group + t
            x.we_in[t, :, a * n.wide:(a + 1) * n.wide] = x.expand_w[:, s * n.wide:(s + 1) * n.wide]
    lead = placed(x.vectors[...], lax.rem(w.me, 128 // n.rows))
    extra = placed(jnp.broadcast_to(x.bias[...], (8, n.units)), lax.rem(w.me, 128 // n.units))
    lead = jnp.where(iota((8, 128), 0) == 5, extra, lead)
    x.small_all[w.me] = low(jnp.concatenate([lead, x.buckets[...].astype(F32), jnp.zeros((8 - ROUNDS, 128), F32)]))
    for h in range(HEADS):
        x.wqv_in[w.f, h, :, :128] = x.query_w[:, h * 128:(h + 1) * 128]
        x.wqv_in[w.f, h, :, 128:] = x.value_w[:, h * 128:(h + 1) * 128]
    x.wo[w.me] = x.wo_in[...]
    for q, ref in enumerate((x.query_w, x.value_w)):
        pltpu.make_async_copy(ref, x.full.at[q, w.me], x.s_loc.at[q]).start()
    x.wc[w.a, w.f] = x.wc_in[...]
    x.we[w.a, w.t, w.f] = x.we_in[w.t]


def vectors_of(n, w, x):
    group = 128 // n.rows
    for q in range(n.width // 128):
        x.vec[:, q * 128:(q + 1) * 128] = jnp.sum(
            x.small_all[q * group:(q + 1) * group].astype(F32), axis=0
        )
    per = 128 // n.units
    for q in range(n.a * n.fsdp // per):
        a, rest = q * per // n.fsdp, q * per % n.fsdp
        first = (a * n.group + w.t) * n.fsdp + rest
        total = sum(x.small_all[first + k].astype(F32) for k in range(per))
        x.shift_part[:, q * 128:(q + 1) * 128] = jnp.broadcast_to(total[5:6], (8, 128))


def front_part(n, w, x, obuf, pmsg, omsg):
    barrier = pltpu.get_barrier_semaphore()
    greet_all(n, w, barrier)
    hat, _ = hat_of(x.second[...])
    x.xh[w.s] = low(hat)
    pack(n, w, x)
    pl.semaphore_wait(barrier, n.all - 1)

    def spot(i, v):
        return (lax.rem(w.a + i, n.a) * n.b + lax.rem(w.b + v, n.b)) * 2 + w.j

    def hat_at(a):
        block = (a * n.b + w.b) * 2 + w.j
        return x.xh.at[block], x.r_n.at[block // 2]

    def hat_chip(a):
        return ((a * n.b + w.b) * 2 + w.j, w.f)

    hats = Line(n, w, lambda k: x.s_n.at[k], n.b)

    def share_hat(block):
        push(x.xh.at[block], x.xh.at[block], x.s_ns.at[block // 2], x.r_ns.at[block // 2], w.sib)

    far_b = [(spot(0, v), w.f) for v in range(1, n.b)]
    hats.start(lambda: hat_at(w.a), hat_chip)
    for k, dev in enumerate(far_b):
        hats.send(*hat_at(w.a), dev, lambda k=k: hats.slot(0, 1 + k))
    share_hat(w.s)
    for m in range(1, n.group):
        t = lax.rem(w.t + m, n.group)
        push(x.we_in.at[t], x.we.at[w.a, w.t, w.f], x.s_ex.at[m], x.r_ex.at[w.t], member(n, w, t))

    mine = pl.ds(w.s * n.fsdp, n.fsdp)
    for q in range(1, n.fsdp):
        far = (w.s, lax.rem(w.f + q, n.fsdp))
        push(x.small_all.at[w.me], x.small_all.at[w.me], x.s_f.at[0, q], x.r_f.at[0, w.f], far)
        push(x.wqv_in.at[w.f], x.wqv_in.at[w.f], x.s_f.at[1, q], x.r_f.at[1, w.f], far)
    for q in range(1, n.fsdp):
        f = lax.rem(w.f + q, n.fsdp)
        wait(x.small_all.at[w.me], x.r_f.at[0, f])

    def send_small(i):
        s = lax.rem(w.s + 1 + i, n.seq)
        push(x.small_all.at[mine], x.small_all.at[mine], x.s_small.at[i], x.r_small.at[w.s], (s, w.f))

    loop(n.seq - 1, send_small)
    for q in range(1, n.fsdp):
        f = lax.rem(w.f + q, n.fsdp)
        wait(x.wqv_in.at[f], x.r_f.at[1, f])

    def send_w(i):
        s = lax.rem(w.s + 1 + i, n.seq)
        push(x.wqv_in.at[:, s // n.sub], x.wqv.at[mine], x.s_wq.at[i], x.r_wq.at[w.s], (s, w.f))

    loop(n.seq - 1, send_w)
    x.wqv[mine] = x.wqv_in[:, w.head]

    def shared_o(ref, uid):
        push(ref, ref, x.s_os.at[uid], x.r_os.at[uid], w.sib)

    def all_index(a, b, f):
        return (a * n.b + b) * n.fsdp + f

    def part_index(a, b, f):
        return a * n.fsdp + f

    g_o = Gather(n, w, lambda a, b, f: x.wo.at[((a * n.b + b) * 2 + w.j) * n.fsdp + f], all_index, lambda i: x.s_go.at[i], lambda u: x.r_go.at[u], True, shared_o)
    g_c = Gather(n, w, lambda a, b, f: x.wc.at[a, f], part_index, lambda i: x.s_gc.at[i], lambda u: x.r_gc.at[u])
    g_e = Gather(n, w, lambda a, b, f: x.we.at[a, :, f], part_index, lambda i: x.s_ge.at[i], lambda u: x.r_ge.at[u])
    gathers = (g_o, g_c, g_e)
    for m in range(1, n.group):
        t = lax.rem(w.t + m, n.group)
        wait(x.we.at[w.a, t, w.f], x.r_ex.at[t])
    shared_o(x.wo.at[w.me], (w.a * n.b + w.b) * n.fsdp + w.f)
    for y in gathers:
        y.column(0)

    def pass_hats(far):
        def take_hat(a):
            ref, recv = hat_at(a)
            wait(ref, recv)
            return ref, recv

        hats.step(far, take_hat, hat_chip, far_b)
        for sign in (-1, 1):
            @pl.when(hats.inside(sign * far))
            def _(sign=sign):
                share_hat(((w.a + sign * far) * n.b + w.b) * 2 + w.j)

    def early():
        def wait_small(i):
            s = lax.rem(w.s + 1 + i, n.seq)
            wait(x.small_all.at[mine], x.r_small.at[s])

        loop(n.seq - 1, wait_small)
        vectors_of(n, w, x)

    pass_hats(1)
    early()
    for far in range(2, n.a - 1):
        pass_hats(far)
    tables(n, w, x.small_all, x.tab)
    if n.a > 2:
        pass_hats(n.a - 1)
    weights = x.wqv.reshape(n.width, 256)

    def project(block):
        normed = low(x.xh[block].astype(F32) * x.vec[0:1] + x.vec[1:2])

        @pl.when(lax.rem(block, n.sub) == w.idx)
        def _():
            x.nown[block // n.sub] = normed

        x.qv[block] = low(dot(normed, weights[...]))

    for y in gathers:
        y.to_a()

    def wait_w(i):
        s = lax.rem(w.s + 1 + i, n.seq)
        wait(x.wqv.at[mine], x.r_wq.at[s])

    loop(n.seq - 1, wait_w)
    project(w.s)
    for i in range(1, n.a):
        project(spot(i, 0))
    for i in range(n.a):
        for v in range(1, n.b):
            block = spot(i, v)
            wait(x.xh.at[block], x.r_n.at[block // 2])
            share_hat(block)
            project(block)

    def from_sibling(c):
        block = 2 * c + 1 - w.j
        wait(x.xh.at[block], x.r_ns.at[c])
        project(block)

    loop(n.chips, from_sibling)

    for m in range(1, n.group):
        t = lax.rem(w.t + m, n.group)
        push(x.ci.at[w.t], x.ci.at[w.t], x.s_ci.at[m], x.r_ci.at[w.t], member(n, w, t))

    tasks = []
    for i in range(n.a):
        if i:
            tasks.append(lambda i=i: [y.column(i) for y in gathers])
        tasks.append(lambda i=i: g_o.corner(i))

    def relay(count):
        for _ in range(count):
            if tasks:
                tasks.pop(0)()

    for r in range(n.rounds):
        loop_by(UNROLL, n.seq, lambda p: fill_block(n, r, p, x.tab, x.qv, x.buf, x.marks))
    relay(RELAYS[0])
    parts = 4
    slot = 1
    for r in range(n.rounds):
        for q in range(parts):
            loop_by(UNROLL, n.seq // parts, lambda g: attend(n, r, q * (n.seq // parts) + g, x.buf, x.marks, obuf))
            relay(RELAYS[slot])
            slot += 1

    blocks = n.seq // n.sub
    for m in range(1, n.sub):
        far = lax.rem(w.idx + m, n.sub)

        def offer(i, m=m, far=far):
            k = (m - 1) * blocks + i
            write_message(pmsg.at[k], *merge_rounds(n, i * n.sub + far, x.tab, obuf))
            push(pmsg.at[k], x.pin.at[k], x.s_p.at[k], x.r_p.at[k], (w.head * n.sub + far, w.f))

        loop_by(UNROLL, blocks, offer)

    def settle(i):
        out, log = merge_rounds(n, i * n.sub + w.idx, x.tab, obuf)
        outs, logs = [out], [log]
        for m in range(1, n.sub):
            k = (m - 1) * blocks + i
            wait(x.pin.at[k], x.r_p.at[k])
            outs.append(x.pin[k, :128].astype(F32))
            logs.append(read_log(x.pin.at[k]))
        write_message(omsg.at[i], *merge(outs, logs))

    def give(i):
        to = lax.rem(w.head + 1 + i, blocks)
        settle(to)
        push(omsg.at[to], x.home.at[w.head], x.s_out.at[i], x.r_out.at[w.head], (to * n.sub + w.idx, w.f))

    loop(blocks - 1, give)
    settle(w.head)
    x.home[w.head] = omsg[w.head]
    relay(len(tasks))

    def take(i):
        h = lax.rem(w.head + 1 + i, HEADS)
        wait(x.home.at[h], x.r_out.at[h])

    loop(HEADS - 1, take)
    g_o.finish()
    loop(n.chips * n.fsdp, lambda u: wait(x.wo.at[w.me], x.r_os.at[u]))

    loop((n.sub - 1) * blocks, lambda k: wait(pmsg.at[0], x.s_p.at[k]))
    loop(blocks - 1, lambda k: wait(omsg.at[0], x.s_out.at[k]))

    def drain():
        g_c.finish()
        g_e.finish()
        for y in gathers:
            y.drain()
        loop(n.chips * n.fsdp, lambda u: wait(x.wo.at[w.me], x.s_os.at[u]))
        for m in range(1, n.group):
            t = lax.rem(w.t + m, n.group)
            wait(x.we_in.at[0], x.s_ex.at[m])
            wait(x.ci.at[t], x.r_ci.at[t])
            wait(x.ci.at[t], x.s_ci.at[m])

        def wait_sends(i):
            wait(x.small_all.at[pl.ds(0, n.fsdp)], x.s_small.at[i])
            wait(x.wqv.at[pl.ds(0, n.fsdp)], x.s_wq.at[i])

        loop(n.seq - 1, wait_sends)
        for q in range(1, n.fsdp):
            wait(x.small_all.at[0], x.s_f.at[0, q])
            wait(x.wqv_in.at[0], x.s_f.at[1, q])
        hats.drain_sends(lambda: x.xh.at[w.s])
        loop(n.chips, lambda c: wait(x.xh.at[w.s], x.s_ns.at[c]))

    return drain


def feed_part(n, w, x, sums, whole, drain, mixed_low, act, gp, out, out2):
    sum_c, sum_e, _ = sums
    for h in range(HEADS):
        mixed_low[:, h * 128:(h + 1) * 128] = x.home[h, :128]
    first_out = x.first[...] + dot(mixed_low[...], x.wo.reshape(n.width, n.width)[...])
    x.first_o[...] = first_out
    hat, scale, normed = normalize(first_out, x.vec[2:3], x.vec[3:4])
    x.n2[w.t] = low(normed)
    k = 0
    for m in range(1, n.b):
        t = lax.rem(w.b + m, n.b) * 2 + w.j
        push(x.n2.at[w.t], x.n2.at[w.t], x.s_x.at[k], x.r_x.at[w.t], member(n, w, t))
        k += 1
    push(x.n2.at[w.t], x.n2.at[w.t], x.s_x.at[k], x.r_x.at[w.t], w.sib)
    k += 1
    for q, ref in enumerate((x.query_w, x.value_w)):
        pltpu.make_async_copy(ref, x.full.at[q, w.me], x.s_loc.at[q]).wait()
    whole.arrived(*whole.own())
    whole.to_a()
    whole.column(0)
    drain()
    for m in range(1, n.b):
        t = lax.rem(w.b + m, n.b) * 2 + w.j
        wait(x.n2.at[t], x.r_x.at[t])
        push(x.n2.at[t], x.n2.at[t], x.s_x.at[k], x.r_x.at[t], w.sib)
        k += 1
    for b in range(n.b):
        t = b * 2 + 1 - w.j
        wait(x.n2.at[t], x.r_x.at[t])
    size = n.group * n.tokens
    step = min(512, n.part)
    tokens = x.n2.reshape(size, n.width)
    cots = x.ci.reshape(size, n.width)
    we = x.we.reshape(n.width, n.part)
    wc = x.wc.reshape(n.part, n.width)
    for q in range(n.part // step):
        at = slice(q * step, (q + 1) * step)
        pre = dot(tokens[...], we[:, at]) + x.shift_part[0:1, at]
        value, slope = gelu_pair(pre)
        act[:, at] = low(value)
        back = low(dot_nt(cots[...], wc[at]) * slope)
        gp[:, at] = back
        x.shift_g[:, at] = jnp.broadcast_to(jnp.sum(back.astype(F32), axis=0, keepdims=True), (8, step))
    gn = GroupSum(n, w, out, x.gn_got1, x.gn_got2, x.s_gn, x.r_gn)
    so = GroupSum(n, w, out2, x.so_got1, x.so_got2, x.s_so, x.r_so)
    pair = 2 * n.tokens
    gn.fill(lambda b: dot_nt(gp[pl.ds(pl.multiple_of(b * pair, pair), pair)], we[...]))
    x.gwc.reshape(n.part, n.width)[...] = low(dot_tn(act[...], cots[...]))
    sum_c.first()
    gn.chips()
    so.fill(lambda b: dot(act[pl.ds(pl.multiple_of(b * pair, pair), pair)], wc[...]))
    x.gwe.reshape(n.width, n.part)[...] = low(dot_tn(tokens[...], gp[...]))
    so.chips()
    sum_e.first()
    grad = gn.total()
    rest = grad * x.vec[2:3]
    mean = jnp.mean(rest, axis=1, keepdims=True)
    tilt = jnp.mean(rest * hat, axis=1, keepdims=True)
    grad1 = x.cot1[...] + scale * (rest - mean - hat * tilt)
    x.grad1_o[...] = grad1
    branch = low(grad1)
    wo = x.wo.reshape(n.width, n.width)
    for h in range(HEADS):
        gm = dot_nt(branch, wo[h * 128:(h + 1) * 128])
        x.message[h, :128] = low(gm)
        delta = jnp.sum(gm * x.home[h, :128].astype(F32), axis=1, keepdims=True)
        logs = x.home[h, 128:].astype(F32)
        x.message[h, 128:] = message_rows((logs[0:1], logs[1:2], logs[2:3]) + split3(to_row(delta)))

    def give(i):
        s = lax.rem(w.s + 1 + i, n.seq)
        push(x.message.at[s // n.sub], x.dtok.at[w.s], x.s_d.at[i], x.r_d.at[w.s], (s, w.f))

    loop(n.seq - 1, give)
    x.dtok[w.s] = x.message[w.head]
    whole.column(1)
    whole.corner(0)
    gwo = low(dot_tn(mixed_low[...], branch)).reshape(n.chips, 2, n.fsdp * n.rows, n.width)
    x.gwo[...] = gwo.reshape(n.chips, 2, n.fsdp, n.rows, n.width)
    push(x.gwo.at[:, 1 - w.j], x.o0, x.s_o0.at[0], x.r_o0.at[0], w.sib)
    zero = jnp.zeros((2, n.width), F32)
    x.vec_g[...] = jnp.concatenate([
        zero,
        jnp.sum(grad * hat, axis=0, keepdims=True),
        jnp.sum(grad, axis=0, keepdims=True),
        jnp.sum(x.ci[w.t].astype(F32), axis=0, keepdims=True),
        zero, zero[:1],
    ])
    x.second_o[...] = x.second[...] + so.total() + x.vec[4:5]
    for i in range(k):
        wait(x.n2.at[0], x.s_x.at[i])
    gn.drain()
    so.drain()


def back_attention(n, w, x, sums, whole, dbuf, gbuf, gout):
    sum_c, sum_e, sum_o = sums
    blocks = n.seq // n.sub
    wait(x.o0, x.r_o0.at[0])

    def join_o(c):
        x.o0[c] = low(x.o0[c].astype(F32) + x.gwo[c, w.j].astype(F32))

    loop(n.chips, join_o)
    sum_o.first()

    def take(i):
        p = lax.rem(w.s + 1 + i, n.seq)
        wait(x.dtok.at[p], x.r_d.at[p])

    loop(n.seq - 1, take)
    tasks = []
    for i in range(n.a):
        tasks.append(lambda i=i: (sum_c.second(i), sum_e.second(i)))
        if 0 < i < n.a - 1:
            tasks.append(lambda i=i: whole.column(i + 1))
        if i:
            tasks.append(lambda i=i: whole.corner(i))
        if i == 1:
            tasks.append(sum_o.second)
    tasks.append(sum_o.third)

    def relay(count):
        for _ in range(count):
            if tasks:
                tasks.pop(0)()

    slot = 0
    parts = 4
    for r in range(n.rounds):
        loop_by(UNROLL, n.seq, lambda p: spread(n, r, p, x.tab, x.dtok, dbuf, x.marks))
        for q in range(parts):
            loop_by(UNROLL, n.seq // parts, lambda g: attend_back(n, r, q * (n.seq // parts) + g, x.buf, x.marks, dbuf, gbuf))
            relay(SUMS[slot])
            slot += 1
    relay(len(tasks))

    def tokens_of(p):
        total = None
        for r in range(n.rounds):
            got = dot(picks_back(n, x.tab[r, p]), rows_of(n, gbuf.at[r, p]))
            total = got if total is None else total + got
        return total

    for m in range(1, n.sub):
        far = lax.rem(w.idx + m, n.sub)

        def offer(i, m=m, far=far):
            k = (m - 1) * blocks + i
            gout[k] = low(tokens_of(i * n.sub + far))
            push(gout.at[k], x.gin.at[k], x.s_g.at[k], x.r_g.at[k], (w.head * n.sub + far, w.f))

        loop_by(UNROLL, blocks, offer)

    def keep(i):
        x.gown[i] = tokens_of(i * n.sub + w.idx)

    loop_by(UNROLL, blocks, keep)
    loop((n.sub - 1) * blocks, lambda k: wait(gout.at[0], x.s_g.at[k]))


def back_rest(n, w, x, sums, whole, dqv, wsum, wout, esw, vsend, full):
    sum_c, sum_e, sum_o = sums
    blocks = n.seq // n.sub
    whole.finish()
    loop(n.chips * n.fsdp, lambda u: wait(whole.own()[0], x.r_ps.at[u]))
    load = pltpu.make_async_copy(x.full, full, x.s_loc.at[0])
    load.start()

    def finish_block(i):
        total = x.gown[i]
        for m in range(1, n.sub):
            k = (m - 1) * blocks + i
            wait(x.gin.at[k], x.r_g.at[k])
            total += x.gin[k].astype(F32)
        dqv[i] = low(total)

    def arrived(h):
        return x.xh.at[h, :, pl.ds(0, 256)]

    def send_home(k):
        i = lax.rem(w.head + 1 + k, blocks)
        finish_block(i)
        push(dqv.at[i], arrived(w.head), x.s_h.at[k], x.r_h.at[w.head], (i * n.sub + w.idx, w.f))

    loop(blocks - 1, send_home)
    finish_block(w.head)
    x.xh[w.head, :, :256] = dqv[w.head]

    for i in range(blocks):
        got = dot_tn(x.nown[i], dqv[i])
        wsum[...] = got if i == 0 else wsum[...] + got
    wout[...] = low(wsum[...]).reshape(n.all, n.rows, 256)

    def rows_out(i):
        d, dev = peer(n, w, i + 1)
        push(wout.at[d], x.win.at[w.me], x.s_w2.at[i], x.r_w2.at[w.me], dev)

    loop(n.all - 1, rows_out)
    x.win[w.me] = wout[w.me]

    esw[...] = sum_e.total()
    x.egot[w.t] = esw[w.t]
    for m in range(1, n.group):
        t = lax.rem(w.t + m, n.group)
        push(esw.at[t], x.egot.at[w.t], x.s_y.at[m], x.r_y.at[w.t], member(n, w, t))
    x.go_o[...] = sum_o.total()
    x.gc_o[...] = sum_c.total()

    hat, scale = hat_of(x.second[...])

    def take_home(k):
        h = lax.rem(w.head + 1 + k, HEADS)
        wait(arrived(h), x.r_h.at[h])

    loop(HEADS - 1, take_home)
    for h in range(HEADS):
        for q in range(2):
            x.xh[HEADS + q, :, h * 128:(h + 1) * 128] = x.xh[h, :, q * 128:(q + 1) * 128]
    load.wait()
    grad = sum(dot_nt(x.xh[HEADS + q], full[q].reshape(n.width, n.width)) for q in range(2))
    rest = grad * x.vec[0:1]
    mean = jnp.mean(rest, axis=1, keepdims=True)
    tilt = jnp.mean(rest * hat, axis=1, keepdims=True)
    x.grad2_o[...] = x.cot2[...] + scale * (rest - mean - hat * tilt)
    gain_g = jnp.sum(grad * hat, axis=0, keepdims=True)
    shift1_g = jnp.sum(grad, axis=0, keepdims=True)
    group = 128 // n.rows
    per = 128 // n.units
    at = iota((8, 128), 0)

    def rolled(tile, lanes):
        return pltpu.roll(tile, 128 - lanes, 1) if lanes else tile

    for q in range(n.width // 128):
        cut = slice(q * 128, (q + 1) * 128)
        tile = jnp.where(at == 0, gain_g[:, cut], jnp.where(at == 1, shift1_g[:, cut], x.vec_g[:, cut]))
        for k in range(group):
            vsend[q * group + k] = rolled(tile, k * n.rows)
    for q in range(n.a * n.fsdp // per):
        for k in range(per):
            u = q * per + k
            d = (u // n.fsdp * n.group + w.t) * n.fsdp + u % n.fsdp
            tile = rolled(x.shift_g[:, q * 128:(q + 1) * 128], k * n.units)
            vsend[d] = jnp.where(at == 5, tile, vsend[d])

    def vec_out(i):
        d, dev = peer(n, w, i + 1)
        push(vsend.at[d], x.vgot.at[w.me], x.s_v.at[i], x.r_v.at[w.me], dev)

    loop(n.all - 1, vec_out)
    x.vgot[w.me] = vsend[w.me]

    def take_rows(i):
        d, _ = peer(n, w, i + 1)
        wait(x.win.at[d], x.r_w2.at[d])

    loop(n.all - 1, take_rows)
    for h in range(HEADS):
        total = 0.0
        for i in range(n.sub * n.fsdp):
            total += x.win[h * n.sub * n.fsdp + i].astype(F32)
        x.gq_o[:, h * 128:(h + 1) * 128] = total[:, :128]
        x.gv_o[:, h * 128:(h + 1) * 128] = total[:, 128:]
    for m in range(1, n.group):
        t = lax.rem(w.t + m, n.group)
        wait(x.egot.at[t], x.r_y.at[t])
    for t in range(n.group):
        for a in range(n.a):
            c = (a * n.group + t) * n.wide
            x.ge_o[:, c:c + n.wide] = x.egot[t, :, a * n.wide:(a + 1) * n.wide]

    wait(x.o0, x.s_o0.at[0])
    for m in range(1, n.group):
        wait(x.egot.at[0], x.s_y.at[m])
    loop(n.seq - 1, lambda i: wait(x.dtok.at[0], x.s_d.at[i]))
    for y in (sum_c, sum_e, sum_o):
        y.drain()
    loop(blocks - 1, lambda k: wait(dqv.at[0], x.s_h.at[k]))
    whole.drain()
    loop(n.chips * n.fsdp, lambda u: wait(whole.own()[0], x.s_ps.at[u]))

    def wait_all(i):
        wait(x.win.at[0], x.s_w2.at[i])
        wait(x.vgot.at[0], x.s_v.at[i])

    loop(n.all - 1, wait_all)

    def take_vec(i):
        d, _ = peer(n, w, i + 1)
        wait(x.vgot.at[d], x.r_v.at[d])

    loop(n.all - 1, take_vec)
    x.small_o[...] = jnp.sum(x.vgot[...], axis=0)


def layer_kernel(n, names, *refs):
    x = types.SimpleNamespace(**dict(zip(names, refs, strict=True)))
    w = place(n)
    t, d, g = n.tokens, n.width, n.group
    blocks = n.seq // n.sub
    pairs = (n.rounds, n.seq, n.seq, n.cap, 256)
    sums = (
        PlaneScatter(n, w, lambda a, f: x.gwc.at[a, f], x.c1, x.c2, x.s_c, x.r_c),
        PlaneScatter(n, w, lambda a, f: x.gwe.at[a, :, f], x.e1, x.e2, x.s_e, x.r_e),
        Scatter(n, w, "f", lambda a, b, f: x.o0.at[a * n.b + b, f], x.o1, x.o2, x.o3, x.s_o, x.r_o),
    )
    drains = []

    def shared(ref, uid):
        push(ref, ref, x.s_ps.at[uid], x.r_ps.at[uid], w.sib)

    whole = Gather(
        n, w, lambda a, b, f: x.full.at[:, ((a * n.b + b) * 2 + w.j) * n.fsdp + f], lambda a, b, f: (a * n.b + b) * n.fsdp + f,
        lambda i: x.s_gp.at[i], lambda u: x.r_gp.at[u], True, shared,
    )
    pl.run_scoped(
        lambda *r: drains.append(front_part(n, w, x, *r)),
        VM(pairs, BF), VM(((n.sub - 1) * blocks, MSG, 128), BF), VM((blocks, MSG, 128), BF),
    )
    pl.run_scoped(
        lambda *r: feed_part(n, w, x, sums, whole, drains[0], *r),
        VM((t, d), BF), VM((g * t, n.part), BF), VM((g * t, n.part), BF),
        VM((g, t, d), BF), VM((g, t, d), BF),
    )
    pl.run_scoped(
        lambda *r: back_attention(n, w, x, sums, whole, *r),
        VM(pairs[:-1] + (128,), BF), VM(pairs, BF), VM(((n.sub - 1) * blocks, 128, 256), BF),
    )
    pl.run_scoped(
        lambda *r: back_rest(n, w, x, sums, whole, *r),
        VM((blocks, 128, 256), BF), VM((d, 256), F32), VM((n.all, n.rows, 256), BF), VM((g, n.rows, n.part), F32),
        VM((n.all, 8, 128), F32), VM((2, n.all, n.rows, d), BF),
    )


def layer(n, inputs):
    inside = pl.BlockSpec(memory_space=VM)
    t, d, g, a = n.tokens, n.width, n.group, n.a
    units = n.chips * n.fsdp
    blocks = n.seq // n.sub
    f1, b1 = max(n.fsdp - 1, 1), max(n.b - 1, 1)
    pairs = (n.rounds, n.seq, n.seq, n.cap)
    unit_c, unit_e, unit_o = (n.units, d), (g, n.rows, n.part), (n.rows, d)
    count_f = (n.fsdp - 1) * a * n.b + (n.b - 1) * a + a - 1
    count_p = (n.fsdp - 1) * a + a - 1
    outputs = {
        "first_o": (t, d), "second_o": (t, d), "grad1_o": (t, d), "grad2_o": (t, d),
        "gq_o": (n.rows, d), "gv_o": (n.rows, d), "go_o": (n.rows, d), "ge_o": (n.rows, n.hidden), "gc_o": (n.units, d),
        "small_o": (8, 128),
    }
    scratch = {
        "xh": VM((n.seq, 128, d), BF),
        "nown": VM((blocks, 128, d), BF), "qv": VM((n.seq, 128, 256), BF),
        "wqv": VM((n.all, n.rows, 256), BF), "wqv_in": VM((n.fsdp, HEADS, n.rows, 256), BF), "we_in": VM((g, n.rows, n.part), BF),
        "small_all": VM((n.all, 16, 128), BF), "tab": VM((n.rounds, n.seq, 8, 128), F32), "vec": VM((16, d), F32),
        "shift_part": VM((8, n.part), F32), "ci": VM((g, t, d), BF),
        "buf": VM(pairs + (256,), BF), "marks": VM(pairs + (128,), BF),
        "pin": VM(((n.sub - 1) * blocks, MSG, 128), BF),
        "home": VM((HEADS, MSG, 128), BF), "dtok": VM((n.seq, MSG, 128), BF),
        "wo": VM((n.all, n.rows, d), BF), "wc": VM((a, n.fsdp, n.units, d), BF), "we": VM((a, g, n.fsdp, n.rows, n.part), BF),
        "n2": VM((g, t, d), BF),
        "gn_got1": VM((n.b, t, d), BF), "gn_got2": VM((b1, t, d), BF), "so_got1": VM((n.b, t, d), BF), "so_got2": VM((b1, t, d), BF),
        "gwc": VM((a, n.fsdp, n.units, d), BF), "gwe": VM((a, g, n.fsdp, n.rows, n.part), BF),
        "gwo": VM((n.chips, 2, n.fsdp, n.rows, d), BF), "message": VM((HEADS, MSG, 128), BF),
        "vec_g": VM((8, d), F32), "shift_g": VM((8, n.part), F32),
        "gown": VM((blocks, 128, 256), F32),
        "gin": VM(((n.sub - 1) * blocks, 128, 256), BF), "win": VM((n.all, n.rows, 256), BF),
        "c1": VM((f1, a) + unit_c, BF), "c2": VM((a - 1,) + unit_c, BF),
        "e1": VM((f1, a) + unit_e, BF), "e2": VM((a - 1,) + unit_e, BF),
        "o0": VM((n.chips, n.fsdp) + unit_o, BF), "o1": VM((f1, a, n.b) + unit_o, BF),
        "o2": VM((b1, a) + unit_o, BF), "o3": VM((a - 1,) + unit_o, BF),
        "egot": VM(unit_e, F32), "vgot": VM((n.all, 8, 128), F32),
    }
    sems = {
        "small": n.seq, "wq": n.seq, "f": (2, n.fsdp), "ns": n.chips, "os": units, "ex": g, "ci": g,
        "p": (n.sub - 1) * blocks, "out": HEADS, "x": 2 * n.b, "gn": 2 * n.b, "so": 2 * n.b, "d": n.seq, "o0": 1,
        "c": count_p, "e": count_p, "o": count_f, "g": (n.sub - 1) * blocks, "w2": n.all, "h": HEADS, "ps": units,
        "v": n.all, "y": g,
    }
    for key, count in sems.items():
        for side in ("s_", "r_"):
            if key == "x" and side == "r_":
                count = g
            scratch[side + key] = DMA(count if isinstance(count, tuple) else (count,))
    scratch["s_loc"] = DMA((2,))
    part, every = 2 + a * n.fsdp, 2 + a * (n.fsdp + n.b - 1) + a * (n.fsdp - 1) * (n.b - 1)
    for key, sends, gets in (("n", 2 + n.chips, n.chips), ("go", every, units), ("gp", every, units), ("gc", part, a * n.fsdp), ("ge", part, a * n.fsdp)):
        scratch["s_" + key], scratch["r_" + key] = DMA((sends,)), DMA((gets,))
    names = list(inputs) + list(outputs) + ["full"] + list(scratch)
    return pl.pallas_call(
        functools.partial(layer_kernel, n, names),
        out_shape=tuple(jax.ShapeDtypeStruct(s, F32) for s in outputs.values()) + (jax.ShapeDtypeStruct((2, n.all, n.rows, d), BF),),
        in_specs=[inside] * len(inputs),
        out_specs=(inside,) * len(outputs) + (pl.BlockSpec(memory_space=pl.ANY),),
        scratch_shapes=list(scratch.values()),
        compiler_params=pltpu.CompilerParams(collective_id=1, has_side_effects=True, vmem_limit_bytes=60 << 20),
        name="layer",
    )(*inputs.values())


def deliver_kernel(n, count, *refs):
    arrays, small, outs = refs[:count], refs[count], refs[count + 1:2 * count + 1]
    vectors, held, come, leave = refs[2 * count + 1:-count - 2], refs[-count - 2:-2], refs[-2], refs[-1]
    ins = [pltpu.make_async_copy(arrays[i], held[i], come.at[i]) for i in range(count)]
    ends = [pltpu.make_async_copy(held[i], outs[i], leave.at[i]) for i in range(count)]
    for cp in ins:
        cp.start()
    for row, ref in zip((0, 1, 2, 3, 5, 4), vectors, strict=True):
        ref[...] = small[row:row + 1, :ref.shape[1]]
    for before, after in zip(ins, ends, strict=True):
        before.wait()
        after.start()
    for cp in ends:
        cp.wait()


def deliver(n, arrays, small):
    anywhere = pl.BlockSpec(memory_space=pl.ANY)
    inside = pl.BlockSpec(memory_space=VM)
    shape = jax.ShapeDtypeStruct
    sizes = (n.rows, n.rows, n.rows, n.rows, n.units, n.rows)
    count = len(arrays)
    return pl.pallas_call(
        functools.partial(deliver_kernel, n, count),
        out_shape=tuple(shape(y.shape, F32) for y in arrays) + tuple(shape((1, k), F32) for k in sizes),
        in_specs=[anywhere] * count + [inside],
        out_specs=(anywhere,) * count + (inside,) * len(sizes),
        scratch_shapes=[VM(y.shape, F32) for y in arrays] + [DMA((count,)), DMA((count,))],
        compiler_params=pltpu.CompilerParams(vmem_limit_bytes=60 << 20),
        name="deliver",
    )(*arrays, small)


def on_device(
    first_half,
    second_half,
    first_cotangent,
    second_cotangent,
    bucket_ids,
    slot_source,
    live_slots,
    mixer_gain,
    mixer_shift,
    query_weight,
    value_weight,
    output_weight,
    feed_gain,
    feed_shift,
    expand_weight,
    expand_bias,
    contract_weight,
    contract_bias,
):
    seq, fsdp = lax.axis_size("seq"), lax.axis_size("fsdp")
    n = setup(seq, fsdp, first_half.shape[2], expand_weight.shape[1], first_half.shape[1])
    vectors = jnp.stack([mixer_gain, mixer_shift, feed_gain, feed_shift, contract_bias] + [jnp.zeros_like(mixer_gain)] * 3)
    *arrays, small, _ = layer(n, {
        "first": first_half[0], "second": second_half[0], "cot1": first_cotangent[0], "cot2": second_cotangent[0],
        "vectors": vectors, "bias": expand_bias.reshape(1, -1), "buckets": bucket_ids[0],
        "query_w": query_weight, "value_w": value_weight, "expand_w": expand_weight,
        "wo_in": output_weight, "wc_in": contract_weight,
    })
    outs = deliver(n, arrays, small)
    first_out, second_out, grad1, grad2, gq, gv, go, ge, gc = outs[:9]
    gain1, shift1, gain2, shift2, up_bias, down_bias = [y.reshape(-1) for y in outs[9:]]
    return (
        first_out[None], second_out[None], grad1[None], grad2[None],
        gain1, shift1, gq, gv, go, gain2, shift2, ge, up_bias, gc, down_bias,
    )


def solution(mesh):
    tokens, slots = P("fsdp", "seq", None), P("fsdp", None, "seq")
    vector, matrix = P(("seq", "fsdp")), P(("seq", "fsdp"), None)
    return jax.shard_map(
        on_device,
        mesh=mesh,
        in_specs=(tokens,) * 4 + (slots,) * 3 + (vector, vector, matrix, matrix, matrix, vector, vector, matrix, vector, matrix, vector),
        out_specs=(tokens,) * 4 + (vector, vector, matrix, matrix, matrix, vector, vector, matrix, vector, matrix, vector),
        check_vma=False,
    )
```

```python
import functools
import types

import jax
import jax.numpy as jnp
from jax import lax
from jax.experimental import pallas as pl
from jax.experimental.pallas import tpu as pltpu
from jax.sharding import PartitionSpec as P

HEADS = 8
HEAD_DIM = 128
ROUNDS = 4
SPAN = 64
BF = jnp.bfloat16
F32 = jnp.float32
MESH = pl.DeviceIdType.MESH
DMA = pltpu.SemaphoreType.DMA
VM = pltpu.VMEM
MSG = 144


def dot(a, b):
    return lax.dot_general(a, b, (((1,), (0,)), ((), ())), preferred_element_type=F32)


def dot_nt(a, b):
    return lax.dot_general(a, b, (((1,), (1,)), ((), ())), preferred_element_type=F32)


def dot_tn(a, b):
    return lax.dot_general(a, b, (((0,), (0,)), ((), ())), preferred_element_type=F32)


def iota(shape, dim):
    return lax.broadcasted_iota(jnp.int32, shape, dim)


def iotaf(shape, dim):
    return iota(shape, dim).astype(F32)


def low(x):
    return x.astype(BF)


def split3(x):
    hi = x.astype(BF).astype(F32)
    rest = x - hi
    mid = rest.astype(BF).astype(F32)
    return hi, mid, rest - mid


def loop(count, body):
    def step(i, carry):
        body(i)
        return carry

    lax.fori_loop(0, count, step, 0)


def loop_by(k, count, body):
    k = k if count % k == 0 else 1

    def several(i):
        for u in range(k):
            body(i * k + u)

    loop(count // k, several)


def push(src, dst, send, recv, dev):
    pltpu.make_async_remote_copy(
        src_ref=src, dst_ref=dst, send_sem=send, recv_sem=recv, device_id=dev, device_id_type=MESH
    ).start()


def wait(ref, sem):
    pltpu.make_async_copy(ref, ref, sem).wait()


def to_column(row):
    size = row.shape[1]
    eye = iota((size, size), 0) == iota((size, size), 1)
    return jnp.sum(jnp.where(eye, row, 0.0), axis=1, keepdims=True)


def to_row(column):
    size = column.shape[0]
    eye = iota((size, size), 0) == iota((size, size), 1)
    return jnp.sum(jnp.where(eye, column, 0.0), axis=0, keepdims=True)


def message_rows(rows):
    at = iota((MSG - 128, 128), 0)
    out = jnp.zeros((MSG - 128, 128), F32)
    for i, row in enumerate(rows):
        out = jnp.where(at == i, row, out)
    return low(out)


def setup(seq, fsdp, width, hidden, tokens):
    n = types.SimpleNamespace()
    n.seq, n.fsdp, n.all = seq, fsdp, seq * fsdp
    n.chips = seq // 2
    n.b = 2 if n.chips <= 8 else 4
    n.a = n.chips // n.b
    n.sub = seq // HEADS
    n.rounds = ROUNDS // n.sub
    n.cap = 4 * SPAN // seq
    n.width, n.hidden, n.tokens = width, hidden, tokens
    n.rows = width // n.all
    n.units = hidden // n.all
    n.group = 2 * n.b
    n.part = hidden // n.group
    n.wide = hidden // seq
    return n


def place(n):
    w = types.SimpleNamespace()
    w.s, w.f = lax.axis_index("seq"), lax.axis_index("fsdp")
    w.c, w.j = w.s // 2, lax.rem(w.s, 2)
    w.a, w.b = w.c // n.b, lax.rem(w.c, n.b)
    w.me = w.s * n.fsdp + w.f
    w.head, w.idx = w.s // n.sub, lax.rem(w.s, n.sub)
    w.sib = (w.s + 1 - 2 * w.j, w.f)
    w.t = w.b * 2 + w.j
    return w


def plane(n, w, a, b, f):
    return ((a * n.b + b) * 2 + w.j, f)


def member(n, w, t):
    return ((w.a * n.b) * 2 + t, w.f)


def peer(n, w, i):
    d = lax.rem(w.me + i, n.all)
    return d, (d // n.fsdp, lax.rem(d, n.fsdp))


def meet_all(n, w):
    barrier = pltpu.get_barrier_semaphore()

    def greet(i):
        pl.semaphore_signal(barrier, inc=1, device_id=peer(n, w, i + 1)[1], device_id_type=MESH)

    loop(n.all - 1, greet)
    pl.semaphore_wait(barrier, n.all - 1)


class Line:
    def __init__(self, n, w, send_sem, per_unit):
        self.n, self.w, self.send_sem, self.per_unit, self.sent = n, w, send_sem, per_unit, []

    def inside(self, shift):
        a = self.w.a + shift
        return (a >= 0) & (a < self.n.a)

    def slot(self, shift, k):
        return 2 + (self.w.a + shift) * self.per_unit + k

    def send(self, ref, recv, dev, slot, *shifts):
        push(ref, ref, self.send_sem(slot()), recv, dev)
        self.sent.append((slot, shifts))

    def both(self, shifts):
        return functools.reduce(jnp.logical_and, [self.inside(v) for v in shifts])

    def start(self, own, neighbour):
        for sign in (-1, 1):
            @pl.when(self.inside(-sign))
            def _(sign=sign):
                self.send(*own(), neighbour(self.w.a - sign), lambda: (1 + sign) // 2, -sign)

    def step(self, far, take, neighbour, more):
        for sign in (-1, 1):
            @pl.when(self.inside(sign * far))
            def _(sign=sign):
                ref, recv = take(self.w.a + sign * far)
                if far < self.n.a - 1:
                    @pl.when(self.inside(-sign))
                    def _():
                        self.send(ref, recv, neighbour(self.w.a - sign), lambda: self.slot(sign * far, 0), sign * far, -sign)
                for k, dev in enumerate(more):
                    self.send(ref, recv, dev, lambda k=k: self.slot(sign * far, 1 + k), sign * far)

    def drain_sends(self, ref):
        for slot, shifts in self.sent:
            if shifts:
                @pl.when(self.both(shifts))
                def _(slot=slot):
                    wait(ref(), self.send_sem(slot()))
            else:
                wait(ref(), self.send_sem(slot()))


class Gather(Line):
    def __init__(self, n, w, unit, index, send_sem, recv_sem, over_b=False, arrived=None):
        super().__init__(n, w, send_sem, n.fsdp + (n.b - 1 if over_b else 0))
        self.unit, self.index, self.recv_sem = unit, index, recv_sem
        self.over_b, self.arrived = over_b, arrived

    def entry(self, a, b, f):
        return self.unit(a, b, f), self.recv_sem(self.index(a, b, f))

    def own(self):
        w = self.w
        return self.unit(w.a, w.b, w.f), self.index(w.a, w.b, w.f)

    def take(self, a, b, f):
        ref, recv = self.entry(a, b, f)
        wait(ref, recv)
        if self.arrived:
            self.arrived(ref, self.index(a, b, f))
        return ref, recv

    def neighbour(self, a):
        return plane(self.n, self.w, a, self.w.b, self.w.f)

    def others(self, over_f=True):
        n, w = self.n, self.w
        out = []
        if over_f:
            out += [plane(n, w, w.a, w.b, lax.rem(w.f + m, n.fsdp)) for m in range(1, n.fsdp)]
        if self.over_b:
            out += [plane(n, w, w.a, lax.rem(w.b + m, n.b), w.f) for m in range(1, n.b)]
        return out

    def to_a(self):
        self.start(lambda: self.entry(self.w.a, self.w.b, self.w.f), self.neighbour)

    def column(self, far):
        w = self.w
        if far == 0:
            for k, dev in enumerate(self.others()):
                self.send(*self.entry(w.a, w.b, w.f), dev, lambda k=k: self.slot(0, 1 + k))
        else:
            self.step(far, lambda a: self.take(a, w.b, w.f), self.neighbour, self.others())

    def corner_slot(self, shift, q, k):
        base = 2 + self.n.a * self.per_unit
        return base + ((self.w.a + shift) * (self.n.fsdp - 1) + q - 1) * (self.n.b - 1) + k

    def corner(self, far):
        if not self.over_b:
            return

        def pass_on(shift, *shifts):
            for q in range(1, self.n.fsdp):
                ref, recv = self.take(self.w.a + shift, self.w.b, lax.rem(self.w.f + q, self.n.fsdp))
                for k, dev in enumerate(self.others(False)):
                    self.send(ref, recv, dev, lambda q=q, k=k: self.corner_slot(shift, q, k), *shifts)

        if far == 0:
            pass_on(0)
        else:
            for sign in (-1, 1):
                @pl.when(self.inside(sign * far))
                def _(sign=sign):
                    pass_on(sign * far, sign * far)

    def finish(self):
        n, w = self.n, self.w
        for i in range(n.a):
            a = lax.rem(w.a + i, n.a)
            for q in range(n.fsdp):
                for v in range(n.b):
                    if (v if self.over_b else q) != 0 and (self.over_b or v == 0):
                        self.take(a, lax.rem(w.b + v, n.b), lax.rem(w.f + q, n.fsdp))

    def drain(self):
        self.drain_sends(lambda: self.unit(self.w.a, self.w.b, self.w.f))


def tables(n, w, small_all, tab):
    nb = 2 * n.seq
    before = low((iota((128, 128), 0) < iota((128, 128), 1)).astype(F32))
    for r in range(n.rounds):
        def bucket_row(p):
            tile = small_all[p * n.fsdp + w.f].astype(F32)
            keep = iota((16, 128), 0) == 8 + w.idx * n.rounds + r
            return jnp.sum(jnp.where(keep, tile, 0.0), axis=0, keepdims=True)

        def count(p, run):
            row = bucket_row(p)
            hot = (iotaf((nb, 128), 0) == row).astype(F32)
            ahead = dot(low(hot), before)
            pos = jnp.sum(hot * (ahead + run), axis=0, keepdims=True)
            group = jnp.floor(row * 0.5)
            hotg = (iotaf((n.seq, 128), 0) == group).astype(F32)
            rank = jnp.sum(hotg * dot(low(hotg), before), axis=0, keepdims=True)
            line = group * n.cap + rank
            at = iota((8, 128), 0)
            tab[r, p] = jnp.where(at == 0, line, jnp.where(at == 1, pos, jnp.where(at == 2, row, 0.0)))
            return run + jnp.sum(hot, axis=1, keepdims=True)

        totals = lax.fori_loop(0, n.seq, count, jnp.zeros((nb, 1), F32))

        def settle(p):
            tile = tab[r, p]
            row = tile[2:3]
            odd = row - 2.0 * jnp.floor(row * 0.5)
            hot = (iotaf((nb, 128), 0) == row - 1.0).astype(F32)
            slot = tile[1:2] + odd * jnp.sum(hot * totals, axis=0, keepdims=True)
            block = jnp.floor(slot * (1.0 / SPAN))
            tab[r, p] = jnp.where(iota((8, 128), 0) == 1, block, tile)

        loop(n.seq, settle)


def picks(n, tile):
    return low((iotaf((n.seq * n.cap, 128), 0) == tile[0:1]).astype(F32))


def picks_back(n, tile):
    return low((iotaf((128, n.seq * n.cap), 1) == to_column(tile[0:1])).astype(F32))


def block_marks(tile):
    return low((iotaf((128, 128), 1) == to_column(tile[1:2])).astype(F32))


FAR = 2.0 ** 30


def with_blocks(marks, query, key):
    i, k = iota((128, 128), 0), iota((128, 128), 1)
    seen = dot(marks, low((((k == i) | (k == i + 1)) & (i < 4)).astype(F32)))
    lane = iota(marks.shape, 1)
    ask = low(jnp.where(lane < 4, marks.astype(F32) * -FAR, 0.0))
    answer = low(jnp.where(lane < 4, 1.0 - seen, 0.0))
    return jnp.concatenate([query, ask], axis=1), jnp.concatenate([key, answer], axis=1)


def halves(wide_query, wide_key):
    size = wide_query.shape[0]
    cut = size // 2
    row, col = iota((cut, cut), 0), iota((cut, cut), 1)

    def ordered(raw):
        return jnp.where(col < row, raw, jnp.where(col == row, -1e4, -1e9))

    first = ordered(dot_nt(wide_query[:cut], wide_key[:cut]))
    rest = dot_nt(wide_query[cut:], wide_key)
    return first, jnp.concatenate([rest[:, :cut], ordered(rest[:, cut:])], axis=1)


def rows_of(n, ref):
    got = ref[...]
    if n.cap % 16:
        return low(got.astype(F32).reshape(n.seq * n.cap, got.shape[-1]))
    return got.reshape(n.seq * n.cap, got.shape[-1])


def put_rows(n, ref, value):
    ref[...] = value.reshape(n.seq, n.cap, value.shape[-1]).astype(ref.dtype)


def keys_of(query):
    wide = query.astype(F32)
    scale = lax.rsqrt(jnp.sum(wide * wide, axis=1, keepdims=True) + 1e-06)
    return low(wide * scale), scale


def fill_block(n, r, p, tab, qv, buf, marks):
    tile = tab[r, p]
    hot = picks(n, tile)
    got = dot(hot, jnp.concatenate([qv[p], block_marks(tile)], axis=1))
    put_rows(n, buf.at[r, :, p], got[:, :256])
    put_rows(n, marks.at[r, :, p], got[:, 256:])


def attend(n, r, g, buf, marks, obuf):
    both = rows_of(n, buf.at[r, g])
    query, value = both[:, :128], both[:, 128:]
    key, _ = keys_of(query)
    cut = query.shape[0] // 2
    outs = []
    for score, values in zip(halves(*with_blocks(rows_of(n, marks.at[r, g]), query, key)), (value[:cut], value)):
        top = jnp.max(score, axis=1, keepdims=True)
        expo = jnp.exp(score - top)
        total = jnp.sum(expo, axis=1, keepdims=True)
        out = dot(low(expo), values) / total
        hi, mid, rest = split3(top + jnp.log(total))
        lane = iota((cut, 128), 1)
        logs = jnp.where(lane == 0, hi, jnp.where(lane == 1, mid, jnp.where(lane == 2, rest, 0.0)))
        outs.append(jnp.concatenate([out, logs], axis=1))
    put_rows(n, obuf.at[r, :, g], jnp.concatenate(outs, axis=0))


def merge(outs, logs):
    top = functools.reduce(jnp.maximum, logs)
    weights = [jnp.exp(v - top) for v in logs]
    total = sum(weights)
    return sum(x * y for x, y in zip(weights, outs)) / total, top + jnp.log(total)


def merge_rounds(n, p, tab, obuf):
    outs, logs = [], []
    for r in range(n.rounds):
        got = dot(picks_back(n, tab[r, p]), rows_of(n, obuf.at[r, p]))
        outs.append(got[:, :128])
        logs.append(jnp.sum(got[:, 128:], axis=1, keepdims=True))
    return merge(outs, logs)


def write_message(ref, out, log):
    ref[:128] = low(out)
    ref[128:] = message_rows(split3(to_row(log)))


def read_log(ref):
    return to_column(jnp.sum(ref[128:].astype(F32), axis=0, keepdims=True))


def hat_of(x):
    center = x - jnp.mean(x, axis=1, keepdims=True)
    scale = lax.rsqrt(jnp.mean(center * center, axis=1, keepdims=True) + 1e-05)
    return center * scale, scale


def normalize(x, gain, shift):
    hat, scale = hat_of(x)
    return hat, scale, hat * gain + shift


def placed(row, spot):
    size = row.shape[1]
    put = (iota((size, 128), 1) == iota((size, 128), 0) + spot * size).astype(F32)
    return dot(row, low(put))


def gelu_pair(x):
    k = 0.7978845608028654
    square = x * x
    t = jnp.tanh(k * (x + 0.044715 * (square * x)))
    half = 0.5 * (1.0 + t)
    return x * half, half + 0.5 * x * (1.0 - t * t) * (k * (1.0 + 0.134145 * square))


class GroupSum:
    def __init__(self, n, w, out, got1, got2, send, recv):
        self.n, self.w, self.out, self.got1, self.got2 = n, w, out, got1, got2
        self.send, self.recv = send, recv

    def fill(self, product):
        n, w = self.n, self.w
        for m in range(n.b):
            b = lax.rem(w.b + 1 + m, n.b)
            self.out[pl.ds(2 * b, 2)] = low(product(b)).reshape(2, n.tokens, n.width)
            t = b * 2 + 1 - w.j
            push(self.out.at[t], self.got1.at[b], self.send.at[m], self.recv.at[b], w.sib)

    def chips(self):
        n, w = self.n, self.w
        for m in range(1, n.b):
            b = lax.rem(w.b + m, n.b)
            t = b * 2 + w.j
            wait(self.got1.at[b], self.recv.at[b])
            self.out[t] = low(self.out[t].astype(F32) + self.got1[b].astype(F32))
            k = n.b + m - 1
            push(self.out.at[t], self.got2.at[m - 1], self.send.at[k], self.recv.at[k], member(n, w, t))

    def total(self):
        n, w = self.n, self.w
        wait(self.got1.at[w.b], self.recv.at[w.b])
        total = self.out[w.t].astype(F32) + self.got1[w.b].astype(F32)
        for m in range(1, n.b):
            wait(self.got2.at[m - 1], self.recv.at[n.b + m - 1])
            total += self.got2[m - 1].astype(F32)
        return total

    def drain(self):
        for k in range(2 * self.n.b - 1):
            wait(self.got1.at[0], self.send.at[k])


class Scatter:
    def __init__(self, n, w, outer, part, got1, got2, got3, send, recv):
        self.n, self.w, self.outer, self.part = n, w, outer, part
        self.got1, self.got2, self.got3 = got1, got2, got3
        self.send, self.recv = send, recv
        self.one, self.two = (n.fsdp, n.b) if outer == "f" else (n.b, n.fsdp)
        self.me1, self.me2 = (w.f, w.b) if outer == "f" else (w.b, w.f)
        self.base2 = (self.one - 1) * n.a * self.two
        self.base3 = self.base2 + (self.two - 1) * n.a

    def mine(self, a, one, two):
        return self.part(a, two, one) if self.outer == "f" else self.part(a, one, two)

    def dev(self, a, one, two):
        if self.outer == "f":
            return plane(self.n, self.w, a, two, one)
        return plane(self.n, self.w, a, one, two)

    def first(self):
        for m in range(1, self.one):
            far = lax.rem(self.me1 + m, self.one)

            def body(i, m=m, far=far):
                a, two = i // self.two, lax.rem(i, self.two)
                k = (m - 1) * self.n.a * self.two + i
                push(self.mine(a, far, two), self.got1.at[m - 1, a, two], self.send.at[k], self.recv.at[k],
                     self.dev(self.w.a, far, self.me2))

            loop(self.n.a * self.two, body)

    def second(self):
        def body(i):
            m2, a = i // self.n.a, lax.rem(i, self.n.a)
            two = lax.rem(self.me2 + 1 + m2, self.two)
            for m in range(1, self.one):
                k = (m - 1) * self.n.a * self.two + a * self.two + two
                wait(self.got1.at[m - 1, a, two], self.recv.at[k])
            self.fold1(a, two)

            @pl.when(m2 < self.two - 1)
            def _():
                k = self.base2 + m2 * self.n.a + a
                push(self.got1.at[0, a, two], self.got2.at[m2, a], self.send.at[k], self.recv.at[k],
                     self.dev(self.w.a, self.me1, two))

        loop(self.n.a * self.two, body)

    def fold1(self, a, two):
        total = self.mine(a, self.me1, two)[...].astype(F32)
        for m in range(1, self.one):
            total += self.got1[m - 1, a, two].astype(F32)
        self.got1[0, a, two] = low(total)

    def third(self):
        def body(i):
            a = lax.rem(self.w.a + 1 + i, self.n.a)
            for m2 in range(self.two - 1):
                wait(self.got2.at[m2, a], self.recv.at[self.base2 + m2 * self.n.a + a])
            total = self.got1[0, a, self.me2].astype(F32)
            for m2 in range(self.two - 1):
                total += self.got2[m2, a].astype(F32)
            self.got2[0, a] = low(total)

            @pl.when(i < self.n.a - 1)
            def _():
                k = self.base3 + i
                push(self.got2.at[0, a], self.got3.at[i], self.send.at[k], self.recv.at[k],
                     self.dev(a, self.me1, self.me2))

        loop(self.n.a, body)

    def total(self):
        total = self.got2[0, self.w.a].astype(F32)
        for i in range(self.n.a - 1):
            wait(self.got3.at[i], self.recv.at[self.base3 + i])
            total += self.got3[i].astype(F32)
        return total

    def drain(self):
        loop(self.base3 + self.n.a - 1, lambda k: wait(self.got3.at[0], self.send.at[k]))


class PlaneScatter:
    def __init__(self, n, w, part, got1, got2, send, recv):
        self.n, self.w, self.part, self.got1, self.got2, self.send, self.recv = n, w, part, got1, got2, send, recv
        self.base = (n.fsdp - 1) * n.a

    def first(self):
        n, w = self.n, self.w
        for m in range(1, n.fsdp):
            far = lax.rem(w.f + m, n.fsdp)

            def body(i, m=m, far=far):
                a = lax.rem(w.a + 1 + i, n.a)
                k = (m - 1) * n.a + a
                push(self.part(a, far), self.got1.at[m - 1, a], self.send.at[k], self.recv.at[k], plane(n, w, w.a, w.b, far))

            loop(n.a, body)

    def second(self, i):
        n, w = self.n, self.w
        a = lax.rem(w.a + 1 + i, n.a)
        total = self.part(a, w.f)[...].astype(F32)
        for m in range(1, n.fsdp):
            wait(self.got1.at[m - 1, a], self.recv.at[(m - 1) * n.a + a])
            total += self.got1[m - 1, a].astype(F32)
        self.got1[0, a] = low(total)
        if i < n.a - 1:
            k = self.base + i
            push(self.got1.at[0, a], self.got2.at[i], self.send.at[k], self.recv.at[k], plane(n, w, a, w.b, w.f))

    def total(self):
        total = self.got1[0, self.w.a].astype(F32)
        for i in range(self.n.a - 1):
            wait(self.got2.at[i], self.recv.at[self.base + i])
            total += self.got2[i].astype(F32)
        return total

    def drain(self):
        loop(self.base + self.n.a - 1, lambda k: wait(self.got2.at[0], self.send.at[k]))


def spread(n, r, p, tab, dtok, dbuf, marks):
    tile = tab[r, p]
    shift = low((iota((MSG - 128, 128), 0) + 4 == iota((MSG - 128, 128), 1)).astype(F32))
    marked = block_marks(tile) + low(dot_tn(dtok[p, 128:], shift))
    got = dot(picks(n, tile), jnp.concatenate([dtok[p, :128], marked], axis=1))
    put_rows(n, dbuf.at[r, :, p], got[:, :128])
    put_rows(n, marks.at[r, :, p], got[:, 128:])


def attend_back(n, r, g, buf, marks, dbuf, gbuf):
    both, cot, marked = rows_of(n, buf.at[r, g]), rows_of(n, dbuf.at[r, g]), rows_of(n, marks.at[r, g])
    query, value = both[:, :128], both[:, 128:]
    aux = marked.astype(F32)
    lane = iota(aux.shape, 1)
    log_all = jnp.sum(jnp.where((lane >= 4) & (lane < 7), aux, 0.0), axis=1, keepdims=True)
    delta = jnp.sum(jnp.where(lane >= 7, aux, 0.0), axis=1, keepdims=True)
    key, scale = keys_of(query)
    cut = query.shape[0] // 2
    score0, score1 = halves(*with_blocks(marked, query, key))
    under = iota((cut, cut), 1) < iota((cut, cut), 0)
    prob0 = jnp.exp(score0 - log_all[:cut])
    prob1 = jnp.exp(score1 - log_all[cut:])
    back0 = low(jnp.where(under, prob0 * (dot_nt(cot[:cut], value[:cut]) - delta[:cut]), 0.0))
    back1 = prob1 * (dot_nt(cot[cut:], value) - delta[cut:])
    back1 = low(jnp.concatenate([back1[:, :cut], jnp.where(under, back1[:, cut:], 0.0)], axis=1))
    direct = jnp.concatenate([dot(back0, key[:cut]), dot(back1, key)], axis=0)

    def both_halves(first, rest, rows):
        total = dot_tn(rest, rows[cut:])
        return jnp.concatenate([total[:cut] + dot_tn(first, rows[:cut]), total[cut:]], axis=0)

    back_key = both_halves(back0, back1, query)
    back_value = both_halves(low(prob0), low(prob1), cot)
    wide = query.astype(F32)
    inner = jnp.sum(wide * back_key, axis=1, keepdims=True)
    total = direct + scale * back_key - wide * (scale * scale * scale * inner)
    put_rows(n, gbuf.at[r, :, g], jnp.concatenate([total, back_value], axis=1))


UNROLL = 2
RELAYS = (0, 0, 0, 0, 0, 1, 1, 1, 1)
SUMS = (1, 1, 2, 2, 1, 1, 1, 1)


def greet_all(n, w, barrier):
    def greet(i):
        pl.semaphore_signal(barrier, inc=1, device_id=peer(n, w, i + 1)[1], device_id_type=MESH)

    loop(n.all - 1, greet)


def pack(n, w, x):
    x.ci[w.t] = low(x.cot2[...])
    for t in range(n.group):
        for a in range(n.a):
            s = a * n.group + t
            x.we_in[t, :, a * n.wide:(a + 1) * n.wide] = x.expand_w[:, s * n.wide:(s + 1) * n.wide]
    lead = placed(x.vectors[...], lax.rem(w.me, 128 // n.rows))
    extra = placed(jnp.broadcast_to(x.bias[...], (8, n.units)), lax.rem(w.me, 128 // n.units))
    lead = jnp.where(iota((8, 128), 0) == 5, extra, lead)
    x.small_all[w.me] = low(jnp.concatenate([lead, x.buckets[...].astype(F32), jnp.zeros((8 - ROUNDS, 128), F32)]))
    for h in range(HEADS):
        x.wqv_in[w.f, h, :, :128] = x.query_w[:, h * 128:(h + 1) * 128]
        x.wqv_in[w.f, h, :, 128:] = x.value_w[:, h * 128:(h + 1) * 128]
    x.wo[w.me] = x.wo_in[...]
    for q, ref in enumerate((x.query_w, x.value_w)):
        pltpu.make_async_copy(ref, x.full.at[q, w.me], x.s_loc.at[q]).start()
    x.wc[w.a, w.f] = x.wc_in[...]
    x.we[w.a, w.t, w.f] = x.we_in[w.t]


def vectors_of(n, w, x):
    group = 128 // n.rows
    for q in range(n.width // 128):
        x.vec[:, q * 128:(q + 1) * 128] = jnp.sum(
            x.small_all[q * group:(q + 1) * group].astype(F32), axis=0
        )
    per = 128 // n.units
    for q in range(n.a * n.fsdp // per):
        a, rest = q * per // n.fsdp, q * per % n.fsdp
        first = (a * n.group + w.t) * n.fsdp + rest
        total = sum(x.small_all[first + k].astype(F32) for k in range(per))
        x.shift_part[:, q * 128:(q + 1) * 128] = jnp.broadcast_to(total[5:6], (8, 128))


def front_part(n, w, x, obuf, pmsg, omsg):
    barrier = pltpu.get_barrier_semaphore()
    greet_all(n, w, barrier)
    hat, _ = hat_of(x.second[...])
    x.xh[w.s] = low(hat)
    pack(n, w, x)
    pl.semaphore_wait(barrier, n.all - 1)

    def spot(i, v):
        return (lax.rem(w.a + i, n.a) * n.b + lax.rem(w.b + v, n.b)) * 2 + w.j

    def hat_at(a):
        block = (a * n.b + w.b) * 2 + w.j
        return x.xh.at[block], x.r_n.at[block // 2]

    def hat_chip(a):
        return ((a * n.b + w.b) * 2 + w.j, w.f)

    hats = Line(n, w, lambda k: x.s_n.at[k], n.b)

    def share_hat(block):
        push(x.xh.at[block], x.xh.at[block], x.s_ns.at[block // 2], x.r_ns.at[block // 2], w.sib)

    far_b = [(spot(0, v), w.f) for v in range(1, n.b)]
    hats.start(lambda: hat_at(w.a), hat_chip)
    for k, dev in enumerate(far_b):
        hats.send(*hat_at(w.a), dev, lambda k=k: hats.slot(0, 1 + k))
    share_hat(w.s)
    for m in range(1, n.group):
        t = lax.rem(w.t + m, n.group)
        push(x.we_in.at[t], x.we.at[w.a, w.t, w.f], x.s_ex.at[m], x.r_ex.at[w.t], member(n, w, t))

    mine = pl.ds(w.s * n.fsdp, n.fsdp)
    for q in range(1, n.fsdp):
        far = (w.s, lax.rem(w.f + q, n.fsdp))
        push(x.small_all.at[w.me], x.small_all.at[w.me], x.s_f.at[0, q], x.r_f.at[0, w.f], far)
        push(x.wqv_in.at[w.f], x.wqv_in.at[w.f], x.s_f.at[1, q], x.r_f.at[1, w.f], far)
    for q in range(1, n.fsdp):
        f = lax.rem(w.f + q, n.fsdp)
        wait(x.small_all.at[w.me], x.r_f.at[0, f])

    def send_small(i):
        s = lax.rem(w.s + 1 + i, n.seq)
        push(x.small_all.at[mine], x.small_all.at[mine], x.s_small.at[i], x.r_small.at[w.s], (s, w.f))

    loop(n.seq - 1, send_small)
    for q in range(1, n.fsdp):
        f = lax.rem(w.f + q, n.fsdp)
        wait(x.wqv_in.at[f], x.r_f.at[1, f])

    def send_w(i):
        s = lax.rem(w.s + 1 + i, n.seq)
        push(x.wqv_in.at[:, s // n.sub], x.wqv.at[mine], x.s_wq.at[i], x.r_wq.at[w.s], (s, w.f))

    loop(n.seq - 1, send_w)
    x.wqv[mine] = x.wqv_in[:, w.head]

    def shared_o(ref, uid):
        push(ref, ref, x.s_os.at[uid], x.r_os.at[uid], w.sib)

    def all_index(a, b, f):
        return (a * n.b + b) * n.fsdp + f

    def part_index(a, b, f):
        return a * n.fsdp + f

    g_o = Gather(n, w, lambda a, b, f: x.wo.at[((a * n.b + b) * 2 + w.j) * n.fsdp + f], all_index, lambda i: x.s_go.at[i], lambda u: x.r_go.at[u], True, shared_o)
    g_c = Gather(n, w, lambda a, b, f: x.wc.at[a, f], part_index, lambda i: x.s_gc.at[i], lambda u: x.r_gc.at[u])
    g_e = Gather(n, w, lambda a, b, f: x.we.at[a, :, f], part_index, lambda i: x.s_ge.at[i], lambda u: x.r_ge.at[u])
    gathers = (g_o, g_c, g_e)
    for m in range(1, n.group):
        t = lax.rem(w.t + m, n.group)
        wait(x.we.at[w.a, t, w.f], x.r_ex.at[t])
    shared_o(x.wo.at[w.me], (w.a * n.b + w.b) * n.fsdp + w.f)
    for y in gathers:
        y.column(0)

    def pass_hats(far):
        def take_hat(a):
            ref, recv = hat_at(a)
            wait(ref, recv)
            return ref, recv

        hats.step(far, take_hat, hat_chip, far_b)
        for sign in (-1, 1):
            @pl.when(hats.inside(sign * far))
            def _(sign=sign):
                share_hat(((w.a + sign * far) * n.b + w.b) * 2 + w.j)

    def early():
        def wait_small(i):
            s = lax.rem(w.s + 1 + i, n.seq)
            wait(x.small_all.at[mine], x.r_small.at[s])

        loop(n.seq - 1, wait_small)
        vectors_of(n, w, x)

    pass_hats(1)
    early()
    for far in range(2, n.a - 1):
        pass_hats(far)
    tables(n, w, x.small_all, x.tab)
    if n.a > 2:
        pass_hats(n.a - 1)
    weights = x.wqv.reshape(n.width, 256)

    def project(block):
        normed = low(x.xh[block].astype(F32) * x.vec[0:1] + x.vec[1:2])

        @pl.when(lax.rem(block, n.sub) == w.idx)
        def _():
            x.nown[block // n.sub] = normed

        x.qv[block] = low(dot(normed, weights[...]))

    for y in gathers:
        y.to_a()

    def wait_w(i):
        s = lax.rem(w.s + 1 + i, n.seq)
        wait(x.wqv.at[mine], x.r_wq.at[s])

    loop(n.seq - 1, wait_w)
    project(w.s)
    for i in range(1, n.a):
        project(spot(i, 0))
    for i in range(n.a):
        for v in range(1, n.b):
            block = spot(i, v)
            wait(x.xh.at[block], x.r_n.at[block // 2])
            share_hat(block)
            project(block)

    def from_sibling(c):
        block = 2 * c + 1 - w.j
        wait(x.xh.at[block], x.r_ns.at[c])
        project(block)

    loop(n.chips, from_sibling)

    for m in range(1, n.group):
        t = lax.rem(w.t + m, n.group)
        push(x.ci.at[w.t], x.ci.at[w.t], x.s_ci.at[m], x.r_ci.at[w.t], member(n, w, t))

    tasks = []
    for i in range(n.a):
        if i:
            tasks.append(lambda i=i: [y.column(i) for y in gathers])
        tasks.append(lambda i=i: g_o.corner(i))

    def relay(count):
        for _ in range(count):
            if tasks:
                tasks.pop(0)()

    for r in range(n.rounds):
        loop_by(UNROLL, n.seq, lambda p: fill_block(n, r, p, x.tab, x.qv, x.buf, x.marks))
    relay(RELAYS[0])
    parts = 4
    slot = 1
    for r in range(n.rounds):
        for q in range(parts):
            loop_by(UNROLL, n.seq // parts, lambda g: attend(n, r, q * (n.seq // parts) + g, x.buf, x.marks, obuf))
            relay(RELAYS[slot])
            slot += 1

    blocks = n.seq // n.sub
    for m in range(1, n.sub):
        far = lax.rem(w.idx + m, n.sub)

        def offer(i, m=m, far=far):
            k = (m - 1) * blocks + i
            write_message(pmsg.at[k], *merge_rounds(n, i * n.sub + far, x.tab, obuf))
            push(pmsg.at[k], x.pin.at[k], x.s_p.at[k], x.r_p.at[k], (w.head * n.sub + far, w.f))

        loop_by(UNROLL, blocks, offer)

    def settle(i):
        out, log = merge_rounds(n, i * n.sub + w.idx, x.tab, obuf)
        outs, logs = [out], [log]
        for m in range(1, n.sub):
            k = (m - 1) * blocks + i
            wait(x.pin.at[k], x.r_p.at[k])
            outs.append(x.pin[k, :128].astype(F32))
            logs.append(read_log(x.pin.at[k]))
        write_message(omsg.at[i], *merge(outs, logs))

    def give(i):
        to = lax.rem(w.head + 1 + i, blocks)
        settle(to)
        push(omsg.at[to], x.home.at[w.head], x.s_out.at[i], x.r_out.at[w.head], (to * n.sub + w.idx, w.f))

    loop(blocks - 1, give)
    settle(w.head)
    x.home[w.head] = omsg[w.head]
    relay(len(tasks))

    def take(i):
        h = lax.rem(w.head + 1 + i, HEADS)
        wait(x.home.at[h], x.r_out.at[h])

    loop(HEADS - 1, take)
    g_o.finish()
    loop(n.chips * n.fsdp, lambda u: wait(x.wo.at[w.me], x.r_os.at[u]))

    loop((n.sub - 1) * blocks, lambda k: wait(pmsg.at[0], x.s_p.at[k]))
    loop(blocks - 1, lambda k: wait(omsg.at[0], x.s_out.at[k]))

    def drain():
        g_c.finish()
        g_e.finish()
        for y in gathers:
            y.drain()
        loop(n.chips * n.fsdp, lambda u: wait(x.wo.at[w.me], x.s_os.at[u]))
        for m in range(1, n.group):
            t = lax.rem(w.t + m, n.group)
            wait(x.we_in.at[0], x.s_ex.at[m])
            wait(x.ci.at[t], x.r_ci.at[t])
            wait(x.ci.at[t], x.s_ci.at[m])

        def wait_sends(i):
            wait(x.small_all.at[pl.ds(0, n.fsdp)], x.s_small.at[i])
            wait(x.wqv.at[pl.ds(0, n.fsdp)], x.s_wq.at[i])

        loop(n.seq - 1, wait_sends)
        for q in range(1, n.fsdp):
            wait(x.small_all.at[0], x.s_f.at[0, q])
            wait(x.wqv_in.at[0], x.s_f.at[1, q])
        hats.drain_sends(lambda: x.xh.at[w.s])
        loop(n.chips, lambda c: wait(x.xh.at[w.s], x.s_ns.at[c]))

    return drain


def feed_part(n, w, x, sums, whole, drain, mixed_low, act, gp, out, out2):
    sum_c, sum_e, _ = sums
    for h in range(HEADS):
        mixed_low[:, h * 128:(h + 1) * 128] = x.home[h, :128]
    first_out = x.first[...] + dot(mixed_low[...], x.wo.reshape(n.width, n.width)[...])
    x.first_o[...] = first_out
    hat, scale, normed = normalize(first_out, x.vec[2:3], x.vec[3:4])
    x.n2[w.t] = low(normed)
    k = 0
    for m in range(1, n.b):
        t = lax.rem(w.b + m, n.b) * 2 + w.j
        push(x.n2.at[w.t], x.n2.at[w.t], x.s_x.at[k], x.r_x.at[w.t], member(n, w, t))
        k += 1
    push(x.n2.at[w.t], x.n2.at[w.t], x.s_x.at[k], x.r_x.at[w.t], w.sib)
    k += 1
    for q, ref in enumerate((x.query_w, x.value_w)):
        pltpu.make_async_copy(ref, x.full.at[q, w.me], x.s_loc.at[q]).wait()
    whole.arrived(*whole.own())
    whole.to_a()
    whole.column(0)
    drain()
    for m in range(1, n.b):
        t = lax.rem(w.b + m, n.b) * 2 + w.j
        wait(x.n2.at[t], x.r_x.at[t])
        push(x.n2.at[t], x.n2.at[t], x.s_x.at[k], x.r_x.at[t], w.sib)
        k += 1
    for b in range(n.b):
        t = b * 2 + 1 - w.j
        wait(x.n2.at[t], x.r_x.at[t])
    size = n.group * n.tokens
    step = min(512, n.part)
    tokens = x.n2.reshape(size, n.width)
    cots = x.ci.reshape(size, n.width)
    we = x.we.reshape(n.width, n.part)
    wc = x.wc.reshape(n.part, n.width)
    for q in range(n.part // step):
        at = slice(q * step, (q + 1) * step)
        pre = dot(tokens[...], we[:, at]) + x.shift_part[0:1, at]
        value, slope = gelu_pair(pre)
        act[:, at] = low(value)
        back = low(dot_nt(cots[...], wc[at]) * slope)
        gp[:, at] = back
        x.shift_g[:, at] = jnp.broadcast_to(jnp.sum(back.astype(F32), axis=0, keepdims=True), (8, step))
    gn = GroupSum(n, w, out, x.gn_got1, x.gn_got2, x.s_gn, x.r_gn)
    so = GroupSum(n, w, out2, x.so_got1, x.so_got2, x.s_so, x.r_so)
    pair = 2 * n.tokens
    gn.fill(lambda b: dot_nt(gp[pl.ds(pl.multiple_of(b * pair, pair), pair)], we[...]))
    x.gwc.reshape(n.part, n.width)[...] = low(dot_tn(act[...], cots[...]))
    sum_c.first()
    gn.chips()
    so.fill(lambda b: dot(act[pl.ds(pl.multiple_of(b * pair, pair), pair)], wc[...]))
    x.gwe.reshape(n.width, n.part)[...] = low(dot_tn(tokens[...], gp[...]))
    so.chips()
    sum_e.first()
    grad = gn.total()
    rest = grad * x.vec[2:3]
    mean = jnp.mean(rest, axis=1, keepdims=True)
    tilt = jnp.mean(rest * hat, axis=1, keepdims=True)
    grad1 = x.cot1[...] + scale * (rest - mean - hat * tilt)
    x.grad1_o[...] = grad1
    branch = low(grad1)
    wo = x.wo.reshape(n.width, n.width)
    for h in range(HEADS):
        gm = dot_nt(branch, wo[h * 128:(h + 1) * 128])
        x.message[h, :128] = low(gm)
        delta = jnp.sum(gm * x.home[h, :128].astype(F32), axis=1, keepdims=True)
        logs = x.home[h, 128:].astype(F32)
        x.message[h, 128:] = message_rows((logs[0:1], logs[1:2], logs[2:3]) + split3(to_row(delta)))

    def give(i):
        s = lax.rem(w.s + 1 + i, n.seq)
        push(x.message.at[s // n.sub], x.dtok.at[w.s], x.s_d.at[i], x.r_d.at[w.s], (s, w.f))

    loop(n.seq - 1, give)
    x.dtok[w.s] = x.message[w.head]
    whole.column(1)
    whole.corner(0)
    gwo = low(dot_tn(mixed_low[...], branch)).reshape(n.chips, 2, n.fsdp * n.rows, n.width)
    x.gwo[...] = gwo.reshape(n.chips, 2, n.fsdp, n.rows, n.width)
    push(x.gwo.at[:, 1 - w.j], x.o0, x.s_o0.at[0], x.r_o0.at[0], w.sib)
    zero = jnp.zeros((2, n.width), F32)
    x.vec_g[...] = jnp.concatenate([
        zero,
        jnp.sum(grad * hat, axis=0, keepdims=True),
        jnp.sum(grad, axis=0, keepdims=True),
        jnp.sum(x.ci[w.t].astype(F32), axis=0, keepdims=True),
        zero, zero[:1],
    ])
    x.second_o[...] = x.second[...] + so.total() + x.vec[4:5]
    for i in range(k):
        wait(x.n2.at[0], x.s_x.at[i])
    gn.drain()
    so.drain()


def back_attention(n, w, x, sums, whole, dbuf, gbuf, gout):
    sum_c, sum_e, sum_o = sums
    blocks = n.seq // n.sub
    wait(x.o0, x.r_o0.at[0])

    def join_o(c):
        x.o0[c] = low(x.o0[c].astype(F32) + x.gwo[c, w.j].astype(F32))

    loop(n.chips, join_o)
    sum_o.first()

    def take(i):
        p = lax.rem(w.s + 1 + i, n.seq)
        wait(x.dtok.at[p], x.r_d.at[p])

    loop(n.seq - 1, take)
    tasks = []
    for i in range(n.a):
        tasks.append(lambda i=i: (sum_c.second(i), sum_e.second(i)))
        if 0 < i < n.a - 1:
            tasks.append(lambda i=i: whole.column(i + 1))
        if i:
            tasks.append(lambda i=i: whole.corner(i))
        if i == 1:
            tasks.append(sum_o.second)
    tasks.append(sum_o.third)

    def relay(count):
        for _ in range(count):
            if tasks:
                tasks.pop(0)()

    slot = 0
    parts = 4
    for r in range(n.rounds):
        loop_by(UNROLL, n.seq, lambda p: spread(n, r, p, x.tab, x.dtok, dbuf, x.marks))
        for q in range(parts):
            loop_by(UNROLL, n.seq // parts, lambda g: attend_back(n, r, q * (n.seq // parts) + g, x.buf, x.marks, dbuf, gbuf))
            relay(SUMS[slot])
            slot += 1
    relay(len(tasks))

    def tokens_of(p):
        total = None
        for r in range(n.rounds):
            got = dot(picks_back(n, x.tab[r, p]), rows_of(n, gbuf.at[r, p]))
            total = got if total is None else total + got
        return total

    for m in range(1, n.sub):
        far = lax.rem(w.idx + m, n.sub)

        def offer(i, m=m, far=far):
            k = (m - 1) * blocks + i
            gout[k] = low(tokens_of(i * n.sub + far))
            push(gout.at[k], x.gin.at[k], x.s_g.at[k], x.r_g.at[k], (w.head * n.sub + far, w.f))

        loop_by(UNROLL, blocks, offer)

    def keep(i):
        x.gown[i] = tokens_of(i * n.sub + w.idx)

    loop_by(UNROLL, blocks, keep)
    loop((n.sub - 1) * blocks, lambda k: wait(gout.at[0], x.s_g.at[k]))


def back_rest(n, w, x, sums, whole, dqv, wsum, wout, esw, vsend, full):
    sum_c, sum_e, sum_o = sums
    blocks = n.seq // n.sub
    whole.finish()
    loop(n.chips * n.fsdp, lambda u: wait(whole.own()[0], x.r_ps.at[u]))
    load = pltpu.make_async_copy(x.full, full, x.s_loc.at[0])
    load.start()

    def finish_block(i):
        total = x.gown[i]
        for m in range(1, n.sub):
            k = (m - 1) * blocks + i
            wait(x.gin.at[k], x.r_g.at[k])
            total += x.gin[k].astype(F32)
        dqv[i] = low(total)

    def arrived(h):
        return x.xh.at[h, :, pl.ds(0, 256)]

    def send_home(k):
        i = lax.rem(w.head + 1 + k, blocks)
        finish_block(i)
        push(dqv.at[i], arrived(w.head), x.s_h.at[k], x.r_h.at[w.head], (i * n.sub + w.idx, w.f))

    loop(blocks - 1, send_home)
    finish_block(w.head)
    x.xh[w.head, :, :256] = dqv[w.head]

    for i in range(blocks):
        got = dot_tn(x.nown[i], dqv[i])
        wsum[...] = got if i == 0 else wsum[...] + got
    wout[...] = low(wsum[...]).reshape(n.all, n.rows, 256)

    def rows_out(i):
        d, dev = peer(n, w, i + 1)
        push(wout.at[d], x.win.at[w.me], x.s_w2.at[i], x.r_w2.at[w.me], dev)

    loop(n.all - 1, rows_out)
    x.win[w.me] = wout[w.me]

    esw[...] = sum_e.total()
    x.egot[w.t] = esw[w.t]
    for m in range(1, n.group):
        t = lax.rem(w.t + m, n.group)
        push(esw.at[t], x.egot.at[w.t], x.s_y.at[m], x.r_y.at[w.t], member(n, w, t))

    hat, scale = hat_of(x.second[...])

    def take_home(k):
        h = lax.rem(w.head + 1 + k, HEADS)
        wait(arrived(h), x.r_h.at[h])

    loop(HEADS - 1, take_home)
    for h in range(HEADS):
        for q in range(2):
            x.xh[HEADS + q, :, h * 128:(h + 1) * 128] = x.xh[h, :, q * 128:(q + 1) * 128]
    load.wait()
    grad = sum(dot_nt(x.xh[HEADS + q], full[q].reshape(n.width, n.width)) for q in range(2))
    rest = grad * x.vec[0:1]
    mean = jnp.mean(rest, axis=1, keepdims=True)
    tilt = jnp.mean(rest * hat, axis=1, keepdims=True)
    x.grad2_o[...] = x.cot2[...] + scale * (rest - mean - hat * tilt)
    gain_g = jnp.sum(grad * hat, axis=0, keepdims=True)
    shift1_g = jnp.sum(grad, axis=0, keepdims=True)
    group = 128 // n.rows
    per = 128 // n.units
    at = iota((8, 128), 0)

    def rolled(tile, lanes):
        return pltpu.roll(tile, 128 - lanes, 1) if lanes else tile

    for q in range(n.width // 128):
        cut = slice(q * 128, (q + 1) * 128)
        tile = jnp.where(at == 0, gain_g[:, cut], jnp.where(at == 1, shift1_g[:, cut], x.vec_g[:, cut]))
        for k in range(group):
            vsend[q * group + k] = rolled(tile, k * n.rows)
    for q in range(n.a * n.fsdp // per):
        for k in range(per):
            u = q * per + k
            d = (u // n.fsdp * n.group + w.t) * n.fsdp + u % n.fsdp
            tile = rolled(x.shift_g[:, q * 128:(q + 1) * 128], k * n.units)
            vsend[d] = jnp.where(at == 5, tile, vsend[d])

    def vec_out(i):
        d, dev = peer(n, w, i + 1)
        push(vsend.at[d], x.vgot.at[w.me], x.s_v.at[i], x.r_v.at[w.me], dev)

    loop(n.all - 1, vec_out)
    x.vgot[w.me] = vsend[w.me]
    x.go_o[...] = sum_o.total()
    x.gc_o[...] = sum_c.total()

    def take_rows(i):
        d, _ = peer(n, w, i + 1)
        wait(x.win.at[d], x.r_w2.at[d])

    loop(n.all - 1, take_rows)
    for h in range(HEADS):
        total = 0.0
        for i in range(n.sub * n.fsdp):
            total += x.win[h * n.sub * n.fsdp + i].astype(F32)
        x.gq_o[:, h * 128:(h + 1) * 128] = total[:, :128]
        x.gv_o[:, h * 128:(h + 1) * 128] = total[:, 128:]
    for m in range(1, n.group):
        t = lax.rem(w.t + m, n.group)
        wait(x.egot.at[t], x.r_y.at[t])
    for t in range(n.group):
        for a in range(n.a):
            c = (a * n.group + t) * n.wide
            x.ge_o[:, c:c + n.wide] = x.egot[t, :, a * n.wide:(a + 1) * n.wide]

    wait(x.o0, x.s_o0.at[0])
    for m in range(1, n.group):
        wait(x.egot.at[0], x.s_y.at[m])
    loop(n.seq - 1, lambda i: wait(x.dtok.at[0], x.s_d.at[i]))
    for y in (sum_c, sum_e, sum_o):
        y.drain()
    loop(blocks - 1, lambda k: wait(dqv.at[0], x.s_h.at[k]))
    whole.drain()
    loop(n.chips * n.fsdp, lambda u: wait(whole.own()[0], x.s_ps.at[u]))

    def wait_all(i):
        wait(x.win.at[0], x.s_w2.at[i])
        wait(x.vgot.at[0], x.s_v.at[i])

    loop(n.all - 1, wait_all)

    def take_vec(i):
        d, _ = peer(n, w, i + 1)
        wait(x.vgot.at[d], x.r_v.at[d])

    loop(n.all - 1, take_vec)
    x.small_o[...] = jnp.sum(x.vgot[...], axis=0)


def layer_kernel(n, names, *refs):
    x = types.SimpleNamespace(**dict(zip(names, refs, strict=True)))
    w = place(n)
    t, d, g = n.tokens, n.width, n.group
    blocks = n.seq // n.sub
    pairs = (n.rounds, n.seq, n.seq, n.cap, 256)
    sums = (
        PlaneScatter(n, w, lambda a, f: x.gwc.at[a, f], x.c1, x.c2, x.s_c, x.r_c),
        PlaneScatter(n, w, lambda a, f: x.gwe.at[a, :, f], x.e1, x.e2, x.s_e, x.r_e),
        Scatter(n, w, "f", lambda a, b, f: x.o0.at[a * n.b + b, f], x.o1, x.o2, x.o3, x.s_o, x.r_o),
    )
    drains = []

    def shared(ref, uid):
        push(ref, ref, x.s_ps.at[uid], x.r_ps.at[uid], w.sib)

    whole = Gather(
        n, w, lambda a, b, f: x.full.at[:, ((a * n.b + b) * 2 + w.j) * n.fsdp + f], lambda a, b, f: (a * n.b + b) * n.fsdp + f,
        lambda i: x.s_gp.at[i], lambda u: x.r_gp.at[u], True, shared,
    )
    pl.run_scoped(
        lambda *r: drains.append(front_part(n, w, x, *r)),
        VM(pairs, BF), VM(((n.sub - 1) * blocks, MSG, 128), BF), VM((blocks, MSG, 128), BF),
    )
    pl.run_scoped(
        lambda *r: feed_part(n, w, x, sums, whole, drains[0], *r),
        VM((t, d), BF), VM((g * t, n.part), BF), VM((g * t, n.part), BF),
        VM((g, t, d), BF), VM((g, t, d), BF),
    )
    pl.run_scoped(
        lambda *r: back_attention(n, w, x, sums, whole, *r),
        VM(pairs[:-1] + (128,), BF), VM(pairs, BF), VM(((n.sub - 1) * blocks, 128, 256), BF),
    )
    pl.run_scoped(
        lambda *r: back_rest(n, w, x, sums, whole, *r),
        VM((blocks, 128, 256), BF), VM((d, 256), F32), VM((n.all, n.rows, 256), BF), VM((g, n.rows, n.part), F32),
        VM((n.all, 8, 128), F32), VM((2, n.all, n.rows, d), BF),
    )


def layer(n, inputs):
    inside = pl.BlockSpec(memory_space=VM)
    t, d, g, a = n.tokens, n.width, n.group, n.a
    units = n.chips * n.fsdp
    blocks = n.seq // n.sub
    f1, b1 = max(n.fsdp - 1, 1), max(n.b - 1, 1)
    pairs = (n.rounds, n.seq, n.seq, n.cap)
    unit_c, unit_e, unit_o = (n.units, d), (g, n.rows, n.part), (n.rows, d)
    count_f = (n.fsdp - 1) * a * n.b + (n.b - 1) * a + a - 1
    count_p = (n.fsdp - 1) * a + a - 1
    outputs = {
        "first_o": (t, d), "second_o": (t, d), "grad1_o": (t, d), "grad2_o": (t, d),
        "gq_o": (n.rows, d), "gv_o": (n.rows, d), "go_o": (n.rows, d), "ge_o": (n.rows, n.hidden), "gc_o": (n.units, d),
        "small_o": (8, 128),
    }
    scratch = {
        "xh": VM((n.seq, 128, d), BF),
        "nown": VM((blocks, 128, d), BF), "qv": VM((n.seq, 128, 256), BF),
        "wqv": VM((n.all, n.rows, 256), BF), "wqv_in": VM((n.fsdp, HEADS, n.rows, 256), BF), "we_in": VM((g, n.rows, n.part), BF),
        "small_all": VM((n.all, 16, 128), BF), "tab": VM((n.rounds, n.seq, 8, 128), F32), "vec": VM((16, d), F32),
        "shift_part": VM((8, n.part), F32), "ci": VM((g, t, d), BF),
        "buf": VM(pairs + (256,), BF), "marks": VM(pairs + (128,), BF),
        "pin": VM(((n.sub - 1) * blocks, MSG, 128), BF),
        "home": VM((HEADS, MSG, 128), BF), "dtok": VM((n.seq, MSG, 128), BF),
        "wo": VM((n.all, n.rows, d), BF), "wc": VM((a, n.fsdp, n.units, d), BF), "we": VM((a, g, n.fsdp, n.rows, n.part), BF),
        "n2": VM((g, t, d), BF),
        "gn_got1": VM((n.b, t, d), BF), "gn_got2": VM((b1, t, d), BF), "so_got1": VM((n.b, t, d), BF), "so_got2": VM((b1, t, d), BF),
        "gwc": VM((a, n.fsdp, n.units, d), BF), "gwe": VM((a, g, n.fsdp, n.rows, n.part), BF),
        "gwo": VM((n.chips, 2, n.fsdp, n.rows, d), BF), "message": VM((HEADS, MSG, 128), BF),
        "vec_g": VM((8, d), F32), "shift_g": VM((8, n.part), F32),
        "gown": VM((blocks, 128, 256), F32),
        "gin": VM(((n.sub - 1) * blocks, 128, 256), BF), "win": VM((n.all, n.rows, 256), BF),
        "c1": VM((f1, a) + unit_c, BF), "c2": VM((a - 1,) + unit_c, BF),
        "e1": VM((f1, a) + unit_e, BF), "e2": VM((a - 1,) + unit_e, BF),
        "o0": VM((n.chips, n.fsdp) + unit_o, BF), "o1": VM((f1, a, n.b) + unit_o, BF),
        "o2": VM((b1, a) + unit_o, BF), "o3": VM((a - 1,) + unit_o, BF),
        "egot": VM(unit_e, F32), "vgot": VM((n.all, 8, 128), F32),
    }
    sems = {
        "small": n.seq, "wq": n.seq, "f": (2, n.fsdp), "ns": n.chips, "os": units, "ex": g, "ci": g,
        "p": (n.sub - 1) * blocks, "out": HEADS, "x": 2 * n.b, "gn": 2 * n.b, "so": 2 * n.b, "d": n.seq, "o0": 1,
        "c": count_p, "e": count_p, "o": count_f, "g": (n.sub - 1) * blocks, "w2": n.all, "h": HEADS, "ps": units,
        "v": n.all, "y": g,
    }
    for key, count in sems.items():
        for side in ("s_", "r_"):
            if key == "x" and side == "r_":
                count = g
            scratch[side + key] = DMA(count if isinstance(count, tuple) else (count,))
    scratch["s_loc"] = DMA((2,))
    part, every = 2 + a * n.fsdp, 2 + a * (n.fsdp + n.b - 1) + a * (n.fsdp - 1) * (n.b - 1)
    for key, sends, gets in (("n", 2 + n.chips, n.chips), ("go", every, units), ("gp", every, units), ("gc", part, a * n.fsdp), ("ge", part, a * n.fsdp)):
        scratch["s_" + key], scratch["r_" + key] = DMA((sends,)), DMA((gets,))
    names = list(inputs) + list(outputs) + ["full"] + list(scratch)
    return pl.pallas_call(
        functools.partial(layer_kernel, n, names),
        out_shape=tuple(jax.ShapeDtypeStruct(s, F32) for s in outputs.values()) + (jax.ShapeDtypeStruct((2, n.all, n.rows, d), BF),),
        in_specs=[inside] * len(inputs),
        out_specs=(inside,) * len(outputs) + (pl.BlockSpec(memory_space=pl.ANY),),
        scratch_shapes=list(scratch.values()),
        compiler_params=pltpu.CompilerParams(collective_id=1, has_side_effects=True, vmem_limit_bytes=60 << 20),
        name="layer",
    )(*inputs.values())


def deliver_kernel(n, count, *refs):
    arrays, small, outs = refs[:count], refs[count], refs[count + 1:2 * count + 1]
    vectors, held, come, leave = refs[2 * count + 1:-count - 2], refs[-count - 2:-2], refs[-2], refs[-1]
    ins = [pltpu.make_async_copy(arrays[i], held[i], come.at[i]) for i in range(count)]
    ends = [pltpu.make_async_copy(held[i], outs[i], leave.at[i]) for i in range(count)]
    for cp in ins:
        cp.start()
    for row, ref in zip((0, 1, 2, 3, 5, 4), vectors, strict=True):
        ref[...] = small[row:row + 1, :ref.shape[1]]
    for before, after in zip(ins, ends, strict=True):
        before.wait()
        after.start()
    for cp in ends:
        cp.wait()


def deliver(n, arrays, small):
    anywhere = pl.BlockSpec(memory_space=pl.ANY)
    inside = pl.BlockSpec(memory_space=VM)
    shape = jax.ShapeDtypeStruct
    sizes = (n.rows, n.rows, n.rows, n.rows, n.units, n.rows)
    count = len(arrays)
    return pl.pallas_call(
        functools.partial(deliver_kernel, n, count),
        out_shape=tuple(shape(y.shape, F32) for y in arrays) + tuple(shape((1, k), F32) for k in sizes),
        in_specs=[anywhere] * count + [inside],
        out_specs=(anywhere,) * count + (inside,) * len(sizes),
        scratch_shapes=[VM(y.shape, F32) for y in arrays] + [DMA((count,)), DMA((count,))],
        compiler_params=pltpu.CompilerParams(vmem_limit_bytes=60 << 20),
        name="deliver",
    )(*arrays, small)


def on_device(
    first_half,
    second_half,
    first_cotangent,
    second_cotangent,
    bucket_ids,
    slot_source,
    live_slots,
    mixer_gain,
    mixer_shift,
    query_weight,
    value_weight,
    output_weight,
    feed_gain,
    feed_shift,
    expand_weight,
    expand_bias,
    contract_weight,
    contract_bias,
):
    seq, fsdp = lax.axis_size("seq"), lax.axis_size("fsdp")
    n = setup(seq, fsdp, first_half.shape[2], expand_weight.shape[1], first_half.shape[1])
    vectors = jnp.stack([mixer_gain, mixer_shift, feed_gain, feed_shift, contract_bias] + [jnp.zeros_like(mixer_gain)] * 3)
    *arrays, small, _ = layer(n, {
        "first": first_half[0], "second": second_half[0], "cot1": first_cotangent[0], "cot2": second_cotangent[0],
        "vectors": vectors, "bias": expand_bias.reshape(1, -1), "buckets": bucket_ids[0],
        "query_w": query_weight, "value_w": value_weight, "expand_w": expand_weight,
        "wo_in": output_weight, "wc_in": contract_weight,
    })
    outs = deliver(n, arrays, small)
    first_out, second_out, grad1, grad2, gq, gv, go, ge, gc = outs[:9]
    gain1, shift1, gain2, shift2, up_bias, down_bias = [y.reshape(-1) for y in outs[9:]]
    return (
        first_out[None], second_out[None], grad1[None], grad2[None],
        gain1, shift1, gq, gv, go, gain2, shift2, ge, up_bias, gc, down_bias,
    )


def solution(mesh):
    tokens, slots = P("fsdp", "seq", None), P("fsdp", None, "seq")
    vector, matrix = P(("seq", "fsdp")), P(("seq", "fsdp"), None)
    return jax.shard_map(
        on_device,
        mesh=mesh,
        in_specs=(tokens,) * 4 + (slots,) * 3 + (vector, vector, matrix, matrix, matrix, vector, vector, matrix, vector, matrix, vector),
        out_specs=(tokens,) * 4 + (vector, vector, matrix, matrix, matrix, vector, vector, matrix, vector, matrix, vector),
        check_vma=False,
    )
```
